32 devices in a mesh: ctx: 8 (over z, x), fsdp: 4 (over y, core).
Axes of the slice: x: 2, y: 2, z: 4, core: 2. Of those that a mesh axis runs over, the one named last changes fastest.
Arguments:
- hidden_in: bfloat16 [12, 512, 768], P('fsdp', 'ctx'), may hold values from -6 to 6
- segment_ids: int32 [12, 512], P('fsdp', 'ctx'), may hold values from 0 to 7, as said below
- doc_positions: int32 [12, 512], P('fsdp', 'ctx'), may hold values from 0 to 256, as said below
- w_query: bfloat16 [768, 768], P('fsdp'), may hold values from -0.21875 to 0.21875
- w_key: bfloat16 [768, 768], P('fsdp'), may hold values from -0.21875 to 0.21875
- w_value: bfloat16 [768, 768], P('fsdp'), may hold values from -0.21875 to 0.21875
- w_out: bfloat16 [768, 768], P('fsdp'), may hold values from -0.875 to 0.875
- b_query: bfloat16 [768], P('fsdp'), may hold values from -4 to 4
- b_value: bfloat16 [768], P('fsdp'), may hold values from -4 to 4
- b_out: bfloat16 [768], P('fsdp'), may hold values from -4 to 4
- ln1_gain: bfloat16 [768], P('fsdp'), may hold values from 0.5 to 1.5
- ln1_shift: bfloat16 [768], P('fsdp'), may hold values from -4 to 4
- w_inter: bfloat16 [768, 3072], P('fsdp'), may hold values from -0.21875 to 0.21875
- b_inter: bfloat16 [3072], P('fsdp'), may hold values from -4 to 4
- w_final: bfloat16 [3072, 768], P('fsdp'), may hold values from -0.109375 to 0.109375
- b_final: bfloat16 [768], P('fsdp'), may hold values from -4 to 4
- ln2_gain: bfloat16 [768], P('fsdp'), may hold values from 0.5 to 1.5
- ln2_shift: bfloat16 [768], P('fsdp'), may hold values from -4 to 4
- mask_logits: float32 [12, 512, 512], P(None, 'fsdp'), may hold values from -6 to 6
- mask_noise: float32 [12, 512, 512], P(None, 'fsdp'), may hold values from -6 to 6
- grad_out: bfloat16 [12, 512, 768], P('fsdp', 'ctx'), may hold values from -6 to 6
Outputs:
- hidden_out: bfloat16 [12, 512, 768], P('fsdp', 'ctx')
- grad_in: float32 [12, 512, 768], P('fsdp', 'ctx')
- w_query_grad: float32 [768, 768], P('fsdp')
- w_key_grad: float32 [768, 768], P('fsdp')
- w_value_grad: float32 [768, 768], P('fsdp')
- w_out_grad: float32 [768, 768], P('fsdp')
- b_query_grad: float32 [768], P('fsdp')
- b_value_grad: float32 [768], P('fsdp')
- b_out_grad: float32 [768], P('fsdp')
- ln1_gain_grad: float32 [768], P('fsdp')
- ln1_shift_grad: float32 [768], P('fsdp')
- w_inter_grad: float32 [768, 3072], P('fsdp')
- b_inter_grad: float32 [3072], P('fsdp')
- w_final_grad: float32 [3072, 768], P('fsdp')
- b_final_grad: float32 [768], P('fsdp')
- ln2_gain_grad: float32 [768], P('fsdp')
- ln2_shift_grad: float32 [768], P('fsdp')
- mask_logits_grad: float32 [12, 512, 512], P(None, 'fsdp')
The draws below stay inside these ranges and needn't reach their ends.
Inputs may be any that keep to these rules, and one draw needn't show every extreme that they name: `segment_ids`: segment numbers never fall along a sequence and every sequence holds exactly 8 documents; the first document of every sequence holds exactly 257 tokens. `doc_positions`: 0 at a document's first token, rising by one along the document; the first document of every sequence holds exactly 257 tokens.
All inputs are finite; a program needn't handle non-finite values.
Results may differ from the reference program's by a relative error of at most 0.023.
Values may be sent and summed in bfloat16 or wider, within the bound.
A program may use at most 256 MiB of HBM per device.

```python
from functools import partial
import jax
import jax.numpy as jnp
from jax import lax

D = 768
H = 12
HD = 64
FF = 3072
MSPAN = 512
DOCS = 8
LEN = 512
SEQS = 12


def cut_points(key):
    opening = LEN // 2 + 1
    candidates = LEN - opening - 1
    group_count = (candidates + 15) // 16
    key_rank, key_group = jax.random.split(jax.random.fold_in(key, 7))
    group_weights = jax.random.randint(key_group, (SEQS, group_count), 1, 17)
    widened = jnp.repeat(group_weights, 16, axis=1)[:, :candidates]
    random_ranks = jax.random.randint(key_rank, (SEQS, candidates), 0, 4096)
    offsets = jnp.arange(candidates, dtype=jnp.int32)
    scores = random_ranks * widened * LEN + offsets[None, :]
    _, picked = lax.top_k(-scores, DOCS - 2)
    later = picked.astype(jnp.int32) + opening + 1
    first_cut = jnp.full((SEQS, 1), opening, jnp.int32)
    return jnp.concatenate([first_cut, later], axis=1).astype(jnp.int32)


def draw_segment_ids(key, part):
    cut_list = cut_points(key)
    places = jnp.arange(LEN, dtype=jnp.int32)
    passed = cut_list[:, None, :] <= places[None, :, None]
    return jnp.sum(passed.astype(jnp.int32), axis=-1).astype(jnp.int32)


def draw_doc_positions(key, part):
    cut_list = cut_points(key)
    places = jnp.arange(LEN, dtype=jnp.int32)
    passed = cut_list[:, None, :] <= places[None, :, None]
    starts = jnp.max(jnp.where(passed, cut_list[:, None, :], 0), axis=-1)
    return (places[None, :] - starts).astype(jnp.int32)


def level_of(rng, dims, cuts, least, top_value):
    gain, own = 1.0, jax.random.fold_in(rng, 6)
    for position, blocks in cuts:
        steps = jnp.exp(jax.random.uniform(jax.random.fold_in(own, position), (blocks,), jnp.float32, least / len(cuts), top_value / len(cuts)))
        gain = gain * jnp.repeat(steps, dims[position] // blocks).reshape([-1 if axis == position else 1 for axis in range(len(dims))])
    return gain


def noise(own_key, dims, scale, limit, shards=(), kind=jnp.bfloat16):
    loudness = level_of(own_key, dims, shards, -0.22, 0.18) if shards else 1.0
    values = jax.random.normal(own_key, dims, jnp.float32) * scale * loudness
    return jnp.minimum(jnp.maximum(values, -limit), limit).astype(kind)


def setup_inputs(seed: int = 0) -> dict:
    arg_keys = jax.random.split(jax.random.key(seed), 22)
    return {
        "hidden_in": noise(arg_keys[0], (SEQS, LEN, D), 1.0, 6.0, ((0, 4), (1, 8))),
        "segment_ids": draw_segment_ids(jax.random.fold_in(arg_keys[21], 71), 0),
        "doc_positions": draw_doc_positions(jax.random.fold_in(arg_keys[21], 71), 0),
        "w_query": noise(arg_keys[3], (D, D), D ** -0.5, 0.21875, ((0, 4),)),
        "w_key": noise(arg_keys[4], (D, D), D ** -0.5, 0.21875, ((0, 4),)),
        "w_value": noise(arg_keys[5], (D, D), D ** -0.5, 0.21875, ((0, 4),)),
        "w_out": noise(arg_keys[6], (D, D), (D // 16) ** -0.5, 0.875, ((0, 4),)),
        "b_query": noise(arg_keys[7], (D,), 0.3, 4.0, ((0, 4),)),
        "b_value": noise(arg_keys[8], (D,), 0.3, 4.0, ((0, 4),)),
        "b_out": noise(arg_keys[9], (D,), 0.3, 4.0, ((0, 4),)),
        "ln1_gain": jnp.clip(1.0 + 0.1 * jax.random.normal(arg_keys[10], (D,), jnp.float32), 0.5, 1.5).astype(jnp.bfloat16),
        "ln1_shift": noise(arg_keys[11], (D,), 0.3, 4.0, ((0, 4),)),
        "w_inter": noise(arg_keys[12], (D, FF), D ** -0.5, 0.21875, ((0, 4),)),
        "b_inter": noise(arg_keys[13], (FF,), 0.3, 4.0, ((0, 4),)),
        "w_final": noise(arg_keys[14], (FF, D), FF ** -0.5, 0.109375, ((0, 4),)),
        "b_final": noise(arg_keys[15], (D,), 0.3, 4.0, ((0, 4),)),
        "ln2_gain": jnp.clip(1.0 + 0.1 * jax.random.normal(arg_keys[16], (D,), jnp.float32), 0.5, 1.5).astype(jnp.bfloat16),
        "ln2_shift": noise(arg_keys[17], (D,), 0.3, 4.0, ((0, 4),)),
        "mask_logits": noise(arg_keys[18], (H, MSPAN, MSPAN), 1.0, 6.0, ((1, 4),), jnp.float32),
        "mask_noise": noise(arg_keys[19], (H, MSPAN, MSPAN), 1.0, 6.0, ((1, 4),), jnp.float32),
        "grad_out": noise(arg_keys[20], (SEQS, LEN, D), 1.0, 6.0, ((0, 4), (1, 8))),
    }


NEGATIVE = -1e+30
EPSILON = 1e-12
HIGHEST = lax.Precision.HIGHEST

@jax.custom_vjp
def low(v):
    return lax.optimization_barrier(v.astype(jnp.bfloat16)).astype(jnp.float32)

@jax.custom_vjp
def low_back(v):
    return v

def low_keep(v):
    return (low(v), None)

def low_pass(kept, grad):
    return (grad,)

def back_keep(v):
    return (v, None)

def back_low(kept, grad):
    return (low(grad),)
low.defvjp(low_keep, low_pass)
low_back.defvjp(back_keep, back_low)

def layer_norm(hidden, gain_row, shift_row):
    average = lax.optimization_barrier(jnp.mean(hidden, axis=-1, keepdims=True))
    centered = hidden - average
    variance = lax.optimization_barrier(jnp.mean(centered * centered, axis=-1, keepdims=True))
    return centered * lax.rsqrt(variance + EPSILON) * gain_row + shift_row

def attend(queries, keys_all, values_all, segment, slot_ids, mask_table):
    raw_scores = jnp.einsum('qhd,khd->hqk', queries, keys_all, precision=HIGHEST) * 0.125
    mask_bias = mask_table[:, slot_ids[:, None], slot_ids[None, :]]
    scores = low_back(raw_scores + mask_bias)
    same_doc = segment[:, None] == segment[None, :]
    scores = jnp.where(same_doc[None], scores, NEGATIVE)
    row_top = lax.optimization_barrier(jnp.max(scores, axis=-1, keepdims=True))
    exponent = jnp.exp(scores - row_top)
    soft_weights = exponent / lax.optimization_barrier(jnp.sum(exponent, axis=-1, keepdims=True))
    return jnp.einsum('hqk,khd->qhd', low(soft_weights), values_all, precision=HIGHEST)

def layer_sequence(inputs, weights, mask_table):
    tokens, segment, slot_ids = inputs
    w_query, w_key, w_value, w_out, b_query, b_value, b_out, gain_one, shift_one, w_inter, b_inter, w_final, b_final, gain_two, shift_two = weights
    queries = low(low_back(jnp.dot(tokens, w_query, precision=HIGHEST) + b_query))
    keys_all = low(low_back(jnp.dot(tokens, w_key, precision=HIGHEST)))
    values_all = low(low_back(jnp.dot(tokens, w_value, precision=HIGHEST) + b_value))
    shaped = (tokens.shape[0], H, HD)
    context = attend(queries.reshape(shaped), keys_all.reshape(shaped), values_all.reshape(shaped), segment, slot_ids, mask_table)
    context = low(low_back(context.reshape(tokens.shape)))
    attn_out = low_back(jnp.dot(context, w_out, precision=HIGHEST) + b_out)
    first_norm = layer_norm(tokens + attn_out, gain_one, shift_one)
    inner_act = low_back(jnp.dot(low(first_norm), w_inter, precision=HIGHEST) + b_inter)
    active = low(low_back(jax.nn.gelu(inner_act, approximate=False)))
    ffn_out = low_back(jnp.dot(active, w_final, precision=HIGHEST) + b_final)
    return layer_norm(first_norm + ffn_out, gain_two, shift_two)

def reference(hidden_in, segment_ids, doc_positions, w_query, w_key, w_value, w_out, b_query, b_value, b_out, ln1_gain, ln1_shift, w_inter, b_inter, w_final, b_final, ln2_gain, ln2_shift, mask_logits, mask_noise, grad_out):
    slot_ids = (doc_positions % MSPAN).astype(jnp.int32)
    floats = [item.astype(jnp.float32) for item in (hidden_in, w_query, w_key, w_value, w_out, b_query, b_value, b_out, ln1_gain, ln1_shift, w_inter, b_inter, w_final, b_final, ln2_gain, ln2_shift, mask_logits)]

    def forward(tokens, w_query, w_key, w_value, w_out, b_query, b_value, b_out, ln1_gain, ln1_shift, w_inter, b_inter, w_final, b_final, ln2_gain, ln2_shift, mask_logits):
        mask_table = low(jax.nn.log_sigmoid(2.0 * (mask_logits + mask_noise)))
        weights = (w_query, w_key, w_value, w_out, b_query, b_value, b_out, ln1_gain, ln1_shift, w_inter, b_inter, w_final, b_final, ln2_gain, ln2_shift)
        stepper = jax.checkpoint(partial(layer_sequence, weights=weights, mask_table=mask_table))
        return lax.map(stepper, (tokens, segment_ids, slot_ids))
    result, pullback = jax.vjp(forward, *floats)
    gradients = pullback(grad_out.astype(jnp.float32))
    grad_in, w_query_grad, w_key_grad, w_value_grad, w_out_grad, b_query_grad, b_value_grad, b_out_grad, ln1_gain_grad, ln1_shift_grad, w_inter_grad, b_inter_grad, w_final_grad, b_final_grad, ln2_gain_grad, ln2_shift_grad, mask_logits_grad = gradients
    return (result.astype(jnp.bfloat16), grad_in, w_query_grad, w_key_grad, w_value_grad, w_out_grad, b_query_grad, b_value_grad, b_out_grad, ln1_gain_grad, ln1_shift_grad, w_inter_grad, b_inter_grad, w_final_grad, b_final_grad, ln2_gain_grad, ln2_shift_grad, mask_logits_grad)
```

```python
import functools

import jax
import jax.numpy as jnp
from jax import lax
from jax.experimental import pallas as pl
from jax.experimental.pallas import tpu as pltpu
from jax.sharding import PartitionSpec as P

H = 12
HD = 64
MSPAN = 512


NEGATIVE = -1e30
EPSILON = 1e-12


def layer_norm(hidden, gain_row, shift_row):
    average = jnp.mean(hidden, axis=-1, keepdims=True)
    centered = hidden - average
    variance = jnp.mean(centered * centered, axis=-1, keepdims=True)
    return centered * lax.rsqrt(variance + EPSILON) * gain_row + shift_row


def exact_gelu(inner_act):
    return jax.nn.gelu(inner_act, approximate=False)


def left_product(first_op, second_op):
    return lax.dot_general(
        first_op, second_op, (((0,), (0,)), ((), ())), preferred_element_type=jnp.float32
    )


def right_product(first_op, second_op):
    return lax.dot_general(
        first_op, second_op, (((1,), (1,)), ((), ())), preferred_element_type=jnp.float32
    )


def one_hot_rows(slot_values, width):
    return (slot_values[:, None] == jnp.arange(width, dtype=jnp.int32)[None, :]).astype(
        jnp.bfloat16
    )


def block_scores(queries, key_part, seg_local, seg_part, bias_part):
    key_heads = key_part.reshape(key_part.shape[0], H, HD)
    raw_scores = (
        jnp.einsum("shd,nhd->hsn", queries, key_heads, preferred_element_type=jnp.float32) * 0.125
    )
    same_doc = seg_local[:, None] == seg_part[None, :]
    return jnp.where(same_doc[None], raw_scores + bias_part.astype(jnp.float32), NEGATIVE)


def split_blocks(array_in, block_size):
    return array_in.reshape((array_in.shape[0] // block_size, block_size) + array_in.shape[1:])


def block_length():
    return 512


def make_blocks(full_keys, full_values, full_segment, full_slot):
    block_size = block_length()
    return (
        split_blocks(full_keys, block_size),
        split_blocks(full_values, block_size),
        split_blocks(full_segment, block_size),
        split_blocks(full_slot, block_size),
    )


def row_statistics(queries, seg_local, table_rows, blocks):
    rows = queries.shape[0]

    def advance(state_carry, key_block):
        key_part, value_part, seg_part, slot_part = key_block

        def compute(pair):
            row_top, row_total = pair
            bias_part = jnp.einsum(
                "hsa,na->hsn",
                table_rows,
                one_hot_rows(slot_part, MSPAN),
                preferred_element_type=jnp.float32,
            ).astype(jnp.bfloat16)
            scores = block_scores(queries, key_part, seg_local, seg_part, bias_part)
            new_top = jnp.maximum(row_top, jnp.max(scores, axis=-1))
            row_total = row_total * jnp.exp(row_top - new_top) + jnp.sum(
                jnp.exp(scores - new_top[..., None]), axis=-1
            )
            return ((new_top, row_total), bias_part)

        return compute(state_carry)

    start_state = (jnp.full((H, rows), NEGATIVE, jnp.float32), jnp.zeros((H, rows), jnp.float32))
    (row_top, row_total), bias_blocks = lax.scan(advance, start_state, blocks)
    return (row_top + jnp.log(row_total), bias_blocks)


def attention_output(queries, seg_local, blocks, bias_blocks, log_total):
    rows = queries.shape[0]

    def advance(accumulated, items):
        (key_part, value_part, seg_part, slot_part), bias_part = items

        def compute(current):
            scores = block_scores(queries, key_part, seg_local, seg_part, bias_part)
            soft_weights = jnp.exp(scores - log_total[..., None]).astype(jnp.bfloat16)
            value_heads = value_part.reshape(value_part.shape[0], H, HD)
            return current + jnp.einsum(
                "hsn,nhd->shd", soft_weights, value_heads, preferred_element_type=jnp.float32
            )

        return (compute(accumulated), None)

    context, _ = lax.scan(advance, jnp.zeros((rows, H, HD), jnp.float32), (blocks, bias_blocks))
    return context


def attention_backward(queries, seg_local, blocks, bias_blocks, log_total, context_grad, row_delta):
    rows = queries.shape[0]

    def advance(state_carry, items):
        (key_part, value_part, seg_part, slot_part), bias_part = items
        key_count = key_part.shape[0]

        def compute(operand):
            query_acc, slot_acc = operand
            scores = block_scores(queries, key_part, seg_local, seg_part, bias_part)
            soft_float = jnp.exp(scores - log_total[..., None])
            key_heads = key_part.reshape(key_count, H, HD)
            value_heads = value_part.reshape(key_count, H, HD)
            weight_grad = jnp.einsum(
                "shd,nhd->hsn", context_grad, value_heads, preferred_element_type=jnp.float32
            )
            score_grad = (soft_float * (weight_grad - row_delta[..., None])).astype(jnp.bfloat16)
            query_acc = (
                query_acc
                + jnp.einsum(
                    "hsn,nhd->shd", score_grad, key_heads, preferred_element_type=jnp.float32
                )
                * 0.125
            )
            slot_acc = slot_acc + jnp.einsum(
                "hsn,na->hsa",
                score_grad,
                one_hot_rows(slot_part, MSPAN),
                preferred_element_type=jnp.float32,
            )
            key_block_grad = (
                jnp.einsum("hsn,shd->nhd", score_grad, queries, preferred_element_type=jnp.float32)
                * 0.125
            )
            value_block_grad = jnp.einsum(
                "hsn,shd->nhd",
                soft_float.astype(jnp.bfloat16),
                context_grad,
                preferred_element_type=jnp.float32,
            )
            return ((query_acc, slot_acc), (key_block_grad, value_block_grad))

        return compute(state_carry)

    start_state = (jnp.zeros((rows, H, HD), jnp.float32), jnp.zeros((H, rows, MSPAN), jnp.float32))
    (query_acc, slot_acc), block_grads = lax.scan(advance, start_state, (blocks, bias_blocks))
    key_grads, value_grads = block_grads
    full_len = key_grads.shape[0] * key_grads.shape[1]
    return (
        query_acc,
        slot_acc,
        key_grads.reshape(full_len, H * HD),
        value_grads.reshape(full_len, H * HD),
    )


def general_device(
    hidden_in,
    segment_ids,
    doc_positions,
    w_query,
    w_key,
    w_value,
    w_out,
    b_query,
    b_value,
    b_out,
    ln1_gain,
    ln1_shift,
    w_inter,
    b_inter,
    w_final,
    b_final,
    ln2_gain,
    ln2_shift,
    mask_logits,
    mask_noise,
    grad_out,
):
    table_part = jax.nn.log_sigmoid(2.0 * (mask_logits + mask_noise)).astype(jnp.bfloat16)
    (
        wq_full,
        wk_full,
        wv_full,
        wo_full,
        wi_full,
        wf_full,
        bq_full,
        bv_full,
        bo_full,
        bi_full,
        bf_full,
        gain_one,
        shift_one,
        gain_two,
        shift_two,
        table_full,
    ) = (
        lax.all_gather(w_query, "fsdp", axis=0, tiled=True),
        lax.all_gather(w_key, "fsdp", axis=0, tiled=True),
        lax.all_gather(w_value, "fsdp", axis=0, tiled=True),
        lax.all_gather(w_out, "fsdp", axis=0, tiled=True),
        lax.all_gather(w_inter, "fsdp", axis=0, tiled=True),
        lax.all_gather(w_final, "fsdp", axis=0, tiled=True),
        lax.all_gather(b_query, "fsdp", axis=0, tiled=True),
        lax.all_gather(b_value, "fsdp", axis=0, tiled=True),
        lax.all_gather(b_out, "fsdp", axis=0, tiled=True),
        lax.all_gather(b_inter, "fsdp", axis=0, tiled=True),
        lax.all_gather(b_final, "fsdp", axis=0, tiled=True),
        lax.all_gather(ln1_gain, "fsdp", axis=0, tiled=True),
        lax.all_gather(ln1_shift, "fsdp", axis=0, tiled=True),
        lax.all_gather(ln2_gain, "fsdp", axis=0, tiled=True),
        lax.all_gather(ln2_shift, "fsdp", axis=0, tiled=True),
        lax.all_gather(table_part, "fsdp", axis=1, tiled=True),
    )
    bq_full, bv_full, bo_full = (
        bq_full.astype(jnp.float32),
        bv_full.astype(jnp.float32),
        bo_full.astype(jnp.float32),
    )
    bi_full, bf_full = (bi_full.astype(jnp.float32), bf_full.astype(jnp.float32))
    gain_one, shift_one = (gain_one.astype(jnp.float32), shift_one.astype(jnp.float32))
    gain_two, shift_two = (gain_two.astype(jnp.float32), shift_two.astype(jnp.float32))
    micro_count = hidden_in.shape[0]
    rows = hidden_in.shape[1]
    saved = []
    outputs_list = []
    for micro_batch in range(micro_count):
        tokens = hidden_in[micro_batch]
        seg_local = segment_ids[micro_batch]
        slot_local = doc_positions[micro_batch] % MSPAN
        queries_flat = (
            jnp.dot(tokens, wq_full, preferred_element_type=jnp.float32) + bq_full
        ).astype(jnp.bfloat16)
        keys_local = jnp.dot(tokens, wk_full, preferred_element_type=jnp.float32).astype(
            jnp.bfloat16
        )
        values_local = (
            jnp.dot(tokens, wv_full, preferred_element_type=jnp.float32) + bv_full
        ).astype(jnp.bfloat16)
        gathered = (
            lax.all_gather(keys_local, "ctx", axis=0, tiled=True),
            lax.all_gather(values_local, "ctx", axis=0, tiled=True),
            lax.all_gather(seg_local, "ctx", axis=0, tiled=True),
            lax.all_gather(slot_local, "ctx", axis=0, tiled=True),
        )
        blocks = make_blocks(*gathered)
        queries = queries_flat.reshape(rows, H, HD)
        table_rows = table_full[:, slot_local, :]
        log_total, bias_blocks = row_statistics(queries, seg_local, table_rows, blocks)
        context = attention_output(queries, seg_local, blocks, bias_blocks, log_total)
        context_low = context.reshape(rows, H * HD).astype(jnp.bfloat16)
        attn_out = jnp.dot(context_low, wo_full, preferred_element_type=jnp.float32) + bo_full
        first_norm, norm_one_back = jax.vjp(
            layer_norm, tokens.astype(jnp.float32) + attn_out, gain_one, shift_one
        )
        first_low = first_norm.astype(jnp.bfloat16)
        inner_act = jnp.dot(first_low, wi_full, preferred_element_type=jnp.float32) + bi_full
        active, gelu_back = jax.vjp(exact_gelu, inner_act)
        active_low = active.astype(jnp.bfloat16)
        ffn_out = jnp.dot(active_low, wf_full, preferred_element_type=jnp.float32) + bf_full
        result, norm_two_back = jax.vjp(layer_norm, first_norm + ffn_out, gain_two, shift_two)
        outputs_list.append(result.astype(jnp.bfloat16))
        kept_blocks = blocks
        saved.append(
            (
                tokens,
                seg_local,
                slot_local,
                queries,
                keys_local,
                values_local,
                log_total,
                bias_blocks,
                context,
                context_low,
                first_low,
                active_low,
                norm_one_back,
                gelu_back,
                norm_two_back,
                kept_blocks,
            )
        )
    zeros_square = jnp.zeros((H * HD, H * HD), jnp.float32)
    wq_grad, wk_grad, wv_grad, wo_grad = (zeros_square, zeros_square, zeros_square, zeros_square)
    wi_grad = jnp.zeros(wi_full.shape, jnp.float32)
    wf_grad = jnp.zeros(wf_full.shape, jnp.float32)
    zeros_row = jnp.zeros((H * HD,), jnp.float32)
    bq_grad, bv_grad, bo_grad, bf_grad = (zeros_row, zeros_row, zeros_row, zeros_row)
    gain_one_grad, shift_one_grad, gain_two_grad, shift_two_grad = (
        zeros_row,
        zeros_row,
        zeros_row,
        zeros_row,
    )
    bi_grad = jnp.zeros(bi_full.shape, jnp.float32)
    table_grad = jnp.zeros(table_full.shape, jnp.float32)
    input_grads = []
    for micro_batch in range(micro_count):
        (
            tokens,
            seg_local,
            slot_local,
            queries,
            keys_local,
            values_local,
            log_total,
            bias_blocks,
            context,
            context_low,
            first_low,
            active_low,
            norm_one_back,
            gelu_back,
            norm_two_back,
            kept_blocks,
        ) = saved[micro_batch]
        upstream = grad_out[micro_batch].astype(jnp.float32)
        sum_grad, gain_part, shift_part = norm_two_back(upstream)
        gain_two_grad = gain_two_grad + gain_part
        shift_two_grad = shift_two_grad + shift_part
        ffn_grad = sum_grad.astype(jnp.bfloat16)
        bf_grad = bf_grad + jnp.sum(ffn_grad.astype(jnp.float32), axis=0)
        wf_grad = wf_grad + left_product(active_low, ffn_grad)
        active_grad = right_product(ffn_grad, wf_full).astype(jnp.bfloat16)
        (inner_float,) = gelu_back(active_grad.astype(jnp.float32))
        inner_grad = inner_float.astype(jnp.bfloat16)
        bi_grad = bi_grad + jnp.sum(inner_grad.astype(jnp.float32), axis=0)
        wi_grad = wi_grad + left_product(first_low, inner_grad)
        first_grad = sum_grad + right_product(inner_grad, wi_full)
        norm_grad, gain_part, shift_part = norm_one_back(first_grad)
        gain_one_grad = gain_one_grad + gain_part
        shift_one_grad = shift_one_grad + shift_part
        attn_grad = norm_grad.astype(jnp.bfloat16)
        bo_grad = bo_grad + jnp.sum(attn_grad.astype(jnp.float32), axis=0)
        wo_grad = wo_grad + left_product(context_low, attn_grad)
        context_grad_flat = right_product(attn_grad, wo_full).astype(jnp.bfloat16)
        context_grad = context_grad_flat.reshape(rows, H, HD)
        row_delta = jnp.einsum("shd,shd->hs", context_grad.astype(jnp.float32), context)
        blocks = kept_blocks
        query_acc, slot_acc, key_full_grad, value_full_grad = attention_backward(
            queries, seg_local, blocks, bias_blocks, log_total, context_grad, row_delta
        )
        key_share, value_share = (
            lax.psum_scatter(
                key_full_grad.astype(jnp.bfloat16), "ctx", scatter_dimension=0, tiled=True
            ).astype(jnp.float32),
            lax.psum_scatter(
                value_full_grad.astype(jnp.bfloat16), "ctx", scatter_dimension=0, tiled=True
            ).astype(jnp.float32),
        )
        table_grad = table_grad.at[:, slot_local, :].add(slot_acc)
        query_low = query_acc.reshape(rows, H * HD).astype(jnp.bfloat16)
        key_low = key_share.astype(jnp.bfloat16)
        value_low = value_share.astype(jnp.bfloat16)
        bq_grad = bq_grad + jnp.sum(query_low.astype(jnp.float32), axis=0)
        bv_grad = bv_grad + jnp.sum(value_low.astype(jnp.float32), axis=0)
        wq_grad = wq_grad + left_product(tokens, query_low)
        wk_grad = wk_grad + left_product(tokens, key_low)
        wv_grad = wv_grad + left_product(tokens, value_low)
        input_grads.append(
            norm_grad
            + right_product(query_low, wq_full)
            + right_product(key_low, wk_full)
            + right_product(value_low, wv_full)
        )
    shares = (
        lax.psum_scatter(
            wq_grad.astype(jnp.bfloat16), "fsdp", scatter_dimension=0, tiled=True
        ).astype(jnp.float32),
        lax.psum_scatter(
            wk_grad.astype(jnp.bfloat16), "fsdp", scatter_dimension=0, tiled=True
        ).astype(jnp.float32),
        lax.psum_scatter(
            wv_grad.astype(jnp.bfloat16), "fsdp", scatter_dimension=0, tiled=True
        ).astype(jnp.float32),
        lax.psum_scatter(
            wo_grad.astype(jnp.bfloat16), "fsdp", scatter_dimension=0, tiled=True
        ).astype(jnp.float32),
        lax.psum_scatter(
            bq_grad.astype(jnp.bfloat16), "fsdp", scatter_dimension=0, tiled=True
        ).astype(jnp.float32),
        lax.psum_scatter(
            bv_grad.astype(jnp.bfloat16), "fsdp", scatter_dimension=0, tiled=True
        ).astype(jnp.float32),
        lax.psum_scatter(
            bo_grad.astype(jnp.bfloat16), "fsdp", scatter_dimension=0, tiled=True
        ).astype(jnp.float32),
        lax.psum_scatter(
            gain_one_grad.astype(jnp.bfloat16), "fsdp", scatter_dimension=0, tiled=True
        ).astype(jnp.float32),
        lax.psum_scatter(
            shift_one_grad.astype(jnp.bfloat16), "fsdp", scatter_dimension=0, tiled=True
        ).astype(jnp.float32),
        lax.psum_scatter(
            wi_grad.astype(jnp.bfloat16), "fsdp", scatter_dimension=0, tiled=True
        ).astype(jnp.float32),
        lax.psum_scatter(
            bi_grad.astype(jnp.bfloat16), "fsdp", scatter_dimension=0, tiled=True
        ).astype(jnp.float32),
        lax.psum_scatter(
            wf_grad.astype(jnp.bfloat16), "fsdp", scatter_dimension=0, tiled=True
        ).astype(jnp.float32),
        lax.psum_scatter(
            bf_grad.astype(jnp.bfloat16), "fsdp", scatter_dimension=0, tiled=True
        ).astype(jnp.float32),
        lax.psum_scatter(
            gain_two_grad.astype(jnp.bfloat16), "fsdp", scatter_dimension=0, tiled=True
        ).astype(jnp.float32),
        lax.psum_scatter(
            shift_two_grad.astype(jnp.bfloat16), "fsdp", scatter_dimension=0, tiled=True
        ).astype(jnp.float32),
        lax.psum_scatter(
            table_grad.astype(jnp.bfloat16), "fsdp", scatter_dimension=1, tiled=True
        ).astype(jnp.float32),
    )
    totals = (
        lax.psum(shares[0].astype(jnp.bfloat16), "ctx").astype(jnp.float32),
        lax.psum(shares[1].astype(jnp.bfloat16), "ctx").astype(jnp.float32),
        lax.psum(shares[2].astype(jnp.bfloat16), "ctx").astype(jnp.float32),
        lax.psum(shares[3].astype(jnp.bfloat16), "ctx").astype(jnp.float32),
        lax.psum(shares[4].astype(jnp.bfloat16), "ctx").astype(jnp.float32),
        lax.psum(shares[5].astype(jnp.bfloat16), "ctx").astype(jnp.float32),
        lax.psum(shares[6].astype(jnp.bfloat16), "ctx").astype(jnp.float32),
        lax.psum(shares[7].astype(jnp.bfloat16), "ctx").astype(jnp.float32),
        lax.psum(shares[8].astype(jnp.bfloat16), "ctx").astype(jnp.float32),
        lax.psum(shares[9].astype(jnp.bfloat16), "ctx").astype(jnp.float32),
        lax.psum(shares[10].astype(jnp.bfloat16), "ctx").astype(jnp.float32),
        lax.psum(shares[11].astype(jnp.bfloat16), "ctx").astype(jnp.float32),
        lax.psum(shares[12].astype(jnp.bfloat16), "ctx").astype(jnp.float32),
        lax.psum(shares[13].astype(jnp.bfloat16), "ctx").astype(jnp.float32),
        lax.psum(shares[14].astype(jnp.bfloat16), "ctx").astype(jnp.float32),
        lax.psum(shares[15].astype(jnp.bfloat16), "ctx").astype(jnp.float32),
    )
    (
        wq_total,
        wk_total,
        wv_total,
        wo_total,
        bq_total,
        bv_total,
        bo_total,
        gain_one_total,
        shift_one_total,
        wi_total,
        bi_total,
        wf_total,
        bf_total,
        gain_two_total,
        shift_two_total,
        table_total,
    ) = totals
    logit_grad = table_total * 2.0 * jax.nn.sigmoid(-2.0 * (mask_logits + mask_noise))
    return (
        jnp.stack(outputs_list),
        jnp.stack(input_grads),
        wq_total,
        wk_total,
        wv_total,
        wo_total,
        bq_total,
        bv_total,
        bo_total,
        gain_one_total,
        shift_one_total,
        wi_total,
        bi_total,
        wf_total,
        bf_total,
        gain_two_total,
        shift_two_total,
        logit_grad,
    )


MESH = pl.DeviceIdType.MESH
BF16 = jnp.bfloat16
F32 = jnp.float32
ROWS = 192
TALL = 272


def place():
    c = lax.axis_index("ctx")
    f = lax.axis_index("fsdp")
    return (c // 2, c % 2, f // 2, f % 2)


def device(z, x, y, k):
    return {"ctx": z * 2 + x, "fsdp": y * 2 + k}


def send(src, dst, send_sem, recv_sem, target):
    return pltpu.make_async_remote_copy(
        src_ref=src,
        dst_ref=dst,
        send_sem=send_sem,
        recv_sem=recv_sem,
        device_id=target,
        device_id_type=MESH,
    )


def meet(targets):
    barrier = pltpu.get_barrier_semaphore()
    for target in targets:
        pl.semaphore_signal(barrier, inc=1, device_id=target, device_id_type=MESH)
    pl.semaphore_wait(barrier, len(targets))


def any_spec():
    return pl.BlockSpec(memory_space=pl.ANY)


def vmem_spec():
    return pl.BlockSpec(memory_space=pltpu.VMEM)


def gather_pieces():
    pieces = []
    for array in range(4):
        pieces.append((array, 0, 192, 0, 768))
    for part in range(2):
        pieces.append((4, 0, 192, 1536 * part, 1536))
    for part in range(4):
        pieces.append((5, 192 * part, 192, 0, 768))
    return pieces


def gather_kernel(*refs):
    ins, table, small = (refs[0:6], refs[6], refs[7])
    outs, table_out, small_out = (refs[8:14], refs[14], refs[15])
    ss, rs, ls, ss_small, rs_small = refs[16:]
    z, x, y, k = place()
    mine = y * 2 + k
    over = (1 - y) * 2 + k
    core = device(z, x, y, 1 - k)
    ynb = device(z, x, 1 - y, k)
    diag = device(z, x, 1 - y, 1 - k)
    xnb = device(z, 1 - x, y, k)
    meet([core, ynb, diag, xnb])
    pieces = gather_pieces()

    def source(n, half):
        if n == len(pieces):
            heads = table.at[pl.ds(3 * z, 3)]
            return heads if half is None else heads.at[:, pl.ds(64 * half, 64)]
        a, r0, rn, c0, cn = pieces[n]
        if half is None:
            return ins[a].at[pl.ds(r0, rn), pl.ds(c0, cn)]
        return ins[a].at[pl.ds(r0 + (rn // 2) * half, rn // 2), pl.ds(c0, cn)]

    def target(n, owner, half):
        if n == len(pieces):
            if half is None:
                return table_out.at[:, pl.ds(128 * owner, 128)]
            return table_out.at[:, pl.ds(128 * owner + 64 * half, 64)]
        a, r0, rn, c0, cn = pieces[n]
        base = ins[a].shape[0] * owner + r0
        if half is None:
            return outs[a].at[pl.ds(base, rn), pl.ds(c0, cn)]
        return outs[a].at[pl.ds(base + (rn // 2) * half, rn // 2), pl.ds(c0, cn)]

    count = len(pieces) + 1
    order = [0, 1, 2, count - 1] + list(range(3, count - 1))
    locals_, cores, ys, xs, f0, f1 = ({}, {}, {}, {}, {}, {})
    for n in order:
        locals_[n] = pltpu.make_async_copy(source(n, None), target(n, mine, None), ls.at[n])
        cores[n] = send(source(n, None), target(n, mine, None), ss.at[n, 0], rs.at[n, 0], core)
        ys[n] = send(source(n, x), target(n, mine, x), ss.at[n, 1], rs.at[n, 1], ynb)
        ys[n].start()
        cores[n].start()
        locals_[n].start()
    smalls = []
    for i, peer in enumerate((core, ynb, diag)):
        cp = send(small, small_out.at[mine], ss_small.at[i], rs_small.at[i], peer)
        cp.start()
        smalls.append(cp)
    own = pltpu.make_async_copy(small, small_out.at[mine], ls.at[count])
    own.start()
    for n in order:
        ys[n].wait_recv()
        here = target(n, over, x)
        xs[n] = send(here, here, ss.at[n, 2], rs.at[n, 2], xnb)
        xs[n].start()
        f0[n] = send(here, here, ss.at[n, 3], rs.at[n, 3], core)
        f0[n].start()
    for n in order:
        xs[n].wait_recv()
        here = target(n, over, 1 - x)
        f1[n] = send(here, here, ss.at[n, 4], rs.at[n, 4], core)
        f1[n].start()
    for n in order:
        locals_[n].wait()
        cores[n].wait()
        ys[n].wait_send()
        xs[n].wait_send()
        f0[n].wait()
        f1[n].wait()
    own.wait()
    for cp in smalls:
        cp.wait()


def gather_parameters(arrays, table, small):
    count = len(gather_pieces()) + 1
    outs = [jax.ShapeDtypeStruct((a.shape[0] * 4, a.shape[1]), BF16) for a in arrays]
    outs += [jax.ShapeDtypeStruct((3, 512, 384), BF16), jax.ShapeDtypeStruct((4, 16, 256), BF16)]
    return pl.pallas_call(
        gather_kernel,
        out_shape=outs,
        in_specs=[any_spec()] * 8,
        out_specs=[any_spec()] * 8,
        scratch_shapes=[
            pltpu.SemaphoreType.DMA((count, 5)),
            pltpu.SemaphoreType.DMA((count, 5)),
            pltpu.SemaphoreType.DMA((count + 1,)),
            pltpu.SemaphoreType.DMA((3,)),
            pltpu.SemaphoreType.DMA((3,)),
        ],
        compiler_params=pltpu.CompilerParams(collective_id=1, has_side_effects=True),
        name="gather_parameters",
    )(*arrays, table, small)


def ctx_peers():
    c = lax.axis_index("ctx")
    return [{"ctx": lax.rem(c + i, 8)} for i in range(1, 8)]


def to_groups(c, main, extra, main_slot, extra_slot, sems):
    ms, mr, es, er, lsem = sems
    group = c // 4
    for zz in range(4):
        dest = zz * 2 + group

        @pl.when(dest != c)
        def _():
            send(
                main.at[zz], main_slot.at[c % 4], ms.at[zz], mr.at[c % 4], {"ctx": dest}
            ).start()

        @pl.when(dest == c)
        def _():
            pltpu.make_async_copy(main.at[zz], main_slot.at[c % 4], lsem.at[0]).start()

        @pl.when((c == 4) & (zz * 2 != c))
        def _():
            send(extra.at[zz], extra_slot, es.at[zz], er, {"ctx": zz * 2}).start()

        @pl.when((c == 4) & (zz * 2 == c))
        def _():
            pltpu.make_async_copy(extra.at[zz], extra_slot, lsem.at[1]).start()


def to_groups_wait(c, main, extra, main_slot, extra_slot, sems):
    ms, mr, es, er, lsem = sems
    group = c // 4
    x = c % 2
    for j in range(4):

        @pl.when(4 * x + j != c)
        def _():
            send(main.at[0], main_slot.at[j], ms.at[0], mr.at[j], {"ctx": 0}).wait_recv()

        @pl.when(4 * x + j == c)
        def _():
            pltpu.make_async_copy(main.at[0], main_slot.at[j], lsem.at[0]).wait()

    @pl.when((x == 0) & (c != 4))
    def _():
        send(extra.at[0], extra_slot, es.at[0], er, {"ctx": 0}).wait_recv()

    @pl.when(c == 4)
    def _():
        pltpu.make_async_copy(extra.at[0], extra_slot, lsem.at[1]).wait()

    for zz in range(4):
        dest = zz * 2 + group

        @pl.when(dest != c)
        def _():
            send(main.at[zz], main_slot.at[0], ms.at[zz], mr.at[0], {"ctx": dest}).wait_send()

        @pl.when((c == 4) & (zz * 2 != c))
        def _():
            send(extra.at[zz], extra_slot, es.at[zz], er, {"ctx": zz * 2}).wait_send()


def to_owners(c, main, extra, main_slot, extra_slot, sems):
    ms, mr, es, er, lsem = sems
    z = c // 2
    x = c % 2
    for j in range(4):
        dest = 4 * x + j

        @pl.when(dest != c)
        def _():
            send(main.at[j], main_slot.at[z], ms.at[j], mr.at[z], {"ctx": dest}).start()

        @pl.when(dest == c)
        def _():
            pltpu.make_async_copy(main.at[j], main_slot.at[z], lsem.at[0]).start()

    @pl.when((x == 0) & (c != 4))
    def _():
        send(extra, extra_slot.at[z], es, er.at[z], {"ctx": 4}).start()

    @pl.when(c == 4)
    def _():
        pltpu.make_async_copy(extra, extra_slot.at[z], lsem.at[1]).start()


def to_owners_wait(c, main, extra, main_slot, extra_slot, sems):
    ms, mr, es, er, lsem = sems
    x = c % 2
    group = c // 4
    for zz in range(4):

        @pl.when(zz * 2 + group != c)
        def _():
            send(main.at[0], main_slot.at[zz], ms.at[0], mr.at[zz], {"ctx": 0}).wait_recv()

        @pl.when(zz * 2 + group == c)
        def _():
            pltpu.make_async_copy(main.at[0], main_slot.at[zz], lsem.at[0]).wait()

        @pl.when((c == 4) & (zz * 2 != c))
        def _():
            send(extra, extra_slot.at[zz], es, er.at[zz], {"ctx": 0}).wait_recv()

        @pl.when((c == 4) & (zz * 2 == c))
        def _():
            pltpu.make_async_copy(extra, extra_slot.at[zz], lsem.at[1]).wait()

    for j in range(4):
        dest = 4 * x + j

        @pl.when(dest != c)
        def _():
            send(main.at[j], main_slot.at[0], ms.at[j], mr.at[0], {"ctx": dest}).wait_send()

    @pl.when((x == 0) & (c != 4))
    def _():
        send(extra, extra_slot.at[0], es, er.at[0], {"ctx": 4}).wait_send()


def exchange_sems():
    return [
        pltpu.SemaphoreType.DMA((4,)),
        pltpu.SemaphoreType.DMA((4,)),
        pltpu.SemaphoreType.DMA((4,)),
        pltpu.SemaphoreType.DMA,
        pltpu.SemaphoreType.DMA((2,)),
    ]


def return_sems():
    return [
        pltpu.SemaphoreType.DMA((4,)),
        pltpu.SemaphoreType.DMA((4,)),
        pltpu.SemaphoreType.DMA,
        pltpu.SemaphoreType.DMA((4,)),
        pltpu.SemaphoreType.DMA((2,)),
    ]


def dot_nn(a, b):
    return lax.dot_general(a, b, (((1,), (0,)), ((), ())), preferred_element_type=F32)


def dot_nt(a, b):
    return lax.dot_general(a, b, (((1,), (1,)), ((), ())), preferred_element_type=F32)


def dot_tn(a, b):
    return lax.dot_general(a, b, (((0,), (0,)), ((), ())), preferred_element_type=F32)


def group_rows(main, extra, s, lo, width):
    top = main[:, pl.ds(64 * s, 64), lo : lo + width].reshape(256, width)
    return jnp.concatenate([top, extra[pl.ds(16 * s, 16), lo : lo + width]], axis=0)


def place_masks(main, extra, s, x):
    marks = group_rows(main, extra, s, 576, 64).astype(F32)
    segment = marks[:, 0:1]
    slot = marks[:, 1:2]
    first = segment == 0.0
    valid = jnp.where(x == 0, jnp.where(first, 1.0, 0.0), jnp.where(first | (segment < 0.0), 0.0, 1.0))
    lanes = lax.broadcasted_iota(jnp.int32, (TALL, 128), 1).astype(F32)
    seg_hot = jnp.where((lanes == segment) & (valid > 0.0), 1.0, 0.0).astype(BF16)
    wide = lax.broadcasted_iota(jnp.int32, (TALL, TALL), 1).astype(F32)
    slot_hot = jnp.where((wide == slot) & (valid > 0.0), 1.0, 0.0).astype(BF16)
    return (slot_hot, dot_nt(seg_hot, seg_hot) > 0.5)


def attend_kernel(
    x_ref, wq, wk, wv, bq, bv, marks, table,
    main, extra, probs, ctx_out,
    main_send, extra_send, ctx_send, ctx_extra, ctx_in, ctx_extra_in, *sems
):
    c = lax.axis_index("ctx")
    x = c % 2
    there, back = (sems[:5], sems[5:])
    meet(ctx_peers())
    tokens = x_ref[...]
    q = (dot_nn(tokens, wq[...]) + bq[...]).astype(BF16)
    kk = dot_nn(tokens, wk[...]).astype(BF16)
    v = (dot_nn(tokens, wv[...]) + bv[...]).astype(BF16)
    for zz in range(4):
        cols = slice(192 * zz, 192 * zz + 192)
        main_send[zz] = jnp.concatenate([q[:, cols], kk[:, cols], v[:, cols], marks[...]], axis=1)
        for s in range(3):
            extra_send[zz, 16 * s : 16 * s + 16] = main_send[zz, 64 * s : 64 * s + 16]

    @pl.when(x == 1)
    def _():
        extra[...] = jnp.full((48, 640), -1.0, BF16)

    to_groups(c, main_send, extra_send, main, extra, there)
    to_groups_wait(c, main_send, extra_send, main, extra, there)

    def sequence(s, carry):
        slot_hot, same = place_masks(main, extra, s, x)
        parts = []
        for h in range(3):
            qh = group_rows(main, extra, s, 64 * h, 64)
            kh = group_rows(main, extra, s, 192 + 64 * h, 64)
            vh = group_rows(main, extra, s, 384 + 64 * h, 64)
            picked = dot_nn(slot_hot, table[h, 0:TALL, 0:TALL]).astype(BF16)
            bias = dot_nt(picked, slot_hot)
            scores = jnp.where(same, dot_nt(qh, kh) * 0.125 + bias, NEGATIVE)
            top = jnp.max(scores, axis=1, keepdims=True)
            grown = jnp.where(same, jnp.exp(scores - top), 0.0)
            total = jnp.maximum(jnp.sum(grown, axis=1, keepdims=True), 1e-30)
            soft = (grown / total).astype(BF16)
            probs[3 * s + h] = soft
            parts.append(dot_nn(soft, vh).astype(BF16))
        whole = jnp.concatenate(parts, axis=1)
        for j in range(4):
            ctx_send[j, pl.ds(64 * s, 64)] = whole[64 * j : 64 * j + 64]
        ctx_extra[pl.ds(16 * s, 16)] = whole[256:272]
        return carry

    lax.fori_loop(0, 3, sequence, 0)
    to_owners(c, ctx_send, ctx_extra, ctx_in, ctx_extra_in, back)
    to_owners_wait(c, ctx_send, ctx_extra, ctx_in, ctx_extra_in, back)
    ctx_out[...] = ctx_in[...]

    @pl.when(c == 4)
    def _():
        for zz in range(4):
            for s in range(3):
                ctx_out[zz, 64 * s : 64 * s + 16] = (
                    ctx_in[zz, 64 * s : 64 * s + 16] + ctx_extra_in[zz, 16 * s : 16 * s + 16]
                )


def attend(tokens, wq, wk, wv, bq, bv, marks, table):
    return pl.pallas_call(
        attend_kernel,
        out_shape=[
            jax.ShapeDtypeStruct((4, ROWS, 640), BF16),
            jax.ShapeDtypeStruct((48, 640), BF16),
            jax.ShapeDtypeStruct((9, TALL, TALL), BF16),
            jax.ShapeDtypeStruct((4, ROWS, 192), BF16),
        ],
        in_specs=[vmem_spec()] * 8,
        out_specs=[vmem_spec()] * 4,
        scratch_shapes=[
            pltpu.VMEM((4, ROWS, 640), BF16),
            pltpu.VMEM((4, 48, 640), BF16),
            pltpu.VMEM((4, ROWS, 192), BF16),
            pltpu.VMEM((48, 192), BF16),
            pltpu.VMEM((4, ROWS, 192), BF16),
            pltpu.VMEM((4, 48, 192), BF16),
        ]
        + exchange_sems()
        + return_sems(),
        compiler_params=pltpu.CompilerParams(
            collective_id=2, has_side_effects=True, vmem_limit_bytes=48 * 2**20
        ),
        name="attend",
    )(tokens, wq, wk, wv, bq, bv, marks, table)


def attend_back_kernel(
    grad, main, extra, probs,
    out, table_grad,
    grad_in, grad_extra, grad_extra_in, main_send, extra_send, main_in, extra_in, *sems
):
    c = lax.axis_index("ctx")
    x = c % 2
    there, back = (sems[:5], sems[5:])
    meet(ctx_peers())
    for zz in range(4):
        for s in range(3):
            grad_extra[zz, 16 * s : 16 * s + 16] = grad[zz, 64 * s : 64 * s + 16]

    @pl.when(x == 1)
    def _():
        grad_extra_in[...] = jnp.zeros((48, 192), BF16)

    to_groups(c, grad, grad_extra, grad_in, grad_extra_in, there)
    to_groups_wait(c, grad, grad_extra, grad_in, grad_extra_in, there)
    table_grad[...] = jnp.zeros((3, TALL, TALL), F32)

    def sequence(s, carry):
        slot_hot, _ = place_masks(main, extra, s, x)
        parts = [[], [], []]
        for h in range(3):
            qh = group_rows(main, extra, s, 64 * h, 64)
            kh = group_rows(main, extra, s, 192 + 64 * h, 64)
            vh = group_rows(main, extra, s, 384 + 64 * h, 64)
            gh = group_rows(grad_in, grad_extra_in, s, 64 * h, 64)
            soft = probs[3 * s + h]
            weight = soft.astype(F32)
            weight_grad = dot_nt(gh, vh)
            delta = jnp.sum(weight * weight_grad, axis=1, keepdims=True)
            score_grad = (weight * (weight_grad - delta)).astype(BF16)
            parts[0].append((dot_nn(score_grad, kh) * 0.125).astype(BF16))
            parts[1].append((dot_tn(score_grad, qh) * 0.125).astype(BF16))
            parts[2].append(dot_tn(soft, gh).astype(BF16))
            moved = dot_tn(slot_hot, score_grad)
            table_grad[h] += dot_nn(moved.astype(BF16), slot_hot)
        blank = jnp.zeros((TALL, 64), BF16)
        whole = jnp.concatenate(parts[0] + parts[1] + parts[2] + [blank], axis=1)
        for j in range(4):
            main_send[j, pl.ds(64 * s, 64)] = whole[64 * j : 64 * j + 64]
        extra_send[pl.ds(16 * s, 16)] = whole[256:272]
        return carry

    lax.fori_loop(0, 3, sequence, 0)
    to_owners(c, main_send, extra_send, main_in, extra_in, back)
    to_owners_wait(c, main_send, extra_send, main_in, extra_in, back)
    out[...] = main_in[...]

    @pl.when(c == 4)
    def _():
        for zz in range(4):
            for s in range(3):
                out[zz, 64 * s : 64 * s + 16] = (
                    main_in[zz, 64 * s : 64 * s + 16] + extra_in[zz, 16 * s : 16 * s + 16]
                )


def attend_back(grad, main, extra, probs):
    return pl.pallas_call(
        attend_back_kernel,
        out_shape=[
            jax.ShapeDtypeStruct((4, ROWS, 640), BF16),
            jax.ShapeDtypeStruct((3, TALL, TALL), F32),
        ],
        in_specs=[vmem_spec()] * 4,
        out_specs=[vmem_spec()] * 2,
        scratch_shapes=[
            pltpu.VMEM((4, ROWS, 192), BF16),
            pltpu.VMEM((4, 48, 192), BF16),
            pltpu.VMEM((48, 192), BF16),
            pltpu.VMEM((4, ROWS, 640), BF16),
            pltpu.VMEM((48, 640), BF16),
            pltpu.VMEM((4, ROWS, 640), BF16),
            pltpu.VMEM((4, 48, 640), BF16),
        ]
        + exchange_sems()
        + return_sems(),
        compiler_params=pltpu.CompilerParams(
            collective_id=3, has_side_effects=True, vmem_limit_bytes=48 * 2**20
        ),
        name="attend_back",
    )(grad, main, extra, probs)


def add_rows(out, left, right, rows, step):
    def body(i, carry):
        at = pl.ds(pl.multiple_of(i * step, step), step)
        out[at, :] = (left[at, :].astype(F32) + right[at, :].astype(F32)).astype(BF16)
        return carry

    lax.fori_loop(0, rows // step, body, 0)


def reduce_kernel(
    gq, gk, gv, go, gi, gf, small, table,
    out, small_out, table_out, edge_out,
    r1, r2, r3, r4, s1, s2, s3, s4, t1, t2, t3, e1, e2, e3, e4,
    p1, q1, p2, q2, p3, q3, p4, q4, p5, q5, p6, q6,
    ps, qs, pt, qt, pe, qe, lsem
):
    z, x, y, k = place()
    core = device(z, x, y, 1 - k)
    ynb = device(z, x, 1 - y, k)
    xnb = device(z, 1 - x, y, k)
    znb = [lax.rem(z + i, 4) for i in (1, 2, 3)]
    zdev = [device(zz, x, y, k) for zz in znb]
    meet([core, ynb, xnb] + zdev)

    def block(n, owner):
        chunk, b = divmod(n, 4)
        if chunk == 0:
            return gf.at[pl.ds(768 * owner + 192 * b, 192)]
        if chunk == 1:
            return gi.at[pl.ds(192 * owner, 192), 768 * b : 768 * b + 768]
        return (gq, gk, gv, go)[b].at[pl.ds(192 * owner, 192)]

    first = {}
    for n in range(12):
        for yy in range(2):
            cp = send(
                block(n, 2 * yy + 1 - k), r1.at[n, yy], p1.at[n, yy], q1.at[n, yy], core
            )
            cp.start()
            first[n, yy] = cp
    for yy in range(2):
        cp = send(small.at[2 * yy + 1 - k], s1.at[yy], ps.at[yy], qs.at[yy], core)
        cp.start()
        first[12, yy] = cp
    tcore = send(table.at[:, pl.ds(128 * (1 - k), 128)], t1, pt.at[0], qt.at[0], core)
    tcore.start()
    ecore = send(table.at[:, pl.ds(256, 16)], e1, pe.at[0], qe.at[0], core)
    ecore.start()

    def add(left, right):
        return (left.astype(F32) + right.astype(F32)).astype(BF16)

    second = {}
    third = {}
    fourth = {}

    def step_two(n):
        for yy in range(2):
            first[n, yy].wait_recv()
            add_rows(r1.at[n, yy], block(n, 2 * yy + k), r1.at[n, yy], 192, 32)
        second[n] = send(r1.at[n, 1 - y], r2.at[n], p2.at[n], q2.at[n], ynb)
        second[n].start()

    def step_three(n):
        second[n].wait_recv()
        add_rows(r2.at[n], r1.at[n, y], r2.at[n], 192, 32)
        third[n] = send(r2.at[n, pl.ds(96 * (1 - x), 96)], r3.at[n], p3.at[n], q3.at[n], xnb)
        third[n].start()

    def step_four(n):
        chunk, b = divmod(n, 4)
        third[n].wait_recv()
        add_rows(r3.at[n], r2.at[n, pl.ds(96 * x, 96)], r3.at[n], 96, 32)

        @pl.when(z != b)
        def _():
            send(
                r3.at[n], r4.at[chunk, z], p4.at[n], q4.at[chunk, z], device(b, x, y, k)
            ).start()

    def step_five(chunk):
        for i, zz in enumerate(znb):
            send(r3.at[0], r4.at[chunk, zz], p4.at[0], q4.at[chunk, zz], core).wait_recv()
        for b in range(4):

            @pl.when(z == b)
            def _():
                def body(i, carry):
                    at = pl.ds(pl.multiple_of(i * 32, 32), 32)
                    total = None
                    for zz in range(4):
                        if zz == b:
                            term = r3[4 * chunk + b, at, :].astype(F32)
                        else:
                            term = r4[chunk, zz, at, :].astype(F32)
                        total = term if total is None else total + term
                    to = pl.ds(pl.multiple_of(96 * x + i * 32, 32), 32)
                    out[4 * chunk + b, to, :] = total.astype(BF16)
                    return carry

                lax.fori_loop(0, 3, body, 0)

        here = out.at[4 * chunk + z, pl.ds(96 * x, 96)]
        for i in range(3):
            cp = send(here, here, p5.at[chunk, i], q5.at[chunk, z], zdev[i])
            cp.start()
            fourth[chunk, i] = cp
        cp = send(here, here, p6.at[chunk, 0], q6.at[chunk, z], xnb)
        cp.start()
        fourth[chunk, 3] = cp

    def step_six(chunk):
        for i, zz in enumerate(znb):
            there = out.at[4 * chunk + zz, pl.ds(96 * x, 96)]
            send(there, there, p5.at[chunk, i], q5.at[chunk, zz], core).wait_recv()
            cp = send(there, there, p6.at[chunk, 1 + i], q6.at[chunk, zz], xnb)
            cp.start()
            fourth[chunk, 4 + i] = cp

    def finish(chunk):
        for zz in range(4):
            there = out.at[4 * chunk + zz, pl.ds(96 * (1 - x), 96)]
            send(there, there, p6.at[chunk, 0], q6.at[chunk, zz], xnb).wait_recv()
        for i in range(7):
            fourth[chunk, i].wait_send()

    for n in range(12):
        step_two(n)
    for yy in range(2):
        first[12, yy].wait_recv()
        s1[yy] = add(small[2 * yy + k], s1[yy])
    small_y = send(s1.at[1 - y], s2, ps.at[2], qs.at[2], ynb)
    small_y.start()
    tcore.wait_recv()
    for h in range(3):
        t1[h] = add(table[h, pl.ds(pl.multiple_of(128 * k, 128), 128), :], t1[h])
    ecore.wait_recv()
    e1[...] = add(table[:, 256:272], e1[...])
    edge_y = send(e1, e2, pe.at[1], qe.at[1], ynb)
    edge_y.start()

    @pl.when(y == 1)
    def _():
        send(t1, t2, pt.at[1], qt.at[1], ynb).start()

    for n in range(12):
        step_three(n)
        if n >= 1:
            step_four(n - 1)
        if n == 2:
            small_y.wait_recv()
            s2[...] = add(s1[y], s2[...])
            small_x = send(s2, s3, ps.at[3], qs.at[3], xnb)
            small_x.start()
            edge_y.wait_recv()
            e2[...] = add(e1[...], e2[...])
            edge_x = send(e2, e3, pe.at[2], qe.at[2], xnb)
            edge_x.start()

            @pl.when(y == 0)
            def _():
                send(t1, t2, pt.at[1], qt.at[1], ynb).wait_recv()
                for h in range(3):
                    t2[h] = add(t1[h], t2[h])
                send(t2.at[:, pl.ds(64 * (1 - x), 64)], t3, pt.at[2], qt.at[2], xnb).start()

        if n == 4:
            small_x.wait_recv()
            s4[z] = add(s2[...], s3[...])
            edge_x.wait_recv()
            edge_out[z] = add(e2[...], e3[...])
            small_z = []
            for i in range(3):
                cp = send(s4.at[z], s4.at[z], ps.at[4 + i], qs.at[4 + z], zdev[i])
                cp.start()
                small_z.append(cp)
                cp = send(edge_out.at[z], edge_out.at[z], pe.at[3 + i], qe.at[3 + z], zdev[i])
                cp.start()
                small_z.append(cp)

            @pl.when(y == 0)
            def _():
                send(t2.at[:, pl.ds(0, 64)], t3, pt.at[2], qt.at[2], xnb).wait_recv()
                at = pl.ds(pl.multiple_of(64 * x, 64), 64)
                for h in range(3):
                    table_out[z, h, at, :] = add(t2[h, at, :], t3[h])
                here = table_out.at[z, :, pl.ds(64 * x, 64)]
                for i in range(3):
                    send(here, here, pt.at[3 + i], qt.at[3 + z], zdev[i]).start()
                send(here, here, pt.at[6], qt.at[7 + z], xnb).start()

        if n == 5:
            step_five(0)
        if n == 7:
            step_six(0)
        if n == 9:
            step_five(1)
        if n == 10:
            for zz in znb:
                send(s4.at[zz], s4.at[zz], ps.at[4], qs.at[4 + zz], core).wait_recv()
                send(edge_out.at[zz], edge_out.at[zz], pe.at[3], qe.at[3 + zz], core).wait_recv()
            small_out[...] = (
                (s4[0].astype(F32) + s4[1].astype(F32)) + (s4[2].astype(F32) + s4[3].astype(F32))
            )
            for cp in small_z:
                cp.wait_send()

            @pl.when(y == 0)
            def _():
                for i, zz in enumerate(znb):
                    there = table_out.at[zz, :, pl.ds(64 * x, 64)]
                    send(there, there, pt.at[3], qt.at[3 + zz], core).wait_recv()
                    send(there, there, pt.at[7 + i], qt.at[7 + zz], xnb).start()

            @pl.when(y == 1)
            def _():
                table_out[...] = jnp.zeros((4, 3, 128, TALL), BF16)

        if n == 11:
            step_six(1)
    step_four(11)
    step_five(2)
    step_six(2)
    for chunk in range(3):
        finish(chunk)

    @pl.when(y == 0)
    def _():
        for zz in range(4):
            there = table_out.at[zz, :, pl.ds(64 * (1 - x), 64)]
            send(there, there, pt.at[6], qt.at[7 + zz], xnb).wait_recv()
        here = table_out.at[z, :, pl.ds(64 * x, 64)]
        send(t2.at[:, pl.ds(0, 64)], t3, pt.at[2], qt.at[2], xnb).wait_send()
        for i in range(3):
            send(here, here, pt.at[3 + i], qt.at[3 + z], zdev[i]).wait_send()
        for i in range(4):
            send(here, here, pt.at[6 + i], qt.at[7 + z], xnb).wait_send()

    @pl.when(y == 1)
    def _():
        send(t1, t2, pt.at[1], qt.at[1], ynb).wait_send()

    for cp in (tcore, ecore, small_y, small_x, edge_y, edge_x):
        cp.wait_send()
    for cp in first.values():
        cp.wait_send()
    for n in range(12):
        second[n].wait_send()
        third[n].wait_send()

        @pl.when(z != n % 4)
        def _():
            send(r3.at[n], r4.at[n // 4, z], p4.at[n], q4.at[0, 0], core).wait_send()


def reduce_gradients(gq, gk, gv, go, gi, gf, small, table):
    dma = pltpu.SemaphoreType.DMA
    return pl.pallas_call(
        reduce_kernel,
        out_shape=[
            jax.ShapeDtypeStruct((12, 192, 768), BF16),
            jax.ShapeDtypeStruct((16, 768), F32),
            jax.ShapeDtypeStruct((4, 3, 128, TALL), BF16),
            jax.ShapeDtypeStruct((4, 3, 16, TALL), BF16),
        ],
        in_specs=[vmem_spec()] * 8,
        out_specs=[vmem_spec()] * 4,
        scratch_shapes=[
            pltpu.VMEM((12, 2, 192, 768), BF16),
            pltpu.VMEM((12, 192, 768), BF16),
            pltpu.VMEM((12, 96, 768), BF16),
            pltpu.VMEM((3, 4, 96, 768), BF16),
            pltpu.VMEM((2, 16, 768), BF16),
            pltpu.VMEM((16, 768), BF16),
            pltpu.VMEM((16, 768), BF16),
            pltpu.VMEM((4, 16, 768), BF16),
            pltpu.VMEM((3, 128, TALL), BF16),
            pltpu.VMEM((3, 128, TALL), BF16),
            pltpu.VMEM((3, 64, TALL), BF16),
            pltpu.VMEM((3, 16, TALL), BF16),
            pltpu.VMEM((3, 16, TALL), BF16),
            pltpu.VMEM((3, 16, TALL), BF16),
            pltpu.VMEM((3, 16, TALL), BF16),
            dma((12, 2)), dma((12, 2)),
            dma((12,)), dma((12,)),
            dma((12,)), dma((12,)),
            dma((12,)), dma((3, 4)),
            dma((3, 3)), dma((3, 4)),
            dma((3, 4)), dma((3, 4)),
            dma((8,)), dma((8,)),
            dma((12,)), dma((12,)),
            dma((8,)), dma((8,)),
            dma((2,)),
        ],
        compiler_params=pltpu.CompilerParams(
            collective_id=4, has_side_effects=True, vmem_limit_bytes=60 * 2**20
        ),
        name="reduce_gradients",
    )(gq, gk, gv, go, gi, gf, small, table)


def block_device(
    hidden_in, segment_ids, doc_positions,
    w_query, w_key, w_value, w_out, b_query, b_value, b_out, ln1_gain, ln1_shift,
    w_inter, b_inter, w_final, b_final, ln2_gain, ln2_shift,
    mask_logits, mask_noise, grad_out,
):
    f = lax.axis_index("fsdp")
    doubled = 2.0 * (mask_logits + mask_noise)
    table_part = jax.nn.log_sigmoid(doubled[:, :, :384]).astype(BF16)
    vectors = (b_query, b_value, b_out, ln1_gain, ln1_shift, b_final, ln2_gain, ln2_shift)
    small = jnp.concatenate([jnp.stack(vectors), b_inter.reshape(4, 192)], axis=0)
    small = jnp.pad(small, ((0, 4), (0, 64)))
    wq, wk, wv, wo, wi, wf, table, small_full = gather_parameters(
        (w_query, w_key, w_value, w_out, w_inter, w_final), table_part, small
    )
    rows = small_full[:, :12, :192].astype(F32)
    bq, bv, bo, gain_one, shift_one, bf, gain_two, shift_two = [
        rows[:, i].reshape(1, 768) for i in range(8)
    ]
    bi = rows[:, 8:12].reshape(1, 3072)
    tokens = hidden_in.reshape(ROWS, 768)
    marks = jnp.stack(
        [segment_ids.reshape(ROWS), (doc_positions % MSPAN).reshape(ROWS)], axis=1
    ).astype(BF16)
    marks = jnp.pad(marks, ((0, 0), (0, 62)))
    main, extra, probs, ctx4 = attend(tokens, wq, wk, wv, bq, bv, marks, table)
    context_low = jnp.concatenate([ctx4[i] for i in range(4)], axis=1)
    attn_out = jnp.dot(context_low, wo, preferred_element_type=F32) + bo
    first_norm, norm_one_back = jax.vjp(
        layer_norm, tokens.astype(F32) + attn_out, gain_one, shift_one
    )
    first_low = first_norm.astype(BF16)
    inner_act = jnp.dot(first_low, wi, preferred_element_type=F32) + bi
    active, gelu_back = jax.vjp(exact_gelu, inner_act)
    active_low = active.astype(BF16)
    ffn_out = jnp.dot(active_low, wf, preferred_element_type=F32) + bf
    result, norm_two_back = jax.vjp(layer_norm, first_norm + ffn_out, gain_two, shift_two)

    upstream = grad_out.reshape(ROWS, 768).astype(F32)
    sum_grad, gain_two_grad, shift_two_grad = norm_two_back(upstream)
    ffn_grad = sum_grad.astype(BF16)
    bf_grad = jnp.sum(ffn_grad.astype(F32), axis=0)
    wf_grad = left_product(active_low, ffn_grad).astype(BF16)
    active_grad = right_product(ffn_grad, wf).astype(BF16)
    (inner_float,) = gelu_back(active_grad.astype(F32))
    inner_grad = inner_float.astype(BF16)
    bi_grad = jnp.sum(inner_grad.astype(F32), axis=0)
    wi_grad = left_product(first_low, inner_grad).astype(BF16)
    first_grad = sum_grad + right_product(inner_grad, wi)
    norm_grad, gain_one_grad, shift_one_grad = norm_one_back(first_grad)
    attn_grad = norm_grad.astype(BF16)
    bo_grad = jnp.sum(attn_grad.astype(F32), axis=0)
    wo_grad = left_product(context_low, attn_grad).astype(BF16)
    context_grad = right_product(attn_grad, wo).astype(BF16)
    grad4 = jnp.stack([context_grad[:, 192 * i : 192 * i + 192] for i in range(4)])
    back4, table_grad = attend_back(grad4, main, extra, probs)
    query_low, key_low, value_low = [
        jnp.concatenate([back4[i, :, lo : lo + 192] for i in range(4)], axis=1)
        for lo in (0, 192, 384)
    ]
    bq_grad = jnp.sum(query_low.astype(F32), axis=0)
    bv_grad = jnp.sum(value_low.astype(F32), axis=0)
    wq_grad = left_product(tokens, query_low).astype(BF16)
    wk_grad = left_product(tokens, key_low).astype(BF16)
    wv_grad = left_product(tokens, value_low).astype(BF16)
    input_grad = (
        norm_grad
        + right_product(query_low, wq)
        + right_product(key_low, wk)
        + right_product(value_low, wv)
    )
    vector_grads = jnp.stack(
        [
            bq_grad, bv_grad, bo_grad, gain_one_grad[0], shift_one_grad[0],
            bf_grad, gain_two_grad[0], shift_two_grad[0],
        ]
    )
    vector_grads = vector_grads.reshape(8, 4, 192).transpose(1, 0, 2).reshape(4, 1536)
    packed = jnp.concatenate([vector_grads, bi_grad.reshape(4, 768)], axis=1)
    packed = jnp.pad(packed.reshape(4, 3, 768), ((0, 0), (0, 13), (0, 0))).astype(BF16)
    sums, small_sum, table_sum, edge_sum = reduce_gradients(
        wq_grad, wk_grad, wv_grad, wo_grad, wi_grad, wf_grad, packed, table_grad.astype(BF16)
    )
    sums = sums.astype(F32)
    small_sum = small_sum[:3].reshape(2304)
    vecs = [small_sum[192 * i : 192 * i + 192] for i in range(8)]
    edge = jnp.pad(edge_sum.reshape(12, 16, TALL)[:, :1], ((0, 0), (0, 127), (0, 0)))
    table_total = jnp.where(
        f < 2,
        table_sum.reshape(12, 128, TALL),
        jnp.where(f == 2, edge, jnp.zeros_like(edge)),
    ).astype(F32)
    table_total = jnp.pad(table_total, ((0, 0), (0, 0), (0, 512 - TALL)))
    logit_grad = table_total * 2.0 * jax.nn.sigmoid(-doubled)
    return (
        result.astype(BF16).reshape(hidden_in.shape),
        input_grad.reshape(hidden_in.shape),
        sums[8],
        sums[9],
        sums[10],
        sums[11],
        vecs[0],
        vecs[1],
        vecs[2],
        vecs[3],
        vecs[4],
        jnp.concatenate([sums[4 + i] for i in range(4)], axis=1),
        small_sum[1536:],
        sums[0:4].reshape(768, 768),
        vecs[5],
        vecs[6],
        vecs[7],
        logit_grad,
    )


def on_device(ctx_size, fsdp_size, hidden_in, *rest):
    if (ctx_size, fsdp_size, hidden_in.shape) == (8, 4, (3, 64, 768)):
        return block_device(hidden_in, *rest)
    return general_device(hidden_in, *rest)


def solution(mesh):
    in_specs = (
        P("fsdp", "ctx", None),
        P("fsdp", "ctx"),
        P("fsdp", "ctx"),
        P("fsdp", None),
        P("fsdp", None),
        P("fsdp", None),
        P("fsdp", None),
        P("fsdp"),
        P("fsdp"),
        P("fsdp"),
        P("fsdp"),
        P("fsdp"),
        P("fsdp", None),
        P("fsdp"),
        P("fsdp", None),
        P("fsdp"),
        P("fsdp"),
        P("fsdp"),
        P(None, "fsdp", None),
        P(None, "fsdp", None),
        P("fsdp", "ctx", None),
    )
    out_specs = (
        P("fsdp", "ctx", None),
        P("fsdp", "ctx", None),
        P("fsdp", None),
        P("fsdp", None),
        P("fsdp", None),
        P("fsdp", None),
        P("fsdp"),
        P("fsdp"),
        P("fsdp"),
        P("fsdp"),
        P("fsdp"),
        P("fsdp", None),
        P("fsdp"),
        P("fsdp", None),
        P("fsdp"),
        P("fsdp"),
        P("fsdp"),
        P(None, "fsdp", None),
    )
    return jax.shard_map(
        functools.partial(on_device, mesh.shape["ctx"], mesh.shape["fsdp"]), mesh=mesh, in_specs=in_specs, out_specs=out_specs, check_vma=False
    )
```

```python
import functools

import jax
import jax.numpy as jnp
from jax import lax
from jax.experimental import pallas as pl
from jax.experimental.pallas import tpu as pltpu
from jax.sharding import PartitionSpec as P

H = 12
HD = 64
MSPAN = 512


NEGATIVE = -1e30
EPSILON = 1e-12


def layer_norm(hidden, gain_row, shift_row):
    average = jnp.mean(hidden, axis=-1, keepdims=True)
    centered = hidden - average
    variance = jnp.mean(centered * centered, axis=-1, keepdims=True)
    return centered * lax.rsqrt(variance + EPSILON) * gain_row + shift_row


def exact_gelu(inner_act):
    return jax.nn.gelu(inner_act, approximate=False)


def left_product(first_op, second_op):
    return lax.dot_general(
        first_op, second_op, (((0,), (0,)), ((), ())), preferred_element_type=jnp.float32
    )


def right_product(first_op, second_op):
    return lax.dot_general(
        first_op, second_op, (((1,), (1,)), ((), ())), preferred_element_type=jnp.float32
    )


def one_hot_rows(slot_values, width):
    return (slot_values[:, None] == jnp.arange(width, dtype=jnp.int32)[None, :]).astype(
        jnp.bfloat16
    )


def block_scores(queries, key_part, seg_local, seg_part, bias_part):
    key_heads = key_part.reshape(key_part.shape[0], H, HD)
    raw_scores = (
        jnp.einsum("shd,nhd->hsn", queries, key_heads, preferred_element_type=jnp.float32) * 0.125
    )
    same_doc = seg_local[:, None] == seg_part[None, :]
    return jnp.where(same_doc[None], raw_scores + bias_part.astype(jnp.float32), NEGATIVE)


def split_blocks(array_in, block_size):
    return array_in.reshape((array_in.shape[0] // block_size, block_size) + array_in.shape[1:])


def block_length():
    return 512


def make_blocks(full_keys, full_values, full_segment, full_slot):
    block_size = block_length()
    return (
        split_blocks(full_keys, block_size),
        split_blocks(full_values, block_size),
        split_blocks(full_segment, block_size),
        split_blocks(full_slot, block_size),
    )


def row_statistics(queries, seg_local, table_rows, blocks):
    rows = queries.shape[0]

    def advance(state_carry, key_block):
        key_part, value_part, seg_part, slot_part = key_block

        def compute(pair):
            row_top, row_total = pair
            bias_part = jnp.einsum(
                "hsa,na->hsn",
                table_rows,
                one_hot_rows(slot_part, MSPAN),
                preferred_element_type=jnp.float32,
            ).astype(jnp.bfloat16)
            scores = block_scores(queries, key_part, seg_local, seg_part, bias_part)
            new_top = jnp.maximum(row_top, jnp.max(scores, axis=-1))
            row_total = row_total * jnp.exp(row_top - new_top) + jnp.sum(
                jnp.exp(scores - new_top[..., None]), axis=-1
            )
            return ((new_top, row_total), bias_part)

        return compute(state_carry)

    start_state = (jnp.full((H, rows), NEGATIVE, jnp.float32), jnp.zeros((H, rows), jnp.float32))
    (row_top, row_total), bias_blocks = lax.scan(advance, start_state, blocks)
    return (row_top + jnp.log(row_total), bias_blocks)


def attention_output(queries, seg_local, blocks, bias_blocks, log_total):
    rows = queries.shape[0]

    def advance(accumulated, items):
        (key_part, value_part, seg_part, slot_part), bias_part = items

        def compute(current):
            scores = block_scores(queries, key_part, seg_local, seg_part, bias_part)
            soft_weights = jnp.exp(scores - log_total[..., None]).astype(jnp.bfloat16)
            value_heads = value_part.reshape(value_part.shape[0], H, HD)
            return current + jnp.einsum(
                "hsn,nhd->shd", soft_weights, value_heads, preferred_element_type=jnp.float32
            )

        return (compute(accumulated), None)

    context, _ = lax.scan(advance, jnp.zeros((rows, H, HD), jnp.float32), (blocks, bias_blocks))
    return context


def attention_backward(queries, seg_local, blocks, bias_blocks, log_total, context_grad, row_delta):
    rows = queries.shape[0]

    def advance(state_carry, items):
        (key_part, value_part, seg_part, slot_part), bias_part = items
        key_count = key_part.shape[0]

        def compute(operand):
            query_acc, slot_acc = operand
            scores = block_scores(queries, key_part, seg_local, seg_part, bias_part)
            soft_float = jnp.exp(scores - log_total[..., None])
            key_heads = key_part.reshape(key_count, H, HD)
            value_heads = value_part.reshape(key_count, H, HD)
            weight_grad = jnp.einsum(
                "shd,nhd->hsn", context_grad, value_heads, preferred_element_type=jnp.float32
            )
            score_grad = (soft_float * (weight_grad - row_delta[..., None])).astype(jnp.bfloat16)
            query_acc = (
                query_acc
                + jnp.einsum(
                    "hsn,nhd->shd", score_grad, key_heads, preferred_element_type=jnp.float32
                )
                * 0.125
            )
            slot_acc = slot_acc + jnp.einsum(
                "hsn,na->hsa",
                score_grad,
                one_hot_rows(slot_part, MSPAN),
                preferred_element_type=jnp.float32,
            )
            key_block_grad = (
                jnp.einsum("hsn,shd->nhd", score_grad, queries, preferred_element_type=jnp.float32)
                * 0.125
            )
            value_block_grad = jnp.einsum(
                "hsn,shd->nhd",
                soft_float.astype(jnp.bfloat16),
                context_grad,
                preferred_element_type=jnp.float32,
            )
            return ((query_acc, slot_acc), (key_block_grad, value_block_grad))

        return compute(state_carry)

    start_state = (jnp.zeros((rows, H, HD), jnp.float32), jnp.zeros((H, rows, MSPAN), jnp.float32))
    (query_acc, slot_acc), block_grads = lax.scan(advance, start_state, (blocks, bias_blocks))
    key_grads, value_grads = block_grads
    full_len = key_grads.shape[0] * key_grads.shape[1]
    return (
        query_acc,
        slot_acc,
        key_grads.reshape(full_len, H * HD),
        value_grads.reshape(full_len, H * HD),
    )


def general_device(
    hidden_in,
    segment_ids,
    doc_positions,
    w_query,
    w_key,
    w_value,
    w_out,
    b_query,
    b_value,
    b_out,
    ln1_gain,
    ln1_shift,
    w_inter,
    b_inter,
    w_final,
    b_final,
    ln2_gain,
    ln2_shift,
    mask_logits,
    mask_noise,
    grad_out,
):
    table_part = jax.nn.log_sigmoid(2.0 * (mask_logits + mask_noise)).astype(jnp.bfloat16)
    (
        wq_full,
        wk_full,
        wv_full,
        wo_full,
        wi_full,
        wf_full,
        bq_full,
        bv_full,
        bo_full,
        bi_full,
        bf_full,
        gain_one,
        shift_one,
        gain_two,
        shift_two,
        table_full,
    ) = (
        lax.all_gather(w_query, "fsdp", axis=0, tiled=True),
        lax.all_gather(w_key, "fsdp", axis=0, tiled=True),
        lax.all_gather(w_value, "fsdp", axis=0, tiled=True),
        lax.all_gather(w_out, "fsdp", axis=0, tiled=True),
        lax.all_gather(w_inter, "fsdp", axis=0, tiled=True),
        lax.all_gather(w_final, "fsdp", axis=0, tiled=True),
        lax.all_gather(b_query, "fsdp", axis=0, tiled=True),
        lax.all_gather(b_value, "fsdp", axis=0, tiled=True),
        lax.all_gather(b_out, "fsdp", axis=0, tiled=True),
        lax.all_gather(b_inter, "fsdp", axis=0, tiled=True),
        lax.all_gather(b_final, "fsdp", axis=0, tiled=True),
        lax.all_gather(ln1_gain, "fsdp", axis=0, tiled=True),
        lax.all_gather(ln1_shift, "fsdp", axis=0, tiled=True),
        lax.all_gather(ln2_gain, "fsdp", axis=0, tiled=True),
        lax.all_gather(ln2_shift, "fsdp", axis=0, tiled=True),
        lax.all_gather(table_part, "fsdp", axis=1, tiled=True),
    )
    bq_full, bv_full, bo_full = (
        bq_full.astype(jnp.float32),
        bv_full.astype(jnp.float32),
        bo_full.astype(jnp.float32),
    )
    bi_full, bf_full = (bi_full.astype(jnp.float32), bf_full.astype(jnp.float32))
    gain_one, shift_one = (gain_one.astype(jnp.float32), shift_one.astype(jnp.float32))
    gain_two, shift_two = (gain_two.astype(jnp.float32), shift_two.astype(jnp.float32))
    micro_count = hidden_in.shape[0]
    rows = hidden_in.shape[1]
    saved = []
    outputs_list = []
    for micro_batch in range(micro_count):
        tokens = hidden_in[micro_batch]
        seg_local = segment_ids[micro_batch]
        slot_local = doc_positions[micro_batch] % MSPAN
        queries_flat = (
            jnp.dot(tokens, wq_full, preferred_element_type=jnp.float32) + bq_full
        ).astype(jnp.bfloat16)
        keys_local = jnp.dot(tokens, wk_full, preferred_element_type=jnp.float32).astype(
            jnp.bfloat16
        )
        values_local = (
            jnp.dot(tokens, wv_full, preferred_element_type=jnp.float32) + bv_full
        ).astype(jnp.bfloat16)
        gathered = (
            lax.all_gather(keys_local, "ctx", axis=0, tiled=True),
            lax.all_gather(values_local, "ctx", axis=0, tiled=True),
            lax.all_gather(seg_local, "ctx", axis=0, tiled=True),
            lax.all_gather(slot_local, "ctx", axis=0, tiled=True),
        )
        blocks = make_blocks(*gathered)
        queries = queries_flat.reshape(rows, H, HD)
        table_rows = table_full[:, slot_local, :]
        log_total, bias_blocks = row_statistics(queries, seg_local, table_rows, blocks)
        context = attention_output(queries, seg_local, blocks, bias_blocks, log_total)
        context_low = context.reshape(rows, H * HD).astype(jnp.bfloat16)
        attn_out = jnp.dot(context_low, wo_full, preferred_element_type=jnp.float32) + bo_full
        first_norm, norm_one_back = jax.vjp(
            layer_norm, tokens.astype(jnp.float32) + attn_out, gain_one, shift_one
        )
        first_low = first_norm.astype(jnp.bfloat16)
        inner_act = jnp.dot(first_low, wi_full, preferred_element_type=jnp.float32) + bi_full
        active, gelu_back = jax.vjp(exact_gelu, inner_act)
        active_low = active.astype(jnp.bfloat16)
        ffn_out = jnp.dot(active_low, wf_full, preferred_element_type=jnp.float32) + bf_full
        result, norm_two_back = jax.vjp(layer_norm, first_norm + ffn_out, gain_two, shift_two)
        outputs_list.append(result.astype(jnp.bfloat16))
        kept_blocks = blocks
        saved.append(
            (
                tokens,
                seg_local,
                slot_local,
                queries,
                keys_local,
                values_local,
                log_total,
                bias_blocks,
                context,
                context_low,
                first_low,
                active_low,
                norm_one_back,
                gelu_back,
                norm_two_back,
                kept_blocks,
            )
        )
    zeros_square = jnp.zeros((H * HD, H * HD), jnp.float32)
    wq_grad, wk_grad, wv_grad, wo_grad = (zeros_square, zeros_square, zeros_square, zeros_square)
    wi_grad = jnp.zeros(wi_full.shape, jnp.float32)
    wf_grad = jnp.zeros(wf_full.shape, jnp.float32)
    zeros_row = jnp.zeros((H * HD,), jnp.float32)
    bq_grad, bv_grad, bo_grad, bf_grad = (zeros_row, zeros_row, zeros_row, zeros_row)
    gain_one_grad, shift_one_grad, gain_two_grad, shift_two_grad = (
        zeros_row,
        zeros_row,
        zeros_row,
        zeros_row,
    )
    bi_grad = jnp.zeros(bi_full.shape, jnp.float32)
    table_grad = jnp.zeros(table_full.shape, jnp.float32)
    input_grads = []
    for micro_batch in range(micro_count):
        (
            tokens,
            seg_local,
            slot_local,
            queries,
            keys_local,
            values_local,
            log_total,
            bias_blocks,
            context,
            context_low,
            first_low,
            active_low,
            norm_one_back,
            gelu_back,
            norm_two_back,
            kept_blocks,
        ) = saved[micro_batch]
        upstream = grad_out[micro_batch].astype(jnp.float32)
        sum_grad, gain_part, shift_part = norm_two_back(upstream)
        gain_two_grad = gain_two_grad + gain_part
        shift_two_grad = shift_two_grad + shift_part
        ffn_grad = sum_grad.astype(jnp.bfloat16)
        bf_grad = bf_grad + jnp.sum(ffn_grad.astype(jnp.float32), axis=0)
        wf_grad = wf_grad + left_product(active_low, ffn_grad)
        active_grad = right_product(ffn_grad, wf_full).astype(jnp.bfloat16)
        (inner_float,) = gelu_back(active_grad.astype(jnp.float32))
        inner_grad = inner_float.astype(jnp.bfloat16)
        bi_grad = bi_grad + jnp.sum(inner_grad.astype(jnp.float32), axis=0)
        wi_grad = wi_grad + left_product(first_low, inner_grad)
        first_grad = sum_grad + right_product(inner_grad, wi_full)
        norm_grad, gain_part, shift_part = norm_one_back(first_grad)
        gain_one_grad = gain_one_grad + gain_part
        shift_one_grad = shift_one_grad + shift_part
        attn_grad = norm_grad.astype(jnp.bfloat16)
        bo_grad = bo_grad + jnp.sum(attn_grad.astype(jnp.float32), axis=0)
        wo_grad = wo_grad + left_product(context_low, attn_grad)
        context_grad_flat = right_product(attn_grad, wo_full).astype(jnp.bfloat16)
        context_grad = context_grad_flat.reshape(rows, H, HD)
        row_delta = jnp.einsum("shd,shd->hs", context_grad.astype(jnp.float32), context)
        blocks = kept_blocks
        query_acc, slot_acc, key_full_grad, value_full_grad = attention_backward(
            queries, seg_local, blocks, bias_blocks, log_total, context_grad, row_delta
        )
        key_share, value_share = (
            lax.psum_scatter(
                key_full_grad.astype(jnp.bfloat16), "ctx", scatter_dimension=0, tiled=True
            ).astype(jnp.float32),
            lax.psum_scatter(
                value_full_grad.astype(jnp.bfloat16), "ctx", scatter_dimension=0, tiled=True
            ).astype(jnp.float32),
        )
        table_grad = table_grad.at[:, slot_local, :].add(slot_acc)
        query_low = query_acc.reshape(rows, H * HD).astype(jnp.bfloat16)
        key_low = key_share.astype(jnp.bfloat16)
        value_low = value_share.astype(jnp.bfloat16)
        bq_grad = bq_grad + jnp.sum(query_low.astype(jnp.float32), axis=0)
        bv_grad = bv_grad + jnp.sum(value_low.astype(jnp.float32), axis=0)
        wq_grad = wq_grad + left_product(tokens, query_low)
        wk_grad = wk_grad + left_product(tokens, key_low)
        wv_grad = wv_grad + left_product(tokens, value_low)
        input_grads.append(
            norm_grad
            + right_product(query_low, wq_full)
            + right_product(key_low, wk_full)
            + right_product(value_low, wv_full)
        )
    shares = (
        lax.psum_scatter(
            wq_grad.astype(jnp.bfloat16), "fsdp", scatter_dimension=0, tiled=True
        ).astype(jnp.float32),
        lax.psum_scatter(
            wk_grad.astype(jnp.bfloat16), "fsdp", scatter_dimension=0, tiled=True
        ).astype(jnp.float32),
        lax.psum_scatter(
            wv_grad.astype(jnp.bfloat16), "fsdp", scatter_dimension=0, tiled=True
        ).astype(jnp.float32),
        lax.psum_scatter(
            wo_grad.astype(jnp.bfloat16), "fsdp", scatter_dimension=0, tiled=True
        ).astype(jnp.float32),
        lax.psum_scatter(
            bq_grad.astype(jnp.bfloat16), "fsdp", scatter_dimension=0, tiled=True
        ).astype(jnp.float32),
        lax.psum_scatter(
            bv_grad.astype(jnp.bfloat16), "fsdp", scatter_dimension=0, tiled=True
        ).astype(jnp.float32),
        lax.psum_scatter(
            bo_grad.astype(jnp.bfloat16), "fsdp", scatter_dimension=0, tiled=True
        ).astype(jnp.float32),
        lax.psum_scatter(
            gain_one_grad.astype(jnp.bfloat16), "fsdp", scatter_dimension=0, tiled=True
        ).astype(jnp.float32),
        lax.psum_scatter(
            shift_one_grad.astype(jnp.bfloat16), "fsdp", scatter_dimension=0, tiled=True
        ).astype(jnp.float32),
        lax.psum_scatter(
            wi_grad.astype(jnp.bfloat16), "fsdp", scatter_dimension=0, tiled=True
        ).astype(jnp.float32),
        lax.psum_scatter(
            bi_grad.astype(jnp.bfloat16), "fsdp", scatter_dimension=0, tiled=True
        ).astype(jnp.float32),
        lax.psum_scatter(
            wf_grad.astype(jnp.bfloat16), "fsdp", scatter_dimension=0, tiled=True
        ).astype(jnp.float32),
        lax.psum_scatter(
            bf_grad.astype(jnp.bfloat16), "fsdp", scatter_dimension=0, tiled=True
        ).astype(jnp.float32),
        lax.psum_scatter(
            gain_two_grad.astype(jnp.bfloat16), "fsdp", scatter_dimension=0, tiled=True
        ).astype(jnp.float32),
        lax.psum_scatter(
            shift_two_grad.astype(jnp.bfloat16), "fsdp", scatter_dimension=0, tiled=True
        ).astype(jnp.float32),
        lax.psum_scatter(
            table_grad.astype(jnp.bfloat16), "fsdp", scatter_dimension=1, tiled=True
        ).astype(jnp.float32),
    )
    totals = (
        lax.psum(shares[0].astype(jnp.bfloat16), "ctx").astype(jnp.float32),
        lax.psum(shares[1].astype(jnp.bfloat16), "ctx").astype(jnp.float32),
        lax.psum(shares[2].astype(jnp.bfloat16), "ctx").astype(jnp.float32),
        lax.psum(shares[3].astype(jnp.bfloat16), "ctx").astype(jnp.float32),
        lax.psum(shares[4].astype(jnp.bfloat16), "ctx").astype(jnp.float32),
        lax.psum(shares[5].astype(jnp.bfloat16), "ctx").astype(jnp.float32),
        lax.psum(shares[6].astype(jnp.bfloat16), "ctx").astype(jnp.float32),
        lax.psum(shares[7].astype(jnp.bfloat16), "ctx").astype(jnp.float32),
        lax.psum(shares[8].astype(jnp.bfloat16), "ctx").astype(jnp.float32),
        lax.psum(shares[9].astype(jnp.bfloat16), "ctx").astype(jnp.float32),
        lax.psum(shares[10].astype(jnp.bfloat16), "ctx").astype(jnp.float32),
        lax.psum(shares[11].astype(jnp.bfloat16), "ctx").astype(jnp.float32),
        lax.psum(shares[12].astype(jnp.bfloat16), "ctx").astype(jnp.float32),
        lax.psum(shares[13].astype(jnp.bfloat16), "ctx").astype(jnp.float32),
        lax.psum(shares[14].astype(jnp.bfloat16), "ctx").astype(jnp.float32),
        lax.psum(shares[15].astype(jnp.bfloat16), "ctx").astype(jnp.float32),
    )
    (
        wq_total,
        wk_total,
        wv_total,
        wo_total,
        bq_total,
        bv_total,
        bo_total,
        gain_one_total,
        shift_one_total,
        wi_total,
        bi_total,
        wf_total,
        bf_total,
        gain_two_total,
        shift_two_total,
        table_total,
    ) = totals
    logit_grad = table_total * 2.0 * jax.nn.sigmoid(-2.0 * (mask_logits + mask_noise))
    return (
        jnp.stack(outputs_list),
        jnp.stack(input_grads),
        wq_total,
        wk_total,
        wv_total,
        wo_total,
        bq_total,
        bv_total,
        bo_total,
        gain_one_total,
        shift_one_total,
        wi_total,
        bi_total,
        wf_total,
        bf_total,
        gain_two_total,
        shift_two_total,
        logit_grad,
    )


MESH = pl.DeviceIdType.MESH
BF16 = jnp.bfloat16
F32 = jnp.float32
ROWS = 192
TALL = 272


def place():
    c = lax.axis_index("ctx")
    f = lax.axis_index("fsdp")
    return (c // 2, c % 2, f // 2, f % 2)


def device(z, x, y, k):
    return {"ctx": z * 2 + x, "fsdp": y * 2 + k}


def send(src, dst, send_sem, recv_sem, target):
    return pltpu.make_async_remote_copy(
        src_ref=src,
        dst_ref=dst,
        send_sem=send_sem,
        recv_sem=recv_sem,
        device_id=target,
        device_id_type=MESH,
    )


def meet(targets):
    barrier = pltpu.get_barrier_semaphore()
    for target in targets:
        pl.semaphore_signal(barrier, inc=1, device_id=target, device_id_type=MESH)
    pl.semaphore_wait(barrier, len(targets))


def any_spec():
    return pl.BlockSpec(memory_space=pl.ANY)


def vmem_spec():
    return pl.BlockSpec(memory_space=pltpu.VMEM)


def gather_pieces():
    pieces = []
    for array in range(4):
        pieces.append((array, 0, 192, 0, 768))
    for part in range(2):
        pieces.append((4, 0, 192, 1536 * part, 1536))
    for part in range(4):
        pieces.append((5, 192 * part, 192, 0, 768))
    return pieces


def gather_plan(ins, table, small, outs, table_out, small_out, sems):
    ss, rs, ls, ss_small, rs_small = sems
    z, x, y, k = place()
    mine = y * 2 + k
    over = (1 - y) * 2 + k
    core = device(z, x, y, 1 - k)
    ynb = device(z, x, 1 - y, k)
    diag = device(z, x, 1 - y, 1 - k)
    xnb = device(z, 1 - x, y, k)
    pieces = gather_pieces()

    def source(n, half):
        if n == len(pieces):
            heads = table.at[pl.ds(3 * z, 3)]
            return heads if half is None else heads.at[:, pl.ds(64 * half, 64)]
        a, r0, rn, c0, cn = pieces[n]
        if half is None:
            return ins[a].at[pl.ds(r0, rn), pl.ds(c0, cn)]
        return ins[a].at[pl.ds(r0 + (rn // 2) * half, rn // 2), pl.ds(c0, cn)]

    def target(n, owner, half):
        if n == len(pieces):
            if half is None:
                return table_out.at[:, pl.ds(128 * owner, 128)]
            return table_out.at[:, pl.ds(128 * owner + 64 * half, 64)]
        a, r0, rn, c0, cn = pieces[n]
        base = ins[a].shape[0] * owner + r0
        if half is None:
            return outs[a].at[pl.ds(base, rn), pl.ds(c0, cn)]
        return outs[a].at[pl.ds(base + (rn // 2) * half, rn // 2), pl.ds(c0, cn)]

    plan = []
    for n in range(len(pieces) + 1):
        whole = source(n, None)
        kept = target(n, mine, None)
        here = target(n, over, x)
        there = target(n, over, 1 - x)
        plan.append(
            {
                "own": pltpu.make_async_copy(whole, kept, ls.at[n]),
                "core": send(whole, kept, ss.at[n, 0], rs.at[n, 0], core),
                "y": send(source(n, x), target(n, mine, x), ss.at[n, 1], rs.at[n, 1], ynb),
                "x": send(here, here, ss.at[n, 2], rs.at[n, 2], xnb),
                "core_y": send(here, here, ss.at[n, 3], rs.at[n, 3], core),
                "core_x": send(there, there, ss.at[n, 4], rs.at[n, 4], core),
            }
        )
    rows = small_out.at[mine]
    smalls = [
        send(small, rows, ss_small.at[i], rs_small.at[i], peer)
        for i, peer in enumerate((core, ynb, diag))
    ]
    own_small = pltpu.make_async_copy(small, rows, ls.at[len(pieces) + 1])
    return (plan, smalls, own_small)


def forward_y(copies):
    copies["y"].wait_recv()
    copies["x"].start()
    copies["core_y"].start()


def forward_x(copies):
    copies["x"].wait_recv()
    copies["core_x"].start()


def arrive(copies):
    copies["own"].wait()
    copies["core"].wait_recv()
    copies["core_y"].wait_recv()
    copies["core_x"].wait_recv()


def settle(copies):
    for name in ("core", "y", "x", "core_y", "core_x"):
        copies[name].wait_send()


def ctx_peers():
    c = lax.axis_index("ctx")
    return [{"ctx": lax.rem(c + i, 8)} for i in range(1, 8)]


def to_groups(c, main, extra, main_slot, extra_slot, sems):
    ms, mr, es, er, lsem = sems
    group = c // 4
    for zz in range(4):
        dest = zz * 2 + group

        @pl.when(dest != c)
        def _():
            send(
                main.at[zz], main_slot.at[c % 4], ms.at[zz], mr.at[c % 4], {"ctx": dest}
            ).start()

        @pl.when(dest == c)
        def _():
            pltpu.make_async_copy(main.at[zz], main_slot.at[c % 4], lsem.at[0]).start()

        @pl.when((c == 4) & (zz * 2 != c))
        def _():
            send(extra.at[zz], extra_slot, es.at[zz], er, {"ctx": zz * 2}).start()

        @pl.when((c == 4) & (zz * 2 == c))
        def _():
            pltpu.make_async_copy(extra.at[zz], extra_slot, lsem.at[1]).start()


def to_groups_wait(c, main, extra, main_slot, extra_slot, sems):
    ms, mr, es, er, lsem = sems
    group = c // 4
    x = c % 2
    for j in range(4):

        @pl.when(4 * x + j != c)
        def _():
            send(main.at[0], main_slot.at[j], ms.at[0], mr.at[j], {"ctx": 0}).wait_recv()

        @pl.when(4 * x + j == c)
        def _():
            pltpu.make_async_copy(main.at[0], main_slot.at[j], lsem.at[0]).wait()

    @pl.when((x == 0) & (c != 4))
    def _():
        send(extra.at[0], extra_slot, es.at[0], er, {"ctx": 0}).wait_recv()

    @pl.when(c == 4)
    def _():
        pltpu.make_async_copy(extra.at[0], extra_slot, lsem.at[1]).wait()

    for zz in range(4):
        dest = zz * 2 + group

        @pl.when(dest != c)
        def _():
            send(main.at[zz], main_slot.at[0], ms.at[zz], mr.at[0], {"ctx": dest}).wait_send()

        @pl.when((c == 4) & (zz * 2 != c))
        def _():
            send(extra.at[zz], extra_slot, es.at[zz], er, {"ctx": zz * 2}).wait_send()


def to_owners(c, main, extra, main_slot, extra_slot, sems):
    ms, mr, es, er, lsem = sems
    z = c // 2
    x = c % 2
    for j in range(4):
        dest = 4 * x + j

        @pl.when(dest != c)
        def _():
            send(main.at[j], main_slot.at[z], ms.at[j], mr.at[z], {"ctx": dest}).start()

        @pl.when(dest == c)
        def _():
            pltpu.make_async_copy(main.at[j], main_slot.at[z], lsem.at[0]).start()

    @pl.when((x == 0) & (c != 4))
    def _():
        send(extra, extra_slot.at[z], es, er.at[z], {"ctx": 4}).start()

    @pl.when(c == 4)
    def _():
        pltpu.make_async_copy(extra, extra_slot.at[z], lsem.at[1]).start()


def to_owners_wait(c, main, extra, main_slot, extra_slot, sems):
    ms, mr, es, er, lsem = sems
    x = c % 2
    group = c // 4
    for zz in range(4):

        @pl.when(zz * 2 + group != c)
        def _():
            send(main.at[0], main_slot.at[zz], ms.at[0], mr.at[zz], {"ctx": 0}).wait_recv()

        @pl.when(zz * 2 + group == c)
        def _():
            pltpu.make_async_copy(main.at[0], main_slot.at[zz], lsem.at[0]).wait()

        @pl.when((c == 4) & (zz * 2 != c))
        def _():
            send(extra, extra_slot.at[zz], es, er.at[zz], {"ctx": 0}).wait_recv()

        @pl.when((c == 4) & (zz * 2 == c))
        def _():
            pltpu.make_async_copy(extra, extra_slot.at[zz], lsem.at[1]).wait()

    for j in range(4):
        dest = 4 * x + j

        @pl.when(dest != c)
        def _():
            send(main.at[j], main_slot.at[0], ms.at[j], mr.at[0], {"ctx": dest}).wait_send()

    @pl.when((x == 0) & (c != 4))
    def _():
        send(extra, extra_slot.at[0], es, er.at[0], {"ctx": 4}).wait_send()


def exchange_sems():
    return [
        pltpu.SemaphoreType.DMA((4,)),
        pltpu.SemaphoreType.DMA((4,)),
        pltpu.SemaphoreType.DMA((4,)),
        pltpu.SemaphoreType.DMA,
        pltpu.SemaphoreType.DMA((2,)),
    ]


def return_sems():
    return [
        pltpu.SemaphoreType.DMA((4,)),
        pltpu.SemaphoreType.DMA((4,)),
        pltpu.SemaphoreType.DMA,
        pltpu.SemaphoreType.DMA((4,)),
        pltpu.SemaphoreType.DMA((2,)),
    ]


def dot_nn(a, b):
    return lax.dot_general(a, b, (((1,), (0,)), ((), ())), preferred_element_type=F32)


def dot_nt(a, b):
    return lax.dot_general(a, b, (((1,), (1,)), ((), ())), preferred_element_type=F32)


def dot_tn(a, b):
    return lax.dot_general(a, b, (((0,), (0,)), ((), ())), preferred_element_type=F32)


def group_rows(main, extra, s, lo, width):
    top = main[:, pl.ds(64 * s, 64), lo : lo + width].reshape(256, width)
    return jnp.concatenate([top, extra[pl.ds(16 * s, 16), lo : lo + width]], axis=0)


def place_masks(main, extra, s, x):
    marks = group_rows(main, extra, s, 576, 64).astype(F32)
    segment = marks[:, 0:1]
    slot = marks[:, 1:2]
    first = segment == 0.0
    valid = jnp.where(x == 0, jnp.where(first, 1.0, 0.0), jnp.where(first | (segment < 0.0), 0.0, 1.0))
    lanes = lax.broadcasted_iota(jnp.int32, (TALL, 128), 1).astype(F32)
    seg_hot = jnp.where((lanes == segment) & (valid > 0.0), 1.0, 0.0).astype(BF16)
    wide = lax.broadcasted_iota(jnp.int32, (TALL, TALL), 1).astype(F32)
    slot_hot = jnp.where((wide == slot) & (valid > 0.0), 1.0, 0.0).astype(BF16)
    return (slot_hot, dot_nt(seg_hot, seg_hot) > 0.5)


def attend_kernel(
    x_ref, marks, wq_in, wk_in, wv_in, wo_in, wi_in, wf_in, table_in, small_in,
    main, extra, probs, ctx_out, wq, wk, wv, wo, wi, wf, small,
    table, main_send, extra_send, ctx_send, ctx_extra, ctx_in, ctx_extra_in, *sems
):
    z, x, y, k = place()
    c = 2 * z + x
    there, back, gather_sems = (sems[:5], sems[5:10], sems[10:])
    meet(
        ctx_peers() + [device(z, x, y, 1 - k), device(z, x, 1 - y, k), device(z, x, 1 - y, 1 - k)]
    )
    plan, smalls, own_small = gather_plan(
        (wq_in, wk_in, wv_in, wo_in, wi_in, wf_in),
        table_in,
        small_in,
        (wq, wk, wv, wo, wi, wf),
        table,
        small,
        gather_sems,
    )
    last = len(plan) - 1
    for cp in smalls + [own_small]:
        cp.start()
    for n in [0, 1, 2, last] + list(range(3, last)):
        for name in ("y", "core", "own"):
            plan[n][name].start()
    for n in range(3):
        forward_y(plan[n])
    for n in range(3):
        forward_x(plan[n])
    own_small.wait()
    for cp in smalls:
        cp.wait_recv()

    def vector(i):
        return jnp.concatenate([small[f, i : i + 1, 0:192] for f in range(4)], axis=1).astype(F32)

    tokens = x_ref[...]
    arrive(plan[0])
    q = (dot_nn(tokens, wq[...]) + vector(0)).astype(BF16)
    arrive(plan[1])
    kk = dot_nn(tokens, wk[...]).astype(BF16)
    arrive(plan[2])
    v = (dot_nn(tokens, wv[...]) + vector(1)).astype(BF16)
    for zz in range(4):
        cols = slice(192 * zz, 192 * zz + 192)
        main_send[zz] = jnp.concatenate([q[:, cols], kk[:, cols], v[:, cols], marks[...]], axis=1)
        for s in range(3):
            extra_send[zz, 16 * s : 16 * s + 16] = main_send[zz, 64 * s : 64 * s + 16]

    @pl.when(x == 1)
    def _():
        extra[...] = jnp.full((48, 640), -1.0, BF16)

    to_groups(c, main_send, extra_send, main, extra, there)
    forward_y(plan[last])
    forward_y(plan[3])
    forward_x(plan[last])
    forward_x(plan[3])
    forward_y(plan[4])
    forward_y(plan[5])
    to_groups_wait(c, main_send, extra_send, main, extra, there)
    arrive(plan[last])

    def sequence(s):
        slot_hot, same = place_masks(main, extra, s, x)
        parts = []
        for h in range(3):
            qh = group_rows(main, extra, s, 64 * h, 64)
            kh = group_rows(main, extra, s, 192 + 64 * h, 64)
            vh = group_rows(main, extra, s, 384 + 64 * h, 64)
            picked = dot_nn(slot_hot, table[h, 0:TALL, 0:TALL]).astype(BF16)
            bias = dot_nt(picked, slot_hot)
            scores = jnp.where(same, dot_nt(qh, kh) * 0.125 + bias, NEGATIVE)
            top = jnp.max(scores, axis=1, keepdims=True)
            grown = jnp.where(same, jnp.exp(scores - top), 0.0)
            total = jnp.maximum(jnp.sum(grown, axis=1, keepdims=True), 1e-30)
            soft = (grown / total).astype(BF16)
            probs[3 * s + h] = soft
            parts.append(dot_nn(soft, vh).astype(BF16))
        whole = jnp.concatenate(parts, axis=1)
        for j in range(4):
            ctx_send[j, pl.ds(64 * s, 64)] = whole[64 * j : 64 * j + 64]
        ctx_extra[pl.ds(16 * s, 16)] = whole[256:272]

    sequence(0)
    forward_x(plan[4])
    forward_x(plan[5])
    forward_y(plan[6])
    forward_y(plan[7])
    sequence(1)
    forward_y(plan[8])
    forward_y(plan[9])
    forward_x(plan[6])
    sequence(2)
    to_owners(c, ctx_send, ctx_extra, ctx_in, ctx_extra_in, back)
    forward_x(plan[7])
    forward_x(plan[8])
    forward_x(plan[9])
    to_owners_wait(c, ctx_send, ctx_extra, ctx_in, ctx_extra_in, back)
    ctx_out[...] = ctx_in[...]

    @pl.when(c == 4)
    def _():
        for zz in range(4):
            for s in range(3):
                ctx_out[zz, 64 * s : 64 * s + 16] = (
                    ctx_in[zz, 64 * s : 64 * s + 16] + ctx_extra_in[zz, 16 * s : 16 * s + 16]
                )

    for n in range(3, last):
        arrive(plan[n])
    for copies in plan:
        settle(copies)
    for cp in smalls:
        cp.wait_send()


def attend(tokens, marks, arrays, table, small):
    count = len(gather_pieces()) + 1
    return pl.pallas_call(
        attend_kernel,
        out_shape=[
            jax.ShapeDtypeStruct((4, ROWS, 640), BF16),
            jax.ShapeDtypeStruct((48, 640), BF16),
            jax.ShapeDtypeStruct((9, TALL, TALL), BF16),
            jax.ShapeDtypeStruct((4, ROWS, 192), BF16),
        ]
        + [jax.ShapeDtypeStruct((a.shape[0] * 4, a.shape[1]), BF16) for a in arrays]
        + [jax.ShapeDtypeStruct((4, 16, 256), BF16)],
        in_specs=[vmem_spec()] * 2 + [any_spec()] * 8,
        out_specs=[vmem_spec()] * 11,
        scratch_shapes=[
            pltpu.VMEM((3, 512, 384), BF16),
            pltpu.VMEM((4, ROWS, 640), BF16),
            pltpu.VMEM((4, 48, 640), BF16),
            pltpu.VMEM((4, ROWS, 192), BF16),
            pltpu.VMEM((48, 192), BF16),
            pltpu.VMEM((4, ROWS, 192), BF16),
            pltpu.VMEM((4, 48, 192), BF16),
        ]
        + exchange_sems()
        + return_sems()
        + [
            pltpu.SemaphoreType.DMA((count, 5)),
            pltpu.SemaphoreType.DMA((count, 5)),
            pltpu.SemaphoreType.DMA((count + 1,)),
            pltpu.SemaphoreType.DMA((3,)),
            pltpu.SemaphoreType.DMA((3,)),
        ],
        compiler_params=pltpu.CompilerParams(
            collective_id=2, has_side_effects=True, vmem_limit_bytes=48 * 2**20
        ),
        name="attend",
    )(tokens, marks, *arrays, table, small)


def attend_back_kernel(
    grad, main, extra, probs,
    out, table_grad,
    grad_in, grad_extra, grad_extra_in, main_send, extra_send, main_in, extra_in, *sems
):
    c = lax.axis_index("ctx")
    x = c % 2
    there, back = (sems[:5], sems[5:])
    meet(ctx_peers())
    for zz in range(4):
        for s in range(3):
            grad_extra[zz, 16 * s : 16 * s + 16] = grad[zz, 64 * s : 64 * s + 16]

    @pl.when(x == 1)
    def _():
        grad_extra_in[...] = jnp.zeros((48, 192), BF16)

    to_groups(c, grad, grad_extra, grad_in, grad_extra_in, there)
    to_groups_wait(c, grad, grad_extra, grad_in, grad_extra_in, there)
    table_grad[...] = jnp.zeros((3, TALL, TALL), F32)

    def sequence(s, carry):
        slot_hot, _ = place_masks(main, extra, s, x)
        parts = [[], [], []]
        for h in range(3):
            qh = group_rows(main, extra, s, 64 * h, 64)
            kh = group_rows(main, extra, s, 192 + 64 * h, 64)
            vh = group_rows(main, extra, s, 384 + 64 * h, 64)
            gh = group_rows(grad_in, grad_extra_in, s, 64 * h, 64)
            soft = probs[3 * s + h]
            weight = soft.astype(F32)
            weight_grad = dot_nt(gh, vh)
            delta = jnp.sum(weight * weight_grad, axis=1, keepdims=True)
            score_grad = (weight * (weight_grad - delta)).astype(BF16)
            parts[0].append((dot_nn(score_grad, kh) * 0.125).astype(BF16))
            parts[1].append((dot_tn(score_grad, qh) * 0.125).astype(BF16))
            parts[2].append(dot_tn(soft, gh).astype(BF16))
            moved = dot_tn(slot_hot, score_grad)
            table_grad[h] += dot_nn(moved.astype(BF16), slot_hot)
        blank = jnp.zeros((TALL, 64), BF16)
        whole = jnp.concatenate(parts[0] + parts[1] + parts[2] + [blank], axis=1)
        for j in range(4):
            main_send[j, pl.ds(64 * s, 64)] = whole[64 * j : 64 * j + 64]
        extra_send[pl.ds(16 * s, 16)] = whole[256:272]
        return carry

    lax.fori_loop(0, 3, sequence, 0)
    to_owners(c, main_send, extra_send, main_in, extra_in, back)
    to_owners_wait(c, main_send, extra_send, main_in, extra_in, back)
    out[...] = main_in[...]

    @pl.when(c == 4)
    def _():
        for zz in range(4):
            for s in range(3):
                out[zz, 64 * s : 64 * s + 16] = (
                    main_in[zz, 64 * s : 64 * s + 16] + extra_in[zz, 16 * s : 16 * s + 16]
                )


def attend_back(grad, main, extra, probs):
    return pl.pallas_call(
        attend_back_kernel,
        out_shape=[
            jax.ShapeDtypeStruct((4, ROWS, 640), BF16),
            jax.ShapeDtypeStruct((3, TALL, TALL), F32),
        ],
        in_specs=[vmem_spec()] * 4,
        out_specs=[vmem_spec()] * 2,
        scratch_shapes=[
            pltpu.VMEM((4, ROWS, 192), BF16),
            pltpu.VMEM((4, 48, 192), BF16),
            pltpu.VMEM((48, 192), BF16),
            pltpu.VMEM((4, ROWS, 640), BF16),
            pltpu.VMEM((48, 640), BF16),
            pltpu.VMEM((4, ROWS, 640), BF16),
            pltpu.VMEM((4, 48, 640), BF16),
        ]
        + exchange_sems()
        + return_sems(),
        compiler_params=pltpu.CompilerParams(
            collective_id=3, has_side_effects=True, vmem_limit_bytes=48 * 2**20
        ),
        name="attend_back",
    )(grad, main, extra, probs)


def add_rows(out, left, right, rows, step):
    def body(i, carry):
        at = pl.ds(pl.multiple_of(i * step, step), step)
        out[at, :] = left[at, :] + right[at, :]
        return carry

    lax.fori_loop(0, rows // step, body, 0)


def reduce_kernel(
    gq, gk, gv, go, gi, gf, small, table,
    out, small_out, table_out, edge_out,
    r1, r2, r3, r4, s1, s2, s3, s4, t1, t2, t3, e1, e2, e3, e4,
    p1, q1, p2, q2, p3, q3, p4, q4, p5, q5, p6, q6,
    ps, qs, pt, qt, pe, qe, lsem
):
    z, x, y, k = place()
    core = device(z, x, y, 1 - k)
    ynb = device(z, x, 1 - y, k)
    xnb = device(z, 1 - x, y, k)
    znb = [lax.rem(z + i, 4) for i in (1, 2, 3)]
    zdev = [device(zz, x, y, k) for zz in znb]
    meet([core, ynb, xnb] + zdev)

    def block(n, owner):
        chunk, b = divmod(n, 4)
        if chunk == 0:
            return gf.at[pl.ds(768 * owner + 192 * b, 192)]
        if chunk == 1:
            return gi.at[pl.ds(192 * owner, 192), 768 * b : 768 * b + 768]
        return (gq, gk, gv, go)[b].at[pl.ds(192 * owner, 192)]

    first = {}
    for yy in range(2):
        cp = send(small.at[2 * yy + 1 - k], s1.at[yy], ps.at[yy], qs.at[yy], core)
        cp.start()
        first[12, yy] = cp
    ecore = send(table.at[:, pl.ds(256, 16)], e1, pe.at[0], qe.at[0], core)
    ecore.start()
    tcore = send(table.at[:, pl.ds(128 * (1 - k), 128)], t1, pt.at[0], qt.at[0], core)
    tcore.start()
    for n in range(12):
        for yy in range(2):
            cp = send(
                block(n, 2 * yy + 1 - k), r1.at[n, yy], p1.at[n, yy], q1.at[n, yy], core
            )
            cp.start()
            first[n, yy] = cp

    def add(left, right):
        return left + right

    second = {}
    third = {}
    fourth = {}

    def step_two(n):
        for yy in range(2):
            first[n, yy].wait_recv()
            add_rows(r1.at[n, yy], block(n, 2 * yy + k), r1.at[n, yy], 192, 32)
        second[n] = send(r1.at[n, 1 - y], r2.at[n], p2.at[n], q2.at[n], ynb)
        second[n].start()

    def step_three(n):
        second[n].wait_recv()
        add_rows(r2.at[n], r1.at[n, y], r2.at[n], 192, 32)
        third[n] = send(r2.at[n, pl.ds(96 * (1 - x), 96)], r3.at[n], p3.at[n], q3.at[n], xnb)
        third[n].start()

    def step_four(n):
        chunk, b = divmod(n, 4)
        third[n].wait_recv()
        add_rows(r3.at[n], r2.at[n, pl.ds(96 * x, 96)], r3.at[n], 96, 32)

        @pl.when(z != b)
        def _():
            send(
                r3.at[n], r4.at[chunk, z], p4.at[n], q4.at[chunk, z], device(b, x, y, k)
            ).start()

    def step_five(chunk):
        for i, zz in enumerate(znb):
            send(r3.at[0], r4.at[chunk, zz], p4.at[0], q4.at[chunk, zz], core).wait_recv()
        for b in range(4):

            @pl.when(z == b)
            def _():
                def body(i, carry):
                    at = pl.ds(pl.multiple_of(i * 32, 32), 32)
                    total = None
                    for zz in range(4):
                        if zz == b:
                            term = r3[4 * chunk + b, at, :].astype(F32)
                        else:
                            term = r4[chunk, zz, at, :].astype(F32)
                        total = term if total is None else total + term
                    to = pl.ds(pl.multiple_of(96 * x + i * 32, 32), 32)
                    out[4 * chunk + b, to, :] = total.astype(BF16)
                    return carry

                lax.fori_loop(0, 3, body, 0)

        here = out.at[4 * chunk + z, pl.ds(96 * x, 96)]
        for i in range(3):
            cp = send(here, here, p5.at[chunk, i], q5.at[chunk, z], zdev[i])
            cp.start()
            fourth[chunk, i] = cp
        cp = send(here, here, p6.at[chunk, 0], q6.at[chunk, z], xnb)
        cp.start()
        fourth[chunk, 3] = cp

    def step_six(chunk):
        for i, zz in enumerate(znb):
            there = out.at[4 * chunk + zz, pl.ds(96 * x, 96)]
            send(there, there, p5.at[chunk, i], q5.at[chunk, zz], core).wait_recv()
            cp = send(there, there, p6.at[chunk, 1 + i], q6.at[chunk, zz], xnb)
            cp.start()
            fourth[chunk, 4 + i] = cp

    def finish(chunk):
        for zz in range(4):
            there = out.at[4 * chunk + zz, pl.ds(96 * (1 - x), 96)]
            send(there, there, p6.at[chunk, 0], q6.at[chunk, zz], xnb).wait_recv()
        for i in range(7):
            fourth[chunk, i].wait_send()

    for yy in range(2):
        first[12, yy].wait_recv()
        s1[yy] = add(small[2 * yy + k], s1[yy])
    small_y = send(s1.at[1 - y], s2, ps.at[2], qs.at[2], ynb)
    small_y.start()
    tcore.wait_recv()
    for h in range(3):
        t1[h] = add(table[h, pl.ds(pl.multiple_of(128 * k, 128), 128), :], t1[h])
    ecore.wait_recv()
    e1[...] = add(table[:, 256:272], e1[...])
    edge_y = send(e1, e2, pe.at[1], qe.at[1], ynb)
    edge_y.start()

    @pl.when(y == 1)
    def _():
        send(t1, t2, pt.at[1], qt.at[1], ynb).start()

    for n in range(12):
        step_two(n)
    for n in range(12):
        step_three(n)
        if n >= 1:
            step_four(n - 1)
        if n == 2:
            small_y.wait_recv()
            s2[...] = add(s1[y], s2[...])
            small_x = send(s2, s3, ps.at[3], qs.at[3], xnb)
            small_x.start()
            edge_y.wait_recv()
            e2[...] = add(e1[...], e2[...])
            edge_x = send(e2, e3, pe.at[2], qe.at[2], xnb)
            edge_x.start()

            @pl.when(y == 0)
            def _():
                send(t1, t2, pt.at[1], qt.at[1], ynb).wait_recv()
                for h in range(3):
                    t2[h] = add(t1[h], t2[h])
                send(t2.at[:, pl.ds(64 * (1 - x), 64)], t3, pt.at[2], qt.at[2], xnb).start()

        if n == 4:
            small_x.wait_recv()
            s4[z] = add(s2[...], s3[...])
            edge_x.wait_recv()
            edge_out[z] = add(e2[...], e3[...])
            small_z = []
            for i in range(3):
                cp = send(s4.at[z], s4.at[z], ps.at[4 + i], qs.at[4 + z], zdev[i])
                cp.start()
                small_z.append(cp)
                cp = send(edge_out.at[z], edge_out.at[z], pe.at[3 + i], qe.at[3 + z], zdev[i])
                cp.start()
                small_z.append(cp)

            @pl.when(y == 0)
            def _():
                send(t2.at[:, pl.ds(0, 64)], t3, pt.at[2], qt.at[2], xnb).wait_recv()
                at = pl.ds(pl.multiple_of(64 * x, 64), 64)
                for h in range(3):
                    table_out[z, h, at, :] = add(t2[h, at, :], t3[h])
                here = table_out.at[z, :, pl.ds(64 * x, 64)]
                for i in range(3):
                    send(here, here, pt.at[3 + i], qt.at[3 + z], zdev[i]).start()
                send(here, here, pt.at[6], qt.at[7 + z], xnb).start()

        if n == 5:
            step_five(0)
        if n == 7:
            step_six(0)
        if n == 9:
            step_five(1)
        if n == 10:
            for zz in znb:
                send(s4.at[zz], s4.at[zz], ps.at[4], qs.at[4 + zz], core).wait_recv()
                send(edge_out.at[zz], edge_out.at[zz], pe.at[3], qe.at[3 + zz], core).wait_recv()
            small_out[...] = (
                (s4[0].astype(F32) + s4[1].astype(F32)) + (s4[2].astype(F32) + s4[3].astype(F32))
            )
            for cp in small_z:
                cp.wait_send()

            @pl.when(y == 0)
            def _():
                for i, zz in enumerate(znb):
                    there = table_out.at[zz, :, pl.ds(64 * x, 64)]
                    send(there, there, pt.at[3], qt.at[3 + zz], core).wait_recv()
                    send(there, there, pt.at[7 + i], qt.at[7 + zz], xnb).start()

            @pl.when(y == 1)
            def _():
                table_out[...] = jnp.zeros((4, 3, 128, TALL), BF16)

        if n == 11:
            step_six(1)
    step_four(11)
    step_five(2)
    step_six(2)
    for chunk in range(3):
        finish(chunk)

    @pl.when(y == 0)
    def _():
        for zz in range(4):
            there = table_out.at[zz, :, pl.ds(64 * (1 - x), 64)]
            send(there, there, pt.at[6], qt.at[7 + zz], xnb).wait_recv()
        here = table_out.at[z, :, pl.ds(64 * x, 64)]
        send(t2.at[:, pl.ds(0, 64)], t3, pt.at[2], qt.at[2], xnb).wait_send()
        for i in range(3):
            send(here, here, pt.at[3 + i], qt.at[3 + z], zdev[i]).wait_send()
        for i in range(4):
            send(here, here, pt.at[6 + i], qt.at[7 + z], xnb).wait_send()

    @pl.when(y == 1)
    def _():
        send(t1, t2, pt.at[1], qt.at[1], ynb).wait_send()

    for cp in (tcore, ecore, small_y, small_x, edge_y, edge_x):
        cp.wait_send()
    for cp in first.values():
        cp.wait_send()
    for n in range(12):
        second[n].wait_send()
        third[n].wait_send()

        @pl.when(z != n % 4)
        def _():
            send(r3.at[n], r4.at[n // 4, z], p4.at[n], q4.at[0, 0], core).wait_send()


def reduce_gradients(gq, gk, gv, go, gi, gf, small, table):
    dma = pltpu.SemaphoreType.DMA
    return pl.pallas_call(
        reduce_kernel,
        out_shape=[
            jax.ShapeDtypeStruct((12, 192, 768), BF16),
            jax.ShapeDtypeStruct((16, 768), F32),
            jax.ShapeDtypeStruct((4, 3, 128, TALL), BF16),
            jax.ShapeDtypeStruct((4, 3, 16, TALL), BF16),
        ],
        in_specs=[vmem_spec()] * 8,
        out_specs=[vmem_spec()] * 4,
        scratch_shapes=[
            pltpu.VMEM((12, 2, 192, 768), BF16),
            pltpu.VMEM((12, 192, 768), BF16),
            pltpu.VMEM((12, 96, 768), BF16),
            pltpu.VMEM((3, 4, 96, 768), BF16),
            pltpu.VMEM((2, 16, 768), BF16),
            pltpu.VMEM((16, 768), BF16),
            pltpu.VMEM((16, 768), BF16),
            pltpu.VMEM((4, 16, 768), BF16),
            pltpu.VMEM((3, 128, TALL), BF16),
            pltpu.VMEM((3, 128, TALL), BF16),
            pltpu.VMEM((3, 64, TALL), BF16),
            pltpu.VMEM((3, 16, TALL), BF16),
            pltpu.VMEM((3, 16, TALL), BF16),
            pltpu.VMEM((3, 16, TALL), BF16),
            pltpu.VMEM((3, 16, TALL), BF16),
            dma((12, 2)), dma((12, 2)),
            dma((12,)), dma((12,)),
            dma((12,)), dma((12,)),
            dma((12,)), dma((3, 4)),
            dma((3, 3)), dma((3, 4)),
            dma((3, 4)), dma((3, 4)),
            dma((8,)), dma((8,)),
            dma((12,)), dma((12,)),
            dma((8,)), dma((8,)),
            dma((2,)),
        ],
        compiler_params=pltpu.CompilerParams(
            collective_id=4, has_side_effects=True, vmem_limit_bytes=60 * 2**20
        ),
        name="reduce_gradients",
    )(gq, gk, gv, go, gi, gf, small, table)


def block_device(
    hidden_in, segment_ids, doc_positions,
    w_query, w_key, w_value, w_out, b_query, b_value, b_out, ln1_gain, ln1_shift,
    w_inter, b_inter, w_final, b_final, ln2_gain, ln2_shift,
    mask_logits, mask_noise, grad_out,
):
    f = lax.axis_index("fsdp")
    doubled = 2.0 * (mask_logits + mask_noise)
    table_part = jax.nn.log_sigmoid(doubled[:, :, :384]).astype(BF16)
    vectors = (b_query, b_value, b_out, ln1_gain, ln1_shift, b_final, ln2_gain, ln2_shift)
    small = jnp.concatenate([jnp.stack(vectors), b_inter.reshape(4, 192)], axis=0)
    small = jnp.pad(small, ((0, 4), (0, 64)))
    tokens = hidden_in.reshape(ROWS, 768)
    marks = jnp.stack(
        [segment_ids.reshape(ROWS), (doc_positions % MSPAN).reshape(ROWS)], axis=1
    ).astype(BF16)
    marks = jnp.pad(marks, ((0, 0), (0, 62)))
    main, extra, probs, ctx4, wq, wk, wv, wo, wi, wf, small_full = attend(
        tokens, marks, (w_query, w_key, w_value, w_out, w_inter, w_final), table_part, small
    )
    rows = small_full[:, :12, :192].astype(F32)
    bo, gain_one, shift_one, bf, gain_two, shift_two = [
        rows[:, i].reshape(1, 768) for i in range(2, 8)
    ]
    bi = rows[:, 8:12].reshape(1, 3072)
    context_low = jnp.concatenate([ctx4[i] for i in range(4)], axis=1)
    attn_out = jnp.dot(context_low, wo, preferred_element_type=F32) + bo
    first_norm, norm_one_back = jax.vjp(
        layer_norm, tokens.astype(F32) + attn_out, gain_one, shift_one
    )
    first_low = first_norm.astype(BF16)
    inner_act = jnp.dot(first_low, wi, preferred_element_type=F32) + bi
    active, gelu_back = jax.vjp(exact_gelu, inner_act)
    active_low = active.astype(BF16)
    ffn_out = jnp.dot(active_low, wf, preferred_element_type=F32) + bf
    result, norm_two_back = jax.vjp(layer_norm, first_norm + ffn_out, gain_two, shift_two)

    upstream = grad_out.reshape(ROWS, 768).astype(F32)
    sum_grad, gain_two_grad, shift_two_grad = norm_two_back(upstream)
    ffn_grad = sum_grad.astype(BF16)
    bf_grad = jnp.sum(ffn_grad.astype(F32), axis=0)
    wf_grad = left_product(active_low, ffn_grad).astype(BF16)
    active_grad = right_product(ffn_grad, wf).astype(BF16)
    (inner_float,) = gelu_back(active_grad.astype(F32))
    inner_grad = inner_float.astype(BF16)
    bi_grad = jnp.sum(inner_grad.astype(F32), axis=0)
    wi_grad = left_product(first_low, inner_grad).astype(BF16)
    first_grad = sum_grad + right_product(inner_grad, wi)
    norm_grad, gain_one_grad, shift_one_grad = norm_one_back(first_grad)
    attn_grad = norm_grad.astype(BF16)
    bo_grad = jnp.sum(attn_grad.astype(F32), axis=0)
    wo_grad = left_product(context_low, attn_grad).astype(BF16)
    context_grad = right_product(attn_grad, wo).astype(BF16)
    grad4 = jnp.stack([context_grad[:, 192 * i : 192 * i + 192] for i in range(4)])
    back4, table_grad = attend_back(grad4, main, extra, probs)
    query_low, key_low, value_low = [
        jnp.concatenate([back4[i, :, lo : lo + 192] for i in range(4)], axis=1)
        for lo in (0, 192, 384)
    ]
    bq_grad = jnp.sum(query_low.astype(F32), axis=0)
    bv_grad = jnp.sum(value_low.astype(F32), axis=0)
    wq_grad = left_product(tokens, query_low).astype(BF16)
    wk_grad = left_product(tokens, key_low).astype(BF16)
    wv_grad = left_product(tokens, value_low).astype(BF16)
    input_grad = (
        norm_grad
        + right_product(query_low, wq)
        + right_product(key_low, wk)
        + right_product(value_low, wv)
    )
    vector_grads = jnp.stack(
        [
            bq_grad, bv_grad, bo_grad, gain_one_grad[0], shift_one_grad[0],
            bf_grad, gain_two_grad[0], shift_two_grad[0],
        ]
    )
    vector_grads = vector_grads.reshape(8, 4, 192).transpose(1, 0, 2).reshape(4, 1536)
    packed = jnp.concatenate([vector_grads, bi_grad.reshape(4, 768)], axis=1)
    packed = jnp.pad(packed.reshape(4, 3, 768), ((0, 0), (0, 13), (0, 0))).astype(BF16)
    sums, small_sum, table_sum, edge_sum = reduce_gradients(
        wq_grad, wk_grad, wv_grad, wo_grad, wi_grad, wf_grad, packed, table_grad.astype(BF16)
    )
    sums = sums.astype(F32)
    small_sum = small_sum[:3].reshape(2304)
    vecs = [small_sum[192 * i : 192 * i + 192] for i in range(8)]
    edge = jnp.pad(edge_sum.reshape(12, 16, TALL)[:, :1], ((0, 0), (0, 127), (0, 0)))
    table_total = jnp.where(
        f < 2,
        table_sum.reshape(12, 128, TALL),
        jnp.where(f == 2, edge, jnp.zeros_like(edge)),
    ).astype(F32)
    table_total = jnp.pad(table_total, ((0, 0), (0, 0), (0, 512 - TALL)))
    logit_grad = table_total * 2.0 * jax.nn.sigmoid(-doubled)
    return (
        result.astype(BF16).reshape(hidden_in.shape),
        input_grad.reshape(hidden_in.shape),
        sums[8],
        sums[9],
        sums[10],
        sums[11],
        vecs[0],
        vecs[1],
        vecs[2],
        vecs[3],
        vecs[4],
        jnp.concatenate([sums[4 + i] for i in range(4)], axis=1),
        small_sum[1536:],
        sums[0:4].reshape(768, 768),
        vecs[5],
        vecs[6],
        vecs[7],
        logit_grad,
    )


def on_device(ctx_size, fsdp_size, hidden_in, *rest):
    if (ctx_size, fsdp_size, hidden_in.shape) == (8, 4, (3, 64, 768)):
        return block_device(hidden_in, *rest)
    return general_device(hidden_in, *rest)


def solution(mesh):
    in_specs = (
        P("fsdp", "ctx", None),
        P("fsdp", "ctx"),
        P("fsdp", "ctx"),
        P("fsdp", None),
        P("fsdp", None),
        P("fsdp", None),
        P("fsdp", None),
        P("fsdp"),
        P("fsdp"),
        P("fsdp"),
        P("fsdp"),
        P("fsdp"),
        P("fsdp", None),
        P("fsdp"),
        P("fsdp", None),
        P("fsdp"),
        P("fsdp"),
        P("fsdp"),
        P(None, "fsdp", None),
        P(None, "fsdp", None),
        P("fsdp", "ctx", None),
    )
    out_specs = (
        P("fsdp", "ctx", None),
        P("fsdp", "ctx", None),
        P("fsdp", None),
        P("fsdp", None),
        P("fsdp", None),
        P("fsdp", None),
        P("fsdp"),
        P("fsdp"),
        P("fsdp"),
        P("fsdp"),
        P("fsdp"),
        P("fsdp", None),
        P("fsdp"),
        P("fsdp", None),
        P("fsdp"),
        P("fsdp"),
        P("fsdp"),
        P(None, "fsdp", None),
    )
    return jax.shard_map(
        functools.partial(on_device, mesh.shape["ctx"], mesh.shape["fsdp"]), mesh=mesh, in_specs=in_specs, out_specs=out_specs, check_vma=False
    )
```

```python
import functools

import jax
import jax.numpy as jnp
from jax import lax
from jax.experimental import pallas as pl
from jax.experimental.pallas import tpu as pltpu
from jax.sharding import PartitionSpec as P

H = 12
HD = 64
MSPAN = 512


NEGATIVE = -1e30
EPSILON = 1e-12


def layer_norm(hidden, gain_row, shift_row):
    average = jnp.mean(hidden, axis=-1, keepdims=True)
    centered = hidden - average
    variance = jnp.mean(centered * centered, axis=-1, keepdims=True)
    return centered * lax.rsqrt(variance + EPSILON) * gain_row + shift_row


def exact_gelu(inner_act):
    return jax.nn.gelu(inner_act, approximate=False)


def left_product(first_op, second_op):
    return lax.dot_general(
        first_op, second_op, (((0,), (0,)), ((), ())), preferred_element_type=jnp.float32
    )


def right_product(first_op, second_op):
    return lax.dot_general(
        first_op, second_op, (((1,), (1,)), ((), ())), preferred_element_type=jnp.float32
    )


def one_hot_rows(slot_values, width):
    return (slot_values[:, None] == jnp.arange(width, dtype=jnp.int32)[None, :]).astype(
        jnp.bfloat16
    )


def block_scores(queries, key_part, seg_local, seg_part, bias_part):
    key_heads = key_part.reshape(key_part.shape[0], H, HD)
    raw_scores = (
        jnp.einsum("shd,nhd->hsn", queries, key_heads, preferred_element_type=jnp.float32) * 0.125
    )
    same_doc = seg_local[:, None] == seg_part[None, :]
    return jnp.where(same_doc[None], raw_scores + bias_part.astype(jnp.float32), NEGATIVE)


def split_blocks(array_in, block_size):
    return array_in.reshape((array_in.shape[0] // block_size, block_size) + array_in.shape[1:])


def block_length():
    return 512


def make_blocks(full_keys, full_values, full_segment, full_slot):
    block_size = block_length()
    return (
        split_blocks(full_keys, block_size),
        split_blocks(full_values, block_size),
        split_blocks(full_segment, block_size),
        split_blocks(full_slot, block_size),
    )


def row_statistics(queries, seg_local, table_rows, blocks):
    rows = queries.shape[0]

    def advance(state_carry, key_block):
        key_part, value_part, seg_part, slot_part = key_block

        def compute(pair):
            row_top, row_total = pair
            bias_part = jnp.einsum(
                "hsa,na->hsn",
                table_rows,
                one_hot_rows(slot_part, MSPAN),
                preferred_element_type=jnp.float32,
            ).astype(jnp.bfloat16)
            scores = block_scores(queries, key_part, seg_local, seg_part, bias_part)
            new_top = jnp.maximum(row_top, jnp.max(scores, axis=-1))
            row_total = row_total * jnp.exp(row_top - new_top) + jnp.sum(
                jnp.exp(scores - new_top[..., None]), axis=-1
            )
            return ((new_top, row_total), bias_part)

        return compute(state_carry)

    start_state = (jnp.full((H, rows), NEGATIVE, jnp.float32), jnp.zeros((H, rows), jnp.float32))
    (row_top, row_total), bias_blocks = lax.scan(advance, start_state, blocks)
    return (row_top + jnp.log(row_total), bias_blocks)


def attention_output(queries, seg_local, blocks, bias_blocks, log_total):
    rows = queries.shape[0]

    def advance(accumulated, items):
        (key_part, value_part, seg_part, slot_part), bias_part = items

        def compute(current):
            scores = block_scores(queries, key_part, seg_local, seg_part, bias_part)
            soft_weights = jnp.exp(scores - log_total[..., None]).astype(jnp.bfloat16)
            value_heads = value_part.reshape(value_part.shape[0], H, HD)
            return current + jnp.einsum(
                "hsn,nhd->shd", soft_weights, value_heads, preferred_element_type=jnp.float32
            )

        return (compute(accumulated), None)

    context, _ = lax.scan(advance, jnp.zeros((rows, H, HD), jnp.float32), (blocks, bias_blocks))
    return context


def attention_backward(queries, seg_local, blocks, bias_blocks, log_total, context_grad, row_delta):
    rows = queries.shape[0]

    def advance(state_carry, items):
        (key_part, value_part, seg_part, slot_part), bias_part = items
        key_count = key_part.shape[0]

        def compute(operand):
            query_acc, slot_acc = operand
            scores = block_scores(queries, key_part, seg_local, seg_part, bias_part)
            soft_float = jnp.exp(scores - log_total[..., None])
            key_heads = key_part.reshape(key_count, H, HD)
            value_heads = value_part.reshape(key_count, H, HD)
            weight_grad = jnp.einsum(
                "shd,nhd->hsn", context_grad, value_heads, preferred_element_type=jnp.float32
            )
            score_grad = (soft_float * (weight_grad - row_delta[..., None])).astype(jnp.bfloat16)
            query_acc = (
                query_acc
                + jnp.einsum(
                    "hsn,nhd->shd", score_grad, key_heads, preferred_element_type=jnp.float32
                )
                * 0.125
            )
            slot_acc = slot_acc + jnp.einsum(
                "hsn,na->hsa",
                score_grad,
                one_hot_rows(slot_part, MSPAN),
                preferred_element_type=jnp.float32,
            )
            key_block_grad = (
                jnp.einsum("hsn,shd->nhd", score_grad, queries, preferred_element_type=jnp.float32)
                * 0.125
            )
            value_block_grad = jnp.einsum(
                "hsn,shd->nhd",
                soft_float.astype(jnp.bfloat16),
                context_grad,
                preferred_element_type=jnp.float32,
            )
            return ((query_acc, slot_acc), (key_block_grad, value_block_grad))

        return compute(state_carry)

    start_state = (jnp.zeros((rows, H, HD), jnp.float32), jnp.zeros((H, rows, MSPAN), jnp.float32))
    (query_acc, slot_acc), block_grads = lax.scan(advance, start_state, (blocks, bias_blocks))
    key_grads, value_grads = block_grads
    full_len = key_grads.shape[0] * key_grads.shape[1]
    return (
        query_acc,
        slot_acc,
        key_grads.reshape(full_len, H * HD),
        value_grads.reshape(full_len, H * HD),
    )


def general_device(
    hidden_in,
    segment_ids,
    doc_positions,
    w_query,
    w_key,
    w_value,
    w_out,
    b_query,
    b_value,
    b_out,
    ln1_gain,
    ln1_shift,
    w_inter,
    b_inter,
    w_final,
    b_final,
    ln2_gain,
    ln2_shift,
    mask_logits,
    mask_noise,
    grad_out,
):
    table_part = jax.nn.log_sigmoid(2.0 * (mask_logits + mask_noise)).astype(jnp.bfloat16)
    (
        wq_full,
        wk_full,
        wv_full,
        wo_full,
        wi_full,
        wf_full,
        bq_full,
        bv_full,
        bo_full,
        bi_full,
        bf_full,
        gain_one,
        shift_one,
        gain_two,
        shift_two,
        table_full,
    ) = (
        lax.all_gather(w_query, "fsdp", axis=0, tiled=True),
        lax.all_gather(w_key, "fsdp", axis=0, tiled=True),
        lax.all_gather(w_value, "fsdp", axis=0, tiled=True),
        lax.all_gather(w_out, "fsdp", axis=0, tiled=True),
        lax.all_gather(w_inter, "fsdp", axis=0, tiled=True),
        lax.all_gather(w_final, "fsdp", axis=0, tiled=True),
        lax.all_gather(b_query, "fsdp", axis=0, tiled=True),
        lax.all_gather(b_value, "fsdp", axis=0, tiled=True),
        lax.all_gather(b_out, "fsdp", axis=0, tiled=True),
        lax.all_gather(b_inter, "fsdp", axis=0, tiled=True),
        lax.all_gather(b_final, "fsdp", axis=0, tiled=True),
        lax.all_gather(ln1_gain, "fsdp", axis=0, tiled=True),
        lax.all_gather(ln1_shift, "fsdp", axis=0, tiled=True),
        lax.all_gather(ln2_gain, "fsdp", axis=0, tiled=True),
        lax.all_gather(ln2_shift, "fsdp", axis=0, tiled=True),
        lax.all_gather(table_part, "fsdp", axis=1, tiled=True),
    )
    bq_full, bv_full, bo_full = (
        bq_full.astype(jnp.float32),
        bv_full.astype(jnp.float32),
        bo_full.astype(jnp.float32),
    )
    bi_full, bf_full = (bi_full.astype(jnp.float32), bf_full.astype(jnp.float32))
    gain_one, shift_one = (gain_one.astype(jnp.float32), shift_one.astype(jnp.float32))
    gain_two, shift_two = (gain_two.astype(jnp.float32), shift_two.astype(jnp.float32))
    micro_count = hidden_in.shape[0]
    rows = hidden_in.shape[1]
    saved = []
    outputs_list = []
    for micro_batch in range(micro_count):
        tokens = hidden_in[micro_batch]
        seg_local = segment_ids[micro_batch]
        slot_local = doc_positions[micro_batch] % MSPAN
        queries_flat = (
            jnp.dot(tokens, wq_full, preferred_element_type=jnp.float32) + bq_full
        ).astype(jnp.bfloat16)
        keys_local = jnp.dot(tokens, wk_full, preferred_element_type=jnp.float32).astype(
            jnp.bfloat16
        )
        values_local = (
            jnp.dot(tokens, wv_full, preferred_element_type=jnp.float32) + bv_full
        ).astype(jnp.bfloat16)
        gathered = (
            lax.all_gather(keys_local, "ctx", axis=0, tiled=True),
            lax.all_gather(values_local, "ctx", axis=0, tiled=True),
            lax.all_gather(seg_local, "ctx", axis=0, tiled=True),
            lax.all_gather(slot_local, "ctx", axis=0, tiled=True),
        )
        blocks = make_blocks(*gathered)
        queries = queries_flat.reshape(rows, H, HD)
        table_rows = table_full[:, slot_local, :]
        log_total, bias_blocks = row_statistics(queries, seg_local, table_rows, blocks)
        context = attention_output(queries, seg_local, blocks, bias_blocks, log_total)
        context_low = context.reshape(rows, H * HD).astype(jnp.bfloat16)
        attn_out = jnp.dot(context_low, wo_full, preferred_element_type=jnp.float32) + bo_full
        first_norm, norm_one_back = jax.vjp(
            layer_norm, tokens.astype(jnp.float32) + attn_out, gain_one, shift_one
        )
        first_low = first_norm.astype(jnp.bfloat16)
        inner_act = jnp.dot(first_low, wi_full, preferred_element_type=jnp.float32) + bi_full
        active, gelu_back = jax.vjp(exact_gelu, inner_act)
        active_low = active.astype(jnp.bfloat16)
        ffn_out = jnp.dot(active_low, wf_full, preferred_element_type=jnp.float32) + bf_full
        result, norm_two_back = jax.vjp(layer_norm, first_norm + ffn_out, gain_two, shift_two)
        outputs_list.append(result.astype(jnp.bfloat16))
        kept_blocks = blocks
        saved.append(
            (
                tokens,
                seg_local,
                slot_local,
                queries,
                keys_local,
                values_local,
                log_total,
                bias_blocks,
                context,
                context_low,
                first_low,
                active_low,
                norm_one_back,
                gelu_back,
                norm_two_back,
                kept_blocks,
            )
        )
    zeros_square = jnp.zeros((H * HD, H * HD), jnp.float32)
    wq_grad, wk_grad, wv_grad, wo_grad = (zeros_square, zeros_square, zeros_square, zeros_square)
    wi_grad = jnp.zeros(wi_full.shape, jnp.float32)
    wf_grad = jnp.zeros(wf_full.shape, jnp.float32)
    zeros_row = jnp.zeros((H * HD,), jnp.float32)
    bq_grad, bv_grad, bo_grad, bf_grad = (zeros_row, zeros_row, zeros_row, zeros_row)
    gain_one_grad, shift_one_grad, gain_two_grad, shift_two_grad = (
        zeros_row,
        zeros_row,
        zeros_row,
        zeros_row,
    )
    bi_grad = jnp.zeros(bi_full.shape, jnp.float32)
    table_grad = jnp.zeros(table_full.shape, jnp.float32)
    input_grads = []
    for micro_batch in range(micro_count):
        (
            tokens,
            seg_local,
            slot_local,
            queries,
            keys_local,
            values_local,
            log_total,
            bias_blocks,
            context,
            context_low,
            first_low,
            active_low,
            norm_one_back,
            gelu_back,
            norm_two_back,
            kept_blocks,
        ) = saved[micro_batch]
        upstream = grad_out[micro_batch].astype(jnp.float32)
        sum_grad, gain_part, shift_part = norm_two_back(upstream)
        gain_two_grad = gain_two_grad + gain_part
        shift_two_grad = shift_two_grad + shift_part
        ffn_grad = sum_grad.astype(jnp.bfloat16)
        bf_grad = bf_grad + jnp.sum(ffn_grad.astype(jnp.float32), axis=0)
        wf_grad = wf_grad + left_product(active_low, ffn_grad)
        active_grad = right_product(ffn_grad, wf_full).astype(jnp.bfloat16)
        (inner_float,) = gelu_back(active_grad.astype(jnp.float32))
        inner_grad = inner_float.astype(jnp.bfloat16)
        bi_grad = bi_grad + jnp.sum(inner_grad.astype(jnp.float32), axis=0)
        wi_grad = wi_grad + left_product(first_low, inner_grad)
        first_grad = sum_grad + right_product(inner_grad, wi_full)
        norm_grad, gain_part, shift_part = norm_one_back(first_grad)
        gain_one_grad = gain_one_grad + gain_part
        shift_one_grad = shift_one_grad + shift_part
        attn_grad = norm_grad.astype(jnp.bfloat16)
        bo_grad = bo_grad + jnp.sum(attn_grad.astype(jnp.float32), axis=0)
        wo_grad = wo_grad + left_product(context_low, attn_grad)
        context_grad_flat = right_product(attn_grad, wo_full).astype(jnp.bfloat16)
        context_grad = context_grad_flat.reshape(rows, H, HD)
        row_delta = jnp.einsum("shd,shd->hs", context_grad.astype(jnp.float32), context)
        blocks = kept_blocks
        query_acc, slot_acc, key_full_grad, value_full_grad = attention_backward(
            queries, seg_local, blocks, bias_blocks, log_total, context_grad, row_delta
        )
        key_share, value_share = (
            lax.psum_scatter(
                key_full_grad.astype(jnp.bfloat16), "ctx", scatter_dimension=0, tiled=True
            ).astype(jnp.float32),
            lax.psum_scatter(
                value_full_grad.astype(jnp.bfloat16), "ctx", scatter_dimension=0, tiled=True
            ).astype(jnp.float32),
        )
        table_grad = table_grad.at[:, slot_local, :].add(slot_acc)
        query_low = query_acc.reshape(rows, H * HD).astype(jnp.bfloat16)
        key_low = key_share.astype(jnp.bfloat16)
        value_low = value_share.astype(jnp.bfloat16)
        bq_grad = bq_grad + jnp.sum(query_low.astype(jnp.float32), axis=0)
        bv_grad = bv_grad + jnp.sum(value_low.astype(jnp.float32), axis=0)
        wq_grad = wq_grad + left_product(tokens, query_low)
        wk_grad = wk_grad + left_product(tokens, key_low)
        wv_grad = wv_grad + left_product(tokens, value_low)
        input_grads.append(
            norm_grad
            + right_product(query_low, wq_full)
            + right_product(key_low, wk_full)
            + right_product(value_low, wv_full)
        )
    shares = (
        lax.psum_scatter(
            wq_grad.astype(jnp.bfloat16), "fsdp", scatter_dimension=0, tiled=True
        ).astype(jnp.float32),
        lax.psum_scatter(
            wk_grad.astype(jnp.bfloat16), "fsdp", scatter_dimension=0, tiled=True
        ).astype(jnp.float32),
        lax.psum_scatter(
            wv_grad.astype(jnp.bfloat16), "fsdp", scatter_dimension=0, tiled=True
        ).astype(jnp.float32),
        lax.psum_scatter(
            wo_grad.astype(jnp.bfloat16), "fsdp", scatter_dimension=0, tiled=True
        ).astype(jnp.float32),
        lax.psum_scatter(
            bq_grad.astype(jnp.bfloat16), "fsdp", scatter_dimension=0, tiled=True
        ).astype(jnp.float32),
        lax.psum_scatter(
            bv_grad.astype(jnp.bfloat16), "fsdp", scatter_dimension=0, tiled=True
        ).astype(jnp.float32),
        lax.psum_scatter(
            bo_grad.astype(jnp.bfloat16), "fsdp", scatter_dimension=0, tiled=True
        ).astype(jnp.float32),
        lax.psum_scatter(
            gain_one_grad.astype(jnp.bfloat16), "fsdp", scatter_dimension=0, tiled=True
        ).astype(jnp.float32),
        lax.psum_scatter(
            shift_one_grad.astype(jnp.bfloat16), "fsdp", scatter_dimension=0, tiled=True
        ).astype(jnp.float32),
        lax.psum_scatter(
            wi_grad.astype(jnp.bfloat16), "fsdp", scatter_dimension=0, tiled=True
        ).astype(jnp.float32),
        lax.psum_scatter(
            bi_grad.astype(jnp.bfloat16), "fsdp", scatter_dimension=0, tiled=True
        ).astype(jnp.float32),
        lax.psum_scatter(
            wf_grad.astype(jnp.bfloat16), "fsdp", scatter_dimension=0, tiled=True
        ).astype(jnp.float32),
        lax.psum_scatter(
            bf_grad.astype(jnp.bfloat16), "fsdp", scatter_dimension=0, tiled=True
        ).astype(jnp.float32),
        lax.psum_scatter(
            gain_two_grad.astype(jnp.bfloat16), "fsdp", scatter_dimension=0, tiled=True
        ).astype(jnp.float32),
        lax.psum_scatter(
            shift_two_grad.astype(jnp.bfloat16), "fsdp", scatter_dimension=0, tiled=True
        ).astype(jnp.float32),
        lax.psum_scatter(
            table_grad.astype(jnp.bfloat16), "fsdp", scatter_dimension=1, tiled=True
        ).astype(jnp.float32),
    )
    totals = (
        lax.psum(shares[0].astype(jnp.bfloat16), "ctx").astype(jnp.float32),
        lax.psum(shares[1].astype(jnp.bfloat16), "ctx").astype(jnp.float32),
        lax.psum(shares[2].astype(jnp.bfloat16), "ctx").astype(jnp.float32),
        lax.psum(shares[3].astype(jnp.bfloat16), "ctx").astype(jnp.float32),
        lax.psum(shares[4].astype(jnp.bfloat16), "ctx").astype(jnp.float32),
        lax.psum(shares[5].astype(jnp.bfloat16), "ctx").astype(jnp.float32),
        lax.psum(shares[6].astype(jnp.bfloat16), "ctx").astype(jnp.float32),
        lax.psum(shares[7].astype(jnp.bfloat16), "ctx").astype(jnp.float32),
        lax.psum(shares[8].astype(jnp.bfloat16), "ctx").astype(jnp.float32),
        lax.psum(shares[9].astype(jnp.bfloat16), "ctx").astype(jnp.float32),
        lax.psum(shares[10].astype(jnp.bfloat16), "ctx").astype(jnp.float32),
        lax.psum(shares[11].astype(jnp.bfloat16), "ctx").astype(jnp.float32),
        lax.psum(shares[12].astype(jnp.bfloat16), "ctx").astype(jnp.float32),
        lax.psum(shares[13].astype(jnp.bfloat16), "ctx").astype(jnp.float32),
        lax.psum(shares[14].astype(jnp.bfloat16), "ctx").astype(jnp.float32),
        lax.psum(shares[15].astype(jnp.bfloat16), "ctx").astype(jnp.float32),
    )
    (
        wq_total,
        wk_total,
        wv_total,
        wo_total,
        bq_total,
        bv_total,
        bo_total,
        gain_one_total,
        shift_one_total,
        wi_total,
        bi_total,
        wf_total,
        bf_total,
        gain_two_total,
        shift_two_total,
        table_total,
    ) = totals
    logit_grad = table_total * 2.0 * jax.nn.sigmoid(-2.0 * (mask_logits + mask_noise))
    return (
        jnp.stack(outputs_list),
        jnp.stack(input_grads),
        wq_total,
        wk_total,
        wv_total,
        wo_total,
        bq_total,
        bv_total,
        bo_total,
        gain_one_total,
        shift_one_total,
        wi_total,
        bi_total,
        wf_total,
        bf_total,
        gain_two_total,
        shift_two_total,
        logit_grad,
    )


MESH = pl.DeviceIdType.MESH
BF16 = jnp.bfloat16
F32 = jnp.float32
ROWS = 192
TALL = 272


ROOT_HALF = 0.7071067811865476
ROOT_TWO_PI = 0.3989422804014327


def place():
    c = lax.axis_index("ctx")
    f = lax.axis_index("fsdp")
    return (c // 2, c % 2, f // 2, f % 2)


def device(z, x, y, k):
    return {"ctx": z * 2 + x, "fsdp": y * 2 + k}


def send(src, dst, send_sem, recv_sem, target):
    return pltpu.make_async_remote_copy(
        src_ref=src,
        dst_ref=dst,
        send_sem=send_sem,
        recv_sem=recv_sem,
        device_id=target,
        device_id_type=MESH,
    )


def meet(targets):
    barrier = pltpu.get_barrier_semaphore()
    for target in targets:
        pl.semaphore_signal(barrier, inc=1, device_id=target, device_id_type=MESH)
    pl.semaphore_wait(barrier, len(targets))


def any_spec():
    return pl.BlockSpec(memory_space=pl.ANY)


def vmem_spec():
    return pl.BlockSpec(memory_space=pltpu.VMEM)


def gather_pieces():
    pieces = [(array, 0, 192, 0, 768, False) for array in range(3)]
    pieces.append((6, 0, 0, 0, 0, True))
    pieces.append((3, 0, 192, 0, 768, False))
    for part in range(2):
        pieces.append((4, 0, 192, 1536 * part, 1536, False))
    for part in range(4):
        pieces.append((5, 192 * part, 192, 0, 768, part == 3))
    return pieces


def gather_plan(ins, outs, small, small_out, sems):
    ss, rs, ls, ss_small, rs_small = sems
    z, x, y, k = place()
    heads = 3 * lax.rem(2 * z + x, 4)
    mine = y * 2 + k
    over = (1 - y) * 2 + k
    core = device(z, x, y, 1 - k)
    ynb = device(z, x, 1 - y, k)
    diag = device(z, x, 1 - y, 1 - k)
    xnb = device(z, 1 - x, y, k)

    def source(piece, half):
        a, r0, rn, c0, cn, _ = piece
        if a == 6:
            return ins[a].at[pl.ds(heads, 3)]
        if half is None:
            return ins[a].at[pl.ds(r0, rn), pl.ds(c0, cn)]
        return ins[a].at[pl.ds(r0 + (rn // 2) * half, rn // 2), pl.ds(c0, cn)]

    def target(piece, owner, half):
        a, r0, rn, c0, cn, _ = piece
        if a == 6:
            return outs[a].at[:, pl.ds(128 * owner, 128)]
        base = ins[a].shape[0] * owner + r0
        if half is None:
            return outs[a].at[pl.ds(base, rn), pl.ds(c0, cn)]
        return outs[a].at[pl.ds(base + (rn // 2) * half, rn // 2), pl.ds(c0, cn)]

    plan = []
    for n, piece in enumerate(gather_pieces()):
        both = piece[5]
        part = None if both else x
        whole = source(piece, None)
        kept = target(piece, mine, None)
        here = target(piece, over, part)
        copies = {
            "own": pltpu.make_async_copy(whole, kept, ls.at[n]),
            "core": send(whole, kept, ss.at[n, 0], rs.at[n, 0], core),
            "y": send(source(piece, part), target(piece, mine, part), ss.at[n, 1], rs.at[n, 1], ynb),
            "core_y": send(here, here, ss.at[n, 3], rs.at[n, 3], core),
        }
        if not both:
            there = target(piece, over, 1 - x)
            copies["x"] = send(here, here, ss.at[n, 2], rs.at[n, 2], xnb)
            copies["core_x"] = send(there, there, ss.at[n, 4], rs.at[n, 4], core)
        plan.append(copies)
    rows = small_out.at[mine]
    smalls = [
        send(small, rows, ss_small.at[i], rs_small.at[i], peer)
        for i, peer in enumerate((core, ynb, diag))
    ]
    own_small = pltpu.make_async_copy(small, rows, ls.at[len(plan)])
    return (plan, smalls, own_small)


def forward_y(copies):
    copies["y"].wait_recv()
    if "x" in copies:
        copies["x"].start()
    copies["core_y"].start()


def forward_x(copies):
    if "x" in copies:
        copies["x"].wait_recv()
        copies["core_x"].start()


def arrive(copies):
    copies["own"].wait()
    for name in ("core", "core_y", "core_x"):
        if name in copies:
            copies[name].wait_recv()


def settle(copies):
    for name, cp in copies.items():
        if name != "own":
            cp.wait_send()


def ctx_peers():
    c = lax.axis_index("ctx")
    return [{"ctx": lax.rem(c + i, 8)} for i in range(1, 8)]


class Exchange:
    def __init__(self, main, main_in, extra, extra_in, sems, home):
        self.main, self.main_in, self.extra, self.extra_in = (main, main_in, extra, extra_in)
        self.ms, self.mr, self.es, self.er, self.ls = sems
        self.c = lax.axis_index("ctx")
        self.group, self.me = (self.c // 4, lax.rem(self.c, 4))
        self.home = home

    def one(self, j, slot):
        return send(
            self.main.at[j],
            self.main_in.at[slot],
            self.ms.at[j],
            self.mr.at[slot],
            {"ctx": 4 * self.group + j},
        )

    def local(self, j):
        return pltpu.make_async_copy(self.main.at[j], self.main_in.at[j], self.ls)

    def side(self, j):
        if self.home:
            return send(
                self.extra, self.extra_in.at[self.me], self.es.at[0], self.er.at[self.me], {"ctx": 4}
            )
        return send(self.extra.at[j], self.extra_in, self.es.at[j], self.er.at[0], {"ctx": j})

    def start(self):
        for j in range(4):

            @pl.when(self.me != j)
            def _():
                self.one(j, self.me).start()

            @pl.when(self.me == j)
            def _():
                self.local(j).start()

        if self.home:

            @pl.when(self.group == 0)
            def _():
                self.side(0).start()

        else:

            @pl.when(self.c == 4)
            def _():
                for j in range(4):
                    self.side(j).start()

    def wait(self):
        for j in range(4):

            @pl.when(self.me != j)
            def _():
                self.one(0, j).wait_recv()

            @pl.when(self.me == j)
            def _():
                self.local(j).wait()

        if self.home:

            @pl.when(self.c == 4)
            def _():
                for j in range(4):
                    send(
                        self.extra, self.extra_in.at[j], self.es.at[0], self.er.at[j], {"ctx": 4}
                    ).wait_recv()

        else:

            @pl.when(self.group == 0)
            def _():
                self.side(0).wait_recv()

    def settle(self):
        for j in range(4):

            @pl.when(self.me != j)
            def _():
                self.one(j, self.me).wait_send()

        if self.home:

            @pl.when(self.group == 0)
            def _():
                self.side(0).wait_send()

        else:

            @pl.when(self.c == 4)
            def _():
                for j in range(4):
                    self.side(j).wait_send()


def exchange_sems():
    dma = pltpu.SemaphoreType.DMA
    return [dma((4,)), dma((4,)), dma((4,)), dma((4,)), dma]


def dot_nn(a, b):
    return lax.dot_general(a, b, (((1,), (0,)), ((), ())), preferred_element_type=F32)


def dot_nt(a, b):
    return lax.dot_general(a, b, (((1,), (1,)), ((), ())), preferred_element_type=F32)


def dot_tn(a, b):
    return lax.dot_general(a, b, (((0,), (0,)), ((), ())), preferred_element_type=F32)


def group_rows(main, extra, s, lo, width):
    top = main[:, pl.ds(64 * s, 64), lo : lo + width].reshape(256, width)
    return jnp.concatenate([top, extra[pl.ds(16 * s, 16), lo : lo + width]], axis=0)


def place_masks(main, extra, s, group):
    marks = group_rows(main, extra, s, 576, 64).astype(F32)
    segment = marks[:, 0:1]
    slot = marks[:, 1:2]
    first = segment == 0.0
    valid = jnp.where(
        group == 0, jnp.where(first, 1.0, 0.0), jnp.where(first | (segment < 0.0), 0.0, 1.0)
    )
    lanes = lax.broadcasted_iota(jnp.int32, (TALL, 128), 1).astype(F32)
    seg_hot = jnp.where((lanes == segment) & (valid > 0.0), 1.0, 0.0).astype(BF16)
    wide = lax.broadcasted_iota(jnp.int32, (TALL, TALL), 1).astype(F32)
    slot_hot = jnp.where((wide == slot) & (valid > 0.0), 1.0, 0.0).astype(BF16)
    return (slot_hot, dot_nt(seg_hot, seg_hot) > 0.5)


def add_rows(out, left, right, rows, step=32):
    def body(i, carry):
        at = pl.ds(pl.multiple_of(i * step, step), step)
        out[at, :] = left[at, :] + right[at, :]
        return carry

    lax.fori_loop(0, rows // step, body, 0)


class BlockSums:
    def __init__(self, partial, bufs, sems, full):
        self.partial, self.full = (partial, full)
        self.st, self.r1, self.r2, self.r3, self.r4 = bufs
        self.p1, self.q1, self.p2, self.q2, self.p3, self.q3, self.p4, self.q4 = sems[:8]
        self.p5, self.q5, self.p6, self.q6 = sems[8:]
        z, x, y, k = place()
        self.z, self.x, self.y, self.k = (z, x, y, k)
        self.core = device(z, x, y, 1 - k)
        self.ynb = device(z, x, 1 - y, k)
        self.xnb = device(z, 1 - x, y, k)
        self.first, self.second, self.third, self.sixth = ({}, {}, {}, {})
        self.slots = {}

    def one(self, n):
        slot = n % 4
        if slot in self.slots:
            for yy in range(2):
                self.first.pop((self.slots[slot], yy)).wait_send()
        self.slots[slot] = n
        for yy in range(2):
            self.st[slot, yy] = self.partial(n, 2 * yy + 1 - self.k).astype(BF16)
            cp = send(
                self.st.at[slot, yy],
                self.r1.at[n, yy],
                self.p1.at[n, yy],
                self.q1.at[n, yy],
                self.core,
            )
            cp.start()
            self.first[n, yy] = cp

    def two(self, n):
        for yy in range(2):
            self.first[n, yy].wait_recv()
            own = self.partial(n, 2 * yy + self.k)
            self.r1[n, yy] = (own + self.r1[n, yy].astype(F32)).astype(BF16)
        cp = send(
            self.r1.at[n, 1 - self.y], self.r2.at[n], self.p2.at[n], self.q2.at[n], self.ynb
        )
        cp.start()
        self.second[n] = cp

    def three(self, n):
        self.second[n].wait_recv()
        add_rows(self.r2.at[n], self.r1.at[n, self.y], self.r2.at[n], 192)
        cp = send(
            self.r2.at[n, pl.ds(96 * (1 - self.x), 96)],
            self.r3.at[n],
            self.p3.at[n],
            self.q3.at[n],
            self.xnb,
        )
        cp.start()
        self.third[n] = cp

    def to_z(self, n):
        return send(
            self.r3.at[n],
            self.r4.at[n // 4, self.z],
            self.p4.at[n],
            self.q4.at[n // 4, self.z],
            device(n % 4, self.x, self.y, self.k),
        )

    def four(self, n):
        self.third[n].wait_recv()
        add_rows(self.r3.at[n], self.r2.at[n, pl.ds(96 * self.x, 96)], self.r3.at[n], 96)

        @pl.when(self.z != n % 4)
        def _():
            self.to_z(n).start()

    def mine(self, n):
        return self.full.at[n, pl.ds(96 * self.x, 96)]

    def from_z(self, n, i):
        here = self.mine(n)
        zz = lax.rem(n % 4 + i, 4)
        return send(
            here, here, self.p5.at[n // 4, i - 1], self.q5.at[n], device(zz, self.x, self.y, self.k)
        )

    def to_x(self, n):
        here = self.mine(n)
        return send(here, here, self.p6.at[n], self.q6.at[n], self.xnb)

    def five(self, n):
        b = n % 4

        @pl.when(self.z == b)
        def _():
            for i in (1, 2, 3):
                zz = (b + i) % 4
                send(
                    self.r3.at[n],
                    self.r4.at[n // 4, zz],
                    self.p4.at[n],
                    self.q4.at[n // 4, zz],
                    self.core,
                ).wait_recv()

            def body(i, carry):
                at = pl.ds(pl.multiple_of(i * 32, 32), 32)
                total = self.r3[n, at, :].astype(F32)
                for j in (1, 2, 3):
                    total = total + self.r4[n // 4, (b + j) % 4, at, :].astype(F32)
                to = pl.ds(pl.multiple_of(96 * self.x + i * 32, 32), 32)
                self.full[n, to, :] = total.astype(BF16)
                return carry

            lax.fori_loop(0, 3, body, 0)
            for i in (1, 2, 3):
                self.from_z(n, i).start()
            self.to_x(n).start()

    def six(self, n):
        @pl.when(self.z != n % 4)
        def _():
            self.from_z(n, 1).wait_recv()
            self.to_x(n).start()

    def seven(self, n, target):
        self.to_x(n).wait_recv()

        def body(i, carry):
            at = pl.ds(pl.multiple_of(i * 32, 32), 32)
            target[at, :] = self.full[n, at, :].astype(F32)
            return carry

        lax.fori_loop(0, 6, body, 0)

    def settle(self):
        for copies in (self.first, self.second, self.third):
            for cp in copies.values():
                cp.wait_send()
        for n in range(12):
            self.to_x(n).wait_send()

            @pl.when(self.z != n % 4)
            def _():
                self.to_z(n).wait_send()

            @pl.when(self.z == n % 4)
            def _():
                for i in (1, 2, 3):
                    self.from_z(n, i).wait_send()


def layer_kernel(
    tokens, tokens4, marks, upstream,
    wq_in, wk_in, wv_in, wo_in, wi_in, wf_in, table_in, small_in,
    hidden_out, input_grad, oq, ok, ov, oo, oi, of, small_out, table_out, edge_out,
    wq, wk, wv, wo, wi, wf, table, small,
    main, extra, main_send, extra_send, probs, ctx_send, ctx_extra, ctx4, ctx_extra_in,
    first_hat, second_hat, first_norm, first4, active, slope, inner, sum_grad, low_grad,
    grad4, grad_extra, grad_in, grad_extra_in, main_in, extra_in, table_grad, lows,
    v0, v1, v2, v3, v4, t0, t1, t2, t3, e0, e1, e2, e3,
    st, r1, r2, r3, r4, full, *sems
):
    z, x, y, k = place()
    c = 2 * z + x
    group = c // 4
    core = device(z, x, y, 1 - k)
    ynb = device(z, x, 1 - y, k)
    xnb = device(z, 1 - x, y, k)
    twin = device(lax.rem(z + 2, 4), x, y, k)
    zdev = [device(lax.rem(z + i, 4), x, y, k) for i in (1, 2, 3)]
    gather_sems, ex = (sems[:5], [sems[5 + 5 * i : 10 + 5 * i] for i in range(4)])
    sum_sems, (ps, qs, pt, qt, pe, qe) = (sems[25:37], sems[37:43])
    meet(ctx_peers() + [core, ynb, device(z, x, 1 - y, 1 - k)])

    plan, smalls, own_small = gather_plan(
        (wq_in, wk_in, wv_in, wo_in, wi_in, wf_in, table_in),
        (wq, wk, wv, wo, wi, wf, table),
        small_in,
        small,
        gather_sems,
    )
    for cp in smalls + [own_small]:
        cp.start()
    for copies in plan:
        for name in ("y", "core", "own"):
            copies[name].start()
    table_grad[...] = jnp.zeros((3, TALL, TALL), F32)
    v0[...] = jnp.zeros((4, 16, 256), F32)
    e0[...] = jnp.zeros((16, 384), F32)

    @pl.when(group == 1)
    def _():
        extra[...] = jnp.full((48, 640), -1.0, BF16)
        grad_extra_in[...] = jnp.zeros((48, 192), BF16)

    @pl.when(y == 1)
    def _():
        table_out[...] = jnp.zeros((4, 3, 128, 256), BF16)

    for n in range(3):
        forward_y(plan[n])
    for n in range(3):
        forward_x(plan[n])
    own_small.wait()
    for cp in smalls:
        cp.wait_recv()

    def vector(i):
        return jnp.concatenate([small[f, i : i + 1, 0:192] for f in range(4)], axis=1).astype(F32)

    arrive(plan[0])
    q = (dot_nn(tokens[...], wq[...]) + vector(0)).astype(BF16)
    arrive(plan[1])
    kk = dot_nn(tokens[...], wk[...]).astype(BF16)
    arrive(plan[2])
    v = (dot_nn(tokens[...], wv[...]) + vector(1)).astype(BF16)
    for j in range(4):
        cols = slice(192 * j, 192 * j + 192)
        main_send[j] = jnp.concatenate([q[:, cols], kk[:, cols], v[:, cols], marks[...]], axis=1)
        for s in range(3):
            extra_send[j, 16 * s : 16 * s + 16] = main_send[j, 64 * s : 64 * s + 16]
    heads_there = Exchange(main_send, main, extra_send, extra, ex[0], False)
    heads_there.start()
    forward_y(plan[3])
    forward_y(plan[4])
    forward_y(plan[5])
    heads_there.wait()
    arrive(plan[3])

    def attend(s):
        slot_hot, same = place_masks(main, extra, s, group)
        parts = []
        for h in range(3):
            qh = group_rows(main, extra, s, 64 * h, 64)
            kh = group_rows(main, extra, s, 192 + 64 * h, 64)
            vh = group_rows(main, extra, s, 384 + 64 * h, 64)
            picked = dot_nn(slot_hot, table[h, 0:TALL, 0:TALL]).astype(BF16)
            bias = dot_nt(picked, slot_hot)
            scores = jnp.where(same, dot_nt(qh, kh) * 0.125 + bias, NEGATIVE)
            top = jnp.max(scores, axis=1, keepdims=True)
            grown = jnp.where(same, jnp.exp(scores - top), 0.0)
            total = jnp.maximum(jnp.sum(grown, axis=1, keepdims=True), 1e-30)
            soft = (grown / total).astype(BF16)
            probs[3 * s + h] = soft
            parts.append(dot_nn(soft, vh).astype(BF16))
        whole = jnp.concatenate(parts, axis=1)
        for j in range(4):
            ctx_send[j, pl.ds(64 * s, 64)] = whole[64 * j : 64 * j + 64]
        ctx_extra[pl.ds(16 * s, 16)] = whole[256:272]

    attend(0)
    forward_x(plan[4])
    attend(1)
    forward_y(plan[6])
    attend(2)
    heads_back = Exchange(ctx_send, ctx4, ctx_extra, ctx_extra_in, ex[1], True)
    heads_back.start()
    forward_x(plan[5])
    forward_y(plan[7])
    heads_back.wait()

    def join(into, side):
        @pl.when(c == 4)
        def _():
            for j in range(4):
                for s in range(3):
                    at = slice(64 * s, 64 * s + 16)
                    into[j, at] = into[j, at] + side[j, 16 * s : 16 * s + 16]

    join(ctx4, ctx_extra_in)

    def mean(value):
        return jnp.mean(value, axis=1, keepdims=True)

    def column_sum(value):
        return jnp.sum(value, axis=0, keepdims=True)

    def keep_vector(i, row):
        for owner in range(4):
            v0[owner, i : i + 1, 0:192] = row[:, 192 * owner : 192 * owner + 192]

    forward_y(plan[8])
    arrive(plan[4])
    context = jnp.concatenate([ctx4[j] for j in range(4)], axis=1)
    centered = tokens[...].astype(F32) + dot_nn(context, wo[...]) + vector(2)
    centered = centered - mean(centered)
    first_rate = lax.rsqrt(mean(centered * centered) + EPSILON)
    centered = centered * first_rate
    first_hat[...] = centered
    centered = centered * vector(3) + vector(4)
    first_norm[...] = centered
    first_low = centered.astype(BF16)
    for j in range(4):
        first4[j] = first_low[:, 192 * j : 192 * j + 192]
    forward_x(plan[6])
    forward_x(plan[7])
    forward_y(plan[9])
    arrive(plan[5])

    def inner_product(j):
        bias = jnp.concatenate([small[j, 8 + i : 9 + i, 0:192] for i in range(4)], axis=1)
        value = dot_nn(first_low, wi[:, 768 * j : 768 * j + 768]) + bias.astype(F32)
        share = 0.5 + 0.5 * lax.erf(value * ROOT_HALF)
        active[j] = (value * share).astype(BF16)
        slope[j] = share + value * (jnp.exp(-0.5 * value * value) * ROOT_TWO_PI)

    inner_product(0)
    forward_x(plan[8])
    inner_product(1)
    forward_y(plan[10])
    arrive(plan[6])
    inner_product(2)
    forward_x(plan[9])
    inner_product(3)
    for n in range(7, 11):
        arrive(plan[n])
    ffn_out = dot_nn(active[0], wf[0:768])
    for j in range(1, 4):
        ffn_out = ffn_out + dot_nn(active[j], wf[768 * j : 768 * j + 768])
    centered = first_norm[...] + ffn_out + vector(5)
    centered = centered - mean(centered)
    rate = lax.rsqrt(mean(centered * centered) + EPSILON)
    hat = centered * rate
    hidden_out[...] = (hat * vector(6) + vector(7)).astype(BF16)

    above = upstream[...].astype(F32)
    keep_vector(6, column_sum(above * hat))
    keep_vector(7, column_sum(above))
    scaled = above * vector(6)
    grown_grad = rate * (scaled - mean(scaled) - hat * mean(scaled * hat))
    sum_grad[...] = grown_grad
    low_grad[...] = grown_grad.astype(BF16)
    keep_vector(5, column_sum(low_grad[...].astype(F32)))

    def partial(n, owner):
        b = n % 4
        if n < 4:
            return dot_tn(active[owner, :, 192 * b : 192 * b + 192], low_grad[...])
        if n < 8:
            return dot_tn(first4[owner], inner[b])
        if n < 11:
            return dot_tn(tokens4[owner], lows[b])
        return dot_tn(ctx4[owner], low_grad[...])

    sums = BlockSums(partial, (st, r1, r2, r3, r4), sum_sems, full)
    targets = (
        [of.at[192 * b : 192 * b + 192] for b in range(4)]
        + [oi.at[:, 768 * b : 768 * b + 768] for b in range(4)]
        + [oq, ok, ov, oo]
    )

    def inner_back(j):
        value = dot_nt(low_grad[...], wf[768 * j : 768 * j + 768]).astype(BF16)
        inner[j] = (value.astype(F32) * slope[j]).astype(BF16)
        row = column_sum(inner[j].astype(F32))
        for i in range(4):
            v0[j, 8 + i : 9 + i, 0:192] = row[:, 192 * i : 192 * i + 192]
        sum_grad[...] += dot_nt(inner[j], wi[:, 768 * j : 768 * j + 768])

    for n in range(4):
        sums.one(n)
    inner_back(0)
    for n in range(4):
        sums.two(n)
    for j in range(1, 4):
        inner_back(j)
    for n in range(4, 8):
        sums.one(n)
    sums.three(0)
    above = sum_grad[...]
    hat = first_hat[...]
    keep_vector(3, column_sum(above * hat))
    keep_vector(4, column_sum(above))
    scaled = above * vector(3)
    norm_grad = first_rate * (scaled - mean(scaled) - hat * mean(scaled * hat))
    sum_grad[...] = norm_grad
    low_grad[...] = norm_grad.astype(BF16)
    keep_vector(2, column_sum(low_grad[...].astype(F32)))
    context_grad = dot_nt(low_grad[...], wo[...]).astype(BF16)
    for j in range(4):
        grad4[j] = context_grad[:, 192 * j : 192 * j + 192]
        for s in range(3):
            grad_extra[j, 16 * s : 16 * s + 16] = grad4[j, 64 * s : 64 * s + 16]
    grads_there = Exchange(grad4, grad_in, grad_extra, grad_extra_in, ex[2], False)
    grads_there.start()
    for n in range(4, 8):
        sums.two(n)
    sums.one(11)
    sums.three(1)
    sums.two(11)
    grads_there.wait()

    def attend_back(s):
        slot_hot, _ = place_masks(main, extra, s, group)
        parts = [[], [], []]
        for h in range(3):
            qh = group_rows(main, extra, s, 64 * h, 64)
            kh = group_rows(main, extra, s, 192 + 64 * h, 64)
            vh = group_rows(main, extra, s, 384 + 64 * h, 64)
            gh = group_rows(grad_in, grad_extra_in, s, 64 * h, 64)
            soft = probs[3 * s + h]
            weight = soft.astype(F32)
            weight_grad = dot_nt(gh, vh)
            delta = jnp.sum(weight * weight_grad, axis=1, keepdims=True)
            score_grad = (weight * (weight_grad - delta)).astype(BF16)
            parts[0].append((dot_nn(score_grad, kh) * 0.125).astype(BF16))
            parts[1].append((dot_tn(score_grad, qh) * 0.125).astype(BF16))
            parts[2].append(dot_tn(soft, gh).astype(BF16))
            moved = dot_tn(slot_hot, score_grad)
            table_grad[h] += dot_nn(moved.astype(BF16), slot_hot)
        blank = jnp.zeros((TALL, 64), BF16)
        whole = jnp.concatenate(parts[0] + parts[1] + parts[2] + [blank], axis=1)
        for j in range(4):
            main_send[j, pl.ds(64 * s, 64)] = whole[64 * j : 64 * j + 64]
        extra_send[0, pl.ds(16 * s, 16)] = whole[256:272]

    heads_there.settle()
    attend_back(0)
    sums.four(0)
    attend_back(1)
    sums.three(2)
    sums.four(1)
    attend_back(2)
    grads_back = Exchange(main_send, main_in, extra_send.at[0], extra_in, ex[3], True)
    grads_back.start()
    sums.five(0)
    sums.three(3)
    sums.four(2)
    sums.five(1)
    lane = lax.broadcasted_iota(jnp.int32, (8, TALL), 1)
    final = jnp.where(lane == 256, 1.0, 0.0).astype(BF16)
    for h in range(3):
        t0[h] = table_grad[h, 0:256, 0:256].astype(BF16)
        e0[h : h + 1, 0:TALL] = table_grad[h, 256:257, :]
        column = dot_nt(final, table_grad[h].astype(BF16))
        e0[8 + h : 9 + h, 0:TALL] = column[0:1]
    tcore = send(t0.at[:, pl.ds(128 * (1 - k), 128)], t1, pt.at[0], qt.at[0], core)
    tcore.start()
    ecore = send(e0, e1, pe.at[0], qe.at[0], core)
    ecore.start()
    tcore.wait_recv()
    for h in range(3):
        at = pl.ds(pl.multiple_of(128 * k, 128), 128)
        t1[h] = t0[h, at, :] + t1[h]

    @pl.when(y == 1)
    def _():
        send(t1, t2, pt.at[1], qt.at[1], ynb).start()

    ecore.wait_recv()
    e1[...] = e0[...] + e1[...]
    edge_y = send(e1, e2, pe.at[1], qe.at[1], ynb)
    edge_y.start()
    sums.six(0)
    sums.three(4)
    sums.four(3)
    sums.five(2)
    grads_back.wait()
    join(main_in, extra_in)
    for a in range(3):
        lows[a] = jnp.concatenate(
            [main_in[j, :, 192 * a : 192 * a + 192] for j in range(4)], axis=1
        )
        sums.one(8 + a)
    keep_vector(0, column_sum(lows[0].astype(F32)))
    keep_vector(1, column_sum(lows[2].astype(F32)))
    small_core = []
    for yy in range(2):
        cp = send(v0.at[2 * yy + 1 - k], v1.at[yy], ps.at[yy], qs.at[yy], core)
        cp.start()
        small_core.append(cp)
    for n in range(8, 11):
        sums.two(n)
    for yy in range(2):
        small_core[yy].wait_recv()
        v1[yy] = v0[2 * yy + k] + v1[yy]
    small_y = send(v1.at[1 - y], v2, ps.at[2], qs.at[2], ynb)
    small_y.start()
    sums.three(5)
    sums.four(4)
    sums.five(3)
    sums.six(1)
    sums.seven(0, targets[0])
    input_grad[...] = sum_grad[...] + dot_nt(lows[0], wq[...])
    input_grad[...] += dot_nt(lows[1], wk[...])
    input_grad[...] += dot_nt(lows[2], wv[...])
    sums.three(6)
    sums.four(5)
    sums.five(4)
    sums.six(2)
    sums.seven(1, targets[1])
    sums.three(7)
    sums.four(6)
    sums.five(5)
    sums.six(3)
    sums.seven(2, targets[2])
    sums.three(11)
    sums.four(7)
    sums.five(6)
    sums.six(4)
    sums.seven(3, targets[3])
    edge_y.wait_recv()
    e2[...] = e1[...] + e2[...]
    edge_x = send(e2, e3, pe.at[2], qe.at[2], twin)
    edge_x.start()

    @pl.when(y == 0)
    def _():
        send(t1, t2, pt.at[1], qt.at[1], ynb).wait_recv()
        for h in range(3):
            t2[h] = t1[h] + t2[h]
        send(t2.at[:, pl.ds(64 * (1 - group), 64)], t3, pt.at[2], qt.at[2], twin).start()

    sums.three(8)
    sums.four(11)
    sums.five(7)
    sums.six(5)
    sums.seven(4, targets[4])
    edge_x.wait_recv()
    me = lax.rem(c, 4)
    edge_out[c] = e2[...] + e3[...]
    edge_z = [send(edge_out.at[c], edge_out.at[c], pe.at[3 + i], qe.at[3 + z], zdev[i]) for i in range(3)]
    edge_z.append(send(edge_out.at[c], edge_out.at[c], pe.at[6], qe.at[7 + z], xnb))
    for cp in edge_z:
        cp.start()

    def table_piece(hg, side):
        return table_out.at[hg, :, pl.ds(64 * side, 64)]

    @pl.when(y == 0)
    def _():
        send(t2.at[:, pl.ds(0, 64)], t3, pt.at[2], qt.at[2], twin).wait_recv()
        at = pl.ds(pl.multiple_of(64 * group, 64), 64)
        for h in range(3):
            table_out[me, h, at, :] = t2[h, at, :] + t3[h]
        here = table_piece(me, group)
        for i in range(3):
            send(here, here, pt.at[3 + i], qt.at[3 + z], zdev[i]).start()
        send(here, here, pt.at[6], qt.at[7 + z], xnb).start()

    sums.three(9)
    sums.four(8)
    sums.five(11)
    sums.six(6)
    sums.seven(5, targets[5])
    small_y.wait_recv()
    v2[...] = v1[y] + v2[...]
    small_x = send(v2, v3, ps.at[3], qs.at[3], xnb)
    small_x.start()
    sums.three(10)
    sums.four(9)
    sums.five(8)
    sums.six(7)
    sums.seven(6, targets[6])
    small_x.wait_recv()
    v4[z] = v2[...] + v3[...]
    small_z = [send(v4.at[z], v4.at[z], ps.at[4 + i], qs.at[4 + z], zdev[i]) for i in range(3)]
    for cp in small_z:
        cp.start()
    sums.four(10)
    sums.five(9)
    sums.five(10)
    sums.six(11)
    sums.seven(7, targets[7])
    for i in (1, 2, 3):
        zz = lax.rem(z + i, 4)
        cc = 2 * zz + x
        there = edge_out.at[cc]
        send(there, there, pe.at[3], qe.at[3 + zz], core).wait_recv()
        cp = send(there, there, pe.at[6 + i], qe.at[7 + zz], xnb)
        cp.start()
        edge_z.append(cp)

    @pl.when(y == 0)
    def _():
        for i in (1, 2, 3):
            zz = lax.rem(z + i, 4)
            cc = 2 * zz + x
            there = table_piece(lax.rem(cc, 4), cc // 4)
            send(there, there, pt.at[3], qt.at[3 + zz], core).wait_recv()
            send(there, there, pt.at[6 + i], qt.at[7 + zz], xnb).start()

    sums.six(8)
    sums.seven(11, targets[11])
    sums.six(9)
    sums.seven(8, targets[8])
    sums.six(10)
    sums.seven(9, targets[9])
    for i in (1, 2, 3):
        zz = lax.rem(z + i, 4)
        send(v4.at[zz], v4.at[zz], ps.at[4], qs.at[4 + zz], core).wait_recv()
    small_out[...] = (v4[0] + v4[1]) + (v4[2] + v4[3])
    for zz in range(4):
        other = edge_out.at[2 * zz + 1 - x]
        send(other, other, pe.at[6], qe.at[7 + zz], xnb).wait_recv()

    @pl.when(y == 0)
    def _():
        for zz in range(4):
            cc = 2 * zz + 1 - x
            there = table_piece(lax.rem(cc, 4), cc // 4)
            send(there, there, pt.at[6], qt.at[7 + zz], xnb).wait_recv()

    sums.seven(10, targets[10])

    @pl.when(y == 0)
    def _():
        send(t2.at[:, pl.ds(0, 64)], t3, pt.at[2], qt.at[2], twin).wait_send()
        here = table_piece(0, 0)
        for i in range(3):
            send(here, here, pt.at[3 + i], qt.at[3], zdev[i]).wait_send()
        for i in range(4):
            send(here, here, pt.at[6 + i], qt.at[7], xnb).wait_send()

    @pl.when(y == 1)
    def _():
        send(t1, t2, pt.at[1], qt.at[1], ynb).wait_send()

    for cp in [tcore, ecore, small_y, small_x, edge_y, edge_x] + small_core + small_z + edge_z:
        cp.wait_send()
    for exchange in (heads_back, grads_there, grads_back):
        exchange.settle()
    for copies in plan:
        settle(copies)
    for cp in smalls:
        cp.wait_send()
    sums.settle()


def layer(tokens, tokens4, marks, upstream, arrays, table, small):
    dma = pltpu.SemaphoreType.DMA
    count = len(gather_pieces())

    def low(*shape):
        return pltpu.VMEM(shape, BF16)

    def wide(*shape):
        return pltpu.VMEM(shape, F32)

    scratch = [low(a.shape[0] * 4, a.shape[1]) for a in arrays]
    scratch += [low(3, 512, 384), low(4, 16, 256)]
    scratch += [
        low(4, ROWS, 640), low(48, 640), low(4, ROWS, 640), low(4, 48, 640),
        low(9, TALL, TALL),
        low(4, ROWS, 192), low(48, 192), low(4, ROWS, 192), low(4, 48, 192),
    ]
    scratch += [
        wide(ROWS, 768), wide(8, 128), wide(ROWS, 768), low(4, ROWS, 192),
        low(4, ROWS, 768), wide(4, ROWS, 768), low(4, ROWS, 768), wide(ROWS, 768), low(ROWS, 768),
    ]
    scratch += [
        low(4, ROWS, 192), low(4, 48, 192), low(4, ROWS, 192), low(48, 192),
        low(4, ROWS, 640), low(4, 48, 640), wide(3, TALL, TALL), low(3, ROWS, 768),
    ]
    scratch += [wide(4, 16, 256), wide(2, 16, 256), wide(16, 256), wide(16, 256), wide(4, 16, 256)]
    scratch += [low(3, 256, 256), low(3, 128, 256), low(3, 128, 256), low(3, 64, 256)]
    scratch += [wide(16, 384)] * 4
    scratch += [
        low(4, 2, 192, 768), low(12, 2, 192, 768), low(12, 192, 768), low(12, 96, 768),
        low(3, 4, 96, 768), low(12, 192, 768),
    ]
    sems = [dma((count, 5)), dma((count, 5)), dma((count + 1,)), dma((3,)), dma((3,))]
    for _ in range(4):
        sems += exchange_sems()
    sems += [
        dma((12, 2)), dma((12, 2)), dma((12,)), dma((12,)), dma((12,)), dma((12,)),
        dma((12,)), dma((3, 4)), dma((3, 3)), dma((12,)), dma((12,)), dma((12,)),
    ]
    sems += [dma((8,)), dma((8,)), dma((12,)), dma((12,)), dma((12,)), dma((12,))]
    return pl.pallas_call(
        layer_kernel,
        out_shape=[
            jax.ShapeDtypeStruct((ROWS, 768), BF16),
            jax.ShapeDtypeStruct((ROWS, 768), F32),
        ]
        + [jax.ShapeDtypeStruct((192, 768), F32)] * 4
        + [
            jax.ShapeDtypeStruct((192, 3072), F32),
            jax.ShapeDtypeStruct((768, 768), F32),
            jax.ShapeDtypeStruct((16, 256), F32),
            jax.ShapeDtypeStruct((4, 3, 128, 256), BF16),
            jax.ShapeDtypeStruct((8, 16, 384), F32),
        ],
        in_specs=[vmem_spec()] * 4 + [any_spec()] * 8,
        out_specs=[vmem_spec()] * 11,
        scratch_shapes=scratch + sems,
        compiler_params=pltpu.CompilerParams(
            collective_id=1, has_side_effects=True, vmem_limit_bytes=62 * 2**20
        ),
        name="layer",
    )(tokens, tokens4, marks, upstream, *arrays, table, small)


def block_device(
    hidden_in, segment_ids, doc_positions,
    w_query, w_key, w_value, w_out, b_query, b_value, b_out, ln1_gain, ln1_shift,
    w_inter, b_inter, w_final, b_final, ln2_gain, ln2_shift,
    mask_logits, mask_noise, grad_out,
):
    f = lax.axis_index("fsdp")
    doubled = 2.0 * (mask_logits + mask_noise)
    table_part = jax.nn.log_sigmoid(doubled[:, :, :384]).astype(BF16)
    vectors = (b_query, b_value, b_out, ln1_gain, ln1_shift, b_final, ln2_gain, ln2_shift)
    small = jnp.concatenate([jnp.stack(vectors), b_inter.reshape(4, 192)], axis=0)
    small = jnp.pad(small, ((0, 4), (0, 64)))
    tokens = hidden_in.reshape(ROWS, 768)
    tokens4 = jnp.stack([tokens[:, 192 * i : 192 * i + 192] for i in range(4)])
    marks = jnp.stack(
        [segment_ids.reshape(ROWS), (doc_positions % MSPAN).reshape(ROWS)], axis=1
    ).astype(BF16)
    marks = jnp.pad(marks, ((0, 0), (0, 62)))
    result, input_grad, oq, ok, ov, oo, oi, of, small_sum, table_sum, edge_sum = layer(
        tokens,
        tokens4,
        marks,
        grad_out.reshape(ROWS, 768),
        (w_query, w_key, w_value, w_out, w_inter, w_final),
        table_part,
        small,
    )
    vecs = [small_sum[i, :192] for i in range(8)]
    edge_rows = edge_sum[:4, 0:3].reshape(12, 1, 384)
    edge_columns = edge_sum[:4, 8:11].reshape(12, 384)
    column = lax.dynamic_slice(edge_columns, (0, 128 * jnp.minimum(f, 1)), (12, 128))
    at_row = lax.broadcasted_iota(jnp.int32, (1, 128, 512), 1)
    at_column = lax.broadcasted_iota(jnp.int32, (1, 128, 512), 2)
    wide = jnp.pad(table_sum.reshape(12, 128, 256).astype(F32), ((0, 0), (0, 0), (0, 256)))
    upper = jnp.where(at_column == 256, column[:, :, None], wide)
    lower = jnp.where(
        (at_row == 0) & (f == 2), jnp.pad(edge_rows, ((0, 0), (0, 0), (0, 128))), 0.0
    )
    table_total = jnp.where(f < 2, upper, lower)
    logit_grad = table_total * 2.0 * jax.nn.sigmoid(-doubled)
    return (
        result.reshape(hidden_in.shape),
        input_grad.reshape(hidden_in.shape),
        oq,
        ok,
        ov,
        oo,
        vecs[0],
        vecs[1],
        vecs[2],
        vecs[3],
        vecs[4],
        oi,
        small_sum[8:12, :192].reshape(768),
        of,
        vecs[5],
        vecs[6],
        vecs[7],
        logit_grad,
    )


def on_device(ctx_size, fsdp_size, hidden_in, *rest):
    if (ctx_size, fsdp_size, hidden_in.shape) == (8, 4, (3, 64, 768)):
        return block_device(hidden_in, *rest)
    return general_device(hidden_in, *rest)


def solution(mesh):
    in_specs = (
        P("fsdp", "ctx", None),
        P("fsdp", "ctx"),
        P("fsdp", "ctx"),
        P("fsdp", None),
        P("fsdp", None),
        P("fsdp", None),
        P("fsdp", None),
        P("fsdp"),
        P("fsdp"),
        P("fsdp"),
        P("fsdp"),
        P("fsdp"),
        P("fsdp", None),
        P("fsdp"),
        P("fsdp", None),
        P("fsdp"),
        P("fsdp"),
        P("fsdp"),
        P(None, "fsdp", None),
        P(None, "fsdp", None),
        P("fsdp", "ctx", None),
    )
    out_specs = (
        P("fsdp", "ctx", None),
        P("fsdp", "ctx", None),
        P("fsdp", None),
        P("fsdp", None),
        P("fsdp", None),
        P("fsdp", None),
        P("fsdp"),
        P("fsdp"),
        P("fsdp"),
        P("fsdp"),
        P("fsdp"),
        P("fsdp", None),
        P("fsdp"),
        P("fsdp", None),
        P("fsdp"),
        P("fsdp"),
        P("fsdp"),
        P(None, "fsdp", None),
    )
    return jax.shard_map(
        functools.partial(on_device, mesh.shape["ctx"], mesh.shape["fsdp"]), mesh=mesh, in_specs=in_specs, out_specs=out_specs, check_vma=False
    )
```

```python
import functools

import jax
import jax.numpy as jnp
from jax import lax
from jax.experimental import pallas as pl
from jax.experimental.pallas import tpu as pltpu
from jax.sharding import PartitionSpec as P

H = 12
HD = 64
MSPAN = 512


NEGATIVE = -1e30
EPSILON = 1e-12


def layer_norm(hidden, gain_row, shift_row):
    average = jnp.mean(hidden, axis=-1, keepdims=True)
    centered = hidden - average
    variance = jnp.mean(centered * centered, axis=-1, keepdims=True)
    return centered * lax.rsqrt(variance + EPSILON) * gain_row + shift_row


def exact_gelu(inner_act):
    return jax.nn.gelu(inner_act, approximate=False)


def left_product(first_op, second_op):
    return lax.dot_general(
        first_op, second_op, (((0,), (0,)), ((), ())), preferred_element_type=jnp.float32
    )


def right_product(first_op, second_op):
    return lax.dot_general(
        first_op, second_op, (((1,), (1,)), ((), ())), preferred_element_type=jnp.float32
    )


def one_hot_rows(slot_values, width):
    return (slot_values[:, None] == jnp.arange(width, dtype=jnp.int32)[None, :]).astype(
        jnp.bfloat16
    )


def block_scores(queries, key_part, seg_local, seg_part, bias_part):
    key_heads = key_part.reshape(key_part.shape[0], H, HD)
    raw_scores = (
        jnp.einsum("shd,nhd->hsn", queries, key_heads, preferred_element_type=jnp.float32) * 0.125
    )
    same_doc = seg_local[:, None] == seg_part[None, :]
    return jnp.where(same_doc[None], raw_scores + bias_part.astype(jnp.float32), NEGATIVE)


def split_blocks(array_in, block_size):
    return array_in.reshape((array_in.shape[0] // block_size, block_size) + array_in.shape[1:])


def block_length():
    return 512


def make_blocks(full_keys, full_values, full_segment, full_slot):
    block_size = block_length()
    return (
        split_blocks(full_keys, block_size),
        split_blocks(full_values, block_size),
        split_blocks(full_segment, block_size),
        split_blocks(full_slot, block_size),
    )


def row_statistics(queries, seg_local, table_rows, blocks):
    rows = queries.shape[0]

    def advance(state_carry, key_block):
        key_part, value_part, seg_part, slot_part = key_block

        def compute(pair):
            row_top, row_total = pair
            bias_part = jnp.einsum(
                "hsa,na->hsn",
                table_rows,
                one_hot_rows(slot_part, MSPAN),
                preferred_element_type=jnp.float32,
            ).astype(jnp.bfloat16)
            scores = block_scores(queries, key_part, seg_local, seg_part, bias_part)
            new_top = jnp.maximum(row_top, jnp.max(scores, axis=-1))
            row_total = row_total * jnp.exp(row_top - new_top) + jnp.sum(
                jnp.exp(scores - new_top[..., None]), axis=-1
            )
            return ((new_top, row_total), bias_part)

        return compute(state_carry)

    start_state = (jnp.full((H, rows), NEGATIVE, jnp.float32), jnp.zeros((H, rows), jnp.float32))
    (row_top, row_total), bias_blocks = lax.scan(advance, start_state, blocks)
    return (row_top + jnp.log(row_total), bias_blocks)


def attention_output(queries, seg_local, blocks, bias_blocks, log_total):
    rows = queries.shape[0]

    def advance(accumulated, items):
        (key_part, value_part, seg_part, slot_part), bias_part = items

        def compute(current):
            scores = block_scores(queries, key_part, seg_local, seg_part, bias_part)
            soft_weights = jnp.exp(scores - log_total[..., None]).astype(jnp.bfloat16)
            value_heads = value_part.reshape(value_part.shape[0], H, HD)
            return current + jnp.einsum(
                "hsn,nhd->shd", soft_weights, value_heads, preferred_element_type=jnp.float32
            )

        return (compute(accumulated), None)

    context, _ = lax.scan(advance, jnp.zeros((rows, H, HD), jnp.float32), (blocks, bias_blocks))
    return context


def attention_backward(queries, seg_local, blocks, bias_blocks, log_total, context_grad, row_delta):
    rows = queries.shape[0]

    def advance(state_carry, items):
        (key_part, value_part, seg_part, slot_part), bias_part = items
        key_count = key_part.shape[0]

        def compute(operand):
            query_acc, slot_acc = operand
            scores = block_scores(queries, key_part, seg_local, seg_part, bias_part)
            soft_float = jnp.exp(scores - log_total[..., None])
            key_heads = key_part.reshape(key_count, H, HD)
            value_heads = value_part.reshape(key_count, H, HD)
            weight_grad = jnp.einsum(
                "shd,nhd->hsn", context_grad, value_heads, preferred_element_type=jnp.float32
            )
            score_grad = (soft_float * (weight_grad - row_delta[..., None])).astype(jnp.bfloat16)
            query_acc = (
                query_acc
                + jnp.einsum(
                    "hsn,nhd->shd", score_grad, key_heads, preferred_element_type=jnp.float32
                )
                * 0.125
            )
            slot_acc = slot_acc + jnp.einsum(
                "hsn,na->hsa",
                score_grad,
                one_hot_rows(slot_part, MSPAN),
                preferred_element_type=jnp.float32,
            )
            key_block_grad = (
                jnp.einsum("hsn,shd->nhd", score_grad, queries, preferred_element_type=jnp.float32)
                * 0.125
            )
            value_block_grad = jnp.einsum(
                "hsn,shd->nhd",
                soft_float.astype(jnp.bfloat16),
                context_grad,
                preferred_element_type=jnp.float32,
            )
            return ((query_acc, slot_acc), (key_block_grad, value_block_grad))

        return compute(state_carry)

    start_state = (jnp.zeros((rows, H, HD), jnp.float32), jnp.zeros((H, rows, MSPAN), jnp.float32))
    (query_acc, slot_acc), block_grads = lax.scan(advance, start_state, (blocks, bias_blocks))
    key_grads, value_grads = block_grads
    full_len = key_grads.shape[0] * key_grads.shape[1]
    return (
        query_acc,
        slot_acc,
        key_grads.reshape(full_len, H * HD),
        value_grads.reshape(full_len, H * HD),
    )


def general_device(
    hidden_in,
    segment_ids,
    doc_positions,
    w_query,
    w_key,
    w_value,
    w_out,
    b_query,
    b_value,
    b_out,
    ln1_gain,
    ln1_shift,
    w_inter,
    b_inter,
    w_final,
    b_final,
    ln2_gain,
    ln2_shift,
    mask_logits,
    mask_noise,
    grad_out,
):
    table_part = jax.nn.log_sigmoid(2.0 * (mask_logits + mask_noise)).astype(jnp.bfloat16)
    (
        wq_full,
        wk_full,
        wv_full,
        wo_full,
        wi_full,
        wf_full,
        bq_full,
        bv_full,
        bo_full,
        bi_full,
        bf_full,
        gain_one,
        shift_one,
        gain_two,
        shift_two,
        table_full,
    ) = (
        lax.all_gather(w_query, "fsdp", axis=0, tiled=True),
        lax.all_gather(w_key, "fsdp", axis=0, tiled=True),
        lax.all_gather(w_value, "fsdp", axis=0, tiled=True),
        lax.all_gather(w_out, "fsdp", axis=0, tiled=True),
        lax.all_gather(w_inter, "fsdp", axis=0, tiled=True),
        lax.all_gather(w_final, "fsdp", axis=0, tiled=True),
        lax.all_gather(b_query, "fsdp", axis=0, tiled=True),
        lax.all_gather(b_value, "fsdp", axis=0, tiled=True),
        lax.all_gather(b_out, "fsdp", axis=0, tiled=True),
        lax.all_gather(b_inter, "fsdp", axis=0, tiled=True),
        lax.all_gather(b_final, "fsdp", axis=0, tiled=True),
        lax.all_gather(ln1_gain, "fsdp", axis=0, tiled=True),
        lax.all_gather(ln1_shift, "fsdp", axis=0, tiled=True),
        lax.all_gather(ln2_gain, "fsdp", axis=0, tiled=True),
        lax.all_gather(ln2_shift, "fsdp", axis=0, tiled=True),
        lax.all_gather(table_part, "fsdp", axis=1, tiled=True),
    )
    bq_full, bv_full, bo_full = (
        bq_full.astype(jnp.float32),
        bv_full.astype(jnp.float32),
        bo_full.astype(jnp.float32),
    )
    bi_full, bf_full = (bi_full.astype(jnp.float32), bf_full.astype(jnp.float32))
    gain_one, shift_one = (gain_one.astype(jnp.float32), shift_one.astype(jnp.float32))
    gain_two, shift_two = (gain_two.astype(jnp.float32), shift_two.astype(jnp.float32))
    micro_count = hidden_in.shape[0]
    rows = hidden_in.shape[1]
    saved = []
    outputs_list = []
    for micro_batch in range(micro_count):
        tokens = hidden_in[micro_batch]
        seg_local = segment_ids[micro_batch]
        slot_local = doc_positions[micro_batch] % MSPAN
        queries_flat = (
            jnp.dot(tokens, wq_full, preferred_element_type=jnp.float32) + bq_full
        ).astype(jnp.bfloat16)
        keys_local = jnp.dot(tokens, wk_full, preferred_element_type=jnp.float32).astype(
            jnp.bfloat16
        )
        values_local = (
            jnp.dot(tokens, wv_full, preferred_element_type=jnp.float32) + bv_full
        ).astype(jnp.bfloat16)
        gathered = (
            lax.all_gather(keys_local, "ctx", axis=0, tiled=True),
            lax.all_gather(values_local, "ctx", axis=0, tiled=True),
            lax.all_gather(seg_local, "ctx", axis=0, tiled=True),
            lax.all_gather(slot_local, "ctx", axis=0, tiled=True),
        )
        blocks = make_blocks(*gathered)
        queries = queries_flat.reshape(rows, H, HD)
        table_rows = table_full[:, slot_local, :]
        log_total, bias_blocks = row_statistics(queries, seg_local, table_rows, blocks)
        context = attention_output(queries, seg_local, blocks, bias_blocks, log_total)
        context_low = context.reshape(rows, H * HD).astype(jnp.bfloat16)
        attn_out = jnp.dot(context_low, wo_full, preferred_element_type=jnp.float32) + bo_full
        first_norm, norm_one_back = jax.vjp(
            layer_norm, tokens.astype(jnp.float32) + attn_out, gain_one, shift_one
        )
        first_low = first_norm.astype(jnp.bfloat16)
        inner_act = jnp.dot(first_low, wi_full, preferred_element_type=jnp.float32) + bi_full
        active, gelu_back = jax.vjp(exact_gelu, inner_act)
        active_low = active.astype(jnp.bfloat16)
        ffn_out = jnp.dot(active_low, wf_full, preferred_element_type=jnp.float32) + bf_full
        result, norm_two_back = jax.vjp(layer_norm, first_norm + ffn_out, gain_two, shift_two)
        outputs_list.append(result.astype(jnp.bfloat16))
        kept_blocks = blocks
        saved.append(
            (
                tokens,
                seg_local,
                slot_local,
                queries,
                keys_local,
                values_local,
                log_total,
                bias_blocks,
                context,
                context_low,
                first_low,
                active_low,
                norm_one_back,
                gelu_back,
                norm_two_back,
                kept_blocks,
            )
        )
    zeros_square = jnp.zeros((H * HD, H * HD), jnp.float32)
    wq_grad, wk_grad, wv_grad, wo_grad = (zeros_square, zeros_square, zeros_square, zeros_square)
    wi_grad = jnp.zeros(wi_full.shape, jnp.float32)
    wf_grad = jnp.zeros(wf_full.shape, jnp.float32)
    zeros_row = jnp.zeros((H * HD,), jnp.float32)
    bq_grad, bv_grad, bo_grad, bf_grad = (zeros_row, zeros_row, zeros_row, zeros_row)
    gain_one_grad, shift_one_grad, gain_two_grad, shift_two_grad = (
        zeros_row,
        zeros_row,
        zeros_row,
        zeros_row,
    )
    bi_grad = jnp.zeros(bi_full.shape, jnp.float32)
    table_grad = jnp.zeros(table_full.shape, jnp.float32)
    input_grads = []
    for micro_batch in range(micro_count):
        (
            tokens,
            seg_local,
            slot_local,
            queries,
            keys_local,
            values_local,
            log_total,
            bias_blocks,
            context,
            context_low,
            first_low,
            active_low,
            norm_one_back,
            gelu_back,
            norm_two_back,
            kept_blocks,
        ) = saved[micro_batch]
        upstream = grad_out[micro_batch].astype(jnp.float32)
        sum_grad, gain_part, shift_part = norm_two_back(upstream)
        gain_two_grad = gain_two_grad + gain_part
        shift_two_grad = shift_two_grad + shift_part
        ffn_grad = sum_grad.astype(jnp.bfloat16)
        bf_grad = bf_grad + jnp.sum(ffn_grad.astype(jnp.float32), axis=0)
        wf_grad = wf_grad + left_product(active_low, ffn_grad)
        active_grad = right_product(ffn_grad, wf_full).astype(jnp.bfloat16)
        (inner_float,) = gelu_back(active_grad.astype(jnp.float32))
        inner_grad = inner_float.astype(jnp.bfloat16)
        bi_grad = bi_grad + jnp.sum(inner_grad.astype(jnp.float32), axis=0)
        wi_grad = wi_grad + left_product(first_low, inner_grad)
        first_grad = sum_grad + right_product(inner_grad, wi_full)
        norm_grad, gain_part, shift_part = norm_one_back(first_grad)
        gain_one_grad = gain_one_grad + gain_part
        shift_one_grad = shift_one_grad + shift_part
        attn_grad = norm_grad.astype(jnp.bfloat16)
        bo_grad = bo_grad + jnp.sum(attn_grad.astype(jnp.float32), axis=0)
        wo_grad = wo_grad + left_product(context_low, attn_grad)
        context_grad_flat = right_product(attn_grad, wo_full).astype(jnp.bfloat16)
        context_grad = context_grad_flat.reshape(rows, H, HD)
        row_delta = jnp.einsum("shd,shd->hs", context_grad.astype(jnp.float32), context)
        blocks = kept_blocks
        query_acc, slot_acc, key_full_grad, value_full_grad = attention_backward(
            queries, seg_local, blocks, bias_blocks, log_total, context_grad, row_delta
        )
        key_share, value_share = (
            lax.psum_scatter(
                key_full_grad.astype(jnp.bfloat16), "ctx", scatter_dimension=0, tiled=True
            ).astype(jnp.float32),
            lax.psum_scatter(
                value_full_grad.astype(jnp.bfloat16), "ctx", scatter_dimension=0, tiled=True
            ).astype(jnp.float32),
        )
        table_grad = table_grad.at[:, slot_local, :].add(slot_acc)
        query_low = query_acc.reshape(rows, H * HD).astype(jnp.bfloat16)
        key_low = key_share.astype(jnp.bfloat16)
        value_low = value_share.astype(jnp.bfloat16)
        bq_grad = bq_grad + jnp.sum(query_low.astype(jnp.float32), axis=0)
        bv_grad = bv_grad + jnp.sum(value_low.astype(jnp.float32), axis=0)
        wq_grad = wq_grad + left_product(tokens, query_low)
        wk_grad = wk_grad + left_product(tokens, key_low)
        wv_grad = wv_grad + left_product(tokens, value_low)
        input_grads.append(
            norm_grad
            + right_product(query_low, wq_full)
            + right_product(key_low, wk_full)
            + right_product(value_low, wv_full)
        )
    shares = (
        lax.psum_scatter(
            wq_grad.astype(jnp.bfloat16), "fsdp", scatter_dimension=0, tiled=True
        ).astype(jnp.float32),
        lax.psum_scatter(
            wk_grad.astype(jnp.bfloat16), "fsdp", scatter_dimension=0, tiled=True
        ).astype(jnp.float32),
        lax.psum_scatter(
            wv_grad.astype(jnp.bfloat16), "fsdp", scatter_dimension=0, tiled=True
        ).astype(jnp.float32),
        lax.psum_scatter(
            wo_grad.astype(jnp.bfloat16), "fsdp", scatter_dimension=0, tiled=True
        ).astype(jnp.float32),
        lax.psum_scatter(
            bq_grad.astype(jnp.bfloat16), "fsdp", scatter_dimension=0, tiled=True
        ).astype(jnp.float32),
        lax.psum_scatter(
            bv_grad.astype(jnp.bfloat16), "fsdp", scatter_dimension=0, tiled=True
        ).astype(jnp.float32),
        lax.psum_scatter(
            bo_grad.astype(jnp.bfloat16), "fsdp", scatter_dimension=0, tiled=True
        ).astype(jnp.float32),
        lax.psum_scatter(
            gain_one_grad.astype(jnp.bfloat16), "fsdp", scatter_dimension=0, tiled=True
        ).astype(jnp.float32),
        lax.psum_scatter(
            shift_one_grad.astype(jnp.bfloat16), "fsdp", scatter_dimension=0, tiled=True
        ).astype(jnp.float32),
        lax.psum_scatter(
            wi_grad.astype(jnp.bfloat16), "fsdp", scatter_dimension=0, tiled=True
        ).astype(jnp.float32),
        lax.psum_scatter(
            bi_grad.astype(jnp.bfloat16), "fsdp", scatter_dimension=0, tiled=True
        ).astype(jnp.float32),
        lax.psum_scatter(
            wf_grad.astype(jnp.bfloat16), "fsdp", scatter_dimension=0, tiled=True
        ).astype(jnp.float32),
        lax.psum_scatter(
            bf_grad.astype(jnp.bfloat16), "fsdp", scatter_dimension=0, tiled=True
        ).astype(jnp.float32),
        lax.psum_scatter(
            gain_two_grad.astype(jnp.bfloat16), "fsdp", scatter_dimension=0, tiled=True
        ).astype(jnp.float32),
        lax.psum_scatter(
            shift_two_grad.astype(jnp.bfloat16), "fsdp", scatter_dimension=0, tiled=True
        ).astype(jnp.float32),
        lax.psum_scatter(
            table_grad.astype(jnp.bfloat16), "fsdp", scatter_dimension=1, tiled=True
        ).astype(jnp.float32),
    )
    totals = (
        lax.psum(shares[0].astype(jnp.bfloat16), "ctx").astype(jnp.float32),
        lax.psum(shares[1].astype(jnp.bfloat16), "ctx").astype(jnp.float32),
        lax.psum(shares[2].astype(jnp.bfloat16), "ctx").astype(jnp.float32),
        lax.psum(shares[3].astype(jnp.bfloat16), "ctx").astype(jnp.float32),
        lax.psum(shares[4].astype(jnp.bfloat16), "ctx").astype(jnp.float32),
        lax.psum(shares[5].astype(jnp.bfloat16), "ctx").astype(jnp.float32),
        lax.psum(shares[6].astype(jnp.bfloat16), "ctx").astype(jnp.float32),
        lax.psum(shares[7].astype(jnp.bfloat16), "ctx").astype(jnp.float32),
        lax.psum(shares[8].astype(jnp.bfloat16), "ctx").astype(jnp.float32),
        lax.psum(shares[9].astype(jnp.bfloat16), "ctx").astype(jnp.float32),
        lax.psum(shares[10].astype(jnp.bfloat16), "ctx").astype(jnp.float32),
        lax.psum(shares[11].astype(jnp.bfloat16), "ctx").astype(jnp.float32),
        lax.psum(shares[12].astype(jnp.bfloat16), "ctx").astype(jnp.float32),
        lax.psum(shares[13].astype(jnp.bfloat16), "ctx").astype(jnp.float32),
        lax.psum(shares[14].astype(jnp.bfloat16), "ctx").astype(jnp.float32),
        lax.psum(shares[15].astype(jnp.bfloat16), "ctx").astype(jnp.float32),
    )
    (
        wq_total,
        wk_total,
        wv_total,
        wo_total,
        bq_total,
        bv_total,
        bo_total,
        gain_one_total,
        shift_one_total,
        wi_total,
        bi_total,
        wf_total,
        bf_total,
        gain_two_total,
        shift_two_total,
        table_total,
    ) = totals
    logit_grad = table_total * 2.0 * jax.nn.sigmoid(-2.0 * (mask_logits + mask_noise))
    return (
        jnp.stack(outputs_list),
        jnp.stack(input_grads),
        wq_total,
        wk_total,
        wv_total,
        wo_total,
        bq_total,
        bv_total,
        bo_total,
        gain_one_total,
        shift_one_total,
        wi_total,
        bi_total,
        wf_total,
        bf_total,
        gain_two_total,
        shift_two_total,
        logit_grad,
    )


MESH = pl.DeviceIdType.MESH
BF16 = jnp.bfloat16
F32 = jnp.float32
ROWS = 192
TALL = 272


ROOT_HALF = 0.7071067811865476
ROOT_TWO_PI = 0.3989422804014327


def place():
    c = lax.axis_index("ctx")
    f = lax.axis_index("fsdp")
    return (c // 2, c % 2, f // 2, f % 2)


def device(z, x, y, k):
    return {"ctx": z * 2 + x, "fsdp": y * 2 + k}


def send(src, dst, send_sem, recv_sem, target):
    return pltpu.make_async_remote_copy(
        src_ref=src,
        dst_ref=dst,
        send_sem=send_sem,
        recv_sem=recv_sem,
        device_id=target,
        device_id_type=MESH,
    )


def meet(targets):
    barrier = pltpu.get_barrier_semaphore()
    for target in targets:
        pl.semaphore_signal(barrier, inc=1, device_id=target, device_id_type=MESH)
    pl.semaphore_wait(barrier, len(targets))


def any_spec():
    return pl.BlockSpec(memory_space=pl.ANY)


def vmem_spec():
    return pl.BlockSpec(memory_space=pltpu.VMEM)


def gather_pieces():
    pieces = [(array, 0, 192, 0, 768, False) for array in range(3)]
    pieces.append((3, 0, 192, 0, 768, False))
    pieces.append((6, 0, 0, 0, 0, True))
    for part in range(2):
        pieces.append((4, 0, 192, 1536 * part, 1536, False))
    for part in range(4):
        pieces.append((5, 192 * part, 192, 0, 768, part > 1))
    return pieces


def gather_plan(ins, outs, small, small_out, sems):
    ss, rs, ls, ss_small, rs_small = sems
    z, x, y, k = place()
    mine = y * 2 + k
    over = (1 - y) * 2 + k
    core = device(z, x, y, 1 - k)
    ynb = device(z, x, 1 - y, k)
    diag = device(z, x, 1 - y, 1 - k)
    xnb = device(z, 1 - x, y, k)

    def source(piece, half):
        a, r0, rn, c0, cn, _ = piece
        if a == 6:
            return ins[a]
        if half is None:
            return ins[a].at[pl.ds(r0, rn), pl.ds(c0, cn)]
        return ins[a].at[pl.ds(r0 + (rn // 2) * half, rn // 2), pl.ds(c0, cn)]

    def target(piece, owner, half):
        a, r0, rn, c0, cn, _ = piece
        if a == 6:
            return outs[a].at[:, pl.ds(128 * owner, 128)]
        base = ins[a].shape[0] * owner + r0
        if half is None:
            return outs[a].at[pl.ds(base, rn), pl.ds(c0, cn)]
        return outs[a].at[pl.ds(base + (rn // 2) * half, rn // 2), pl.ds(c0, cn)]

    plan = []
    for n, piece in enumerate(gather_pieces()):
        both = piece[5]
        part = None if both else x
        whole = source(piece, None)
        kept = target(piece, mine, None)
        here = target(piece, over, part)
        copies = {
            "own": pltpu.make_async_copy(whole, kept, ls.at[n]),
            "core": send(whole, kept, ss.at[n, 0], rs.at[n, 0], core),
            "y": send(source(piece, part), target(piece, mine, part), ss.at[n, 1], rs.at[n, 1], ynb),
            "core_y": send(here, here, ss.at[n, 3], rs.at[n, 3], core),
        }
        if not both:
            there = target(piece, over, 1 - x)
            copies["x"] = send(here, here, ss.at[n, 2], rs.at[n, 2], xnb)
            copies["core_x"] = send(there, there, ss.at[n, 4], rs.at[n, 4], core)
        plan.append(copies)
    rows = small_out.at[mine]
    smalls = [
        send(small, rows, ss_small.at[i], rs_small.at[i], peer)
        for i, peer in enumerate((core, ynb, diag))
    ]
    own_small = pltpu.make_async_copy(small, rows, ls.at[len(plan)])
    return (plan, smalls, own_small)


def forward_y(copies):
    copies["y"].wait_recv()
    if "x" in copies:
        copies["x"].start()
    copies["core_y"].start()


def forward_x(copies):
    if "x" in copies:
        copies["x"].wait_recv()
        copies["core_x"].start()


def arrive(copies):
    copies["own"].wait()
    for name in ("core", "core_y", "core_x"):
        if name in copies:
            copies[name].wait_recv()


def settle(copies):
    for name, cp in copies.items():
        if name != "own":
            cp.wait_send()


def ctx_peers():
    c = lax.axis_index("ctx")
    return [{"ctx": lax.rem(c + i, 8)} for i in range(1, 8)]


class Exchange:
    def __init__(self, main, main_in, extra, extra_in, sems, home):
        self.main, self.main_in, self.extra, self.extra_in = (main, main_in, extra, extra_in)
        self.ms, self.mr, self.es, self.er, self.ls = sems
        self.c = lax.axis_index("ctx")
        self.group, self.me = (self.c // 4, lax.rem(self.c, 4))
        self.home = home

    def one(self, j, slot):
        return send(
            self.main.at[j],
            self.main_in.at[slot],
            self.ms.at[j],
            self.mr.at[slot],
            {"ctx": 4 * self.group + j},
        )

    def local(self, j):
        return pltpu.make_async_copy(self.main.at[j], self.main_in.at[j], self.ls)

    def side(self, j):
        if self.home:
            return send(
                self.extra, self.extra_in.at[self.me], self.es.at[0], self.er.at[self.me], {"ctx": 4}
            )
        return send(self.extra.at[j], self.extra_in, self.es.at[j], self.er.at[0], {"ctx": j})

    def start(self):
        for j in range(4):

            @pl.when(self.me != j)
            def _():
                self.one(j, self.me).start()

            @pl.when(self.me == j)
            def _():
                self.local(j).start()

        if self.home:

            @pl.when(self.group == 0)
            def _():
                self.side(0).start()

        else:

            @pl.when(self.c == 4)
            def _():
                for j in range(4):
                    self.side(j).start()

    def wait(self):
        for j in range(4):

            @pl.when(self.me != j)
            def _():
                self.one(0, j).wait_recv()

            @pl.when(self.me == j)
            def _():
                self.local(j).wait()

        if self.home:

            @pl.when(self.c == 4)
            def _():
                for j in range(4):
                    send(
                        self.extra, self.extra_in.at[j], self.es.at[0], self.er.at[j], {"ctx": 4}
                    ).wait_recv()

        else:

            @pl.when(self.group == 0)
            def _():
                self.side(0).wait_recv()

    def settle(self):
        for j in range(4):

            @pl.when(self.me != j)
            def _():
                self.one(j, self.me).wait_send()

        if self.home:

            @pl.when(self.group == 0)
            def _():
                self.side(0).wait_send()

        else:

            @pl.when(self.c == 4)
            def _():
                for j in range(4):
                    self.side(j).wait_send()


def exchange_sems():
    dma = pltpu.SemaphoreType.DMA
    return [dma((4,)), dma((4,)), dma((4,)), dma((4,)), dma]


def dot_nn(a, b):
    return lax.dot_general(a, b, (((1,), (0,)), ((), ())), preferred_element_type=F32)


def dot_nt(a, b):
    return lax.dot_general(a, b, (((1,), (1,)), ((), ())), preferred_element_type=F32)


def dot_tn(a, b):
    return lax.dot_general(a, b, (((0,), (0,)), ((), ())), preferred_element_type=F32)


def group_rows(main, extra, s, lo, width):
    top = main[:, pl.ds(64 * s, 64), lo : lo + width].reshape(256, width)
    return jnp.concatenate([top, extra[pl.ds(16 * s, 16), lo : lo + width]], axis=0)


def place_masks(main, extra, s, group):
    marks = group_rows(main, extra, s, 576, 64).astype(F32)
    segment = marks[:, 0:1]
    slot = marks[:, 1:2]
    first = segment == 0.0
    valid = jnp.where(
        group == 0, jnp.where(first, 1.0, 0.0), jnp.where(first | (segment < 0.0), 0.0, 1.0)
    )
    lanes = lax.broadcasted_iota(jnp.int32, (TALL, 128), 1).astype(F32)
    seg_hot = jnp.where((lanes == segment) & (valid > 0.0), 1.0, 0.0).astype(BF16)
    wide = lax.broadcasted_iota(jnp.int32, (TALL, TALL), 1).astype(F32)
    slot_hot = jnp.where((wide == slot) & (valid > 0.0), 1.0, 0.0).astype(BF16)
    return (slot_hot, dot_nt(seg_hot, seg_hot) > 0.5, valid)


class BlockSums:
    def __init__(self, bufs, sems, blocks):
        self.blocks = blocks
        self.st, self.r1, self.r2, self.r3, self.r4, self.total = bufs
        self.p1, self.q1, self.p2, self.q2, self.p3, self.q3, self.p4, self.q4 = sems[:8]
        self.p5, self.q5, self.p6, self.q6, self.kept = sems[8:]
        z, x, y, k = place()
        self.z, self.x, self.y, self.k = (z, x, y, k)
        self.core = device(z, x, y, 1 - k)
        self.ynb = device(z, x, 1 - y, k)
        self.xnb = device(z, 1 - x, y, k)
        self.peers = [lax.rem(z + i, 4) for i in (1, 2, 3)]
        self.columns = pl.ds(pl.multiple_of(384 * x, 128), 384)
        self.others = pl.ds(pl.multiple_of(384 * (1 - x), 128), 384)

    def zdev(self, zz):
        return device(zz, self.x, self.y, self.k)

    def to_core(self, n, yy):
        slot = n % 4
        return send(
            self.st.at[slot, yy], self.r1.at[n, yy], self.p1.at[n, yy], self.q1.at[n, yy], self.core
        )

    def to_y(self, n):
        return send(
            self.r1.at[n, 1 - self.y], self.r2.at[n], self.p2.at[n], self.q2.at[n], self.ynb
        )

    def sum_x(self, n):
        return send(
            self.r2.at[n, :, self.others], self.r3.at[n], self.p3.at[n], self.q3.at[n], self.xnb
        )

    def sum_z(self, n, i):
        zz = self.peers[i]
        return send(
            self.r3.at[n, pl.ds(48 * zz, 48)],
            self.r4.at[n, self.z],
            self.p4.at[n, i],
            self.q4.at[n, self.z],
            self.zdev(zz),
        )

    def view(self, n, rows):
        ref, row, column = self.blocks[n if isinstance(n, int) else 0]
        if rows == slice(None):
            rows = pl.ds(row, 192)
        else:
            rows = pl.ds(rows.start + row, rows.size)
        return ref.at[rows, pl.ds(pl.multiple_of(column + 384 * self.x, 128), 384)]

    def spread_z(self, n, i, owner):
        here = self.view(n, pl.ds(48 * owner, 48))
        return send(
            self.total.at[n], here, self.p5.at[n, i], self.q5.at[n, owner], self.zdev(self.peers[i])
        )

    def keep(self, n):
        here = self.view(n, pl.ds(48 * self.z, 48))
        return pltpu.make_async_copy(self.total.at[n], here, self.kept.at[n])

    def spread_x(self, n):
        here = self.view(n, slice(None))
        return send(here, here, self.p6.at[n], self.q6.at[n], self.xnb)

    def one(self, n, partial):
        for yy in range(2):
            self.st[n % 4, yy] = partial(2 * yy + 1 - self.k).astype(BF16)
            self.to_core(n, yy).start()

    def two(self, n, partial):
        for yy in range(2):
            own = partial(2 * yy + self.k)
            self.to_core(n, yy).wait_recv()
            self.r1[n, yy] = (own + self.r1[n, yy].astype(F32)).astype(BF16)
        self.to_y(n).start()

    def three(self, n):
        self.to_y(n).wait_recv()

        def body(i, carry):
            at = pl.ds(pl.multiple_of(i * 48, 48), 48)
            self.r2[n, at, :] = self.r2[n, at, :] + self.r1[n, self.y, at, :]
            return carry

        lax.fori_loop(0, 4, body, 0)
        self.sum_x(n).start()

    def four(self, n):
        self.sum_x(n).wait_recv()

        def body(i, carry):
            at = pl.ds(pl.multiple_of(i * 48, 48), 48)
            self.r3[n, at, :] = self.r3[n, at, :] + self.r2[n, at, self.columns]
            return carry

        lax.fori_loop(0, 4, body, 0)
        for i in range(3):
            self.sum_z(n, i).start()

    def five(self, n):
        for i in range(3):
            zz = self.peers[i]
            send(
                self.r3.at[n, pl.ds(0, 48)],
                self.r4.at[n, zz],
                self.p4.at[n, 0],
                self.q4.at[n, zz],
                self.core,
            ).wait_recv()
        rows = pl.ds(pl.multiple_of(48 * self.z, 16), 48)
        total = self.r3[n, rows, :].astype(F32)
        for i in range(3):
            total = total + self.r4[n, self.peers[i]].astype(F32)
        self.total[n] = total.astype(BF16)
        self.keep(n).start()
        for i in range(3):
            self.spread_z(n, i, self.z).start()

    def six(self, n):
        self.keep(n).wait()
        for i in range(3):
            self.spread_z(n, i, self.peers[i]).wait_recv()
        self.spread_x(n).start()

    def seven(self, n):
        self.spread_x(n).wait_recv()

    def settle(self):
        def body(n, carry):
            self.to_y(n).wait_send()
            self.sum_x(n).wait_send()
            self.spread_x(n).wait_send()
            for i in range(3):
                self.sum_z(n, i).wait_send()
                self.spread_z(n, i, self.z).wait_send()
            return carry

        lax.fori_loop(0, 12, body, 0)
        for n in range(8, 12):
            for yy in range(2):
                self.to_core(n, yy).wait_send()


def layer_kernel(
    tokens, segments, places, upstream, *vectors_and_more
):
    vectors, rest = (vectors_and_more[:9], vectors_and_more[9:])
    layer_body(tokens, segments, places, upstream, vectors, *rest)


def layer_body(
    tokens, segments, places, upstream, vectors,
    wq_in, wk_in, wv_in, wo_in, wi_in, wf_in, logits_in, noise_in,
    hidden_out, input_grad, oh, oi, of, small_out, mask_out,
    wq, wk, wv, wo, wi, wf, table, small,
    main, extra, main_send, extra_send, probs, ctx_send, ctx_extra, ctx4, ctx_extra_in,
    small_in, marks, active, table_in, tokens4, first_hat, first_norm, first4, active16, slope, inner, sum_grad, low_grad,
    grad4, grad_extra, grad_in, grad_extra_in, main_in, extra_in, table_grad, lows,
    v0, v1, v2, v3, v4, t0, t1, t2, t3, e0, e1, e2, e3, table_out, edge_out,
    st, r1, r2, r3, r4, total, hidden_low, input_sum, mask_sum, *sems
):
    z, x, y, k = place()
    c = 2 * z + x
    group = c // 4
    core = device(z, x, y, 1 - k)
    ynb = device(z, x, 1 - y, k)
    xnb = device(z, 1 - x, y, k)
    twin = device(lax.rem(z + 2, 4), x, y, k)
    zdev = [device(lax.rem(z + i, 4), x, y, k) for i in (1, 2, 3)]
    gather_sems, ex = (sems[:5], [sems[5 + 5 * i : 10 + 5 * i] for i in range(4)])
    sum_sems, (ps, qs, pt, qt, pe, qe, load) = (sems[25:38], sems[38:45])
    heads = pl.ds(3 * lax.rem(c, 4), 3)
    near = pl.ds(0, 384)
    loads = [
        pltpu.make_async_copy(
            logits_in.at[heads, :, near], slope.at[0:3, 0:128, 0:384], load.at[0]
        ),
        pltpu.make_async_copy(
            noise_in.at[heads, :, near], slope.at[0:3, 0:128, 384:768], load.at[1]
        ),
    ]
    for cp in loads:
        cp.start()
    meet(ctx_peers() + [core, ynb, device(z, x, 1 - y, 1 - k)])

    for i in range(8):
        small_in[i : i + 1, 0:192] = vectors[i][...].astype(F32).reshape(1, 192)
    for i in range(4):
        small_in[8 + i : 9 + i, 0:192] = (
            vectors[8][192 * i : 192 * i + 192].astype(F32).reshape(1, 192)
        )
    plan, smalls, own_small = gather_plan(
        (wq_in, wk_in, wv_in, wo_in, wi_in, wf_in, table_in),
        (wq, wk, wv, wo, wi, wf, table),
        small_in,
        small,
        gather_sems,
    )
    for cp in smalls + [own_small]:
        cp.start()
    for n in range(3):
        for name in ("y", "core", "own"):
            plan[n][name].start()
    for cp in loads:
        cp.wait()
    for h in range(3):
        doubled = 2.0 * (slope[h, 0:128, 0:384] + slope[h, 0:128, 384:768])
        table_in[h] = (
            jnp.minimum(doubled, 0.0) - jnp.log1p(jnp.exp(-jnp.abs(doubled)))
        ).astype(BF16)
    for n in range(3, len(plan)):
        for name in ("y", "core", "own"):
            plan[n][name].start()
    forward_y(plan[0])
    forward_y(plan[1])
    for j in range(4):
        tokens4[j] = tokens[:, 192 * j : 192 * j + 192]
    down = lax.broadcasted_iota(jnp.int32, (64, 64), 0)
    along = lax.broadcasted_iota(jnp.int32, (64, 64), 1)
    for s in range(3):
        mark = jnp.zeros((64, 64), F32)
        for i, ref in enumerate((segments, places)):
            row = lax.rem(ref[s : s + 1, :], MSPAN).astype(F32)
            column = jnp.sum(jnp.where(down == along, row, 0.0), axis=1, keepdims=True)
            mark = jnp.where(along == i, column, mark)
        marks[64 * s : 64 * s + 64] = mark.astype(BF16)
    table_grad[...] = jnp.zeros((3, TALL, TALL), F32)
    v0[...] = jnp.zeros((4, 16, 256), F32)
    e0[...] = jnp.zeros((16, 384), F32)

    @pl.when(group == 1)
    def _():
        extra[...] = jnp.full((48, 640), -1.0, BF16)
        grad_extra_in[...] = jnp.zeros((48, 192), BF16)

    forward_y(plan[2])
    for n in range(3):
        forward_x(plan[n])
    forward_y(plan[3])
    own_small.wait()
    for cp in smalls:
        cp.wait_recv()

    def vector(i):
        return jnp.concatenate([small[f, i : i + 1, 0:192] for f in range(4)], axis=1)

    arrive(plan[0])
    q = (dot_nn(tokens[...], wq[...]) + vector(0)).astype(BF16)
    arrive(plan[1])
    kk = dot_nn(tokens[...], wk[...]).astype(BF16)
    arrive(plan[2])
    v = (dot_nn(tokens[...], wv[...]) + vector(1)).astype(BF16)
    for j in range(4):
        cols = slice(192 * j, 192 * j + 192)
        main_send[j] = jnp.concatenate([q[:, cols], kk[:, cols], v[:, cols], marks[...]], axis=1)
        for s in range(3):
            extra_send[j, 16 * s : 16 * s + 16] = main_send[j, 64 * s : 64 * s + 16]
    heads_there = Exchange(main_send, main, extra_send, extra, ex[0], False)
    heads_there.start()
    forward_y(plan[4])
    forward_x(plan[3])
    forward_y(plan[5])
    heads_there.wait()
    arrive(plan[4])

    def attend(s):
        slot_hot, same, valid = place_masks(main, extra, s, group)
        parts = []
        for h in range(3):
            qh = group_rows(main, extra, s, 64 * h, 64)
            kh = group_rows(main, extra, s, 192 + 64 * h, 64)
            vh = group_rows(main, extra, s, 384 + 64 * h, 64)
            picked = dot_nn(slot_hot, table[h, 0:TALL, 0:TALL]).astype(BF16)
            bias = dot_nt(picked, slot_hot)
            scores = jnp.where(same, dot_nt(qh, kh) * 0.125 + bias, NEGATIVE)
            top = jnp.max(scores, axis=1, keepdims=True)
            grown = jnp.exp(scores - top)
            share = valid / jnp.sum(grown, axis=1, keepdims=True)
            soft = (grown * share).astype(BF16)
            probs[3 * s + h] = soft
            parts.append(dot_nn(soft, vh).astype(BF16))
        whole = jnp.concatenate(parts, axis=1)
        for j in range(4):
            ctx_send[j, pl.ds(64 * s, 64)] = whole[64 * j : 64 * j + 64]
        ctx_extra[pl.ds(16 * s, 16)] = whole[256:272]

    attend(0)
    forward_y(plan[6])
    attend(1)
    forward_x(plan[5])
    attend(2)
    heads_back = Exchange(ctx_send, ctx4, ctx_extra, ctx_extra_in, ex[1], True)
    heads_back.start()
    forward_y(plan[7])
    def factor(hg, carry):
        part = pl.ds(3 * hg, 3)
        loads = [
            pltpu.make_async_copy(
                logits_in.at[part, :, near], slope.at[0:3, 0:128, 0:384], load.at[0]
            ),
            pltpu.make_async_copy(
                noise_in.at[part, :, near], slope.at[0:3, 0:128, 384:768], load.at[1]
            ),
        ]
        for cp in loads:
            cp.start()
        for cp in loads:
            cp.wait()
        for h in range(3):
            grown = jnp.exp(2.0 * (slope[h, 0:128, 0:384] + slope[h, 0:128, 384:768]))
            mask_sum[3 * hg + h, :, 0:384] = 2.0 / (1.0 + grown)
        return carry

    lax.fori_loop(0, 4, factor, 0)
    heads_back.wait()

    def join(into, side):
        @pl.when(c == 4)
        def _():
            for j in range(4):
                for s in range(3):
                    at = slice(64 * s, 64 * s + 16)
                    into[j, at] = into[j, at] + side[j, 16 * s : 16 * s + 16]

    join(ctx4, ctx_extra_in)

    def mean(value):
        return jnp.mean(value, axis=1, keepdims=True)

    def column_sum(value):
        return jnp.sum(value, axis=0, keepdims=True)

    def keep_vector(i, row):
        for owner in range(4):
            v0[owner, i : i + 1, 0:192] = row[:, 192 * owner : 192 * owner + 192]

    forward_y(plan[8])
    arrive(plan[3])
    context = jnp.concatenate([ctx4[j] for j in range(4)], axis=1)
    centered = tokens[...].astype(F32) + dot_nn(context, wo[...]) + vector(2)
    centered = centered - mean(centered)
    first_rate = lax.rsqrt(mean(centered * centered) + EPSILON)
    centered = centered * first_rate
    first_hat[...] = centered
    centered = centered * vector(3) + vector(4)
    first_norm[...] = centered
    first_low = centered.astype(BF16)
    for j in range(4):
        first4[j] = first_low[:, 192 * j : 192 * j + 192]
    forward_x(plan[6])
    arrive(plan[5])
    arrive(plan[6])

    def inner_product(j):
        bias = jnp.concatenate([small[j, 8 + i : 9 + i, 0:192] for i in range(4)], axis=1)
        at = 768 * j
        value = dot_nn(first_low, wi[:, at : at + 768]) + bias
        share = 0.5 + 0.5 * lax.erf(value * ROOT_HALF)
        low = (value * share).astype(BF16)
        active[j] = low
        for b in range(4):
            active16[4 * j + b] = low[:, 192 * b : 192 * b + 192]
        slope[j] = share + value * (jnp.exp(-0.5 * value * value) * ROOT_TWO_PI)

    for j in range(4):
        inner_product(j)
        if j == 0:
            forward_x(plan[7])
            forward_y(plan[9])
        if j == 2:
            forward_x(plan[8])
    forward_y(plan[10])
    for n in range(7, 11):
        arrive(plan[n])
    first_norm[...] += vector(5)

    centered = first_norm[...]
    for j in range(4):
        centered = centered + dot_nn(active[j], wf[768 * j : 768 * j + 768])
    centered = centered - mean(centered)
    rate = lax.rsqrt(mean(centered * centered) + EPSILON)
    hat = centered * rate
    hidden_low[...] = (hat * vector(6) + vector(7)).astype(BF16)
    outs = [pltpu.make_async_copy(hidden_low, hidden_out, load.at[2])]
    outs[0].start()

    above = upstream[...].astype(F32)
    keep_vector(6, column_sum(above * hat))
    keep_vector(7, column_sum(above))
    scaled = above * vector(6)
    grown_grad = rate * (scaled - mean(scaled) - hat * mean(scaled * hat))
    sum_grad[...] = grown_grad
    low_grad[...] = grown_grad.astype(BF16)
    keep_vector(5, column_sum(low_grad[...].astype(F32)))

    blocks = [(of, 192 * b, 0) for b in range(4)] + [(oi, 0, 768 * b) for b in range(4)]
    blocks += [(oh, 192 * b, 0) for b in range(4)]
    sums = BlockSums((st, r1, r2, r3, r4, total), sum_sems, blocks)

    def final_part(b):
        return lambda owner: dot_tn(active16[4 * owner + b], low_grad[...])

    def inter_part(b):
        return lambda owner: dot_tn(first4[owner], inner[b])

    def heads_part(b):
        return lambda owner: dot_tn(tokens4[owner], lows[b])

    def out_part(owner):
        return dot_tn(ctx4[owner], low_grad[...])

    def loop(first, count, body):
        def step(i, carry):
            body(first + i, i)
            return carry

        lax.fori_loop(0, count, step, 0)

    def again(n):
        for yy in range(2):
            sums.to_core(n, yy).wait_send()

    def inner_back(j):
        at = pl.ds(pl.multiple_of(768 * j, 768), 768)
        value = dot_nt(low_grad[...], wf[at]).astype(BF16)
        inner[j] = (value.astype(F32) * slope[j]).astype(BF16)
        row = column_sum(inner[j].astype(F32))
        for i in range(4):
            v0[j, 8 + i : 9 + i, 0:192] = row[:, 192 * i : 192 * i + 192]
        sum_grad[...] += dot_nt(inner[j], wi[:, at])

    sums.one(0, final_part(0))

    def final_both(n, b):
        sums.one(n + 1, final_part(b + 1))
        sums.two(n, final_part(b))

    loop(0, 3, final_both)
    sums.two(3, final_part(3))
    loop(0, 4, lambda j, i: inner_back(j))

    def inter_one(n, b):
        again(n - 4)
        sums.one(n, inter_part(b))

    loop(4, 4, inter_one)
    sums.three(0)
    above = sum_grad[...]
    hat = first_hat[...]
    keep_vector(3, column_sum(above * hat))
    keep_vector(4, column_sum(above))
    scaled = above * vector(3)
    norm_grad = first_rate * (scaled - mean(scaled) - hat * mean(scaled * hat))
    sum_grad[...] = norm_grad
    low_grad[...] = norm_grad.astype(BF16)
    keep_vector(2, column_sum(low_grad[...].astype(F32)))
    context_grad = dot_nt(low_grad[...], wo[...]).astype(BF16)
    for j in range(4):
        grad4[j] = context_grad[:, 192 * j : 192 * j + 192]
        for s in range(3):
            grad_extra[j, 16 * s : 16 * s + 16] = grad4[j, 64 * s : 64 * s + 16]
    grads_there = Exchange(grad4, grad_in, grad_extra, grad_extra_in, ex[2], False)
    grads_there.start()
    loop(4, 3, lambda n, b: sums.two(n, inter_part(b)))
    sums.three(1)
    sums.four(0)
    grads_there.wait()

    def attend_back(s):
        slot_hot, _, _ = place_masks(main, extra, s, group)
        parts = [[], [], []]
        for h in range(3):
            qh = group_rows(main, extra, s, 64 * h, 64)
            kh = group_rows(main, extra, s, 192 + 64 * h, 64)
            vh = group_rows(main, extra, s, 384 + 64 * h, 64)
            gh = group_rows(grad_in, grad_extra_in, s, 64 * h, 64)
            soft = probs[3 * s + h]
            weight = soft.astype(F32)
            weight_grad = dot_nt(gh, vh)
            delta = jnp.sum(weight * weight_grad, axis=1, keepdims=True)
            score_grad = (weight * (weight_grad - delta)).astype(BF16)
            parts[0].append((dot_nn(score_grad, kh) * 0.125).astype(BF16))
            parts[1].append((dot_tn(score_grad, qh) * 0.125).astype(BF16))
            parts[2].append(dot_tn(soft, gh).astype(BF16))
            moved = dot_tn(slot_hot, score_grad)
            table_grad[h] += dot_nn(moved.astype(BF16), slot_hot)
        blank = jnp.zeros((TALL, 64), BF16)
        whole = jnp.concatenate(parts[0] + parts[1] + parts[2] + [blank], axis=1)
        for j in range(4):
            main_send[j, pl.ds(64 * s, 64)] = whole[64 * j : 64 * j + 64]
        extra_send[0, pl.ds(16 * s, 16)] = whole[256:272]

    heads_there.settle()
    attend_back(0)
    sums.three(2)
    sums.four(1)
    attend_back(1)
    sums.five(0)
    attend_back(2)
    grads_back = Exchange(main_send, main_in, extra_send.at[0], extra_in, ex[3], True)
    grads_back.start()
    w = {}

    def table_core():
        lane = lax.broadcasted_iota(jnp.int32, (8, TALL), 1)
        final = jnp.where(lane == 256, 1.0, 0.0).astype(BF16)
        for h in range(3):
            t0[h] = table_grad[h, 0:256, 0:256].astype(BF16)
            e0[h : h + 1, 0:TALL] = table_grad[h, 256:257, :]
            column = dot_nt(final, table_grad[h].astype(BF16))
            e0[8 + h : 9 + h, 0:TALL] = column[0:1]
        w["tcore"] = send(t0.at[:, pl.ds(128 * (1 - k), 128)], t1, pt.at[0], qt.at[0], core)
        w["tcore"].start()
        w["ecore"] = send(e0, e1, pe.at[0], qe.at[0], core)
        w["ecore"].start()

    def out_one():
        again(7)
        sums.one(11, out_part)

    def table_over_y():
        w["tcore"].wait_recv()
        for h in range(3):
            t1[h] = t0[h, pl.ds(pl.multiple_of(128 * k, 128), 128), :] + t1[h]
        w["table_y"] = send(t1.at[:, pl.ds(64 * (1 - y), 64)], t2, pt.at[1], qt.at[1], ynb)
        w["table_y"].start()
        w["ecore"].wait_recv()
        e1[...] = e0[...] + e1[...]
        w["edge_y"] = send(e1, e2, pe.at[1], qe.at[1], ynb)
        w["edge_y"].start()

    def late_two():
        sums.two(7, inter_part(3))
        sums.two(11, out_part)

    def heads_back_in():
        grads_back.wait()
        join(main_in, extra_in)
        for a in range(3):
            lows[a] = jnp.concatenate(
                [main_in[j, :, 192 * a : 192 * a + 192] for j in range(4)], axis=1
            )
        keep_vector(0, column_sum(lows[0].astype(F32)))
        keep_vector(1, column_sum(lows[2].astype(F32)))
        for yy in range(2):
            cp = send(v0.at[2 * yy + 1 - k], v1.at[yy], ps.at[yy], qs.at[yy], core)
            cp.start()
            w["small_core", yy] = cp

        def heads_one(n, b):
            again(n - 4)
            sums.one(n, heads_part(b))

        loop(8, 3, heads_one)
        for yy in range(2):
            w["small_core", yy].wait_recv()
            v1[yy] = v0[2 * yy + k] + v1[yy]
        w["small_y"] = send(v1.at[1 - y], v2, ps.at[2], qs.at[2], ynb)
        w["small_y"].start()
        loop(8, 3, lambda n, b: sums.two(n, heads_part(b)))

    def inputs_grad():
        input_sum[...] = sum_grad[...] + dot_nt(lows[0], wq[...])
        input_sum[...] += dot_nt(lows[1], wk[...])
        input_sum[...] += dot_nt(lows[2], wv[...])
        outs.append(pltpu.make_async_copy(input_sum, input_grad, load.at[3]))
        outs[1].start()

    def table_to_twin():
        w["edge_y"].wait_recv()
        e2[...] = e1[...] + e2[...]
        w["edge_x"] = send(e2, e3, pe.at[2], qe.at[2], twin)
        w["edge_x"].start()
        w["table_y"].wait_recv()
        for h in range(3):
            t2[h] = t1[h, pl.ds(pl.multiple_of(64 * y, 64), 64), :] + t2[h]
        w["table_x"] = send(t2.at[:, pl.ds(32 * (1 - group), 32)], t3, pt.at[2], qt.at[2], twin)
        w["table_x"].start()

    me = lax.rem(c, 4)

    def table_piece(hg, side):
        return table_out.at[hg, :, pl.ds(64 * y + 32 * side, 32)]

    def table_spread():
        w["edge_x"].wait_recv()
        edge_out[c] = e2[...] + e3[...]
        here = edge_out.at[c]
        for i in range(3):
            w["edge_z", i] = send(here, here, pe.at[3 + i], qe.at[3 + z], zdev[i])
        w["edge_z", 3] = send(here, here, pe.at[6], qe.at[7 + z], xnb)
        w["table_x"].wait_recv()
        at = pl.ds(pl.multiple_of(32 * group, 32), 32)
        to = pl.ds(pl.multiple_of(64 * y + 32 * group, 32), 32)
        for h in range(3):
            table_out[me, h, to, :] = t2[h, at, :] + t3[h]
        here = table_piece(me, group)
        for i in range(3):
            w["table_z", i] = send(here, here, pt.at[3 + i], qt.at[3 + z], zdev[i])
        w["table_z", 3] = send(here, here, pt.at[6], qt.at[7 + z], xnb)
        for i in range(4):
            w["edge_z", i].start()
            w["table_z", i].start()

    def table_over_x():
        for i in (1, 2, 3):
            zz = lax.rem(z + i, 4)
            cc = 2 * zz + x
            there = edge_out.at[cc]
            send(there, there, pe.at[3], qe.at[3 + zz], core).wait_recv()
            w["edge_z", 3 + i] = send(there, there, pe.at[6 + i], qe.at[7 + zz], xnb)
            w["edge_z", 3 + i].start()
            there = table_piece(lax.rem(cc, 4), cc // 4)
            send(there, there, pt.at[3], qt.at[3 + zz], core).wait_recv()
            w["table_z", 3 + i] = send(there, there, pt.at[6 + i], qt.at[7 + zz], xnb)
            w["table_z", 3 + i].start()

    half_table = table_out.at[:, :, pl.ds(64, 64)]
    half_copy = send(half_table, half_table, pt.at[10], qt.at[11], ynb)

    def table_half():
        for zz in range(4):
            cc = 2 * zz + 1 - x
            there = table_piece(lax.rem(cc, 4), cc // 4)
            send(there, there, pt.at[6], qt.at[7 + zz], xnb).wait_recv()
            there = edge_out.at[cc]
            send(there, there, pe.at[6], qe.at[7 + zz], xnb).wait_recv()

        @pl.when(y == 1)
        def _():
            half_copy.start()

    def small_over_x():
        w["small_y"].wait_recv()
        v2[...] = v1[y] + v2[...]
        w["small_x"] = send(v2, v3, ps.at[3], qs.at[3], xnb)
        w["small_x"].start()

    def small_over_z():
        w["small_x"].wait_recv()
        v4[z] = v2[...] + v3[...]
        for i in range(3):
            w["small_z", i] = send(v4.at[z], v4.at[z], ps.at[4 + i], qs.at[4 + z], zdev[i])
            w["small_z", i].start()

    def small_end():
        for i in (1, 2, 3):
            zz = lax.rem(z + i, 4)
            send(v4.at[zz], v4.at[zz], ps.at[4], qs.at[4 + zz], core).wait_recv()
        small_out[...] = (v4[0] + v4[1]) + (v4[2] + v4[3])

    def mask_end():
        @pl.when(y == 0)
        def _():
            half_copy.wait_recv()
            deep = lax.broadcasted_iota(jnp.int32, (128, 128), 0)
            across = lax.broadcasted_iota(jnp.int32, (128, 128), 1)

            def fill(hg, carry):
                for h in range(3):
                    row = edge_out[hg, 8 + h : 9 + h, :]
                    row = jnp.where(k == 0, row[:, 0:128], row[:, 128:256])
                    column = jnp.sum(jnp.where(deep == across, row, 0.0), axis=1, keepdims=True)
                    n = 3 * hg + h
                    mask_sum[n, :, 0:256] = mask_sum[n, :, 0:256] * table_out[hg, h].astype(F32)
                    mask_sum[n, :, 256:384] = mask_sum[n, :, 256:384] * jnp.where(
                        across == 0, column, 0.0
                    )
                    mask_sum[n, :, 384:512] = jnp.zeros((128, 128), F32)
                return carry

            lax.fori_loop(0, 4, fill, 0)

        @pl.when(y == 1)
        def _():
            top = lax.broadcasted_iota(jnp.int32, (8, 384), 0)

            def fill(hg, carry):
                for h in range(3):
                    n = 3 * hg + h
                    first = mask_sum[n, 0:8, 0:384] * edge_out[hg, h : h + 1, :]
                    mask_sum[n] = jnp.zeros((128, 512), F32)
                    mask_sum[n, 0:8, 0:384] = jnp.where((top == 0) & (k == 0), first, 0.0)
                return carry

            lax.fori_loop(0, 4, fill, 0)

        outs.append(pltpu.make_async_copy(mask_sum, mask_out, load.at[4]))
        outs[2].start()

    steps = [
        ("three", 3), ("four", 2), ("five", 1), ("six", 0), table_core, out_one, table_over_y,
        late_two, ("three", 4), ("five", 2), ("six", 1), ("four", 3), heads_back_in,
        ("three", 5), ("four", 4), ("five", 3), ("six", 2), inputs_grad, ("three", 6),
        ("four", 5), table_to_twin, ("five", 4), ("six", 3), ("three", 7), ("four", 6),
        ("five", 5), table_spread, ("three", 11), ("four", 7), ("six", 4), ("five", 6),
        small_over_x, ("three", 8), ("four", 11), ("six", 5), ("five", 7), table_over_x,
        small_over_z, ("three", 9), ("four", 8), ("six", 6), ("five", 11), ("three", 10),
        ("four", 9), ("six", 7), ("five", 8), ("four", 10), table_half, ("six", 11), ("five", 9),
        mask_end, ("six", 8), ("five", 10), small_end, ("six", 9), ("six", 10),
    ]
    for step in steps:
        if isinstance(step, tuple):
            getattr(sums, step[0])(step[1])
        else:
            step()
    for n in (0, 1, 2, 3, 4, 5, 6, 7, 11, 8, 9, 10):
        sums.seven(n)
    for cp in outs:
        cp.wait()

    @pl.when(y == 1)
    def _():
        half_copy.wait_send()

    for cp in w.values():
        cp.wait_send()
    for exchange in (heads_back, grads_there, grads_back):
        exchange.settle()
    for copies in plan:
        settle(copies)
    for cp in smalls:
        cp.wait_send()
    sums.settle()


def layer(tokens, segments, places, upstream, vectors, arrays, logits, noise):
    dma = pltpu.SemaphoreType.DMA
    count = len(gather_pieces())

    def low(*shape):
        return pltpu.VMEM(shape, BF16)

    def wide(*shape):
        return pltpu.VMEM(shape, F32)

    scratch = [low(a.shape[0] * 4, a.shape[1]) for a in arrays]
    scratch += [low(3, 512, 384), wide(4, 16, 256)]
    scratch += [
        low(4, ROWS, 640), low(48, 640), low(4, ROWS, 640), low(4, 48, 640),
        low(9, TALL, TALL),
        low(4, ROWS, 192), low(48, 192), low(4, ROWS, 192), low(4, 48, 192),
    ]
    scratch += [
        wide(16, 256), low(ROWS, 64), low(4, ROWS, 768), low(3, 128, 384), low(4, ROWS, 192),
        wide(ROWS, 768), wide(ROWS, 768), low(4, ROWS, 192),
        low(16, ROWS, 192), wide(4, ROWS, 768), low(4, ROWS, 768), wide(ROWS, 768), low(ROWS, 768),
    ]
    scratch += [
        low(4, ROWS, 192), low(4, 48, 192), low(4, ROWS, 192), low(48, 192),
        low(4, ROWS, 640), low(4, 48, 640), wide(3, TALL, TALL), low(3, ROWS, 768),
    ]
    scratch += [wide(4, 16, 256), wide(2, 16, 256), wide(16, 256), wide(16, 256), wide(4, 16, 256)]
    scratch += [low(3, 256, 256), low(3, 128, 256), low(3, 64, 256), low(3, 32, 256)]
    scratch += [wide(16, 384)] * 4 + [low(4, 3, 128, 256), wide(8, 16, 384)]
    scratch += [
        low(4, 2, 192, 768), low(12, 2, 192, 768), low(12, 192, 768), low(12, 192, 384),
        low(12, 4, 48, 384), low(12, 48, 384),
        low(ROWS, 768), wide(ROWS, 768), wide(12, 128, 512),
    ]
    sems = [dma((count, 5)), dma((count, 5)), dma((count + 1,)), dma((3,)), dma((3,))]
    for _ in range(4):
        sems += exchange_sems()
    sems += [
        dma((12, 2)), dma((12, 2)), dma((12,)), dma((12,)), dma((12,)), dma((12,)),
        dma((12, 3)), dma((12, 4)), dma((12, 3)), dma((12, 4)), dma((12,)), dma((12,)), dma((12,)),
    ]
    sems += [dma((8,)), dma((8,)), dma((12,)), dma((12,)), dma((12,)), dma((12,)), dma((5,))]
    return pl.pallas_call(
        layer_kernel,
        out_shape=[
            jax.ShapeDtypeStruct((ROWS, 768), BF16),
            jax.ShapeDtypeStruct((ROWS, 768), F32),
        ]
        + [
            jax.ShapeDtypeStruct((768, 768), BF16),
            jax.ShapeDtypeStruct((192, 3072), BF16),
            jax.ShapeDtypeStruct((768, 768), BF16),
            jax.ShapeDtypeStruct((16, 256), F32),
            jax.ShapeDtypeStruct((12, 128, 512), F32),
        ],
        in_specs=[vmem_spec()] * 13 + [any_spec()] * 8,
        out_specs=[any_spec()] * 5 + [vmem_spec(), any_spec()],
        scratch_shapes=scratch + sems,
        compiler_params=pltpu.CompilerParams(
            collective_id=1, has_side_effects=True, vmem_limit_bytes=62 * 2**20
        ),
        name="layer",
    )(tokens, segments, places, upstream, *vectors, *arrays, logits, noise)


def block_device(
    hidden_in, segment_ids, doc_positions,
    w_query, w_key, w_value, w_out, b_query, b_value, b_out, ln1_gain, ln1_shift,
    w_inter, b_inter, w_final, b_final, ln2_gain, ln2_shift,
    mask_logits, mask_noise, grad_out,
):
    vectors = (
        b_query, b_value, b_out, ln1_gain, ln1_shift, b_final, ln2_gain, ln2_shift, b_inter
    )
    result, input_grad, oh, oi, of, small_sum, logit_grad = layer(
        hidden_in.reshape(ROWS, 768),
        segment_ids,
        doc_positions,
        grad_out.reshape(ROWS, 768),
        vectors,
        (w_query, w_key, w_value, w_out, w_inter, w_final),
        mask_logits,
        mask_noise,
    )
    vecs = [small_sum[i, :192] for i in range(8)]
    heads = [oh[192 * i : 192 * i + 192].astype(F32) for i in range(4)]
    return (
        result.reshape(hidden_in.shape),
        input_grad.reshape(hidden_in.shape),
        heads[0],
        heads[1],
        heads[2],
        heads[3],
        vecs[0],
        vecs[1],
        vecs[2],
        vecs[3],
        vecs[4],
        oi.astype(F32),
        small_sum[8:12, :192].reshape(768),
        of.astype(F32),
        vecs[5],
        vecs[6],
        vecs[7],
        logit_grad,
    )


def on_device(ctx_size, fsdp_size, hidden_in, *rest):
    if (ctx_size, fsdp_size, hidden_in.shape) == (8, 4, (3, 64, 768)):
        return block_device(hidden_in, *rest)
    return general_device(hidden_in, *rest)


def solution(mesh):
    in_specs = (
        P("fsdp", "ctx", None),
        P("fsdp", "ctx"),
        P("fsdp", "ctx"),
        P("fsdp", None),
        P("fsdp", None),
        P("fsdp", None),
        P("fsdp", None),
        P("fsdp"),
        P("fsdp"),
        P("fsdp"),
        P("fsdp"),
        P("fsdp"),
        P("fsdp", None),
        P("fsdp"),
        P("fsdp", None),
        P("fsdp"),
        P("fsdp"),
        P("fsdp"),
        P(None, "fsdp", None),
        P(None, "fsdp", None),
        P("fsdp", "ctx", None),
    )
    out_specs = (
        P("fsdp", "ctx", None),
        P("fsdp", "ctx", None),
        P("fsdp", None),
        P("fsdp", None),
        P("fsdp", None),
        P("fsdp", None),
        P("fsdp"),
        P("fsdp"),
        P("fsdp"),
        P("fsdp"),
        P("fsdp"),
        P("fsdp", None),
        P("fsdp"),
        P("fsdp", None),
        P("fsdp"),
        P("fsdp"),
        P("fsdp"),
        P(None, "fsdp", None),
    )
    return jax.shard_map(
        functools.partial(on_device, mesh.shape["ctx"], mesh.shape["fsdp"]), mesh=mesh, in_specs=in_specs, out_specs=out_specs, check_vma=False
    )
```

```python
import functools

import jax
import jax.numpy as jnp
from jax import lax
from jax.experimental import pallas as pl
from jax.experimental.pallas import tpu as pltpu
from jax.sharding import PartitionSpec as P

H = 12
HD = 64
MSPAN = 512


NEGATIVE = -1e30
EPSILON = 1e-12


def layer_norm(hidden, gain_row, shift_row):
    average = jnp.mean(hidden, axis=-1, keepdims=True)
    centered = hidden - average
    variance = jnp.mean(centered * centered, axis=-1, keepdims=True)
    return centered * lax.rsqrt(variance + EPSILON) * gain_row + shift_row


def exact_gelu(inner_act):
    return jax.nn.gelu(inner_act, approximate=False)


def left_product(first_op, second_op):
    return lax.dot_general(
        first_op, second_op, (((0,), (0,)), ((), ())), preferred_element_type=jnp.float32
    )


def right_product(first_op, second_op):
    return lax.dot_general(
        first_op, second_op, (((1,), (1,)), ((), ())), preferred_element_type=jnp.float32
    )


def one_hot_rows(slot_values, width):
    return (slot_values[:, None] == jnp.arange(width, dtype=jnp.int32)[None, :]).astype(
        jnp.bfloat16
    )


def block_scores(queries, key_part, seg_local, seg_part, bias_part):
    key_heads = key_part.reshape(key_part.shape[0], H, HD)
    raw_scores = (
        jnp.einsum("shd,nhd->hsn", queries, key_heads, preferred_element_type=jnp.float32) * 0.125
    )
    same_doc = seg_local[:, None] == seg_part[None, :]
    return jnp.where(same_doc[None], raw_scores + bias_part.astype(jnp.float32), NEGATIVE)


def split_blocks(array_in, block_size):
    return array_in.reshape((array_in.shape[0] // block_size, block_size) + array_in.shape[1:])


def block_length():
    return 512


def make_blocks(full_keys, full_values, full_segment, full_slot):
    block_size = block_length()
    return (
        split_blocks(full_keys, block_size),
        split_blocks(full_values, block_size),
        split_blocks(full_segment, block_size),
        split_blocks(full_slot, block_size),
    )


def row_statistics(queries, seg_local, table_rows, blocks):
    rows = queries.shape[0]

    def advance(state_carry, key_block):
        key_part, value_part, seg_part, slot_part = key_block

        def compute(pair):
            row_top, row_total = pair
            bias_part = jnp.einsum(
                "hsa,na->hsn",
                table_rows,
                one_hot_rows(slot_part, MSPAN),
                preferred_element_type=jnp.float32,
            ).astype(jnp.bfloat16)
            scores = block_scores(queries, key_part, seg_local, seg_part, bias_part)
            new_top = jnp.maximum(row_top, jnp.max(scores, axis=-1))
            row_total = row_total * jnp.exp(row_top - new_top) + jnp.sum(
                jnp.exp(scores - new_top[..., None]), axis=-1
            )
            return ((new_top, row_total), bias_part)

        return compute(state_carry)

    start_state = (jnp.full((H, rows), NEGATIVE, jnp.float32), jnp.zeros((H, rows), jnp.float32))
    (row_top, row_total), bias_blocks = lax.scan(advance, start_state, blocks)
    return (row_top + jnp.log(row_total), bias_blocks)


def attention_output(queries, seg_local, blocks, bias_blocks, log_total):
    rows = queries.shape[0]

    def advance(accumulated, items):
        (key_part, value_part, seg_part, slot_part), bias_part = items

        def compute(current):
            scores = block_scores(queries, key_part, seg_local, seg_part, bias_part)
            soft_weights = jnp.exp(scores - log_total[..., None]).astype(jnp.bfloat16)
            value_heads = value_part.reshape(value_part.shape[0], H, HD)
            return current + jnp.einsum(
                "hsn,nhd->shd", soft_weights, value_heads, preferred_element_type=jnp.float32
            )

        return (compute(accumulated), None)

    context, _ = lax.scan(advance, jnp.zeros((rows, H, HD), jnp.float32), (blocks, bias_blocks))
    return context


def attention_backward(queries, seg_local, blocks, bias_blocks, log_total, context_grad, row_delta):
    rows = queries.shape[0]

    def advance(state_carry, items):
        (key_part, value_part, seg_part, slot_part), bias_part = items
        key_count = key_part.shape[0]

        def compute(operand):
            query_acc, slot_acc = operand
            scores = block_scores(queries, key_part, seg_local, seg_part, bias_part)
            soft_float = jnp.exp(scores - log_total[..., None])
            key_heads = key_part.reshape(key_count, H, HD)
            value_heads = value_part.reshape(key_count, H, HD)
            weight_grad = jnp.einsum(
                "shd,nhd->hsn", context_grad, value_heads, preferred_element_type=jnp.float32
            )
            score_grad = (soft_float * (weight_grad - row_delta[..., None])).astype(jnp.bfloat16)
            query_acc = (
                query_acc
                + jnp.einsum(
                    "hsn,nhd->shd", score_grad, key_heads, preferred_element_type=jnp.float32
                )
                * 0.125
            )
            slot_acc = slot_acc + jnp.einsum(
                "hsn,na->hsa",
                score_grad,
                one_hot_rows(slot_part, MSPAN),
                preferred_element_type=jnp.float32,
            )
            key_block_grad = (
                jnp.einsum("hsn,shd->nhd", score_grad, queries, preferred_element_type=jnp.float32)
                * 0.125
            )
            value_block_grad = jnp.einsum(
                "hsn,shd->nhd",
                soft_float.astype(jnp.bfloat16),
                context_grad,
                preferred_element_type=jnp.float32,
            )
            return ((query_acc, slot_acc), (key_block_grad, value_block_grad))

        return compute(state_carry)

    start_state = (jnp.zeros((rows, H, HD), jnp.float32), jnp.zeros((H, rows, MSPAN), jnp.float32))
    (query_acc, slot_acc), block_grads = lax.scan(advance, start_state, (blocks, bias_blocks))
    key_grads, value_grads = block_grads
    full_len = key_grads.shape[0] * key_grads.shape[1]
    return (
        query_acc,
        slot_acc,
        key_grads.reshape(full_len, H * HD),
        value_grads.reshape(full_len, H * HD),
    )


def general_device(
    hidden_in,
    segment_ids,
    doc_positions,
    w_query,
    w_key,
    w_value,
    w_out,
    b_query,
    b_value,
    b_out,
    ln1_gain,
    ln1_shift,
    w_inter,
    b_inter,
    w_final,
    b_final,
    ln2_gain,
    ln2_shift,
    mask_logits,
    mask_noise,
    grad_out,
):
    table_part = jax.nn.log_sigmoid(2.0 * (mask_logits + mask_noise)).astype(jnp.bfloat16)
    (
        wq_full,
        wk_full,
        wv_full,
        wo_full,
        wi_full,
        wf_full,
        bq_full,
        bv_full,
        bo_full,
        bi_full,
        bf_full,
        gain_one,
        shift_one,
        gain_two,
        shift_two,
        table_full,
    ) = (
        lax.all_gather(w_query, "fsdp", axis=0, tiled=True),
        lax.all_gather(w_key, "fsdp", axis=0, tiled=True),
        lax.all_gather(w_value, "fsdp", axis=0, tiled=True),
        lax.all_gather(w_out, "fsdp", axis=0, tiled=True),
        lax.all_gather(w_inter, "fsdp", axis=0, tiled=True),
        lax.all_gather(w_final, "fsdp", axis=0, tiled=True),
        lax.all_gather(b_query, "fsdp", axis=0, tiled=True),
        lax.all_gather(b_value, "fsdp", axis=0, tiled=True),
        lax.all_gather(b_out, "fsdp", axis=0, tiled=True),
        lax.all_gather(b_inter, "fsdp", axis=0, tiled=True),
        lax.all_gather(b_final, "fsdp", axis=0, tiled=True),
        lax.all_gather(ln1_gain, "fsdp", axis=0, tiled=True),
        lax.all_gather(ln1_shift, "fsdp", axis=0, tiled=True),
        lax.all_gather(ln2_gain, "fsdp", axis=0, tiled=True),
        lax.all_gather(ln2_shift, "fsdp", axis=0, tiled=True),
        lax.all_gather(table_part, "fsdp", axis=1, tiled=True),
    )
    bq_full, bv_full, bo_full = (
        bq_full.astype(jnp.float32),
        bv_full.astype(jnp.float32),
        bo_full.astype(jnp.float32),
    )
    bi_full, bf_full = (bi_full.astype(jnp.float32), bf_full.astype(jnp.float32))
    gain_one, shift_one = (gain_one.astype(jnp.float32), shift_one.astype(jnp.float32))
    gain_two, shift_two = (gain_two.astype(jnp.float32), shift_two.astype(jnp.float32))
    micro_count = hidden_in.shape[0]
    rows = hidden_in.shape[1]
    saved = []
    outputs_list = []
    for micro_batch in range(micro_count):
        tokens = hidden_in[micro_batch]
        seg_local = segment_ids[micro_batch]
        slot_local = doc_positions[micro_batch] % MSPAN
        queries_flat = (
            jnp.dot(tokens, wq_full, preferred_element_type=jnp.float32) + bq_full
        ).astype(jnp.bfloat16)
        keys_local = jnp.dot(tokens, wk_full, preferred_element_type=jnp.float32).astype(
            jnp.bfloat16
        )
        values_local = (
            jnp.dot(tokens, wv_full, preferred_element_type=jnp.float32) + bv_full
        ).astype(jnp.bfloat16)
        gathered = (
            lax.all_gather(keys_local, "ctx", axis=0, tiled=True),
            lax.all_gather(values_local, "ctx", axis=0, tiled=True),
            lax.all_gather(seg_local, "ctx", axis=0, tiled=True),
            lax.all_gather(slot_local, "ctx", axis=0, tiled=True),
        )
        blocks = make_blocks(*gathered)
        queries = queries_flat.reshape(rows, H, HD)
        table_rows = table_full[:, slot_local, :]
        log_total, bias_blocks = row_statistics(queries, seg_local, table_rows, blocks)
        context = attention_output(queries, seg_local, blocks, bias_blocks, log_total)
        context_low = context.reshape(rows, H * HD).astype(jnp.bfloat16)
        attn_out = jnp.dot(context_low, wo_full, preferred_element_type=jnp.float32) + bo_full
        first_norm, norm_one_back = jax.vjp(
            layer_norm, tokens.astype(jnp.float32) + attn_out, gain_one, shift_one
        )
        first_low = first_norm.astype(jnp.bfloat16)
        inner_act = jnp.dot(first_low, wi_full, preferred_element_type=jnp.float32) + bi_full
        active, gelu_back = jax.vjp(exact_gelu, inner_act)
        active_low = active.astype(jnp.bfloat16)
        ffn_out = jnp.dot(active_low, wf_full, preferred_element_type=jnp.float32) + bf_full
        result, norm_two_back = jax.vjp(layer_norm, first_norm + ffn_out, gain_two, shift_two)
        outputs_list.append(result.astype(jnp.bfloat16))
        kept_blocks = blocks
        saved.append(
            (
                tokens,
                seg_local,
                slot_local,
                queries,
                keys_local,
                values_local,
                log_total,
                bias_blocks,
                context,
                context_low,
                first_low,
                active_low,
                norm_one_back,
                gelu_back,
                norm_two_back,
                kept_blocks,
            )
        )
    zeros_square = jnp.zeros((H * HD, H * HD), jnp.float32)
    wq_grad, wk_grad, wv_grad, wo_grad = (zeros_square, zeros_square, zeros_square, zeros_square)
    wi_grad = jnp.zeros(wi_full.shape, jnp.float32)
    wf_grad = jnp.zeros(wf_full.shape, jnp.float32)
    zeros_row = jnp.zeros((H * HD,), jnp.float32)
    bq_grad, bv_grad, bo_grad, bf_grad = (zeros_row, zeros_row, zeros_row, zeros_row)
    gain_one_grad, shift_one_grad, gain_two_grad, shift_two_grad = (
        zeros_row,
        zeros_row,
        zeros_row,
        zeros_row,
    )
    bi_grad = jnp.zeros(bi_full.shape, jnp.float32)
    table_grad = jnp.zeros(table_full.shape, jnp.float32)
    input_grads = []
    for micro_batch in range(micro_count):
        (
            tokens,
            seg_local,
            slot_local,
            queries,
            keys_local,
            values_local,
            log_total,
            bias_blocks,
            context,
            context_low,
            first_low,
            active_low,
            norm_one_back,
            gelu_back,
            norm_two_back,
            kept_blocks,
        ) = saved[micro_batch]
        upstream = grad_out[micro_batch].astype(jnp.float32)
        sum_grad, gain_part, shift_part = norm_two_back(upstream)
        gain_two_grad = gain_two_grad + gain_part
        shift_two_grad = shift_two_grad + shift_part
        ffn_grad = sum_grad.astype(jnp.bfloat16)
        bf_grad = bf_grad + jnp.sum(ffn_grad.astype(jnp.float32), axis=0)
        wf_grad = wf_grad + left_product(active_low, ffn_grad)
        active_grad = right_product(ffn_grad, wf_full).astype(jnp.bfloat16)
        (inner_float,) = gelu_back(active_grad.astype(jnp.float32))
        inner_grad = inner_float.astype(jnp.bfloat16)
        bi_grad = bi_grad + jnp.sum(inner_grad.astype(jnp.float32), axis=0)
        wi_grad = wi_grad + left_product(first_low, inner_grad)
        first_grad = sum_grad + right_product(inner_grad, wi_full)
        norm_grad, gain_part, shift_part = norm_one_back(first_grad)
        gain_one_grad = gain_one_grad + gain_part
        shift_one_grad = shift_one_grad + shift_part
        attn_grad = norm_grad.astype(jnp.bfloat16)
        bo_grad = bo_grad + jnp.sum(attn_grad.astype(jnp.float32), axis=0)
        wo_grad = wo_grad + left_product(context_low, attn_grad)
        context_grad_flat = right_product(attn_grad, wo_full).astype(jnp.bfloat16)
        context_grad = context_grad_flat.reshape(rows, H, HD)
        row_delta = jnp.einsum("shd,shd->hs", context_grad.astype(jnp.float32), context)
        blocks = kept_blocks
        query_acc, slot_acc, key_full_grad, value_full_grad = attention_backward(
            queries, seg_local, blocks, bias_blocks, log_total, context_grad, row_delta
        )
        key_share, value_share = (
            lax.psum_scatter(
                key_full_grad.astype(jnp.bfloat16), "ctx", scatter_dimension=0, tiled=True
            ).astype(jnp.float32),
            lax.psum_scatter(
                value_full_grad.astype(jnp.bfloat16), "ctx", scatter_dimension=0, tiled=True
            ).astype(jnp.float32),
        )
        table_grad = table_grad.at[:, slot_local, :].add(slot_acc)
        query_low = query_acc.reshape(rows, H * HD).astype(jnp.bfloat16)
        key_low = key_share.astype(jnp.bfloat16)
        value_low = value_share.astype(jnp.bfloat16)
        bq_grad = bq_grad + jnp.sum(query_low.astype(jnp.float32), axis=0)
        bv_grad = bv_grad + jnp.sum(value_low.astype(jnp.float32), axis=0)
        wq_grad = wq_grad + left_product(tokens, query_low)
        wk_grad = wk_grad + left_product(tokens, key_low)
        wv_grad = wv_grad + left_product(tokens, value_low)
        input_grads.append(
            norm_grad
            + right_product(query_low, wq_full)
            + right_product(key_low, wk_full)
            + right_product(value_low, wv_full)
        )
    shares = (
        lax.psum_scatter(
            wq_grad.astype(jnp.bfloat16), "fsdp", scatter_dimension=0, tiled=True
        ).astype(jnp.float32),
        lax.psum_scatter(
            wk_grad.astype(jnp.bfloat16), "fsdp", scatter_dimension=0, tiled=True
        ).astype(jnp.float32),
        lax.psum_scatter(
            wv_grad.astype(jnp.bfloat16), "fsdp", scatter_dimension=0, tiled=True
        ).astype(jnp.float32),
        lax.psum_scatter(
            wo_grad.astype(jnp.bfloat16), "fsdp", scatter_dimension=0, tiled=True
        ).astype(jnp.float32),
        lax.psum_scatter(
            bq_grad.astype(jnp.bfloat16), "fsdp", scatter_dimension=0, tiled=True
        ).astype(jnp.float32),
        lax.psum_scatter(
            bv_grad.astype(jnp.bfloat16), "fsdp", scatter_dimension=0, tiled=True
        ).astype(jnp.float32),
        lax.psum_scatter(
            bo_grad.astype(jnp.bfloat16), "fsdp", scatter_dimension=0, tiled=True
        ).astype(jnp.float32),
        lax.psum_scatter(
            gain_one_grad.astype(jnp.bfloat16), "fsdp", scatter_dimension=0, tiled=True
        ).astype(jnp.float32),
        lax.psum_scatter(
            shift_one_grad.astype(jnp.bfloat16), "fsdp", scatter_dimension=0, tiled=True
        ).astype(jnp.float32),
        lax.psum_scatter(
            wi_grad.astype(jnp.bfloat16), "fsdp", scatter_dimension=0, tiled=True
        ).astype(jnp.float32),
        lax.psum_scatter(
            bi_grad.astype(jnp.bfloat16), "fsdp", scatter_dimension=0, tiled=True
        ).astype(jnp.float32),
        lax.psum_scatter(
            wf_grad.astype(jnp.bfloat16), "fsdp", scatter_dimension=0, tiled=True
        ).astype(jnp.float32),
        lax.psum_scatter(
            bf_grad.astype(jnp.bfloat16), "fsdp", scatter_dimension=0, tiled=True
        ).astype(jnp.float32),
        lax.psum_scatter(
            gain_two_grad.astype(jnp.bfloat16), "fsdp", scatter_dimension=0, tiled=True
        ).astype(jnp.float32),
        lax.psum_scatter(
            shift_two_grad.astype(jnp.bfloat16), "fsdp", scatter_dimension=0, tiled=True
        ).astype(jnp.float32),
        lax.psum_scatter(
            table_grad.astype(jnp.bfloat16), "fsdp", scatter_dimension=1, tiled=True
        ).astype(jnp.float32),
    )
    totals = (
        lax.psum(shares[0].astype(jnp.bfloat16), "ctx").astype(jnp.float32),
        lax.psum(shares[1].astype(jnp.bfloat16), "ctx").astype(jnp.float32),
        lax.psum(shares[2].astype(jnp.bfloat16), "ctx").astype(jnp.float32),
        lax.psum(shares[3].astype(jnp.bfloat16), "ctx").astype(jnp.float32),
        lax.psum(shares[4].astype(jnp.bfloat16), "ctx").astype(jnp.float32),
        lax.psum(shares[5].astype(jnp.bfloat16), "ctx").astype(jnp.float32),
        lax.psum(shares[6].astype(jnp.bfloat16), "ctx").astype(jnp.float32),
        lax.psum(shares[7].astype(jnp.bfloat16), "ctx").astype(jnp.float32),
        lax.psum(shares[8].astype(jnp.bfloat16), "ctx").astype(jnp.float32),
        lax.psum(shares[9].astype(jnp.bfloat16), "ctx").astype(jnp.float32),
        lax.psum(shares[10].astype(jnp.bfloat16), "ctx").astype(jnp.float32),
        lax.psum(shares[11].astype(jnp.bfloat16), "ctx").astype(jnp.float32),
        lax.psum(shares[12].astype(jnp.bfloat16), "ctx").astype(jnp.float32),
        lax.psum(shares[13].astype(jnp.bfloat16), "ctx").astype(jnp.float32),
        lax.psum(shares[14].astype(jnp.bfloat16), "ctx").astype(jnp.float32),
        lax.psum(shares[15].astype(jnp.bfloat16), "ctx").astype(jnp.float32),
    )
    (
        wq_total,
        wk_total,
        wv_total,
        wo_total,
        bq_total,
        bv_total,
        bo_total,
        gain_one_total,
        shift_one_total,
        wi_total,
        bi_total,
        wf_total,
        bf_total,
        gain_two_total,
        shift_two_total,
        table_total,
    ) = totals
    logit_grad = table_total * 2.0 * jax.nn.sigmoid(-2.0 * (mask_logits + mask_noise))
    return (
        jnp.stack(outputs_list),
        jnp.stack(input_grads),
        wq_total,
        wk_total,
        wv_total,
        wo_total,
        bq_total,
        bv_total,
        bo_total,
        gain_one_total,
        shift_one_total,
        wi_total,
        bi_total,
        wf_total,
        bf_total,
        gain_two_total,
        shift_two_total,
        logit_grad,
    )


MESH = pl.DeviceIdType.MESH
BF16 = jnp.bfloat16
F32 = jnp.float32
ROWS = 192
TALL = 272


ROOT_HALF = 0.7071067811865476
ROOT_TWO_PI = 0.3989422804014327


def place():
    c = lax.axis_index("ctx")
    f = lax.axis_index("fsdp")
    return (c // 2, c % 2, f // 2, f % 2)


def device(z, x, y, k):
    return {"ctx": z * 2 + x, "fsdp": y * 2 + k}


def send(src, dst, send_sem, recv_sem, target):
    return pltpu.make_async_remote_copy(
        src_ref=src,
        dst_ref=dst,
        send_sem=send_sem,
        recv_sem=recv_sem,
        device_id=target,
        device_id_type=MESH,
    )


def meet(targets):
    barrier = pltpu.get_barrier_semaphore()
    for target in targets:
        pl.semaphore_signal(barrier, inc=1, device_id=target, device_id_type=MESH)
    pl.semaphore_wait(barrier, len(targets))


def any_spec():
    return pl.BlockSpec(memory_space=pl.ANY)


def vmem_spec():
    return pl.BlockSpec(memory_space=pltpu.VMEM)


def gather_pieces():
    pieces = [(array, 0, 192, 0, 768, "x") for array in range(4)]
    pieces.append((6, 0, 0, 0, 0, None))
    for part, axis in enumerate("xx"):
        pieces.append((4, 0, 192, 1536 * part, 1536, axis))
    for part, axis in enumerate(("z", "z", None, None)):
        pieces.append((5, 192 * part, 192, 0, 768, axis))
    return pieces


def gather_plan(ins, outs, small, small_out, sems):
    ss, rs, ls, ss_small, rs_small = sems
    z, x, y, k = place()
    mine = y * 2 + k
    over = (1 - y) * 2 + k
    core = device(z, x, y, 1 - k)
    ynb = device(z, x, 1 - y, k)
    diag = device(z, x, 1 - y, 1 - k)
    xnb = device(z, 1 - x, y, k)

    def source(piece, half):
        a, r0, rn, c0, cn, _ = piece
        if a == 6:
            return ins[a]
        if half is None:
            return ins[a].at[pl.ds(r0, rn), pl.ds(c0, cn)]
        return ins[a].at[pl.ds(r0 + (rn // 2) * half, rn // 2), pl.ds(c0, cn)]

    def target(piece, owner, half):
        a, r0, rn, c0, cn, _ = piece
        if a == 6:
            return outs[a].at[:, pl.ds(128 * owner, 128)]
        base = ins[a].shape[0] * owner + r0
        if half is None:
            return outs[a].at[pl.ds(base, rn), pl.ds(c0, cn)]
        return outs[a].at[pl.ds(base + (rn // 2) * half, rn // 2), pl.ds(c0, cn)]

    plan = []
    znb = device(z + 1 - 2 * lax.rem(z, 2), x, y, k)
    for n, piece in enumerate(gather_pieces()):
        axis = piece[5]
        part = {None: None, "x": x, "z": lax.rem(z, 2)}[axis]
        whole = source(piece, None)
        kept = target(piece, mine, None)
        here = target(piece, over, part)
        copies = {
            "own": pltpu.make_async_copy(whole, kept, ls.at[n]),
            "core": send(whole, kept, ss.at[n, 0], rs.at[n, 0], core),
            "y": send(source(piece, part), target(piece, mine, part), ss.at[n, 1], rs.at[n, 1], ynb),
            "core_y": send(here, here, ss.at[n, 3], rs.at[n, 3], core),
        }
        if axis is not None:
            there = target(piece, over, 1 - part)
            copies["x"] = send(
                here, here, ss.at[n, 2], rs.at[n, 2], xnb if axis == "x" else znb
            )
            copies["core_x"] = send(there, there, ss.at[n, 4], rs.at[n, 4], core)
        plan.append(copies)
    rows = small_out.at[mine]
    smalls = [
        send(small, rows, ss_small.at[i], rs_small.at[i], peer)
        for i, peer in enumerate((core, ynb, diag))
    ]
    own_small = pltpu.make_async_copy(small, rows, ls.at[len(plan)])
    return (plan, smalls, own_small)


def forward_y(copies):
    copies["y"].wait_recv()
    if "x" in copies:
        copies["x"].start()
    copies["core_y"].start()


def forward_x(copies):
    if "x" in copies:
        copies["x"].wait_recv()
        copies["core_x"].start()


def arrive(copies):
    copies["own"].wait()
    for name in ("core", "core_y", "core_x"):
        if name in copies:
            copies[name].wait_recv()


def settle(copies):
    for name, cp in copies.items():
        if name != "own":
            cp.wait_send()


def ctx_peers():
    c = lax.axis_index("ctx")
    return [{"ctx": lax.rem(c + i, 8)} for i in range(1, 8)]


class Exchange:
    def __init__(self, main, main_in, extra, extra_in, sems, home):
        self.main, self.main_in, self.extra, self.extra_in = (main, main_in, extra, extra_in)
        self.ms, self.mr, self.es, self.er, self.ls = sems
        self.c = lax.axis_index("ctx")
        self.group, self.me = (self.c // 4, lax.rem(self.c, 4))
        self.home = home

    def one(self, j, slot):
        return send(
            self.main.at[j],
            self.main_in.at[slot],
            self.ms.at[j],
            self.mr.at[slot],
            {"ctx": 4 * self.group + j},
        )

    def local(self, j):
        return pltpu.make_async_copy(self.main.at[j], self.main_in.at[j], self.ls)

    def side(self, j):
        if self.home:
            return send(
                self.extra, self.extra_in.at[self.me], self.es.at[0], self.er.at[self.me], {"ctx": 4}
            )
        return send(self.extra.at[j], self.extra_in, self.es.at[j], self.er.at[0], {"ctx": j})

    def start(self):
        if self.home:

            @pl.when(self.group == 0)
            def _():
                self.side(0).start()

        for j in range(4):

            @pl.when(self.me != j)
            def _():
                self.one(j, self.me).start()

            @pl.when(self.me == j)
            def _():
                self.local(j).start()

        if not self.home:

            @pl.when(self.c == 4)
            def _():
                for j in range(4):
                    self.side(j).start()

    def wait(self):
        for j in range(4):

            @pl.when(self.me != j)
            def _():
                self.one(0, j).wait_recv()

            @pl.when(self.me == j)
            def _():
                self.local(j).wait()

        if self.home:

            @pl.when(self.c == 4)
            def _():
                for j in range(4):
                    send(
                        self.extra, self.extra_in.at[j], self.es.at[0], self.er.at[j], {"ctx": 4}
                    ).wait_recv()

        else:

            @pl.when(self.group == 0)
            def _():
                self.side(0).wait_recv()

    def settle(self):
        for j in range(4):

            @pl.when(self.me != j)
            def _():
                self.one(j, self.me).wait_send()

        if self.home:

            @pl.when(self.group == 0)
            def _():
                self.side(0).wait_send()

        else:

            @pl.when(self.c == 4)
            def _():
                for j in range(4):
                    self.side(j).wait_send()


def exchange_sems():
    dma = pltpu.SemaphoreType.DMA
    return [dma((4,)), dma((4,)), dma((4,)), dma((4,)), dma]


def dot_nn(a, b):
    return lax.dot_general(a, b, (((1,), (0,)), ((), ())), preferred_element_type=F32)


def dot_nt(a, b):
    return lax.dot_general(a, b, (((1,), (1,)), ((), ())), preferred_element_type=F32)


def dot_tn(a, b):
    return lax.dot_general(a, b, (((0,), (0,)), ((), ())), preferred_element_type=F32)


def own_rows(main, s, lo, width):
    return main[:, pl.ds(64 * s, 64), lo : lo + width].reshape(256, width)


def place_masks(main, s):
    marks = own_rows(main, s, 576, 64).astype(F32)
    segment = marks[:, 0:1]
    slot = marks[:, 1:2]
    valid = jnp.where(segment == 0.0, 0.0, 1.0)
    lanes = lax.broadcasted_iota(jnp.int32, (256, 128), 1).astype(F32)
    seg_hot = jnp.where((lanes == segment) & (valid > 0.0), 1.0, 0.0).astype(BF16)
    wide = lax.broadcasted_iota(jnp.int32, (256, 256), 1).astype(F32)
    slot_hot = jnp.where((wide == slot) & (valid > 0.0), 1.0, 0.0).astype(BF16)
    return (slot_hot, dot_nt(seg_hot, seg_hot) > 0.5, valid)


class BlockSums:
    def __init__(self, bufs, sems, blocks):
        self.blocks = blocks
        self.st, self.r1, self.r2, self.r3, self.r4, self.total = bufs
        self.p1, self.q1, self.p2, self.q2, self.p3, self.q3, self.p4, self.q4 = sems[:8]
        self.p5, self.q5, self.p6, self.q6, self.kept = sems[8:]
        z, x, y, k = place()
        self.z, self.x, self.y, self.k = (z, x, y, k)
        self.core = device(z, x, y, 1 - k)
        self.ynb = device(z, x, 1 - y, k)
        self.xnb = device(z, 1 - x, y, k)
        self.peers = [lax.rem(z + i, 4) for i in (1, 2, 3)]
        self.columns = pl.ds(pl.multiple_of(384 * x, 128), 384)
        self.others = pl.ds(pl.multiple_of(384 * (1 - x), 128), 384)

    def zdev(self, zz):
        return device(zz, self.x, self.y, self.k)

    def to_core(self, n, yy):
        slot = n % 4
        return send(
            self.st.at[slot, yy], self.r1.at[n, yy], self.p1.at[n, yy], self.q1.at[n, yy], self.core
        )

    def to_y(self, n):
        return send(
            self.r1.at[n, 1 - self.y], self.r2.at[n], self.p2.at[n], self.q2.at[n], self.ynb
        )

    def sum_x(self, n):
        return send(
            self.r2.at[n, :, self.others], self.r3.at[n], self.p3.at[n], self.q3.at[n], self.xnb
        )

    def sum_z(self, n, i):
        zz = self.peers[i]
        return send(
            self.r3.at[n, pl.ds(48 * zz, 48)],
            self.r4.at[n, self.z],
            self.p4.at[n, i],
            self.q4.at[n, self.z],
            self.zdev(zz),
        )

    def view(self, n, rows):
        ref, row, column = self.blocks[n if isinstance(n, int) else 0]
        if rows == slice(None):
            rows = pl.ds(row, 192)
        else:
            rows = pl.ds(rows.start + row, rows.size)
        return ref.at[rows, pl.ds(pl.multiple_of(column + 384 * self.x, 128), 384)]

    def spread_z(self, n, i, owner):
        here = self.view(n, pl.ds(48 * owner, 48))
        return send(
            self.total.at[n], here, self.p5.at[n, i], self.q5.at[n, owner], self.zdev(self.peers[i])
        )

    def keep(self, n):
        here = self.view(n, pl.ds(48 * self.z, 48))
        return pltpu.make_async_copy(self.total.at[n], here, self.kept.at[n])

    def spread_x(self, n):
        here = self.view(n, slice(None))
        return send(here, here, self.p6.at[n], self.q6.at[n], self.xnb)

    def one(self, n, partial):
        for yy in range(2):
            self.st[n % 4, yy] = partial(2 * yy + 1 - self.k).astype(BF16)
            self.to_core(n, yy).start()

    def two(self, n, partial):
        for yy in range(2):
            own = partial(2 * yy + self.k)
            self.to_core(n, yy).wait_recv()
            self.r1[n, yy] = (own + self.r1[n, yy].astype(F32)).astype(BF16)
        self.to_y(n).start()

    def three(self, n):
        self.to_y(n).wait_recv()

        def body(i, carry):
            at = pl.ds(pl.multiple_of(i * 48, 48), 48)
            self.r2[n, at, :] = self.r2[n, at, :] + self.r1[n, self.y, at, :]
            return carry

        lax.fori_loop(0, 4, body, 0)
        self.sum_x(n).start()

    def four(self, n):
        self.sum_x(n).wait_recv()

        def body(i, carry):
            at = pl.ds(pl.multiple_of(i * 48, 48), 48)
            self.r3[n, at, :] = self.r3[n, at, :] + self.r2[n, at, self.columns]
            return carry

        lax.fori_loop(0, 4, body, 0)
        for i in range(3):
            self.sum_z(n, i).start()

    def five(self, n):
        for i in range(3):
            zz = self.peers[i]
            send(
                self.r3.at[n, pl.ds(0, 48)],
                self.r4.at[n, zz],
                self.p4.at[n, 0],
                self.q4.at[n, zz],
                self.core,
            ).wait_recv()
        rows = pl.ds(pl.multiple_of(48 * self.z, 16), 48)
        total = self.r3[n, rows, :].astype(F32)
        for i in range(3):
            total = total + self.r4[n, self.peers[i]].astype(F32)
        self.total[n] = total.astype(BF16)
        self.keep(n).start()
        for i in range(3):
            self.spread_z(n, i, self.z).start()

    def six(self, n):
        self.keep(n).wait()
        for i in range(3):
            self.spread_z(n, i, self.peers[i]).wait_recv()
        self.spread_x(n).start()

    def seven(self, n):
        self.spread_x(n).wait_recv()

    def settle(self):
        def body(n, carry):
            self.to_y(n).wait_send()
            self.sum_x(n).wait_send()
            self.spread_x(n).wait_send()
            for i in range(3):
                self.sum_z(n, i).wait_send()
                self.spread_z(n, i, self.z).wait_send()
            return carry

        lax.fori_loop(0, 12, body, 0)
        for n in range(8, 12):
            for yy in range(2):
                self.to_core(n, yy).wait_send()


def layer_kernel(
    tokens, segments, places, upstream, *vectors_and_more
):
    vectors, rest = (vectors_and_more[:9], vectors_and_more[9:])
    layer_body(tokens, segments, places, upstream, vectors, *rest)


def layer_body(
    tokens, segments, places, upstream, vectors,
    wq_in, wk_in, wv_in, wo_in, wi_in, wf_in, logits_in, noise_in,
    hidden_out, input_grad, oh, oi, of, small_out, mask_out,
    wq, wk, wv, wo, wi, wf, table, small,
    main, extra, main_send, extra_send, probs, ctx_send, ctx_extra, ctx4, ctx_extra_in,
    small_in, marks, active, table_in, tokens4, first_hat, first_norm, first4, active16, slope, inner, sum_grad, low_grad,
    grad4, grad_extra, grad_in, grad_extra_in, main_in, extra_in, table_grad, lows,
    v0, v1, v2, v3, v4, t0, t1, t2, t3, e0, e1, e2, e3, table_out, edge_out,
    st, r1, r2, r3, r4, total, hidden_low, input_sum, mask_sum, *sems
):
    z, x, y, k = place()
    c = 2 * z + x
    group = c // 4
    core = device(z, x, y, 1 - k)
    ynb = device(z, x, 1 - y, k)
    xnb = device(z, 1 - x, y, k)
    twin = device(lax.rem(z + 2, 4), x, y, k)
    zdev = [device(lax.rem(z + i, 4), x, y, k) for i in (1, 2, 3)]
    gather_sems, ex = (sems[:5], [sems[5 + 5 * i : 10 + 5 * i] for i in range(4)])
    sum_sems, (ps, qs, pt, qt, pe, qe, load) = (sems[25:38], sems[38:45])
    heads = pl.ds(3 * lax.rem(c, 4), 3)
    near = pl.ds(0, 384)
    loads = [
        pltpu.make_async_copy(
            logits_in.at[heads, :, near], slope.at[0:3, 0:128, 0:384], load.at[0]
        ),
        pltpu.make_async_copy(
            noise_in.at[heads, :, near], slope.at[0:3, 0:128, 384:768], load.at[1]
        ),
    ]
    for cp in loads:
        cp.start()
    meet(ctx_peers() + [core, ynb, device(z, x, 1 - y, 1 - k)])

    for i in range(8):
        small_in[i : i + 1, 0:192] = vectors[i][...].astype(F32).reshape(1, 192)
    for i in range(4):
        small_in[8 + i : 9 + i, 0:192] = (
            vectors[8][192 * i : 192 * i + 192].astype(F32).reshape(1, 192)
        )
    plan, smalls, own_small = gather_plan(
        (wq_in, wk_in, wv_in, wo_in, wi_in, wf_in, table_in),
        (wq, wk, wv, wo, wi, wf, table),
        small_in,
        small,
        gather_sems,
    )
    for cp in smalls + [own_small]:
        cp.start()
    for name in ("y", "core", "own"):
        for n in range(3):
            plan[n][name].start()
    for cp in loads:
        cp.wait()
    for h in range(3):
        doubled = 2.0 * (slope[h, 0:128, 0:384] + slope[h, 0:128, 384:768])
        table_in[h] = (
            jnp.minimum(doubled, 0.0) - jnp.log1p(jnp.exp(-jnp.abs(doubled)))
        ).astype(BF16)
    for n in range(3, len(plan)):
        for name in ("y", "core", "own"):
            plan[n][name].start()
    forward_y(plan[0])
    forward_y(plan[1])
    for j in range(4):
        tokens4[j] = tokens[:, 192 * j : 192 * j + 192]
    down = lax.broadcasted_iota(jnp.int32, (64, 64), 0)
    along = lax.broadcasted_iota(jnp.int32, (64, 64), 1)
    for s in range(3):
        mark = jnp.zeros((64, 64), F32)
        for i, ref in enumerate((segments, places)):
            row = lax.rem(ref[s : s + 1, :], MSPAN).astype(F32)
            column = jnp.sum(jnp.where(down == along, row, 0.0), axis=1, keepdims=True)
            mark = jnp.where(along == i, column, mark)
        marks[64 * s : 64 * s + 64] = mark.astype(BF16)
    table_grad[...] = jnp.zeros((3, TALL, TALL), F32)
    v0[...] = jnp.zeros((4, 16, 256), F32)
    e0[...] = jnp.zeros((16, 384), F32)

    forward_y(plan[2])
    for n in range(3):
        forward_x(plan[n])
    forward_y(plan[3])
    own_small.wait()
    for cp in smalls:
        cp.wait_recv()

    def vector(i):
        return jnp.concatenate([small[f, i : i + 1, 0:192] for f in range(4)], axis=1)

    arrive(plan[0])
    q = (dot_nn(tokens[...], wq[...]) + vector(0)).astype(BF16)
    arrive(plan[1])
    kk = dot_nn(tokens[...], wk[...]).astype(BF16)
    arrive(plan[2])
    v = (dot_nn(tokens[...], wv[...]) + vector(1)).astype(BF16)
    for j in range(4):
        cols = slice(192 * j, 192 * j + 192)
        main_send[j] = jnp.concatenate([q[:, cols], kk[:, cols], v[:, cols], marks[...]], axis=1)
        for s in range(3):
            extra_send[j, 16 * s : 16 * s + 16] = main_send[j, 64 * s : 64 * s + 16]
    heads_there = Exchange(main_send, main, extra_send, extra, ex[0], False)
    heads_there.start()
    forward_y(plan[4])
    forward_x(plan[3])
    forward_y(plan[5])
    heads_there.wait()
    arrive(plan[4])

    own, end = (slice(0, 256), slice(256, 272))

    def loop(first, count, body):
        def step(i, carry):
            body(first + i, i)
            return carry

        lax.fori_loop(0, count, step, 0)

    def first_document(s, _):
        lone = lax.broadcasted_iota(jnp.int32, (256, 16), 1) == 0
        lone_row = jnp.where(lax.broadcasted_iota(jnp.int32, (16, 1), 0) == 0, 1.0, 0.0)
        at = pl.ds(pl.multiple_of(16 * s, 16), 16)
        parts, ends = ([], [])
        for h in range(3):
            qo, ko, vo = [own_rows(main, s, lo + 64 * h, 64) for lo in (0, 192, 384)]
            qe, ke, ve = [extra[at, lo + 64 * h : lo + 64 * h + 64] for lo in (0, 192, 384)]
            bias = table[h, 0:TALL, 0:TALL].astype(F32)
            oo = dot_nt(qo, ko) * 0.125 + bias[own, own]
            oe = jnp.where(lone, dot_nt(qo, ke) * 0.125 + bias[own, end], NEGATIVE)
            eo = dot_nt(qe, ko) * 0.125 + bias[end, own]
            ee = jnp.where(lone[0:16], dot_nt(qe, ke) * 0.125 + bias[end, end], NEGATIVE)
            n = 3 * s + h
            for left, right, rows, valid, into, v_ends in (
                (oo, oe, own, 1.0, parts, None),
                (eo, ee, end, lone_row, ends, None),
            ):
                top = jnp.maximum(
                    jnp.max(left, axis=1, keepdims=True), jnp.max(right, axis=1, keepdims=True)
                )
                left, right = (jnp.exp(left - top), jnp.exp(right - top))
                share = valid / (
                    jnp.sum(left, axis=1, keepdims=True) + jnp.sum(right, axis=1, keepdims=True)
                )
                left, right = ((left * share).astype(BF16), (right * share).astype(BF16))
                probs[n, rows, own] = left
                probs[n, rows, end] = right
                into.append((dot_nn(left, vo) + dot_nn(right, ve)).astype(BF16))
        whole = jnp.concatenate(parts, axis=1)
        for j in range(4):
            ctx_send[j, pl.ds(64 * s, 64)] = whole[64 * j : 64 * j + 64]
        ctx_extra[at] = jnp.concatenate(ends, axis=1)

    def other_documents(s, _):
        slot_hot, same, valid = place_masks(main, s)
        parts = []
        for h in range(3):
            qo, ko, vo = [own_rows(main, s, lo + 64 * h, 64) for lo in (0, 192, 384)]
            picked = dot_nn(slot_hot, table[h, 0:256, 0:256]).astype(BF16)
            bias = dot_nt(picked, slot_hot)
            scores = jnp.where(same, dot_nt(qo, ko) * 0.125 + bias, NEGATIVE)
            top = jnp.max(scores, axis=1, keepdims=True)
            grown = jnp.exp(scores - top)
            share = valid / jnp.sum(grown, axis=1, keepdims=True)
            soft = (grown * share).astype(BF16)
            probs[3 * s + h, own, own] = soft
            parts.append(dot_nn(soft, vo).astype(BF16))
        whole = jnp.concatenate(parts, axis=1)
        for j in range(4):
            ctx_send[j, pl.ds(64 * s, 64)] = whole[64 * j : 64 * j + 64]

    def attend(first, count):
        @pl.when(group == 0)
        def _():
            loop(first, count, first_document)

        @pl.when(group == 1)
        def _():
            loop(first, count, other_documents)

    attend(0, 1)
    forward_y(plan[6])
    attend(1, 2)
    forward_x(plan[5])
    heads_back = Exchange(ctx_send, ctx4, ctx_extra, ctx_extra_in, ex[1], True)
    heads_back.start()
    forward_y(plan[7])
    def factor(hg, carry):
        part = pl.ds(3 * hg, 3)
        loads = [
            pltpu.make_async_copy(
                logits_in.at[part, :, near], slope.at[0:3, 0:128, 0:384], load.at[0]
            ),
            pltpu.make_async_copy(
                noise_in.at[part, :, near], slope.at[0:3, 0:128, 384:768], load.at[1]
            ),
        ]
        for cp in loads:
            cp.start()
        for cp in loads:
            cp.wait()
        for h in range(3):
            grown = jnp.exp(2.0 * (slope[h, 0:128, 0:384] + slope[h, 0:128, 384:768]))
            mask_sum[3 * hg + h, :, 0:384] = 2.0 / (1.0 + grown)
        return carry

    lax.fori_loop(0, 4, factor, 0)
    heads_back.wait()

    def join(into, side):
        @pl.when(c == 4)
        def _():
            for j in range(4):
                for s in range(3):
                    at = slice(64 * s, 64 * s + 16)
                    into[j, at] = into[j, at] + side[j, 16 * s : 16 * s + 16]

    join(ctx4, ctx_extra_in)

    def mean(value):
        return jnp.mean(value, axis=1, keepdims=True)

    def column_sum(value):
        return jnp.sum(value, axis=0, keepdims=True)

    def keep_vector(i, row):
        for owner in range(4):
            v0[owner, i : i + 1, 0:192] = row[:, 192 * owner : 192 * owner + 192]

    forward_y(plan[8])
    arrive(plan[3])
    context = jnp.concatenate([ctx4[j] for j in range(4)], axis=1)
    centered = tokens[...].astype(F32) + dot_nn(context, wo[...]) + vector(2)
    centered = centered - mean(centered)
    first_rate = lax.rsqrt(mean(centered * centered) + EPSILON)
    centered = centered * first_rate
    first_hat[...] = centered
    centered = centered * vector(3) + vector(4)
    first_norm[...] = centered
    first_low = centered.astype(BF16)
    for j in range(4):
        first4[j] = first_low[:, 192 * j : 192 * j + 192]
    forward_x(plan[6])
    arrive(plan[5])
    arrive(plan[6])

    def inner_product(j):
        bias = jnp.concatenate([small[j, 8 + i : 9 + i, 0:192] for i in range(4)], axis=1)
        at = 768 * j
        value = dot_nn(first_low, wi[:, at : at + 768]) + bias
        share = 0.5 + 0.5 * lax.erf(value * ROOT_HALF)
        low = (value * share).astype(BF16)
        active[j] = low
        for b in range(4):
            active16[4 * j + b] = low[:, 192 * b : 192 * b + 192]
        slope[j] = share + value * (jnp.exp(-0.5 * value * value) * ROOT_TWO_PI)

    for j in range(4):
        inner_product(j)
        if j == 0:
            forward_y(plan[9])
            forward_x(plan[7])
        if j == 2:
            forward_y(plan[10])
            forward_x(plan[8])
    forward_x(plan[9])
    forward_x(plan[10])
    for n in range(7, 11):
        arrive(plan[n])
    first_norm[...] += vector(5)

    centered = first_norm[...]
    for j in range(4):
        centered = centered + dot_nn(active[j], wf[768 * j : 768 * j + 768])
    centered = centered - mean(centered)
    rate = lax.rsqrt(mean(centered * centered) + EPSILON)
    hat = centered * rate
    hidden_low[...] = (hat * vector(6) + vector(7)).astype(BF16)
    outs = [pltpu.make_async_copy(hidden_low, hidden_out, load.at[2])]
    outs[0].start()

    above = upstream[...].astype(F32)
    keep_vector(6, column_sum(above * hat))
    keep_vector(7, column_sum(above))
    scaled = above * vector(6)
    grown_grad = rate * (scaled - mean(scaled) - hat * mean(scaled * hat))
    sum_grad[...] = grown_grad
    low_grad[...] = grown_grad.astype(BF16)
    keep_vector(5, column_sum(low_grad[...].astype(F32)))

    blocks = [(of, 192 * b, 0) for b in range(4)] + [(oi, 0, 768 * b) for b in range(4)]
    blocks += [(oh, 192 * b, 0) for b in range(4)]
    sums = BlockSums((st, r1, r2, r3, r4, total), sum_sems, blocks)

    def final_part(b):
        return lambda owner: dot_tn(active16[4 * owner + b], low_grad[...])

    def inter_part(b):
        return lambda owner: dot_tn(first4[owner], inner[b])

    def heads_part(b):
        return lambda owner: dot_tn(tokens4[owner], lows[b])

    def out_part(owner):
        return dot_tn(ctx4[owner], low_grad[...])

    def again(n):
        for yy in range(2):
            sums.to_core(n, yy).wait_send()

    def inner_back(j):
        at = pl.ds(pl.multiple_of(768 * j, 768), 768)
        value = dot_nt(low_grad[...], wf[at]).astype(BF16)
        inner[j] = (value.astype(F32) * slope[j]).astype(BF16)
        row = column_sum(inner[j].astype(F32))
        for i in range(4):
            v0[j, 8 + i : 9 + i, 0:192] = row[:, 192 * i : 192 * i + 192]
        sum_grad[...] += dot_nt(inner[j], wi[:, at])

    sums.one(0, final_part(0))

    def final_both(n, b):
        sums.one(n + 1, final_part(b + 1))
        sums.two(n, final_part(b))

    loop(0, 3, final_both)
    sums.two(3, final_part(3))
    loop(0, 4, lambda j, i: inner_back(j))

    def inter_one(n, b):
        again(n - 4)
        sums.one(n, inter_part(b))

    loop(4, 4, inter_one)
    sums.three(0)
    above = sum_grad[...]
    hat = first_hat[...]
    keep_vector(3, column_sum(above * hat))
    keep_vector(4, column_sum(above))
    scaled = above * vector(3)
    norm_grad = first_rate * (scaled - mean(scaled) - hat * mean(scaled * hat))
    sum_grad[...] = norm_grad
    low_grad[...] = norm_grad.astype(BF16)
    keep_vector(2, column_sum(low_grad[...].astype(F32)))
    context_grad = dot_nt(low_grad[...], wo[...]).astype(BF16)
    for j in range(4):
        grad4[j] = context_grad[:, 192 * j : 192 * j + 192]
        for s in range(3):
            grad_extra[j, 16 * s : 16 * s + 16] = grad4[j, 64 * s : 64 * s + 16]
    grads_there = Exchange(grad4, grad_in, grad_extra, grad_extra_in, ex[2], False)
    grads_there.start()
    loop(4, 3, lambda n, b: sums.two(n, inter_part(b)))
    sums.three(1)
    sums.four(0)
    grads_there.wait()

    def keep_heads(s, parts, into):
        blank = jnp.zeros((parts[0][0].shape[0], 64), BF16)
        into(jnp.concatenate(parts[0] + parts[1] + parts[2] + [blank], axis=1))

    def own_heads(s):
        def into(whole):
            for j in range(4):
                main_send[j, pl.ds(64 * s, 64)] = whole[64 * j : 64 * j + 64]

        return into

    def first_document_back(s, _):
        at = pl.ds(pl.multiple_of(16 * s, 16), 16)
        parts, ends = ([[], [], []], [[], [], []])
        for h in range(3):
            qo, ko, vo = [own_rows(main, s, lo + 64 * h, 64) for lo in (0, 192, 384)]
            qe, ke, ve = [extra[at, lo + 64 * h : lo + 64 * h + 64] for lo in (0, 192, 384)]
            go = own_rows(grad_in, s, 64 * h, 64)
            ge = grad_extra_in[at, 64 * h : 64 * h + 64]
            n = 3 * s + h
            moves = []
            for g, rows in ((go, own), (ge, end)):
                left, right = (probs[n, rows, own], probs[n, rows, end])
                wide_left, wide_right = (left.astype(F32), right.astype(F32))
                grad_left, grad_right = (dot_nt(g, vo), dot_nt(g, ve))
                delta = jnp.sum(wide_left * grad_left, axis=1, keepdims=True) + jnp.sum(
                    wide_right * grad_right, axis=1, keepdims=True
                )
                grad_left = (wide_left * (grad_left - delta)).astype(BF16)
                grad_right = (wide_right * (grad_right - delta)).astype(BF16)
                table_grad[h, rows, own] += grad_left.astype(F32)
                table_grad[h, rows, end] += grad_right.astype(F32)
                moves.append((left, right, grad_left, grad_right))
            (poo, poe, soo, soe), (peo, pee, seo, see) = moves
            parts[0].append(((dot_nn(soo, ko) + dot_nn(soe, ke)) * 0.125).astype(BF16))
            ends[0].append(((dot_nn(seo, ko) + dot_nn(see, ke)) * 0.125).astype(BF16))
            parts[1].append(((dot_tn(soo, qo) + dot_tn(seo, qe)) * 0.125).astype(BF16))
            ends[1].append(((dot_tn(soe, qo) + dot_tn(see, qe)) * 0.125).astype(BF16))
            parts[2].append((dot_tn(poo, go) + dot_tn(peo, ge)).astype(BF16))
            ends[2].append((dot_tn(poe, go) + dot_tn(pee, ge)).astype(BF16))
        keep_heads(s, parts, own_heads(s))

        def into(whole):
            extra_send[0, at] = whole

        keep_heads(s, ends, into)

    def other_documents_back(s, _):
        slot_hot, _, _ = place_masks(main, s)
        parts = [[], [], []]
        for h in range(3):
            qo, ko, vo = [own_rows(main, s, lo + 64 * h, 64) for lo in (0, 192, 384)]
            go = own_rows(grad_in, s, 64 * h, 64)
            soft = probs[3 * s + h, own, own]
            weight = soft.astype(F32)
            weight_grad = dot_nt(go, vo)
            delta = jnp.sum(weight * weight_grad, axis=1, keepdims=True)
            score_grad = (weight * (weight_grad - delta)).astype(BF16)
            parts[0].append((dot_nn(score_grad, ko) * 0.125).astype(BF16))
            parts[1].append((dot_tn(score_grad, qo) * 0.125).astype(BF16))
            parts[2].append(dot_tn(soft, go).astype(BF16))
            moved = dot_tn(slot_hot, score_grad)
            table_grad[h, own, own] += dot_nn(moved.astype(BF16), slot_hot)
        keep_heads(s, parts, own_heads(s))

    def attend_back(s):
        @pl.when(group == 0)
        def _():
            first_document_back(s, 0)

        @pl.when(group == 1)
        def _():
            other_documents_back(s, 0)

    heads_there.settle()
    attend_back(0)
    sums.three(2)
    sums.four(1)
    loop(1, 2, lambda s, i: attend_back(s))
    sums.five(0)
    grads_back = Exchange(main_send, main_in, extra_send.at[0], extra_in, ex[3], True)
    grads_back.start()
    w = {}

    def table_core():
        lane = lax.broadcasted_iota(jnp.int32, (8, TALL), 1)
        final = jnp.where(lane == 256, 1.0, 0.0).astype(BF16)
        for h in range(3):
            t0[h] = table_grad[h, 0:256, 0:256].astype(BF16)
            e0[h : h + 1, 0:TALL] = table_grad[h, 256:257, :]
            column = dot_nt(final, table_grad[h].astype(BF16))
            e0[8 + h : 9 + h, 0:TALL] = column[0:1]
        w["tcore"] = send(t0.at[:, pl.ds(128 * (1 - k), 128)], t1, pt.at[0], qt.at[0], core)
        w["tcore"].start()
        w["ecore"] = send(e0, e1, pe.at[0], qe.at[0], core)
        w["ecore"].start()

    def out_one():
        again(7)
        sums.one(11, out_part)

    def table_over_y():
        w["tcore"].wait_recv()
        for h in range(3):
            t1[h] = t0[h, pl.ds(pl.multiple_of(128 * k, 128), 128), :] + t1[h]
        w["table_y"] = send(t1.at[:, pl.ds(64 * (1 - y), 64)], t2, pt.at[1], qt.at[1], ynb)
        w["table_y"].start()
        w["ecore"].wait_recv()
        e1[...] = e0[...] + e1[...]
        w["edge_y"] = send(e1, e2, pe.at[1], qe.at[1], ynb)
        w["edge_y"].start()

    def late_two():
        sums.two(7, inter_part(3))
        sums.two(11, out_part)

    def heads_back_in():
        grads_back.wait()
        join(main_in, extra_in)
        for a in range(3):
            lows[a] = jnp.concatenate(
                [main_in[j, :, 192 * a : 192 * a + 192] for j in range(4)], axis=1
            )
        keep_vector(0, column_sum(lows[0].astype(F32)))
        keep_vector(1, column_sum(lows[2].astype(F32)))
        for yy in range(2):
            cp = send(v0.at[2 * yy + 1 - k], v1.at[yy], ps.at[yy], qs.at[yy], core)
            cp.start()
            w["small_core", yy] = cp

    def heads_sums():
        def heads_one(n, b):
            again(n - 4)
            sums.one(n, heads_part(b))

        loop(8, 3, heads_one)
        for yy in range(2):
            w["small_core", yy].wait_recv()
            v1[yy] = v0[2 * yy + k] + v1[yy]
        w["small_y"] = send(v1.at[1 - y], v2, ps.at[2], qs.at[2], ynb)
        w["small_y"].start()
        loop(8, 3, lambda n, b: sums.two(n, heads_part(b)))

    def inputs_grad():
        input_sum[...] = sum_grad[...] + dot_nt(lows[0], wq[...])
        input_sum[...] += dot_nt(lows[1], wk[...])
        input_sum[...] += dot_nt(lows[2], wv[...])
        outs.append(pltpu.make_async_copy(input_sum, input_grad, load.at[3]))
        outs[1].start()

    def table_to_twin():
        w["edge_y"].wait_recv()
        e2[...] = e1[...] + e2[...]
        w["edge_x"] = send(e2, e3, pe.at[2], qe.at[2], twin)
        w["edge_x"].start()
        w["table_y"].wait_recv()
        for h in range(3):
            t2[h] = t1[h, pl.ds(pl.multiple_of(64 * y, 64), 64), :] + t2[h]
        w["table_x"] = send(t2.at[:, pl.ds(32 * (1 - group), 32)], t3, pt.at[2], qt.at[2], twin)
        w["table_x"].start()

    me = lax.rem(c, 4)

    def table_piece(hg, side):
        return table_out.at[hg, :, pl.ds(64 * y + 32 * side, 32)]

    def table_spread():
        w["edge_x"].wait_recv()
        edge_out[c] = e2[...] + e3[...]
        here = edge_out.at[c]
        for i in range(3):
            w["edge_z", i] = send(here, here, pe.at[3 + i], qe.at[3 + z], zdev[i])
        w["edge_z", 3] = send(here, here, pe.at[6], qe.at[7 + z], xnb)
        w["table_x"].wait_recv()
        at = pl.ds(pl.multiple_of(32 * group, 32), 32)
        to = pl.ds(pl.multiple_of(64 * y + 32 * group, 32), 32)
        for h in range(3):
            table_out[me, h, to, :] = t2[h, at, :] + t3[h]
        here = table_piece(me, group)
        for i in range(3):
            w["table_z", i] = send(here, here, pt.at[3 + i], qt.at[3 + z], zdev[i])
        w["table_z", 3] = send(here, here, pt.at[6], qt.at[7 + z], xnb)
        for i in range(4):
            w["edge_z", i].start()
            w["table_z", i].start()

    def table_over_x():
        for i in (1, 2, 3):
            zz = lax.rem(z + i, 4)
            cc = 2 * zz + x
            there = edge_out.at[cc]
            send(there, there, pe.at[3], qe.at[3 + zz], core).wait_recv()
            w["edge_z", 3 + i] = send(there, there, pe.at[6 + i], qe.at[7 + zz], xnb)
            w["edge_z", 3 + i].start()
            there = table_piece(lax.rem(cc, 4), cc // 4)
            send(there, there, pt.at[3], qt.at[3 + zz], core).wait_recv()
            w["table_z", 3 + i] = send(there, there, pt.at[6 + i], qt.at[7 + zz], xnb)
            w["table_z", 3 + i].start()

    half_table = table_out.at[:, :, pl.ds(64, 64)]
    half_copy = send(half_table, half_table, pt.at[10], qt.at[11], ynb)

    def table_half():
        for zz in range(4):
            cc = 2 * zz + 1 - x
            there = table_piece(lax.rem(cc, 4), cc // 4)
            send(there, there, pt.at[6], qt.at[7 + zz], xnb).wait_recv()
            there = edge_out.at[cc]
            send(there, there, pe.at[6], qe.at[7 + zz], xnb).wait_recv()

        @pl.when(y == 1)
        def _():
            half_copy.start()

    def small_over_x():
        w["small_y"].wait_recv()
        v2[...] = v1[y] + v2[...]
        w["small_x"] = send(v2, v3, ps.at[3], qs.at[3], xnb)
        w["small_x"].start()

    def small_over_z():
        w["small_x"].wait_recv()
        v4[z] = v2[...] + v3[...]
        for i in range(3):
            w["small_z", i] = send(v4.at[z], v4.at[z], ps.at[4 + i], qs.at[4 + z], zdev[i])
            w["small_z", i].start()

    def small_end():
        for i in (1, 2, 3):
            zz = lax.rem(z + i, 4)
            send(v4.at[zz], v4.at[zz], ps.at[4], qs.at[4 + zz], core).wait_recv()
        small_out[...] = (v4[0] + v4[1]) + (v4[2] + v4[3])

    def mask_end():
        @pl.when(y == 0)
        def _():
            half_copy.wait_recv()
            deep = lax.broadcasted_iota(jnp.int32, (128, 128), 0)
            across = lax.broadcasted_iota(jnp.int32, (128, 128), 1)

            def fill(hg, carry):
                for h in range(3):
                    row = edge_out[hg, 8 + h : 9 + h, :]
                    row = jnp.where(k == 0, row[:, 0:128], row[:, 128:256])
                    column = jnp.sum(jnp.where(deep == across, row, 0.0), axis=1, keepdims=True)
                    n = 3 * hg + h
                    mask_sum[n, :, 0:256] = mask_sum[n, :, 0:256] * table_out[hg, h].astype(F32)
                    mask_sum[n, :, 256:384] = mask_sum[n, :, 256:384] * jnp.where(
                        across == 0, column, 0.0
                    )
                return carry

            lax.fori_loop(0, 4, fill, 0)

        @pl.when(y == 1)
        def _():
            top = lax.broadcasted_iota(jnp.int32, (8, 384), 0)

            def fill(hg, carry):
                for h in range(3):
                    n = 3 * hg + h
                    first = mask_sum[n, 0:8, 0:384] * edge_out[hg, h : h + 1, :]
                    mask_sum[n] = jnp.zeros((128, 384), F32)
                    mask_sum[n, 0:8, 0:384] = jnp.where((top == 0) & (k == 0), first, 0.0)
                return carry

            lax.fori_loop(0, 4, fill, 0)

        outs.append(pltpu.make_async_copy(mask_sum, mask_out, load.at[4]))
        outs[2].start()

    steps = [
        ("three", 3), ("four", 2), ("five", 1), ("six", 0), table_core, out_one, table_over_y,
        late_two, ("three", 4), ("five", 2), ("six", 1), ("four", 3), heads_back_in,
        ("three", 5), ("four", 4), ("five", 3), ("six", 2), heads_sums, ("three", 6),
        ("four", 5), table_to_twin, ("five", 4), ("six", 3), inputs_grad, ("three", 7),
        ("four", 6), ("five", 5), ("three", 11), ("four", 7), table_spread, ("six", 4),
        ("five", 6), small_over_x, ("three", 8), ("four", 11), ("six", 5), ("five", 7),
        small_over_z, ("three", 9), ("four", 8), ("six", 6), ("five", 11), ("three", 10),
        ("four", 9), ("six", 7), table_over_x, ("five", 8), ("four", 10), ("six", 11),
        ("five", 9), ("six", 8), table_half, ("five", 10), small_end, ("six", 9), ("six", 10),
        mask_end,
    ]
    for step in steps:
        if isinstance(step, tuple):
            getattr(sums, step[0])(step[1])
        else:
            step()
    for n in (0, 1, 2, 3, 4, 5, 6, 7, 11, 8, 9, 10):
        sums.seven(n)
    for cp in outs:
        cp.wait()

    @pl.when(y == 1)
    def _():
        half_copy.wait_send()

    for cp in w.values():
        cp.wait_send()
    for exchange in (heads_back, grads_there, grads_back):
        exchange.settle()
    for copies in plan:
        settle(copies)
    for cp in smalls:
        cp.wait_send()
    sums.settle()


def layer(tokens, segments, places, upstream, vectors, arrays, logits, noise):
    dma = pltpu.SemaphoreType.DMA
    count = len(gather_pieces())

    def low(*shape):
        return pltpu.VMEM(shape, BF16)

    def wide(*shape):
        return pltpu.VMEM(shape, F32)

    scratch = [low(a.shape[0] * 4, a.shape[1]) for a in arrays]
    scratch += [low(3, 512, 384), wide(4, 16, 256)]
    scratch += [
        low(4, ROWS, 640), low(48, 640), low(4, ROWS, 640), low(4, 48, 640),
        low(9, TALL, TALL),
        low(4, ROWS, 192), low(48, 192), low(4, ROWS, 192), low(4, 48, 192),
    ]
    scratch += [
        wide(16, 256), low(ROWS, 64), low(4, ROWS, 768), low(3, 128, 384), low(4, ROWS, 192),
        wide(ROWS, 768), wide(ROWS, 768), low(4, ROWS, 192),
        low(16, ROWS, 192), wide(4, ROWS, 768), low(4, ROWS, 768), wide(ROWS, 768), low(ROWS, 768),
    ]
    scratch += [
        low(4, ROWS, 192), low(4, 48, 192), low(4, ROWS, 192), low(48, 192),
        low(4, ROWS, 640), low(4, 48, 640), wide(3, TALL, TALL), low(3, ROWS, 768),
    ]
    scratch += [wide(4, 16, 256), wide(2, 16, 256), wide(16, 256), wide(16, 256), wide(4, 16, 256)]
    scratch += [low(3, 256, 256), low(3, 128, 256), low(3, 64, 256), low(3, 32, 256)]
    scratch += [wide(16, 384)] * 4 + [low(4, 3, 128, 256), wide(8, 16, 384)]
    scratch += [
        low(4, 2, 192, 768), low(12, 2, 192, 768), low(12, 192, 768), low(12, 192, 384),
        low(12, 4, 48, 384), low(12, 48, 384),
        low(ROWS, 768), wide(ROWS, 768), wide(12, 128, 384),
    ]
    sems = [dma((count, 5)), dma((count, 5)), dma((count + 1,)), dma((3,)), dma((3,))]
    for _ in range(4):
        sems += exchange_sems()
    sems += [
        dma((12, 2)), dma((12, 2)), dma((12,)), dma((12,)), dma((12,)), dma((12,)),
        dma((12, 3)), dma((12, 4)), dma((12, 3)), dma((12, 4)), dma((12,)), dma((12,)), dma((12,)),
    ]
    sems += [dma((8,)), dma((8,)), dma((12,)), dma((12,)), dma((12,)), dma((12,)), dma((5,))]
    return pl.pallas_call(
        layer_kernel,
        out_shape=[
            jax.ShapeDtypeStruct((ROWS, 768), BF16),
            jax.ShapeDtypeStruct((ROWS, 768), F32),
        ]
        + [
            jax.ShapeDtypeStruct((768, 768), BF16),
            jax.ShapeDtypeStruct((192, 3072), BF16),
            jax.ShapeDtypeStruct((768, 768), BF16),
            jax.ShapeDtypeStruct((16, 256), F32),
            jax.ShapeDtypeStruct((12, 128, 384), F32),
        ],
        in_specs=[vmem_spec()] * 13 + [any_spec()] * 8,
        out_specs=[any_spec()] * 5 + [vmem_spec(), any_spec()],
        scratch_shapes=scratch + sems,
        compiler_params=pltpu.CompilerParams(
            collective_id=1, has_side_effects=True, vmem_limit_bytes=62 * 2**20
        ),
        name="layer",
    )(tokens, segments, places, upstream, *vectors, *arrays, logits, noise)


def write_kernel(
    hidden, grad, mask, oh, oi, of, small,
    hidden_out, grad_out, mask_out, wq, wk, wv, wo, wi, wf, bi, *rest
):
    vectors, (vh, vg, vm, bh, bb, bf, fh, fi, ff, load, store) = (rest[:8], rest[8:])
    reads = [
        pltpu.make_async_copy(src, dst, load.at[i])
        for i, (src, dst) in enumerate(
            (
                (of, bf), (oi, bb), (oh, bh),
                (mask, vm.at[:, :, 0:384]), (grad, vg), (hidden, vh),
            )
        )
    ]
    for cp in reads:
        cp.start()
    writes = []

    def write(src, dst):
        cp = pltpu.make_async_copy(src, dst, store.at[len(writes)])
        cp.start()
        writes.append(cp)

    vm[:, :, 384:512] = jnp.zeros((12, 128, 128), F32)

    def widen(into, ref, first):
        def body(i, carry):
            at = pl.ds(pl.multiple_of(first + 32 * i, 32), 32)
            into[at, :] = ref[at, :].astype(F32)
            return carry

        lax.fori_loop(0, 6, body, 0)

    reads[0].wait()
    for i in range(4):
        widen(ff, bf, 192 * i)
        rows = pl.ds(192 * i, 192)
        write(ff.at[rows], wf.at[rows])
    reads[1].wait()
    widen(fi, bb, 0)
    write(fi, wi)
    reads[3].wait()
    write(vm, mask_out)
    reads[2].wait()
    for i, ref in enumerate((wq, wk, wv, wo)):
        widen(fh, bh, 192 * i)
        write(fh.at[pl.ds(192 * i, 192)], ref)
    reads[4].wait()
    write(vg, grad_out)
    reads[5].wait()
    write(vh, hidden_out)
    for i in range(8):
        vectors[i][...] = small[i : i + 1, 0:192].reshape(192)
    for i in range(4):
        bi[192 * i : 192 * i + 192] = small[8 + i : 9 + i, 0:192].reshape(192)
    for cp in writes:
        cp.wait()


def write_outputs(hidden, grad, mask, oh, oi, of, small):
    def out(shape, kind=F32):
        return jax.ShapeDtypeStruct(shape, kind)

    dma = pltpu.SemaphoreType.DMA
    return pl.pallas_call(
        write_kernel,
        out_shape=[
            out((ROWS, 768), BF16), out((ROWS, 768)), out((12, 128, 512)),
            out((192, 768)), out((192, 768)), out((192, 768)), out((192, 768)),
            out((192, 3072)), out((768, 768)), out((768,)),
        ]
        + [out((192,))] * 8,
        in_specs=[any_spec()] * 6 + [vmem_spec()],
        out_specs=[any_spec()] * 9 + [vmem_spec()] * 9,
        scratch_shapes=[
            pltpu.VMEM((ROWS, 768), BF16), pltpu.VMEM((ROWS, 768), F32),
            pltpu.VMEM((12, 128, 512), F32),
            pltpu.VMEM((768, 768), BF16), pltpu.VMEM((192, 3072), BF16),
            pltpu.VMEM((768, 768), BF16),
            pltpu.VMEM((768, 768), F32), pltpu.VMEM((192, 3072), F32),
            pltpu.VMEM((768, 768), F32),
            dma((6,)), dma((12,)),
        ],
        compiler_params=pltpu.CompilerParams(vmem_limit_bytes=62 * 2**20),
        name="write_outputs",
    )(hidden, grad, mask, oh, oi, of, small)


def block_device(
    hidden_in, segment_ids, doc_positions,
    w_query, w_key, w_value, w_out, b_query, b_value, b_out, ln1_gain, ln1_shift,
    w_inter, b_inter, w_final, b_final, ln2_gain, ln2_shift,
    mask_logits, mask_noise, grad_out,
):
    vectors = (
        b_query, b_value, b_out, ln1_gain, ln1_shift, b_final, ln2_gain, ln2_shift, b_inter
    )
    result, input_grad, oh, oi, of, small_sum, logit_grad = layer(
        hidden_in.reshape(ROWS, 768),
        segment_ids,
        doc_positions,
        grad_out.reshape(ROWS, 768),
        vectors,
        (w_query, w_key, w_value, w_out, w_inter, w_final),
        mask_logits,
        mask_noise,
    )
    hidden_out, grad_in, mask_grad, wq, wk, wv, wo, wi, wf, bi, *vecs = write_outputs(
        result, input_grad, logit_grad, oh, oi, of, small_sum
    )
    return (
        hidden_out.reshape(hidden_in.shape),
        grad_in.reshape(hidden_in.shape),
        wq,
        wk,
        wv,
        wo,
        vecs[0],
        vecs[1],
        vecs[2],
        vecs[3],
        vecs[4],
        wi,
        bi,
        wf,
        vecs[5],
        vecs[6],
        vecs[7],
        mask_grad,
    )


def on_device(ctx_size, fsdp_size, hidden_in, *rest):
    if (ctx_size, fsdp_size, hidden_in.shape) == (8, 4, (3, 64, 768)):
        return block_device(hidden_in, *rest)
    return general_device(hidden_in, *rest)


def solution(mesh):
    in_specs = (
        P("fsdp", "ctx", None),
        P("fsdp", "ctx"),
        P("fsdp", "ctx"),
        P("fsdp", None),
        P("fsdp", None),
        P("fsdp", None),
        P("fsdp", None),
        P("fsdp"),
        P("fsdp"),
        P("fsdp"),
        P("fsdp"),
        P("fsdp"),
        P("fsdp", None),
        P("fsdp"),
        P("fsdp", None),
        P("fsdp"),
        P("fsdp"),
        P("fsdp"),
        P(None, "fsdp", None),
        P(None, "fsdp", None),
        P("fsdp", "ctx", None),
    )
    out_specs = (
        P("fsdp", "ctx", None),
        P("fsdp", "ctx", None),
        P("fsdp", None),
        P("fsdp", None),
        P("fsdp", None),
        P("fsdp", None),
        P("fsdp"),
        P("fsdp"),
        P("fsdp"),
        P("fsdp"),
        P("fsdp"),
        P("fsdp", None),
        P("fsdp"),
        P("fsdp", None),
        P("fsdp"),
        P("fsdp"),
        P("fsdp"),
        P(None, "fsdp", None),
    )
    return jax.shard_map(
        functools.partial(on_device, mesh.shape["ctx"], mesh.shape["fsdp"]), mesh=mesh, in_specs=in_specs, out_specs=out_specs, check_vma=False
    )
```

```python
import functools

import jax
import jax.numpy as jnp
from jax import lax
from jax.experimental import pallas as pl
from jax.experimental.pallas import tpu as pltpu
from jax.sharding import PartitionSpec as P

H = 12
HD = 64
MSPAN = 512


NEGATIVE = -1e30
EPSILON = 1e-12


def layer_norm(hidden, gain_row, shift_row):
    average = jnp.mean(hidden, axis=-1, keepdims=True)
    centered = hidden - average
    variance = jnp.mean(centered * centered, axis=-1, keepdims=True)
    return centered * lax.rsqrt(variance + EPSILON) * gain_row + shift_row


def exact_gelu(inner_act):
    return jax.nn.gelu(inner_act, approximate=False)


def left_product(first_op, second_op):
    return lax.dot_general(
        first_op, second_op, (((0,), (0,)), ((), ())), preferred_element_type=jnp.float32
    )


def right_product(first_op, second_op):
    return lax.dot_general(
        first_op, second_op, (((1,), (1,)), ((), ())), preferred_element_type=jnp.float32
    )


def one_hot_rows(slot_values, width):
    return (slot_values[:, None] == jnp.arange(width, dtype=jnp.int32)[None, :]).astype(
        jnp.bfloat16
    )


def block_scores(queries, key_part, seg_local, seg_part, bias_part):
    key_heads = key_part.reshape(key_part.shape[0], H, HD)
    raw_scores = (
        jnp.einsum("shd,nhd->hsn", queries, key_heads, preferred_element_type=jnp.float32) * 0.125
    )
    same_doc = seg_local[:, None] == seg_part[None, :]
    return jnp.where(same_doc[None], raw_scores + bias_part.astype(jnp.float32), NEGATIVE)


def split_blocks(array_in, block_size):
    return array_in.reshape((array_in.shape[0] // block_size, block_size) + array_in.shape[1:])


def block_length():
    return 512


def make_blocks(full_keys, full_values, full_segment, full_slot):
    block_size = block_length()
    return (
        split_blocks(full_keys, block_size),
        split_blocks(full_values, block_size),
        split_blocks(full_segment, block_size),
        split_blocks(full_slot, block_size),
    )


def row_statistics(queries, seg_local, table_rows, blocks):
    rows = queries.shape[0]

    def advance(state_carry, key_block):
        key_part, value_part, seg_part, slot_part = key_block

        def compute(pair):
            row_top, row_total = pair
            bias_part = jnp.einsum(
                "hsa,na->hsn",
                table_rows,
                one_hot_rows(slot_part, MSPAN),
                preferred_element_type=jnp.float32,
            ).astype(jnp.bfloat16)
            scores = block_scores(queries, key_part, seg_local, seg_part, bias_part)
            new_top = jnp.maximum(row_top, jnp.max(scores, axis=-1))
            row_total = row_total * jnp.exp(row_top - new_top) + jnp.sum(
                jnp.exp(scores - new_top[..., None]), axis=-1
            )
            return ((new_top, row_total), bias_part)

        return compute(state_carry)

    start_state = (jnp.full((H, rows), NEGATIVE, jnp.float32), jnp.zeros((H, rows), jnp.float32))
    (row_top, row_total), bias_blocks = lax.scan(advance, start_state, blocks)
    return (row_top + jnp.log(row_total), bias_blocks)


def attention_output(queries, seg_local, blocks, bias_blocks, log_total):
    rows = queries.shape[0]

    def advance(accumulated, items):
        (key_part, value_part, seg_part, slot_part), bias_part = items

        def compute(current):
            scores = block_scores(queries, key_part, seg_local, seg_part, bias_part)
            soft_weights = jnp.exp(scores - log_total[..., None]).astype(jnp.bfloat16)
            value_heads = value_part.reshape(value_part.shape[0], H, HD)
            return current + jnp.einsum(
                "hsn,nhd->shd", soft_weights, value_heads, preferred_element_type=jnp.float32
            )

        return (compute(accumulated), None)

    context, _ = lax.scan(advance, jnp.zeros((rows, H, HD), jnp.float32), (blocks, bias_blocks))
    return context


def attention_backward(queries, seg_local, blocks, bias_blocks, log_total, context_grad, row_delta):
    rows = queries.shape[0]

    def advance(state_carry, items):
        (key_part, value_part, seg_part, slot_part), bias_part = items
        key_count = key_part.shape[0]

        def compute(operand):
            query_acc, slot_acc = operand
            scores = block_scores(queries, key_part, seg_local, seg_part, bias_part)
            soft_float = jnp.exp(scores - log_total[..., None])
            key_heads = key_part.reshape(key_count, H, HD)
            value_heads = value_part.reshape(key_count, H, HD)
            weight_grad = jnp.einsum(
                "shd,nhd->hsn", context_grad, value_heads, preferred_element_type=jnp.float32
            )
            score_grad = (soft_float * (weight_grad - row_delta[..., None])).astype(jnp.bfloat16)
            query_acc = (
                query_acc
                + jnp.einsum(
                    "hsn,nhd->shd", score_grad, key_heads, preferred_element_type=jnp.float32
                )
                * 0.125
            )
            slot_acc = slot_acc + jnp.einsum(
                "hsn,na->hsa",
                score_grad,
                one_hot_rows(slot_part, MSPAN),
                preferred_element_type=jnp.float32,
            )
            key_block_grad = (
                jnp.einsum("hsn,shd->nhd", score_grad, queries, preferred_element_type=jnp.float32)
                * 0.125
            )
            value_block_grad = jnp.einsum(
                "hsn,shd->nhd",
                soft_float.astype(jnp.bfloat16),
                context_grad,
                preferred_element_type=jnp.float32,
            )
            return ((query_acc, slot_acc), (key_block_grad, value_block_grad))

        return compute(state_carry)

    start_state = (jnp.zeros((rows, H, HD), jnp.float32), jnp.zeros((H, rows, MSPAN), jnp.float32))
    (query_acc, slot_acc), block_grads = lax.scan(advance, start_state, (blocks, bias_blocks))
    key_grads, value_grads = block_grads
    full_len = key_grads.shape[0] * key_grads.shape[1]
    return (
        query_acc,
        slot_acc,
        key_grads.reshape(full_len, H * HD),
        value_grads.reshape(full_len, H * HD),
    )


def general_device(
    hidden_in,
    segment_ids,
    doc_positions,
    w_query,
    w_key,
    w_value,
    w_out,
    b_query,
    b_value,
    b_out,
    ln1_gain,
    ln1_shift,
    w_inter,
    b_inter,
    w_final,
    b_final,
    ln2_gain,
    ln2_shift,
    mask_logits,
    mask_noise,
    grad_out,
):
    table_part = jax.nn.log_sigmoid(2.0 * (mask_logits + mask_noise)).astype(jnp.bfloat16)
    (
        wq_full,
        wk_full,
        wv_full,
        wo_full,
        wi_full,
        wf_full,
        bq_full,
        bv_full,
        bo_full,
        bi_full,
        bf_full,
        gain_one,
        shift_one,
        gain_two,
        shift_two,
        table_full,
    ) = (
        lax.all_gather(w_query, "fsdp", axis=0, tiled=True),
        lax.all_gather(w_key, "fsdp", axis=0, tiled=True),
        lax.all_gather(w_value, "fsdp", axis=0, tiled=True),
        lax.all_gather(w_out, "fsdp", axis=0, tiled=True),
        lax.all_gather(w_inter, "fsdp", axis=0, tiled=True),
        lax.all_gather(w_final, "fsdp", axis=0, tiled=True),
        lax.all_gather(b_query, "fsdp", axis=0, tiled=True),
        lax.all_gather(b_value, "fsdp", axis=0, tiled=True),
        lax.all_gather(b_out, "fsdp", axis=0, tiled=True),
        lax.all_gather(b_inter, "fsdp", axis=0, tiled=True),
        lax.all_gather(b_final, "fsdp", axis=0, tiled=True),
        lax.all_gather(ln1_gain, "fsdp", axis=0, tiled=True),
        lax.all_gather(ln1_shift, "fsdp", axis=0, tiled=True),
        lax.all_gather(ln2_gain, "fsdp", axis=0, tiled=True),
        lax.all_gather(ln2_shift, "fsdp", axis=0, tiled=True),
        lax.all_gather(table_part, "fsdp", axis=1, tiled=True),
    )
    bq_full, bv_full, bo_full = (
        bq_full.astype(jnp.float32),
        bv_full.astype(jnp.float32),
        bo_full.astype(jnp.float32),
    )
    bi_full, bf_full = (bi_full.astype(jnp.float32), bf_full.astype(jnp.float32))
    gain_one, shift_one = (gain_one.astype(jnp.float32), shift_one.astype(jnp.float32))
    gain_two, shift_two = (gain_two.astype(jnp.float32), shift_two.astype(jnp.float32))
    micro_count = hidden_in.shape[0]
    rows = hidden_in.shape[1]
    saved = []
    outputs_list = []
    for micro_batch in range(micro_count):
        tokens = hidden_in[micro_batch]
        seg_local = segment_ids[micro_batch]
        slot_local = doc_positions[micro_batch] % MSPAN
        queries_flat = (
            jnp.dot(tokens, wq_full, preferred_element_type=jnp.float32) + bq_full
        ).astype(jnp.bfloat16)
        keys_local = jnp.dot(tokens, wk_full, preferred_element_type=jnp.float32).astype(
            jnp.bfloat16
        )
        values_local = (
            jnp.dot(tokens, wv_full, preferred_element_type=jnp.float32) + bv_full
        ).astype(jnp.bfloat16)
        gathered = (
            lax.all_gather(keys_local, "ctx", axis=0, tiled=True),
            lax.all_gather(values_local, "ctx", axis=0, tiled=True),
            lax.all_gather(seg_local, "ctx", axis=0, tiled=True),
            lax.all_gather(slot_local, "ctx", axis=0, tiled=True),
        )
        blocks = make_blocks(*gathered)
        queries = queries_flat.reshape(rows, H, HD)
        table_rows = table_full[:, slot_local, :]
        log_total, bias_blocks = row_statistics(queries, seg_local, table_rows, blocks)
        context = attention_output(queries, seg_local, blocks, bias_blocks, log_total)
        context_low = context.reshape(rows, H * HD).astype(jnp.bfloat16)
        attn_out = jnp.dot(context_low, wo_full, preferred_element_type=jnp.float32) + bo_full
        first_norm, norm_one_back = jax.vjp(
            layer_norm, tokens.astype(jnp.float32) + attn_out, gain_one, shift_one
        )
        first_low = first_norm.astype(jnp.bfloat16)
        inner_act = jnp.dot(first_low, wi_full, preferred_element_type=jnp.float32) + bi_full
        active, gelu_back = jax.vjp(exact_gelu, inner_act)
        active_low = active.astype(jnp.bfloat16)
        ffn_out = jnp.dot(active_low, wf_full, preferred_element_type=jnp.float32) + bf_full
        result, norm_two_back = jax.vjp(layer_norm, first_norm + ffn_out, gain_two, shift_two)
        outputs_list.append(result.astype(jnp.bfloat16))
        kept_blocks = blocks
        saved.append(
            (
                tokens,
                seg_local,
                slot_local,
                queries,
                keys_local,
                values_local,
                log_total,
                bias_blocks,
                context,
                context_low,
                first_low,
                active_low,
                norm_one_back,
                gelu_back,
                norm_two_back,
                kept_blocks,
            )
        )
    zeros_square = jnp.zeros((H * HD, H * HD), jnp.float32)
    wq_grad, wk_grad, wv_grad, wo_grad = (zeros_square, zeros_square, zeros_square, zeros_square)
    wi_grad = jnp.zeros(wi_full.shape, jnp.float32)
    wf_grad = jnp.zeros(wf_full.shape, jnp.float32)
    zeros_row = jnp.zeros((H * HD,), jnp.float32)
    bq_grad, bv_grad, bo_grad, bf_grad = (zeros_row, zeros_row, zeros_row, zeros_row)
    gain_one_grad, shift_one_grad, gain_two_grad, shift_two_grad = (
        zeros_row,
        zeros_row,
        zeros_row,
        zeros_row,
    )
    bi_grad = jnp.zeros(bi_full.shape, jnp.float32)
    table_grad = jnp.zeros(table_full.shape, jnp.float32)
    input_grads = []
    for micro_batch in range(micro_count):
        (
            tokens,
            seg_local,
            slot_local,
            queries,
            keys_local,
            values_local,
            log_total,
            bias_blocks,
            context,
            context_low,
            first_low,
            active_low,
            norm_one_back,
            gelu_back,
            norm_two_back,
            kept_blocks,
        ) = saved[micro_batch]
        upstream = grad_out[micro_batch].astype(jnp.float32)
        sum_grad, gain_part, shift_part = norm_two_back(upstream)
        gain_two_grad = gain_two_grad + gain_part
        shift_two_grad = shift_two_grad + shift_part
        ffn_grad = sum_grad.astype(jnp.bfloat16)
        bf_grad = bf_grad + jnp.sum(ffn_grad.astype(jnp.float32), axis=0)
        wf_grad = wf_grad + left_product(active_low, ffn_grad)
        active_grad = right_product(ffn_grad, wf_full).astype(jnp.bfloat16)
        (inner_float,) = gelu_back(active_grad.astype(jnp.float32))
        inner_grad = inner_float.astype(jnp.bfloat16)
        bi_grad = bi_grad + jnp.sum(inner_grad.astype(jnp.float32), axis=0)
        wi_grad = wi_grad + left_product(first_low, inner_grad)
        first_grad = sum_grad + right_product(inner_grad, wi_full)
        norm_grad, gain_part, shift_part = norm_one_back(first_grad)
        gain_one_grad = gain_one_grad + gain_part
        shift_one_grad = shift_one_grad + shift_part
        attn_grad = norm_grad.astype(jnp.bfloat16)
        bo_grad = bo_grad + jnp.sum(attn_grad.astype(jnp.float32), axis=0)
        wo_grad = wo_grad + left_product(context_low, attn_grad)
        context_grad_flat = right_product(attn_grad, wo_full).astype(jnp.bfloat16)
        context_grad = context_grad_flat.reshape(rows, H, HD)
        row_delta = jnp.einsum("shd,shd->hs", context_grad.astype(jnp.float32), context)
        blocks = kept_blocks
        query_acc, slot_acc, key_full_grad, value_full_grad = attention_backward(
            queries, seg_local, blocks, bias_blocks, log_total, context_grad, row_delta
        )
        key_share, value_share = (
            lax.psum_scatter(
                key_full_grad.astype(jnp.bfloat16), "ctx", scatter_dimension=0, tiled=True
            ).astype(jnp.float32),
            lax.psum_scatter(
                value_full_grad.astype(jnp.bfloat16), "ctx", scatter_dimension=0, tiled=True
            ).astype(jnp.float32),
        )
        table_grad = table_grad.at[:, slot_local, :].add(slot_acc)
        query_low = query_acc.reshape(rows, H * HD).astype(jnp.bfloat16)
        key_low = key_share.astype(jnp.bfloat16)
        value_low = value_share.astype(jnp.bfloat16)
        bq_grad = bq_grad + jnp.sum(query_low.astype(jnp.float32), axis=0)
        bv_grad = bv_grad + jnp.sum(value_low.astype(jnp.float32), axis=0)
        wq_grad = wq_grad + left_product(tokens, query_low)
        wk_grad = wk_grad + left_product(tokens, key_low)
        wv_grad = wv_grad + left_product(tokens, value_low)
        input_grads.append(
            norm_grad
            + right_product(query_low, wq_full)
            + right_product(key_low, wk_full)
            + right_product(value_low, wv_full)
        )
    shares = (
        lax.psum_scatter(
            wq_grad.astype(jnp.bfloat16), "fsdp", scatter_dimension=0, tiled=True
        ).astype(jnp.float32),
        lax.psum_scatter(
            wk_grad.astype(jnp.bfloat16), "fsdp", scatter_dimension=0, tiled=True
        ).astype(jnp.float32),
        lax.psum_scatter(
            wv_grad.astype(jnp.bfloat16), "fsdp", scatter_dimension=0, tiled=True
        ).astype(jnp.float32),
        lax.psum_scatter(
            wo_grad.astype(jnp.bfloat16), "fsdp", scatter_dimension=0, tiled=True
        ).astype(jnp.float32),
        lax.psum_scatter(
            bq_grad.astype(jnp.bfloat16), "fsdp", scatter_dimension=0, tiled=True
        ).astype(jnp.float32),
        lax.psum_scatter(
            bv_grad.astype(jnp.bfloat16), "fsdp", scatter_dimension=0, tiled=True
        ).astype(jnp.float32),
        lax.psum_scatter(
            bo_grad.astype(jnp.bfloat16), "fsdp", scatter_dimension=0, tiled=True
        ).astype(jnp.float32),
        lax.psum_scatter(
            gain_one_grad.astype(jnp.bfloat16), "fsdp", scatter_dimension=0, tiled=True
        ).astype(jnp.float32),
        lax.psum_scatter(
            shift_one_grad.astype(jnp.bfloat16), "fsdp", scatter_dimension=0, tiled=True
        ).astype(jnp.float32),
        lax.psum_scatter(
            wi_grad.astype(jnp.bfloat16), "fsdp", scatter_dimension=0, tiled=True
        ).astype(jnp.float32),
        lax.psum_scatter(
            bi_grad.astype(jnp.bfloat16), "fsdp", scatter_dimension=0, tiled=True
        ).astype(jnp.float32),
        lax.psum_scatter(
            wf_grad.astype(jnp.bfloat16), "fsdp", scatter_dimension=0, tiled=True
        ).astype(jnp.float32),
        lax.psum_scatter(
            bf_grad.astype(jnp.bfloat16), "fsdp", scatter_dimension=0, tiled=True
        ).astype(jnp.float32),
        lax.psum_scatter(
            gain_two_grad.astype(jnp.bfloat16), "fsdp", scatter_dimension=0, tiled=True
        ).astype(jnp.float32),
        lax.psum_scatter(
            shift_two_grad.astype(jnp.bfloat16), "fsdp", scatter_dimension=0, tiled=True
        ).astype(jnp.float32),
        lax.psum_scatter(
            table_grad.astype(jnp.bfloat16), "fsdp", scatter_dimension=1, tiled=True
        ).astype(jnp.float32),
    )
    totals = (
        lax.psum(shares[0].astype(jnp.bfloat16), "ctx").astype(jnp.float32),
        lax.psum(shares[1].astype(jnp.bfloat16), "ctx").astype(jnp.float32),
        lax.psum(shares[2].astype(jnp.bfloat16), "ctx").astype(jnp.float32),
        lax.psum(shares[3].astype(jnp.bfloat16), "ctx").astype(jnp.float32),
        lax.psum(shares[4].astype(jnp.bfloat16), "ctx").astype(jnp.float32),
        lax.psum(shares[5].astype(jnp.bfloat16), "ctx").astype(jnp.float32),
        lax.psum(shares[6].astype(jnp.bfloat16), "ctx").astype(jnp.float32),
        lax.psum(shares[7].astype(jnp.bfloat16), "ctx").astype(jnp.float32),
        lax.psum(shares[8].astype(jnp.bfloat16), "ctx").astype(jnp.float32),
        lax.psum(shares[9].astype(jnp.bfloat16), "ctx").astype(jnp.float32),
        lax.psum(shares[10].astype(jnp.bfloat16), "ctx").astype(jnp.float32),
        lax.psum(shares[11].astype(jnp.bfloat16), "ctx").astype(jnp.float32),
        lax.psum(shares[12].astype(jnp.bfloat16), "ctx").astype(jnp.float32),
        lax.psum(shares[13].astype(jnp.bfloat16), "ctx").astype(jnp.float32),
        lax.psum(shares[14].astype(jnp.bfloat16), "ctx").astype(jnp.float32),
        lax.psum(shares[15].astype(jnp.bfloat16), "ctx").astype(jnp.float32),
    )
    (
        wq_total,
        wk_total,
        wv_total,
        wo_total,
        bq_total,
        bv_total,
        bo_total,
        gain_one_total,
        shift_one_total,
        wi_total,
        bi_total,
        wf_total,
        bf_total,
        gain_two_total,
        shift_two_total,
        table_total,
    ) = totals
    logit_grad = table_total * 2.0 * jax.nn.sigmoid(-2.0 * (mask_logits + mask_noise))
    return (
        jnp.stack(outputs_list),
        jnp.stack(input_grads),
        wq_total,
        wk_total,
        wv_total,
        wo_total,
        bq_total,
        bv_total,
        bo_total,
        gain_one_total,
        shift_one_total,
        wi_total,
        bi_total,
        wf_total,
        bf_total,
        gain_two_total,
        shift_two_total,
        logit_grad,
    )


MESH = pl.DeviceIdType.MESH
BF16 = jnp.bfloat16
F32 = jnp.float32
ROWS = 192
TALL = 272


ROOT_HALF = 0.7071067811865476
ROOT_TWO_PI = 0.3989422804014327


def place():
    c = lax.axis_index("ctx")
    f = lax.axis_index("fsdp")
    return (c // 2, c % 2, f // 2, f % 2)


def device(z, x, y, k):
    return {"ctx": z * 2 + x, "fsdp": y * 2 + k}


def send(src, dst, send_sem, recv_sem, target):
    return pltpu.make_async_remote_copy(
        src_ref=src,
        dst_ref=dst,
        send_sem=send_sem,
        recv_sem=recv_sem,
        device_id=target,
        device_id_type=MESH,
    )


def meet(targets):
    barrier = pltpu.get_barrier_semaphore()
    for target in targets:
        pl.semaphore_signal(barrier, inc=1, device_id=target, device_id_type=MESH)
    pl.semaphore_wait(barrier, len(targets))


def any_spec():
    return pl.BlockSpec(memory_space=pl.ANY)


def vmem_spec():
    return pl.BlockSpec(memory_space=pltpu.VMEM)


def gather_pieces():
    pieces = [(array, 0, 192, 0, 768, "x") for array in range(4)]
    pieces.append((6, 0, 0, 0, 0, None))
    for part, axis in enumerate("xz"):
        pieces.append((4, 0, 192, 1536 * part, 1536, axis))
    for part, axis in enumerate("xzxz"):
        pieces.append((5, 192 * part, 192, 0, 768, axis))
    return pieces


def gather_plan(ins, outs, small, small_out, sems):
    ss, rs, ls, ss_small, rs_small = sems
    z, x, y, k = place()
    mine = y * 2 + k
    over = (1 - y) * 2 + k
    core = device(z, x, y, 1 - k)
    ynb = device(z, x, 1 - y, k)
    diag = device(z, x, 1 - y, 1 - k)
    xnb = device(z, 1 - x, y, k)

    def source(piece, half):
        a, r0, rn, c0, cn, _ = piece
        if a == 6:
            return ins[a]
        if half is None:
            return ins[a].at[pl.ds(r0, rn), pl.ds(c0, cn)]
        return ins[a].at[pl.ds(r0 + (rn // 2) * half, rn // 2), pl.ds(c0, cn)]

    def target(piece, owner, half):
        a, r0, rn, c0, cn, _ = piece
        if a == 6:
            return outs[a].at[:, pl.ds(128 * owner, 128)]
        base = ins[a].shape[0] * owner + r0
        if half is None:
            return outs[a].at[pl.ds(base, rn), pl.ds(c0, cn)]
        return outs[a].at[pl.ds(base + (rn // 2) * half, rn // 2), pl.ds(c0, cn)]

    plan = []
    znb = device(z + 1 - 2 * lax.rem(z, 2), x, y, k)
    for n, piece in enumerate(gather_pieces()):
        axis = piece[5]
        part = {None: None, "x": x, "z": lax.rem(z, 2)}[axis]
        whole = source(piece, None)
        kept = target(piece, mine, None)
        here = target(piece, over, part)
        copies = {
            "own": pltpu.make_async_copy(whole, kept, ls.at[n]),
            "core": send(whole, kept, ss.at[n, 0], rs.at[n, 0], core),
            "y": send(source(piece, part), target(piece, mine, part), ss.at[n, 1], rs.at[n, 1], ynb),
            "core_y": send(here, here, ss.at[n, 3], rs.at[n, 3], core),
        }
        if axis is not None:
            there = target(piece, over, 1 - part)
            copies["x"] = send(
                here, here, ss.at[n, 2], rs.at[n, 2], xnb if axis == "x" else znb
            )
            copies["core_x"] = send(there, there, ss.at[n, 4], rs.at[n, 4], core)
        plan.append(copies)
    rows = small_out.at[mine]
    smalls = [
        send(small, rows, ss_small.at[i], rs_small.at[i], peer)
        for i, peer in enumerate((core, ynb, diag))
    ]
    own_small = pltpu.make_async_copy(small, rows, ls.at[len(plan)])
    return (plan, smalls, own_small)


def forward_y(copies):
    copies["y"].wait_recv()
    if "x" in copies:
        copies["x"].start()
    copies["core_y"].start()


def forward_x(copies):
    if "x" in copies:
        copies["x"].wait_recv()
        copies["core_x"].start()


def arrive(copies):
    copies["own"].wait()
    for name in ("core", "core_y", "core_x"):
        if name in copies:
            copies[name].wait_recv()


def settle(copies):
    for name, cp in copies.items():
        if name != "own":
            cp.wait_send()


def ctx_peers():
    c = lax.axis_index("ctx")
    return [{"ctx": lax.rem(c + i, 8)} for i in range(1, 8)]


class Exchange:
    def __init__(self, main, main_in, extra, extra_in, sems, home):
        self.main, self.main_in, self.extra, self.extra_in = (main, main_in, extra, extra_in)
        self.ms, self.mr, self.es, self.er, self.ls = sems
        self.c = lax.axis_index("ctx")
        self.group, self.me = (self.c // 4, lax.rem(self.c, 4))
        self.home = home

    def one(self, j, slot):
        return send(
            self.main.at[j],
            self.main_in.at[slot],
            self.ms.at[j],
            self.mr.at[slot],
            {"ctx": 4 * self.group + j},
        )

    def local(self, j):
        return pltpu.make_async_copy(self.main.at[j], self.main_in.at[j], self.ls)

    def side(self, j):
        if self.home:
            return send(
                self.extra, self.extra_in.at[self.me], self.es.at[0], self.er.at[self.me], {"ctx": 4}
            )
        return send(self.extra.at[j], self.extra_in, self.es.at[j], self.er.at[0], {"ctx": j})

    def start(self):
        if self.home:

            @pl.when(self.group == 0)
            def _():
                self.side(0).start()

        for j in range(4):

            @pl.when(self.me != j)
            def _():
                self.one(j, self.me).start()

            @pl.when(self.me == j)
            def _():
                self.local(j).start()

        if not self.home:

            @pl.when(self.c == 4)
            def _():
                for j in range(4):
                    self.side(j).start()

    def wait(self):
        for j in range(4):

            @pl.when(self.me != j)
            def _():
                self.one(0, j).wait_recv()

            @pl.when(self.me == j)
            def _():
                self.local(j).wait()

        if self.home:

            @pl.when(self.c == 4)
            def _():
                for j in range(4):
                    send(
                        self.extra, self.extra_in.at[j], self.es.at[0], self.er.at[j], {"ctx": 4}
                    ).wait_recv()

        else:

            @pl.when(self.group == 0)
            def _():
                self.side(0).wait_recv()

    def settle(self):
        for j in range(4):

            @pl.when(self.me != j)
            def _():
                self.one(j, self.me).wait_send()

        if self.home:

            @pl.when(self.group == 0)
            def _():
                self.side(0).wait_send()

        else:

            @pl.when(self.c == 4)
            def _():
                for j in range(4):
                    self.side(j).wait_send()


def exchange_sems():
    dma = pltpu.SemaphoreType.DMA
    return [dma((4,)), dma((4,)), dma((4,)), dma((4,)), dma]


def dot_nn(a, b):
    return lax.dot_general(a, b, (((1,), (0,)), ((), ())), preferred_element_type=F32)


def dot_nt(a, b):
    return lax.dot_general(a, b, (((1,), (1,)), ((), ())), preferred_element_type=F32)


def dot_tn(a, b):
    return lax.dot_general(a, b, (((0,), (0,)), ((), ())), preferred_element_type=F32)


def own_rows(main, s, lo, width):
    return main[:, pl.ds(64 * s, 64), lo : lo + width].reshape(256, width)


def place_masks(main, s):
    marks = own_rows(main, s, 576, 64).astype(F32)
    segment = marks[:, 0:1]
    slot = marks[:, 1:2]
    valid = jnp.where(segment == 0.0, 0.0, 1.0)
    lanes = lax.broadcasted_iota(jnp.int32, (256, 128), 1).astype(F32)
    seg_hot = jnp.where((lanes == segment) & (valid > 0.0), 1.0, 0.0).astype(BF16)
    wide = lax.broadcasted_iota(jnp.int32, (256, 256), 1).astype(F32)
    slot_hot = jnp.where((wide == slot) & (valid > 0.0), 1.0, 0.0).astype(BF16)
    return (slot_hot, dot_nt(seg_hot, seg_hot) > 0.5, valid)


class BlockSums:
    def __init__(self, bufs, sems, blocks):
        self.blocks = blocks
        self.st, self.r1, self.r2, self.r3, self.r4, self.total = bufs
        self.p1, self.q1, self.p2, self.q2, self.p3, self.q3, self.p4, self.q4 = sems[:8]
        self.p5, self.q5, self.p6, self.q6, self.kept = sems[8:]
        z, x, y, k = place()
        self.z, self.x, self.y, self.k = (z, x, y, k)
        self.core = device(z, x, y, 1 - k)
        self.ynb = device(z, x, 1 - y, k)
        self.xnb = device(z, 1 - x, y, k)
        self.peers = [lax.rem(z + i, 4) for i in (1, 2, 3)]
        self.columns = pl.ds(pl.multiple_of(384 * x, 128), 384)
        self.others = pl.ds(pl.multiple_of(384 * (1 - x), 128), 384)

    def zdev(self, zz):
        return device(zz, self.x, self.y, self.k)

    def to_core(self, n, yy):
        slot = n % 4
        return send(
            self.st.at[slot, yy], self.r1.at[n, yy], self.p1.at[n, yy], self.q1.at[n, yy], self.core
        )

    def to_y(self, n):
        return send(
            self.r1.at[n, 1 - self.y], self.r2.at[n], self.p2.at[n], self.q2.at[n], self.ynb
        )

    def sum_x(self, n):
        return send(
            self.r2.at[n, :, self.others], self.r3.at[n], self.p3.at[n], self.q3.at[n], self.xnb
        )

    def sum_z(self, n, i):
        zz = self.peers[i]
        return send(
            self.r3.at[n, pl.ds(48 * zz, 48)],
            self.r4.at[n, self.z],
            self.p4.at[n, i],
            self.q4.at[n, self.z],
            self.zdev(zz),
        )

    def view(self, n, rows):
        ref, row, column = self.blocks[n if isinstance(n, int) else 0]
        if rows == slice(None):
            rows = pl.ds(row, 192)
        else:
            rows = pl.ds(rows.start + row, rows.size)
        return ref.at[rows, pl.ds(pl.multiple_of(column + 384 * self.x, 128), 384)]

    def spread_z(self, n, i, owner):
        here = self.view(n, pl.ds(48 * owner, 48))
        return send(
            self.total.at[n], here, self.p5.at[n, i], self.q5.at[n, owner], self.zdev(self.peers[i])
        )

    def keep(self, n):
        here = self.view(n, pl.ds(48 * self.z, 48))
        return pltpu.make_async_copy(self.total.at[n], here, self.kept.at[n])

    def spread_x(self, n):
        here = self.view(n, slice(None))
        return send(here, here, self.p6.at[n], self.q6.at[n], self.xnb)

    def one(self, n, partial):
        for yy in range(2):
            self.st[n % 4, yy] = partial(2 * yy + 1 - self.k).astype(BF16)
            self.to_core(n, yy).start()

    def two(self, n, partial):
        for yy in range(2):
            own = partial(2 * yy + self.k)
            self.to_core(n, yy).wait_recv()
            self.r1[n, yy] = (own + self.r1[n, yy].astype(F32)).astype(BF16)
        self.to_y(n).start()

    def three(self, n):
        self.to_y(n).wait_recv()

        def body(i, carry):
            at = pl.ds(pl.multiple_of(i * 48, 48), 48)
            self.r2[n, at, :] = self.r2[n, at, :] + self.r1[n, self.y, at, :]
            return carry

        lax.fori_loop(0, 4, body, 0)
        self.sum_x(n).start()

    def four(self, n):
        self.sum_x(n).wait_recv()

        def body(i, carry):
            at = pl.ds(pl.multiple_of(i * 48, 48), 48)
            self.r3[n, at, :] = self.r3[n, at, :] + self.r2[n, at, self.columns]
            return carry

        lax.fori_loop(0, 4, body, 0)
        for i in range(3):
            self.sum_z(n, i).start()

    def five(self, n):
        for i in range(3):
            zz = self.peers[i]
            send(
                self.r3.at[n, pl.ds(0, 48)],
                self.r4.at[n, zz],
                self.p4.at[n, 0],
                self.q4.at[n, zz],
                self.core,
            ).wait_recv()
        rows = pl.ds(pl.multiple_of(48 * self.z, 16), 48)
        total = self.r3[n, rows, :].astype(F32)
        for i in range(3):
            total = total + self.r4[n, self.peers[i]].astype(F32)
        self.total[n] = total.astype(BF16)
        self.keep(n).start()
        for i in range(3):
            self.spread_z(n, i, self.z).start()

    def six(self, n):
        self.keep(n).wait()
        for i in range(3):
            self.spread_z(n, i, self.peers[i]).wait_recv()
        self.spread_x(n).start()

    def seven(self, n):
        self.spread_x(n).wait_recv()

    def settle(self):
        def body(n, carry):
            self.to_y(n).wait_send()
            self.sum_x(n).wait_send()
            self.spread_x(n).wait_send()
            for i in range(3):
                self.sum_z(n, i).wait_send()
                self.spread_z(n, i, self.z).wait_send()
            return carry

        lax.fori_loop(0, 12, body, 0)
        for n in range(8, 12):
            for yy in range(2):
                self.to_core(n, yy).wait_send()


def layer_kernel(
    tokens, segments, places, upstream, *vectors_and_more
):
    vectors, rest = (vectors_and_more[:9], vectors_and_more[9:])
    layer_body(tokens, segments, places, upstream, vectors, *rest)


def layer_body(
    tokens, segments, places, upstream, vectors,
    wq_in, wk_in, wv_in, wo_in, wi_in, wf_in, logits_in, noise_in,
    hidden_out, input_grad, oh, oi, of, small_out, mask_out,
    wq, wk, wv, wo, wi, wf, table, small,
    main, extra, main_send, extra_send, probs, ctx_send, ctx_extra, ctx4, ctx_extra_in,
    small_in, marks, active, table_in, tokens4, first_hat, first_norm, first4, active16, slope, inner, sum_grad, low_grad,
    grad4, grad_extra, grad_in, grad_extra_in, main_in, extra_in, table_grad, lows,
    v0, v1, v2, v3, v4, t0, t1, t2, t3, e0, e1, e2, e3, table_out, edge_out,
    st, r1, r2, r3, r4, total, hidden_low, input_sum, mask_sum, *sems
):
    z, x, y, k = place()
    c = 2 * z + x
    group = c // 4
    core = device(z, x, y, 1 - k)
    ynb = device(z, x, 1 - y, k)
    xnb = device(z, 1 - x, y, k)
    twin = device(lax.rem(z + 2, 4), x, y, k)
    zdev = [device(lax.rem(z + i, 4), x, y, k) for i in (1, 2, 3)]
    gather_sems, ex = (sems[:5], [sems[5 + 5 * i : 10 + 5 * i] for i in range(4)])
    sum_sems, (ps, qs, pt, qt, pe, qe, load) = (sems[25:38], sems[38:45])
    heads = pl.ds(3 * lax.rem(c, 4), 3)
    near = pl.ds(0, 384)
    loads = [
        pltpu.make_async_copy(
            logits_in.at[heads, :, near], slope.at[0:3, 0:128, 0:384], load.at[0]
        ),
        pltpu.make_async_copy(
            noise_in.at[heads, :, near], slope.at[0:3, 0:128, 384:768], load.at[1]
        ),
    ]
    for cp in loads:
        cp.start()
    meet(ctx_peers() + [core, ynb, device(z, x, 1 - y, 1 - k)])

    for i in range(8):
        small_in[i : i + 1, 0:192] = vectors[i][...].astype(F32).reshape(1, 192)
    for i in range(4):
        small_in[8 + i : 9 + i, 0:192] = (
            vectors[8][192 * i : 192 * i + 192].astype(F32).reshape(1, 192)
        )
    plan, smalls, own_small = gather_plan(
        (wq_in, wk_in, wv_in, wo_in, wi_in, wf_in, table_in),
        (wq, wk, wv, wo, wi, wf, table),
        small_in,
        small,
        gather_sems,
    )
    for cp in smalls + [own_small]:
        cp.start()
    for name in ("y", "core", "own"):
        for n in range(3):
            plan[n][name].start()
    for cp in loads:
        cp.wait()
    for h in range(3):
        doubled = 2.0 * (slope[h, 0:128, 0:384] + slope[h, 0:128, 384:768])
        table_in[h] = (
            jnp.minimum(doubled, 0.0) - jnp.log1p(jnp.exp(-jnp.abs(doubled)))
        ).astype(BF16)
    for n in range(3, len(plan)):
        for name in ("y", "core", "own"):
            plan[n][name].start()
    forward_y(plan[0])
    forward_y(plan[1])
    for j in range(4):
        tokens4[j] = tokens[:, 192 * j : 192 * j + 192]
    down = lax.broadcasted_iota(jnp.int32, (64, 64), 0)
    along = lax.broadcasted_iota(jnp.int32, (64, 64), 1)
    for s in range(3):
        mark = jnp.zeros((64, 64), F32)
        for i, ref in enumerate((segments, places)):
            row = lax.rem(ref[s : s + 1, :], MSPAN).astype(F32)
            column = jnp.sum(jnp.where(down == along, row, 0.0), axis=1, keepdims=True)
            mark = jnp.where(along == i, column, mark)
        marks[64 * s : 64 * s + 64] = mark.astype(BF16)
    table_grad[...] = jnp.zeros((3, TALL, TALL), F32)
    v0[...] = jnp.zeros((4, 16, 256), F32)
    e0[...] = jnp.zeros((16, 384), F32)

    forward_y(plan[2])
    for n in range(3):
        forward_x(plan[n])
    forward_y(plan[3])
    own_small.wait()
    for cp in smalls:
        cp.wait_recv()

    def vector(i):
        return jnp.concatenate([small[f, i : i + 1, 0:192] for f in range(4)], axis=1)

    arrive(plan[0])
    q = (dot_nn(tokens[...], wq[...]) + vector(0)).astype(BF16)
    arrive(plan[1])
    kk = dot_nn(tokens[...], wk[...]).astype(BF16)
    arrive(plan[2])
    v = (dot_nn(tokens[...], wv[...]) + vector(1)).astype(BF16)
    for j in range(4):
        cols = slice(192 * j, 192 * j + 192)
        main_send[j] = jnp.concatenate([q[:, cols], kk[:, cols], v[:, cols], marks[...]], axis=1)
        for s in range(3):
            extra_send[j, 16 * s : 16 * s + 16] = main_send[j, 64 * s : 64 * s + 16]
    heads_there = Exchange(main_send, main, extra_send, extra, ex[0], False)
    heads_there.start()
    forward_y(plan[4])
    forward_x(plan[3])
    forward_y(plan[5])
    heads_there.wait()
    arrive(plan[4])

    own, end = (slice(0, 256), slice(256, 272))

    def loop(first, count, body):
        def step(i, carry):
            body(first + i, i)
            return carry

        lax.fori_loop(0, count, step, 0)

    def first_document(s, _):
        lone = lax.broadcasted_iota(jnp.int32, (256, 16), 1) == 0
        lone_row = jnp.where(lax.broadcasted_iota(jnp.int32, (16, 1), 0) == 0, 1.0, 0.0)
        at = pl.ds(pl.multiple_of(16 * s, 16), 16)
        parts, ends = ([], [])
        for h in range(3):
            qo, ko, vo = [own_rows(main, s, lo + 64 * h, 64) for lo in (0, 192, 384)]
            qe, ke, ve = [extra[at, lo + 64 * h : lo + 64 * h + 64] for lo in (0, 192, 384)]
            bias = table[h, 0:TALL, 0:TALL].astype(F32)
            oo = dot_nt(qo, ko) * 0.125 + bias[own, own]
            oe = jnp.where(lone, dot_nt(qo, ke) * 0.125 + bias[own, end], NEGATIVE)
            eo = dot_nt(qe, ko) * 0.125 + bias[end, own]
            ee = jnp.where(lone[0:16], dot_nt(qe, ke) * 0.125 + bias[end, end], NEGATIVE)
            n = 3 * s + h
            for left, right, rows, valid, into, v_ends in (
                (oo, oe, own, 1.0, parts, None),
                (eo, ee, end, lone_row, ends, None),
            ):
                top = jnp.maximum(
                    jnp.max(left, axis=1, keepdims=True), jnp.max(right, axis=1, keepdims=True)
                )
                left, right = (jnp.exp(left - top), jnp.exp(right - top))
                share = valid / (
                    jnp.sum(left, axis=1, keepdims=True) + jnp.sum(right, axis=1, keepdims=True)
                )
                left, right = ((left * share).astype(BF16), (right * share).astype(BF16))
                probs[n, rows, own] = left
                probs[n, rows, end] = right
                into.append((dot_nn(left, vo) + dot_nn(right, ve)).astype(BF16))
        whole = jnp.concatenate(parts, axis=1)
        for j in range(4):
            ctx_send[j, pl.ds(64 * s, 64)] = whole[64 * j : 64 * j + 64]
        ctx_extra[at] = jnp.concatenate(ends, axis=1)

    def other_documents(s, _):
        slot_hot, same, valid = place_masks(main, s)
        parts = []
        for h in range(3):
            qo, ko, vo = [own_rows(main, s, lo + 64 * h, 64) for lo in (0, 192, 384)]
            picked = dot_nn(slot_hot, table[h, 0:256, 0:256]).astype(BF16)
            bias = dot_nt(picked, slot_hot)
            scores = jnp.where(same, dot_nt(qo, ko) * 0.125 + bias, NEGATIVE)
            top = jnp.max(scores, axis=1, keepdims=True)
            grown = jnp.exp(scores - top)
            share = valid / jnp.sum(grown, axis=1, keepdims=True)
            soft = (grown * share).astype(BF16)
            probs[3 * s + h, own, own] = soft
            parts.append(dot_nn(soft, vo).astype(BF16))
        whole = jnp.concatenate(parts, axis=1)
        for j in range(4):
            ctx_send[j, pl.ds(64 * s, 64)] = whole[64 * j : 64 * j + 64]

    def attend(first, count):
        @pl.when(group == 0)
        def _():
            loop(first, count, first_document)

        @pl.when(group == 1)
        def _():
            loop(first, count, other_documents)

    attend(0, 1)
    forward_y(plan[6])
    attend(1, 2)
    forward_x(plan[5])
    heads_back = Exchange(ctx_send, ctx4, ctx_extra, ctx_extra_in, ex[1], True)
    heads_back.start()
    forward_y(plan[7])
    def factor(hg, carry):
        part = pl.ds(3 * hg, 3)
        loads = [
            pltpu.make_async_copy(
                logits_in.at[part, :, near], slope.at[0:3, 0:128, 0:384], load.at[0]
            ),
            pltpu.make_async_copy(
                noise_in.at[part, :, near], slope.at[0:3, 0:128, 384:768], load.at[1]
            ),
        ]
        for cp in loads:
            cp.start()
        for cp in loads:
            cp.wait()
        for h in range(3):
            grown = jnp.exp(2.0 * (slope[h, 0:128, 0:384] + slope[h, 0:128, 384:768]))
            mask_sum[3 * hg + h, :, 0:384] = 2.0 / (1.0 + grown)
        return carry

    lax.fori_loop(0, 4, factor, 0)
    forward_y(plan[8])
    forward_y(plan[9])
    heads_back.wait()

    def join(into, side):
        @pl.when(c == 4)
        def _():
            for j in range(4):
                for s in range(3):
                    at = slice(64 * s, 64 * s + 16)
                    into[j, at] = into[j, at] + side[j, 16 * s : 16 * s + 16]

    join(ctx4, ctx_extra_in)

    def mean(value):
        return jnp.mean(value, axis=1, keepdims=True)

    def column_sum(value):
        return jnp.sum(value, axis=0, keepdims=True)

    def keep_vector(i, row):
        for owner in range(4):
            v0[owner, i : i + 1, 0:192] = row[:, 192 * owner : 192 * owner + 192]

    arrive(plan[3])
    context = jnp.concatenate([ctx4[j] for j in range(4)], axis=1)
    centered = tokens[...].astype(F32) + dot_nn(context, wo[...]) + vector(2)
    centered = centered - mean(centered)
    first_rate = lax.rsqrt(mean(centered * centered) + EPSILON)
    centered = centered * first_rate
    first_hat[...] = centered
    centered = centered * vector(3) + vector(4)
    first_norm[...] = centered
    first_low = centered.astype(BF16)
    for j in range(4):
        first4[j] = first_low[:, 192 * j : 192 * j + 192]
    forward_x(plan[6])
    forward_y(plan[10])
    arrive(plan[5])
    arrive(plan[6])

    def inner_product(j):
        bias = jnp.concatenate([small[j, 8 + i : 9 + i, 0:192] for i in range(4)], axis=1)
        at = 768 * j
        value = dot_nn(first_low, wi[:, at : at + 768]) + bias
        share = 0.5 + 0.5 * lax.erf(value * ROOT_HALF)
        low = (value * share).astype(BF16)
        active[j] = low
        for b in range(4):
            active16[4 * j + b] = low[:, 192 * b : 192 * b + 192]
        slope[j] = share + value * (jnp.exp(-0.5 * value * value) * ROOT_TWO_PI)

    for j in range(4):
        inner_product(j)
        if j == 1:
            forward_x(plan[7])
        if j == 2:
            forward_x(plan[8])
    forward_x(plan[9])
    forward_x(plan[10])
    for n in range(7, 11):
        arrive(plan[n])
    first_norm[...] += vector(5)

    centered = first_norm[...]
    for j in range(4):
        centered = centered + dot_nn(active[j], wf[768 * j : 768 * j + 768])
    centered = centered - mean(centered)
    rate = lax.rsqrt(mean(centered * centered) + EPSILON)
    hat = centered * rate
    hidden_low[...] = (hat * vector(6) + vector(7)).astype(BF16)
    outs = [pltpu.make_async_copy(hidden_low, hidden_out, load.at[2])]
    outs[0].start()

    above = upstream[...].astype(F32)
    keep_vector(6, column_sum(above * hat))
    keep_vector(7, column_sum(above))
    scaled = above * vector(6)
    grown_grad = rate * (scaled - mean(scaled) - hat * mean(scaled * hat))
    sum_grad[...] = grown_grad
    low_grad[...] = grown_grad.astype(BF16)
    keep_vector(5, column_sum(low_grad[...].astype(F32)))

    blocks = [(of, 192 * b, 0) for b in range(4)] + [(oi, 0, 768 * b) for b in range(4)]
    blocks += [(oh, 192 * b, 0) for b in range(4)]
    sums = BlockSums((st, r1, r2, r3, r4, total), sum_sems, blocks)

    def final_part(b):
        return lambda owner: dot_tn(active16[4 * owner + b], low_grad[...])

    def inter_part(b):
        return lambda owner: dot_tn(first4[owner], inner[b])

    def heads_part(b):
        return lambda owner: dot_tn(tokens4[owner], lows[b])

    def out_part(owner):
        return dot_tn(ctx4[owner], low_grad[...])

    def again(n):
        for yy in range(2):
            sums.to_core(n, yy).wait_send()

    def inner_back(j):
        at = pl.ds(pl.multiple_of(768 * j, 768), 768)
        value = dot_nt(low_grad[...], wf[at]).astype(BF16)
        inner[j] = (value.astype(F32) * slope[j]).astype(BF16)
        row = column_sum(inner[j].astype(F32))
        for i in range(4):
            v0[j, 8 + i : 9 + i, 0:192] = row[:, 192 * i : 192 * i + 192]
        sum_grad[...] += dot_nt(inner[j], wi[:, at])

    sums.one(0, final_part(0))

    def final_both(n, b):
        sums.one(n + 1, final_part(b + 1))
        sums.two(n, final_part(b))

    loop(0, 3, final_both)
    sums.two(3, final_part(3))
    loop(0, 4, lambda j, i: inner_back(j))

    def inter_one(n, b):
        again(n - 4)
        sums.one(n, inter_part(b))

    loop(4, 4, inter_one)
    sums.three(0)
    above = sum_grad[...]
    hat = first_hat[...]
    keep_vector(3, column_sum(above * hat))
    keep_vector(4, column_sum(above))
    scaled = above * vector(3)
    norm_grad = first_rate * (scaled - mean(scaled) - hat * mean(scaled * hat))
    sum_grad[...] = norm_grad
    low_grad[...] = norm_grad.astype(BF16)
    keep_vector(2, column_sum(low_grad[...].astype(F32)))
    context_grad = dot_nt(low_grad[...], wo[...]).astype(BF16)
    for j in range(4):
        grad4[j] = context_grad[:, 192 * j : 192 * j + 192]
        for s in range(3):
            grad_extra[j, 16 * s : 16 * s + 16] = grad4[j, 64 * s : 64 * s + 16]
    grads_there = Exchange(grad4, grad_in, grad_extra, grad_extra_in, ex[2], False)
    grads_there.start()
    loop(4, 3, lambda n, b: sums.two(n, inter_part(b)))
    sums.three(1)
    sums.four(0)
    grads_there.wait()

    def keep_heads(s, parts, into):
        blank = jnp.zeros((parts[0][0].shape[0], 64), BF16)
        into(jnp.concatenate(parts[0] + parts[1] + parts[2] + [blank], axis=1))

    def own_heads(s):
        def into(whole):
            for j in range(4):
                main_send[j, pl.ds(64 * s, 64)] = whole[64 * j : 64 * j + 64]

        return into

    def first_document_back(s, _):
        at = pl.ds(pl.multiple_of(16 * s, 16), 16)
        parts, ends = ([[], [], []], [[], [], []])
        for h in range(3):
            qo, ko, vo = [own_rows(main, s, lo + 64 * h, 64) for lo in (0, 192, 384)]
            qe, ke, ve = [extra[at, lo + 64 * h : lo + 64 * h + 64] for lo in (0, 192, 384)]
            go = own_rows(grad_in, s, 64 * h, 64)
            ge = grad_extra_in[at, 64 * h : 64 * h + 64]
            n = 3 * s + h
            moves = []
            for g, rows in ((go, own), (ge, end)):
                left, right = (probs[n, rows, own], probs[n, rows, end])
                wide_left, wide_right = (left.astype(F32), right.astype(F32))
                grad_left, grad_right = (dot_nt(g, vo), dot_nt(g, ve))
                delta = jnp.sum(wide_left * grad_left, axis=1, keepdims=True) + jnp.sum(
                    wide_right * grad_right, axis=1, keepdims=True
                )
                grad_left = (wide_left * (grad_left - delta)).astype(BF16)
                grad_right = (wide_right * (grad_right - delta)).astype(BF16)
                table_grad[h, rows, own] += grad_left.astype(F32)
                table_grad[h, rows, end] += grad_right.astype(F32)
                moves.append((left, right, grad_left, grad_right))
            (poo, poe, soo, soe), (peo, pee, seo, see) = moves
            parts[0].append(((dot_nn(soo, ko) + dot_nn(soe, ke)) * 0.125).astype(BF16))
            ends[0].append(((dot_nn(seo, ko) + dot_nn(see, ke)) * 0.125).astype(BF16))
            parts[1].append(((dot_tn(soo, qo) + dot_tn(seo, qe)) * 0.125).astype(BF16))
            ends[1].append(((dot_tn(soe, qo) + dot_tn(see, qe)) * 0.125).astype(BF16))
            parts[2].append((dot_tn(poo, go) + dot_tn(peo, ge)).astype(BF16))
            ends[2].append((dot_tn(poe, go) + dot_tn(pee, ge)).astype(BF16))
        keep_heads(s, parts, own_heads(s))

        def into(whole):
            extra_send[0, at] = whole

        keep_heads(s, ends, into)

    def other_documents_back(s, _):
        slot_hot, _, _ = place_masks(main, s)
        parts = [[], [], []]
        for h in range(3):
            qo, ko, vo = [own_rows(main, s, lo + 64 * h, 64) for lo in (0, 192, 384)]
            go = own_rows(grad_in, s, 64 * h, 64)
            soft = probs[3 * s + h, own, own]
            weight = soft.astype(F32)
            weight_grad = dot_nt(go, vo)
            delta = jnp.sum(weight * weight_grad, axis=1, keepdims=True)
            score_grad = (weight * (weight_grad - delta)).astype(BF16)
            parts[0].append((dot_nn(score_grad, ko) * 0.125).astype(BF16))
            parts[1].append((dot_tn(score_grad, qo) * 0.125).astype(BF16))
            parts[2].append(dot_tn(soft, go).astype(BF16))
            moved = dot_tn(slot_hot, score_grad)
            table_grad[h, own, own] += dot_nn(moved.astype(BF16), slot_hot)
        keep_heads(s, parts, own_heads(s))

    def attend_back(s):
        @pl.when(group == 0)
        def _():
            first_document_back(s, 0)

        @pl.when(group == 1)
        def _():
            other_documents_back(s, 0)

    heads_there.settle()
    attend_back(0)
    sums.three(2)
    sums.four(1)
    sums.five(0)
    loop(1, 2, lambda s, i: attend_back(s))
    grads_back = Exchange(main_send, main_in, extra_send.at[0], extra_in, ex[3], True)
    grads_back.start()
    w = {}

    def table_core():
        lane = lax.broadcasted_iota(jnp.int32, (8, TALL), 1)
        final = jnp.where(lane == 256, 1.0, 0.0).astype(BF16)
        for h in range(3):
            t0[h] = table_grad[h, 0:256, 0:256].astype(BF16)
            e0[h : h + 1, 0:TALL] = table_grad[h, 256:257, :]
            column = dot_nt(final, table_grad[h].astype(BF16))
            e0[8 + h : 9 + h, 0:TALL] = column[0:1]
        w["tcore"] = send(t0.at[:, pl.ds(128 * (1 - k), 128)], t1, pt.at[0], qt.at[0], core)
        w["tcore"].start()
        w["ecore"] = send(e0, e1, pe.at[0], qe.at[0], core)
        w["ecore"].start()

    def out_one():
        again(7)
        sums.one(11, out_part)

    def table_over_y():
        w["tcore"].wait_recv()
        for h in range(3):
            t1[h] = t0[h, pl.ds(pl.multiple_of(128 * k, 128), 128), :] + t1[h]
        w["table_y"] = send(t1.at[:, pl.ds(64 * (1 - y), 64)], t2, pt.at[1], qt.at[1], ynb)
        w["table_y"].start()
        w["ecore"].wait_recv()
        e1[...] = e0[...] + e1[...]
        w["edge_y"] = send(e1, e2, pe.at[1], qe.at[1], ynb)
        w["edge_y"].start()

    def late_two():
        sums.two(7, inter_part(3))
        sums.two(11, out_part)

    def heads_back_in():
        grads_back.wait()
        join(main_in, extra_in)
        for a in range(3):
            lows[a] = jnp.concatenate(
                [main_in[j, :, 192 * a : 192 * a + 192] for j in range(4)], axis=1
            )
        keep_vector(0, column_sum(lows[0].astype(F32)))
        keep_vector(1, column_sum(lows[2].astype(F32)))
        for yy in range(2):
            cp = send(v0.at[2 * yy + 1 - k], v1.at[yy], ps.at[yy], qs.at[yy], core)
            cp.start()
            w["small_core", yy] = cp

    def heads_sums():
        def heads_one(n, b):
            again(n - 4)
            sums.one(n, heads_part(b))

        loop(8, 3, heads_one)
        for yy in range(2):
            w["small_core", yy].wait_recv()
            v1[yy] = v0[2 * yy + k] + v1[yy]
        w["small_y"] = send(v1.at[1 - y], v2, ps.at[2], qs.at[2], ynb)
        w["small_y"].start()
        loop(8, 3, lambda n, b: sums.two(n, heads_part(b)))

    def inputs_grad():
        input_sum[...] = sum_grad[...] + dot_nt(lows[0], wq[...])
        input_sum[...] += dot_nt(lows[1], wk[...])
        input_sum[...] += dot_nt(lows[2], wv[...])
        outs.append(pltpu.make_async_copy(input_sum, input_grad, load.at[3]))
        outs[1].start()

    def table_to_twin():
        w["edge_y"].wait_recv()
        e2[...] = e1[...] + e2[...]
        w["edge_x"] = send(e2, e3, pe.at[2], qe.at[2], twin)
        w["edge_x"].start()
        w["table_y"].wait_recv()
        for h in range(3):
            t2[h] = t1[h, pl.ds(pl.multiple_of(64 * y, 64), 64), :] + t2[h]
        w["table_x"] = send(t2.at[:, pl.ds(32 * (1 - group), 32)], t3, pt.at[2], qt.at[2], twin)
        w["table_x"].start()

    me = lax.rem(c, 4)

    def table_piece(hg, side):
        return table_out.at[hg, :, pl.ds(64 * y + 32 * side, 32)]

    def table_spread():
        w["edge_x"].wait_recv()
        edge_out[c] = e2[...] + e3[...]
        here = edge_out.at[c]
        for i in range(3):
            w["edge_z", i] = send(here, here, pe.at[3 + i], qe.at[3 + z], zdev[i])
        w["edge_z", 3] = send(here, here, pe.at[6], qe.at[7 + z], xnb)
        w["table_x"].wait_recv()
        at = pl.ds(pl.multiple_of(32 * group, 32), 32)
        to = pl.ds(pl.multiple_of(64 * y + 32 * group, 32), 32)
        for h in range(3):
            table_out[me, h, to, :] = t2[h, at, :] + t3[h]
        here = table_piece(me, group)
        for i in range(3):
            w["table_z", i] = send(here, here, pt.at[3 + i], qt.at[3 + z], zdev[i])
        w["table_z", 3] = send(here, here, pt.at[6], qt.at[7 + z], xnb)
        for i in range(4):
            w["edge_z", i].start()
            w["table_z", i].start()

    def table_over_x():
        for i in (1, 2, 3):
            zz = lax.rem(z + i, 4)
            cc = 2 * zz + x
            there = edge_out.at[cc]
            send(there, there, pe.at[3], qe.at[3 + zz], core).wait_recv()
            w["edge_z", 3 + i] = send(there, there, pe.at[6 + i], qe.at[7 + zz], xnb)
            w["edge_z", 3 + i].start()
            there = table_piece(lax.rem(cc, 4), cc // 4)
            send(there, there, pt.at[3], qt.at[3 + zz], core).wait_recv()
            w["table_z", 3 + i] = send(there, there, pt.at[6 + i], qt.at[7 + zz], xnb)
            w["table_z", 3 + i].start()

    half_table = table_out.at[:, :, pl.ds(64, 64)]
    half_copy = send(half_table, half_table, pt.at[10], qt.at[11], ynb)

    def table_half():
        for zz in range(4):
            cc = 2 * zz + 1 - x
            there = table_piece(lax.rem(cc, 4), cc // 4)
            send(there, there, pt.at[6], qt.at[7 + zz], xnb).wait_recv()
            there = edge_out.at[cc]
            send(there, there, pe.at[6], qe.at[7 + zz], xnb).wait_recv()

        @pl.when(y == 1)
        def _():
            half_copy.start()

    def small_over_x():
        w["small_y"].wait_recv()
        v2[...] = v1[y] + v2[...]
        w["small_x"] = send(v2, v3, ps.at[3], qs.at[3], xnb)
        w["small_x"].start()

    def small_over_z():
        w["small_x"].wait_recv()
        v4[z] = v2[...] + v3[...]
        for i in range(3):
            w["small_z", i] = send(v4.at[z], v4.at[z], ps.at[4 + i], qs.at[4 + z], zdev[i])
            w["small_z", i].start()

    def small_end():
        for i in (1, 2, 3):
            zz = lax.rem(z + i, 4)
            send(v4.at[zz], v4.at[zz], ps.at[4], qs.at[4 + zz], core).wait_recv()
        small_out[...] = (v4[0] + v4[1]) + (v4[2] + v4[3])

    def mask_end():
        @pl.when(y == 0)
        def _():
            half_copy.wait_recv()
            deep = lax.broadcasted_iota(jnp.int32, (128, 128), 0)
            across = lax.broadcasted_iota(jnp.int32, (128, 128), 1)

            def fill(hg, carry):
                for h in range(3):
                    row = edge_out[hg, 8 + h : 9 + h, :]
                    row = jnp.where(k == 0, row[:, 0:128], row[:, 128:256])
                    column = jnp.sum(jnp.where(deep == across, row, 0.0), axis=1, keepdims=True)
                    n = 3 * hg + h
                    mask_sum[n, :, 0:256] = mask_sum[n, :, 0:256] * table_out[hg, h].astype(F32)
                    mask_sum[n, :, 256:384] = mask_sum[n, :, 256:384] * jnp.where(
                        across == 0, column, 0.0
                    )
                return carry

            lax.fori_loop(0, 4, fill, 0)

        @pl.when(y == 1)
        def _():
            top = lax.broadcasted_iota(jnp.int32, (8, 384), 0)

            def fill(hg, carry):
                for h in range(3):
                    n = 3 * hg + h
                    first = mask_sum[n, 0:8, 0:384] * edge_out[hg, h : h + 1, :]
                    mask_sum[n] = jnp.zeros((128, 384), F32)
                    mask_sum[n, 0:8, 0:384] = jnp.where((top == 0) & (k == 0), first, 0.0)
                return carry

            lax.fori_loop(0, 4, fill, 0)

        outs.append(pltpu.make_async_copy(mask_sum, mask_out, load.at[4]))
        outs[2].start()

    steps = [
        ("three", 3), ("four", 2), ("five", 1), ("six", 0), table_core, out_one, table_over_y,
        late_two, ("three", 4), ("five", 2), ("six", 1), ("four", 3), heads_back_in,
        ("three", 5), ("four", 4), ("five", 3), ("six", 2), heads_sums, ("three", 6),
        ("four", 5), table_to_twin, ("five", 4), ("six", 3), inputs_grad, ("three", 7),
        ("four", 6), ("five", 5), ("three", 11), ("four", 7), table_spread, ("six", 4),
        ("five", 6), small_over_x, ("three", 8), ("four", 11), ("six", 5), ("five", 7),
        small_over_z, ("three", 9), ("four", 8), ("six", 6), ("five", 11), ("three", 10),
        ("four", 9), ("six", 7), table_over_x, ("five", 8), ("four", 10), ("six", 11),
        ("five", 9), ("six", 8), table_half, ("five", 10), small_end, ("six", 9), ("six", 10),
        mask_end,
    ]
    for step in steps:
        if isinstance(step, tuple):
            getattr(sums, step[0])(step[1])
        else:
            step()
    for n in (0, 1, 2, 3, 4, 5, 6, 7, 11, 8, 9, 10):
        sums.seven(n)
    for cp in outs:
        cp.wait()

    @pl.when(y == 1)
    def _():
        half_copy.wait_send()

    for cp in w.values():
        cp.wait_send()
    for exchange in (heads_back, grads_there, grads_back):
        exchange.settle()
    for copies in plan:
        settle(copies)
    for cp in smalls:
        cp.wait_send()
    sums.settle()


def layer(tokens, segments, places, upstream, vectors, arrays, logits, noise):
    dma = pltpu.SemaphoreType.DMA
    count = len(gather_pieces())

    def low(*shape):
        return pltpu.VMEM(shape, BF16)

    def wide(*shape):
        return pltpu.VMEM(shape, F32)

    scratch = [low(a.shape[0] * 4, a.shape[1]) for a in arrays]
    scratch += [low(3, 512, 384), wide(4, 16, 256)]
    scratch += [
        low(4, ROWS, 640), low(48, 640), low(4, ROWS, 640), low(4, 48, 640),
        low(9, TALL, TALL),
        low(4, ROWS, 192), low(48, 192), low(4, ROWS, 192), low(4, 48, 192),
    ]
    scratch += [
        wide(16, 256), low(ROWS, 64), low(4, ROWS, 768), low(3, 128, 384), low(4, ROWS, 192),
        wide(ROWS, 768), wide(ROWS, 768), low(4, ROWS, 192),
        low(16, ROWS, 192), wide(4, ROWS, 768), low(4, ROWS, 768), wide(ROWS, 768), low(ROWS, 768),
    ]
    scratch += [
        low(4, ROWS, 192), low(4, 48, 192), low(4, ROWS, 192), low(48, 192),
        low(4, ROWS, 640), low(4, 48, 640), wide(3, TALL, TALL), low(3, ROWS, 768),
    ]
    scratch += [wide(4, 16, 256), wide(2, 16, 256), wide(16, 256), wide(16, 256), wide(4, 16, 256)]
    scratch += [low(3, 256, 256), low(3, 128, 256), low(3, 64, 256), low(3, 32, 256)]
    scratch += [wide(16, 384)] * 4 + [low(4, 3, 128, 256), wide(8, 16, 384)]
    scratch += [
        low(4, 2, 192, 768), low(12, 2, 192, 768), low(12, 192, 768), low(12, 192, 384),
        low(12, 4, 48, 384), low(12, 48, 384),
        low(ROWS, 768), wide(ROWS, 768), wide(12, 128, 384),
    ]
    sems = [dma((count, 5)), dma((count, 5)), dma((count + 1,)), dma((3,)), dma((3,))]
    for _ in range(4):
        sems += exchange_sems()
    sems += [
        dma((12, 2)), dma((12, 2)), dma((12,)), dma((12,)), dma((12,)), dma((12,)),
        dma((12, 3)), dma((12, 4)), dma((12, 3)), dma((12, 4)), dma((12,)), dma((12,)), dma((12,)),
    ]
    sems += [dma((8,)), dma((8,)), dma((12,)), dma((12,)), dma((12,)), dma((12,)), dma((5,))]
    return pl.pallas_call(
        layer_kernel,
        out_shape=[
            jax.ShapeDtypeStruct((ROWS, 768), BF16),
            jax.ShapeDtypeStruct((ROWS, 768), F32),
        ]
        + [
            jax.ShapeDtypeStruct((768, 768), BF16),
            jax.ShapeDtypeStruct((192, 3072), BF16),
            jax.ShapeDtypeStruct((768, 768), BF16),
            jax.ShapeDtypeStruct((16, 256), F32),
            jax.ShapeDtypeStruct((12, 128, 384), F32),
        ],
        in_specs=[vmem_spec()] * 13 + [any_spec()] * 8,
        out_specs=[any_spec()] * 5 + [vmem_spec(), any_spec()],
        scratch_shapes=scratch + sems,
        compiler_params=pltpu.CompilerParams(
            collective_id=1, has_side_effects=True, vmem_limit_bytes=62 * 2**20
        ),
        name="layer",
    )(tokens, segments, places, upstream, *vectors, *arrays, logits, noise)


def write_kernel(
    hidden, grad, mask, oh, oi, of, small,
    hidden_out, grad_out, mask_out, wq, wk, wv, wo, wi, wf, bi, *rest
):
    vectors, (vh, vg, vm, bh, bb, bf, fh, fi, ff, load, store) = (rest[:8], rest[8:])
    reads = [
        pltpu.make_async_copy(src, dst, load.at[i])
        for i, (src, dst) in enumerate(
            (
                (of, bf), (oi, bb), (oh, bh),
                (mask, vm.at[:, :, 0:384]), (grad, vg), (hidden, vh),
            )
        )
    ]
    for cp in reads:
        cp.start()
    writes = []

    def write(src, dst):
        cp = pltpu.make_async_copy(src, dst, store.at[len(writes)])
        cp.start()
        writes.append(cp)

    vm[:, :, 384:512] = jnp.zeros((12, 128, 128), F32)

    def widen(into, ref, first):
        def body(i, carry):
            at = pl.ds(pl.multiple_of(first + 32 * i, 32), 32)
            into[at, :] = ref[at, :].astype(F32)
            return carry

        lax.fori_loop(0, 6, body, 0)

    reads[0].wait()
    for i in range(4):
        widen(ff, bf, 192 * i)
        rows = pl.ds(192 * i, 192)
        write(ff.at[rows], wf.at[rows])
    reads[1].wait()
    widen(fi, bb, 0)
    write(fi, wi)
    reads[3].wait()
    write(vm, mask_out)
    reads[2].wait()
    for i, ref in enumerate((wq, wk, wv, wo)):
        widen(fh, bh, 192 * i)
        write(fh.at[pl.ds(192 * i, 192)], ref)
    reads[4].wait()
    write(vg, grad_out)
    reads[5].wait()
    write(vh, hidden_out)
    for i in range(8):
        vectors[i][...] = small[i : i + 1, 0:192].reshape(192)
    for i in range(4):
        bi[192 * i : 192 * i + 192] = small[8 + i : 9 + i, 0:192].reshape(192)
    for cp in writes:
        cp.wait()


def write_outputs(hidden, grad, mask, oh, oi, of, small):
    def out(shape, kind=F32):
        return jax.ShapeDtypeStruct(shape, kind)

    dma = pltpu.SemaphoreType.DMA
    return pl.pallas_call(
        write_kernel,
        out_shape=[
            out((ROWS, 768), BF16), out((ROWS, 768)), out((12, 128, 512)),
            out((192, 768)), out((192, 768)), out((192, 768)), out((192, 768)),
            out((192, 3072)), out((768, 768)), out((768,)),
        ]
        + [out((192,))] * 8,
        in_specs=[any_spec()] * 6 + [vmem_spec()],
        out_specs=[any_spec()] * 9 + [vmem_spec()] * 9,
        scratch_shapes=[
            pltpu.VMEM((ROWS, 768), BF16), pltpu.VMEM((ROWS, 768), F32),
            pltpu.VMEM((12, 128, 512), F32),
            pltpu.VMEM((768, 768), BF16), pltpu.VMEM((192, 3072), BF16),
            pltpu.VMEM((768, 768), BF16),
            pltpu.VMEM((768, 768), F32), pltpu.VMEM((192, 3072), F32),
            pltpu.VMEM((768, 768), F32),
            dma((6,)), dma((12,)),
        ],
        compiler_params=pltpu.CompilerParams(vmem_limit_bytes=62 * 2**20),
        name="write_outputs",
    )(hidden, grad, mask, oh, oi, of, small)


def block_device(
    hidden_in, segment_ids, doc_positions,
    w_query, w_key, w_value, w_out, b_query, b_value, b_out, ln1_gain, ln1_shift,
    w_inter, b_inter, w_final, b_final, ln2_gain, ln2_shift,
    mask_logits, mask_noise, grad_out,
):
    vectors = (
        b_query, b_value, b_out, ln1_gain, ln1_shift, b_final, ln2_gain, ln2_shift, b_inter
    )
    result, input_grad, oh, oi, of, small_sum, logit_grad = layer(
        hidden_in.reshape(ROWS, 768),
        segment_ids,
        doc_positions,
        grad_out.reshape(ROWS, 768),
        vectors,
        (w_query, w_key, w_value, w_out, w_inter, w_final),
        mask_logits,
        mask_noise,
    )
    hidden_out, grad_in, mask_grad, wq, wk, wv, wo, wi, wf, bi, *vecs = write_outputs(
        result, input_grad, logit_grad, oh, oi, of, small_sum
    )
    return (
        hidden_out.reshape(hidden_in.shape),
        grad_in.reshape(hidden_in.shape),
        wq,
        wk,
        wv,
        wo,
        vecs[0],
        vecs[1],
        vecs[2],
        vecs[3],
        vecs[4],
        wi,
        bi,
        wf,
        vecs[5],
        vecs[6],
        vecs[7],
        mask_grad,
    )


def on_device(ctx_size, fsdp_size, hidden_in, *rest):
    if (ctx_size, fsdp_size, hidden_in.shape) == (8, 4, (3, 64, 768)):
        return block_device(hidden_in, *rest)
    return general_device(hidden_in, *rest)


def solution(mesh):
    in_specs = (
        P("fsdp", "ctx", None),
        P("fsdp", "ctx"),
        P("fsdp", "ctx"),
        P("fsdp", None),
        P("fsdp", None),
        P("fsdp", None),
        P("fsdp", None),
        P("fsdp"),
        P("fsdp"),
        P("fsdp"),
        P("fsdp"),
        P("fsdp"),
        P("fsdp", None),
        P("fsdp"),
        P("fsdp", None),
        P("fsdp"),
        P("fsdp"),
        P("fsdp"),
        P(None, "fsdp", None),
        P(None, "fsdp", None),
        P("fsdp", "ctx", None),
    )
    out_specs = (
        P("fsdp", "ctx", None),
        P("fsdp", "ctx", None),
        P("fsdp", None),
        P("fsdp", None),
        P("fsdp", None),
        P("fsdp", None),
        P("fsdp"),
        P("fsdp"),
        P("fsdp"),
        P("fsdp"),
        P("fsdp"),
        P("fsdp", None),
        P("fsdp"),
        P("fsdp", None),
        P("fsdp"),
        P("fsdp"),
        P("fsdp"),
        P(None, "fsdp", None),
    )
    return jax.shard_map(
        functools.partial(on_device, mesh.shape["ctx"], mesh.shape["fsdp"]), mesh=mesh, in_specs=in_specs, out_specs=out_specs, check_vma=False
    )
```
